32 devices in a mesh: ctx: 8 (over y, x, core), fsdp: 4 (over z).
Axes of the slice: x: 2, y: 2, z: 4, core: 2. Of those that a mesh axis runs over, the one named last changes fastest.
Arguments:
- block_input: bfloat16 [4, 2048, 1024], P('fsdp', 'ctx'), may hold values from -6 to 6
- doc_starts: int32 [4, 4], P('fsdp'), may hold values from 0 to 2047, as said below
- out_grad: bfloat16 [4, 2048, 1024], P('fsdp', 'ctx'), may hold values from -6 to 6
- query_weight: bfloat16 [1024, 1024], P('fsdp'), may hold values from -0.1875 to 0.1875
- key_weight: bfloat16 [1024, 512], P('fsdp'), may hold values from -0.1875 to 0.1875
- value_weight: bfloat16 [1024, 512], P('fsdp'), may hold values from -0.1875 to 0.1875
- output_weight: bfloat16 [1024, 1024], P('fsdp'), may hold values from -1.5 to 1.5
- gate_weight: bfloat16 [1024, 4608], P('fsdp'), may hold values from -0.1875 to 0.1875
- up_weight: bfloat16 [1024, 4608], P('fsdp'), may hold values from -0.1875 to 0.1875
- down_weight: bfloat16 [4608, 1024], P('fsdp'), may hold values from -0.09375 to 0.09375
- mixer_gain: bfloat16 [1024], P('fsdp'), may hold values from 0.25 to 1.75
- feed_gain: bfloat16 [1024], P('fsdp'), may hold values from 0.25 to 1.75
- query_gain: bfloat16 [64], P('fsdp'), may hold values from 0.25 to 1.75
- key_gain: bfloat16 [64], P('fsdp'), may hold values from 0.25 to 1.75
Outputs:
- block_output: bfloat16 [4, 2048, 1024], P('fsdp', 'ctx')
- input_grad: float32 [4, 2048, 1024], P('fsdp', 'ctx')
- grad_query: float32 [1024, 1024], P('fsdp')
- grad_key: float32 [1024, 512], P('fsdp')
- grad_value: float32 [1024, 512], P('fsdp')
- grad_proj: float32 [1024, 1024], P('fsdp')
- grad_gate: float32 [1024, 4608], P('fsdp')
- grad_up: float32 [1024, 4608], P('fsdp')
- grad_down: float32 [4608, 1024], P('fsdp')
- grad_mixer: float32 [1024], P('fsdp')
- grad_feed: float32 [1024], P('fsdp')
- grad_qgain: float32 [64], P('fsdp')
- grad_kgain: float32 [64], P('fsdp')
The draws below stay inside these ranges and needn't reach their ends.
Inputs may be any that keep to these rules, and one draw needn't show every extreme that they name: `doc_starts`: in each stream the starts begin at 0 and rise; every document (to the next start or the stream's end) has 1 to 1024 positions, and one has exactly 1024.
All inputs are finite; a program needn't handle non-finite values.
Results may differ from the reference program's by a relative error of at most 0.035.
Values may be sent and summed in bfloat16 or wider, within the bound.
No kernel may reach another device: no remote copies, remote signals or barrier semaphores. Data moves between devices by JAX's collectives and lax.ppermute only.
A program may use at most 256 MiB of HBM per device.

```python
import math
import jax
import jax.numpy as jnp
from jax import lax

D = 1024
H = 16
KVH = 8
HD = 64
FF = 4608
TOK_DEV = 256
STREAMS = 4
STREAM = 2048
DOC_MOST = 1024
NDOC = 4
N_CTX = 8


def draw_doc_starts(key, part):
    others_count = NDOC - 1
    remain = STREAM - DOC_MOST
    jitter = max(remain // (2 * others_count) - 1, 0)

    def one_stream(stream_key):
        cut_key, slot_key = jax.random.split(stream_key)
        markers = jnp.arange(1, others_count, dtype=jnp.int32)
        cut_points = markers * remain // others_count + jax.random.randint(cut_key, (others_count - 1,), -jitter, jitter + 1, dtype=jnp.int32)
        bounds = jnp.concatenate([jnp.zeros((1,), jnp.int32), cut_points, jnp.full((1,), remain, jnp.int32)])
        others = bounds[1:] - bounds[:-1]
        long_slot = jax.random.randint(slot_key, (), 0, NDOC, dtype=jnp.int32)
        places = jnp.arange(NDOC, dtype=jnp.int32)
        source = jnp.clip(places - (places > long_slot).astype(jnp.int32), 0, others_count - 1)
        lengths = jnp.where(places == long_slot, jnp.int32(DOC_MOST), others[source]).astype(jnp.int32)
        return (jnp.cumsum(lengths, dtype=jnp.int32) - lengths).astype(jnp.int32)
    return jax.vmap(one_stream)(jax.random.split(key, STREAMS))


def shard_levels(key, dims, shards, low, high):
    gain, own = 1.0, jax.random.fold_in(key, 6)
    for dim, shards_of in shards:
        heights = jnp.exp(jax.random.uniform(jax.random.fold_in(own, dim), (shards_of,), jnp.float32, low / len(shards), high / len(shards)))
        gain = gain * jnp.repeat(heights, dims[dim] // shards_of).reshape([-1 if axis == dim else 1 for axis in range(len(dims))])
    return gain


def bell_draw(own_key, extent, deviation, bound, shards=(), kind=jnp.bfloat16):
    values = deviation * jax.random.normal(own_key, extent, jnp.float32)
    if shards:
        values = values * shard_levels(own_key, extent, shards, -0.22, 0.18)
    return jnp.clip(values, -bound, bound).astype(kind)


def setup_inputs(seed: int = 0) -> dict:
    key_of = jax.random.split(jax.random.key(seed), 15)
    return {
        "block_input": bell_draw(key_of[0], (STREAMS, STREAM, D), 1.0, 6.0, ((0, 4), (1, 8))),
        "doc_starts": draw_doc_starts(jax.random.fold_in(key_of[14], 71), 0),
        "out_grad": bell_draw(key_of[2], (STREAMS, STREAM, D), 1.0, 6.0, ((0, 4), (1, 8))),
        "query_weight": bell_draw(key_of[3], (D, H * HD), D ** -0.5, 0.1875, ((0, 4),)),
        "key_weight": bell_draw(key_of[4], (D, KVH * HD), D ** -0.5, 0.1875, ((0, 4),)),
        "value_weight": bell_draw(key_of[5], (D, KVH * HD), D ** -0.5, 0.1875, ((0, 4),)),
        "output_weight": bell_draw(key_of[6], (H * HD, D), (D // 64) ** -0.5, 1.5, ((0, 4),)),
        "gate_weight": bell_draw(key_of[7], (D, FF), D ** -0.5, 0.1875, ((0, 4),)),
        "up_weight": bell_draw(key_of[8], (D, FF), D ** -0.5, 0.1875, ((0, 4),)),
        "down_weight": bell_draw(key_of[9], (FF, D), FF ** -0.5, 0.09375, ((0, 4),)),
        "mixer_gain": jnp.clip(1.0 + 0.15 * jax.random.normal(key_of[10], (D,), jnp.float32), 0.25, 1.75).astype(jnp.bfloat16),
        "feed_gain": jnp.clip(1.0 + 0.15 * jax.random.normal(key_of[11], (D,), jnp.float32), 0.25, 1.75).astype(jnp.bfloat16),
        "query_gain": jnp.clip(1.0 + 0.15 * jax.random.normal(key_of[12], (HD,), jnp.float32), 0.25, 1.75).astype(jnp.bfloat16),
        "key_gain": jnp.clip(1.0 + 0.15 * jax.random.normal(key_of[13], (HD,), jnp.float32), 0.25, 1.75).astype(jnp.bfloat16),
    }


EPSILON = 1e-05
ROPE_BASE = 1000000.0
FLOOR_SCORE = -1e+30
HIGHEST = lax.Precision.HIGHEST

@jax.custom_vjp
def low(v):
    return lax.optimization_barrier(v.astype(jnp.bfloat16)).astype(jnp.float32)

@jax.custom_vjp
def low_back(v):
    return v

def low_keep(v):
    return (low(v), None)

def low_pass(kept, grad):
    return (grad,)

def back_keep(v):
    return (v, None)

def back_low(kept, grad):
    return (low(grad),)
low.defvjp(low_keep, low_pass)
low_back.defvjp(back_keep, back_low)

def matmul_high(left, right):
    return jnp.dot(left, right, precision=HIGHEST, preferred_element_type=jnp.float32)

def place_rows(row_index):
    half_rows = TOK_DEV // 2
    device = row_index // TOK_DEV
    offset = row_index % TOK_DEV
    early = device * half_rows + offset
    late = (2 * N_CTX - 1 - device) * half_rows + offset - half_rows
    return jnp.where(offset < half_rows, early, late).astype(jnp.int32)

def rows_of(places):
    half_rows = TOK_DEV // 2
    piece = places // half_rows
    offset = places % half_rows
    device = jnp.where(piece < N_CTX, piece, 2 * N_CTX - 1 - piece)
    return (device * TOK_DEV + jnp.where(piece < N_CTX, offset, half_rows + offset)).astype(jnp.int32)

def doc_begin(starts, where_at):
    started = starts[None, :] <= where_at[:, None]
    return lax.optimization_barrier(jnp.max(jnp.where(started, starts[None, :], 0), axis=1)).astype(jnp.int32)

def rotary(positions):
    half_dim = HD // 2
    frequency = ROPE_BASE ** (-(2.0 * jnp.arange(half_dim, dtype=jnp.float32)) / HD)
    angles = positions.astype(jnp.float32)[:, None] * frequency[None, :]
    angles = jnp.concatenate([angles, angles], axis=1)
    return (jnp.cos(angles)[:, None, :], jnp.sin(angles)[:, None, :])

def rotate_pairs(values, cosine, sine_part):
    half_dim = values.shape[-1] // 2
    rolled = jnp.concatenate([-values[..., half_dim:], values[..., :half_dim]], axis=-1)
    return values * cosine + rolled * sine_part

def row_norm(values, gain_row):
    scaling = lax.rsqrt(lax.optimization_barrier(jnp.mean(values * values, axis=-1, keepdims=True)) + EPSILON)
    return values * scaling * gain_row

def attention(query_att, key_att, value_att, where_at, begins):
    block = math.gcd(STREAM, 512)
    span = DOC_MOST + block
    repeat = H // KVH
    scaling = HD ** (-0.5)
    pad_rows = jnp.zeros((DOC_MOST, KVH * HD), jnp.float32)
    keys_pad = jnp.concatenate([pad_rows, key_att], axis=0)
    values_pad = jnp.concatenate([pad_rows, value_att], axis=0)
    at_pad = jnp.concatenate([jnp.full((DOC_MOST,), -1, jnp.int32), where_at.astype(jnp.int32)])
    begin_pad = jnp.concatenate([jnp.full((DOC_MOST,), -1, jnp.int32), begins.astype(jnp.int32)])

    def query_block(index):
        first = (index * block).astype(jnp.int32)
        query_rows = lax.dynamic_slice_in_dim(query_att, first, block, 0).reshape(block, KVH, repeat, HD)
        key_rows = lax.dynamic_slice_in_dim(keys_pad, first, span, 0).reshape(span, KVH, HD)
        value_rows = lax.dynamic_slice_in_dim(values_pad, first, span, 0).reshape(span, KVH, HD)
        query_at = lax.dynamic_slice_in_dim(where_at.astype(jnp.int32), first, block, 0)
        query_doc = lax.dynamic_slice_in_dim(begins.astype(jnp.int32), first, block, 0)
        key_at = lax.dynamic_slice_in_dim(at_pad, first, span, 0)
        key_doc = lax.dynamic_slice_in_dim(begin_pad, first, span, 0)
        visible = (query_doc[:, None] == key_doc[None, :]) & (key_at[None, :] <= query_at[:, None])
        scores = low_back(jnp.einsum('igrd,jgd->grij', query_rows, key_rows, precision=HIGHEST) * scaling)
        scores = jnp.where(visible, scores, FLOOR_SCORE)
        probs = low(jax.nn.softmax(scores, axis=-1))
        mixed_rows = jnp.einsum('grij,jgd->igrd', probs, value_rows, precision=HIGHEST)
        return mixed_rows.reshape(block, H * HD)
    blocks = lax.map(jax.checkpoint(query_block), jnp.arange(STREAM // block, dtype=jnp.int32))
    return blocks.reshape(STREAM, H * HD)

def whole_layer(inputs, where_at, begins, w_query, w_key, w_value, w_output, w_gate, w_up, w_down, gain_mixer, gain_feed, gain_query, gain_key):
    cosine, sine_part = rotary(where_at - begins)
    hidden_in = low(row_norm(inputs, gain_mixer))
    query_lin = low_back(matmul_high(hidden_in, w_query))
    key_lin = low_back(matmul_high(hidden_in, w_key))
    value_lin = low_back(matmul_high(hidden_in, w_value))
    query_att = low(rotate_pairs(row_norm(query_lin.reshape(STREAM, H, HD), gain_query), cosine, sine_part).reshape(STREAM, H * HD))
    key_att = low(rotate_pairs(row_norm(key_lin.reshape(STREAM, KVH, HD), gain_key), cosine, sine_part).reshape(STREAM, KVH * HD))
    value_att = low(value_lin)
    attn_low = low(low_back(attention(query_att, key_att, value_att, where_at, begins)))
    mixed = inputs + low_back(matmul_high(attn_low, w_output))
    hidden_mid = low(row_norm(mixed, gain_feed))
    gate_lin = low_back(matmul_high(hidden_mid, w_gate))
    up_lin = low_back(matmul_high(hidden_mid, w_up))
    activated = low(jax.nn.silu(gate_lin) * up_lin)
    return mixed + low_back(matmul_high(activated, w_down))

def reference(block_input, doc_starts, out_grad, query_weight, key_weight, value_weight, output_weight, gate_weight, up_weight, down_weight, mixer_gain, feed_gain, query_gain, key_gain):
    params = tuple((entry.astype(jnp.float32) for entry in (query_weight, key_weight, value_weight, output_weight, gate_weight, up_weight, down_weight, mixer_gain, feed_gain, query_gain, key_gain)))
    outputs = []
    input_grads = []
    totals = None
    where_at = jnp.arange(STREAM, dtype=jnp.int32)
    order_rows = rows_of(where_at)
    back_rows = place_rows(where_at)
    for stream in range(STREAMS):
        begins = doc_begin(doc_starts[stream].astype(jnp.int32), where_at)
        inputs = block_input[stream].astype(jnp.float32)[order_rows]
        result, pull = jax.vjp(lambda values, *weights: whole_layer(values, where_at, begins, *weights), inputs, *params)
        grads = pull(out_grad[stream].astype(jnp.float32)[order_rows])
        outputs.append(result[back_rows].astype(jnp.bfloat16))
        input_grads.append(grads[0][back_rows])
        if totals is None:
            totals = tuple(grads[1:])
        else:
            totals = tuple((first + second for first, second in zip(totals, grads[1:])))
    return (jnp.stack(outputs), jnp.stack(input_grads), totals[0], totals[1], totals[2], totals[3], totals[4], totals[5], totals[6], totals[7], totals[8], totals[9], totals[10])
```

```python
import functools
import math

import jax
import jax.numpy as jnp
from jax import lax
from jax.experimental import pallas as pl
from jax.experimental.pallas import tpu as pltpu
from jax.sharding import PartitionSpec as P

H = 16
KVH = 8
HD = 64


EPSILON = 1e-05
ROPE_BASE = 1000000.0
FLOOR_SCORE = -1e30


def place_rows(row_index, tokens, ctx_count):
    half_rows = tokens // 2
    device = row_index // tokens
    offset = row_index % tokens
    early = device * half_rows + offset
    late = (2 * ctx_count - 1 - device) * half_rows + offset - half_rows
    return jnp.where(offset < half_rows, early, late)


def doc_begin(starts, where_at):
    started = starts[None, :] <= where_at[:, None]
    return jnp.max(jnp.where(started, starts[None, :], 0), axis=1)


def rotary(positions):
    half_dim = HD // 2
    frequency = ROPE_BASE ** (-(2.0 * jnp.arange(half_dim, dtype=jnp.float32)) / HD)
    angles = positions.astype(jnp.float32)[:, None] * frequency[None, :]
    angles = jnp.concatenate([angles, angles], axis=1)
    return (jnp.cos(angles)[:, None, :], jnp.sin(angles)[:, None, :])


def rotate_pairs(values, cosine, sine_part):
    half_dim = values.shape[-1] // 2
    rolled = jnp.concatenate([-values[..., half_dim:], values[..., :half_dim]], axis=-1)
    return values * cosine + rolled * sine_part


def rotate_back(grads, cosine, sine_part):
    half_dim = grads.shape[-1] // 2
    moved = grads * sine_part
    rolled = jnp.concatenate([moved[..., half_dim:], -moved[..., :half_dim]], axis=-1)
    return grads * cosine + rolled


def unit_norm(values):
    scaling = lax.rsqrt(jnp.mean(values * values, axis=-1, keepdims=True) + EPSILON)
    return (values * scaling, scaling)


def norm_back(grad_out, normed, scaling, gain_row):
    weighted = grad_out * gain_row
    grad_in = scaling * (weighted - normed * jnp.mean(weighted * normed, axis=-1, keepdims=True))
    grad_gain = jnp.sum((grad_out * normed).reshape(-1, normed.shape[-1]), axis=0)
    return (grad_in, grad_gain)


def score_block(query_rows, key_rows, scaling):
    return (
        jnp.einsum("igrd,jgd->grij", query_rows, key_rows, preferred_element_type=jnp.float32)
        * scaling
    )


def visible_pairs(query_at, query_doc, key_at, key_doc):
    return (query_doc[:, None] == key_doc[None, :]) & (key_at[None, :] <= query_at[:, None])


def any_visible(query_at, query_doc, key_at):
    return (jnp.min(key_at) <= jnp.max(query_at)) & (jnp.max(key_at) >= jnp.min(query_doc))


def contract_rows(left, right):
    return lax.dot_general(
        left, right, (((0,), (0,)), ((), ())), preferred_element_type=jnp.float32
    )


def contract_cols(left, right):
    return lax.dot_general(
        left, right, (((1,), (1,)), ((), ())), preferred_element_type=jnp.float32
    )


def keep_same(totals):
    return totals


def local(
    block_input,
    doc_starts,
    out_grad,
    query_weight,
    key_weight,
    value_weight,
    output_weight,
    gate_weight,
    up_weight,
    down_weight,
    mixer_gain,
    feed_gain,
    query_gain,
    key_gain,
):
    tokens = block_input.shape[1]
    ctx_count = lax.axis_size("ctx")
    repeat = H // KVH
    kv_width = KVH * HD
    scaling = HD ** (-0.5)
    inputs = block_input[0].astype(jnp.float32)
    starts = doc_starts[0]
    where_at = place_rows(
        lax.axis_index("ctx") * tokens + jnp.arange(tokens, dtype=jnp.int32), tokens, ctx_count
    )
    begins = doc_begin(starts, where_at)
    cosine, sine_part = rotary(where_at - begins)
    gathered = (
        lax.all_gather(query_weight, "fsdp", axis=0, tiled=True),
        lax.all_gather(key_weight, "fsdp", axis=0, tiled=True),
        lax.all_gather(value_weight, "fsdp", axis=0, tiled=True),
        lax.all_gather(output_weight, "fsdp", axis=0, tiled=True),
        lax.all_gather(gate_weight, "fsdp", axis=0, tiled=True),
        lax.all_gather(up_weight, "fsdp", axis=0, tiled=True),
        lax.all_gather(down_weight, "fsdp", axis=0, tiled=True),
        lax.all_gather(mixer_gain, "fsdp", axis=0, tiled=True),
        lax.all_gather(feed_gain, "fsdp", axis=0, tiled=True),
        lax.all_gather(query_gain, "fsdp", axis=0, tiled=True),
        lax.all_gather(key_gain, "fsdp", axis=0, tiled=True),
    )
    full_query, full_key, full_value, full_proj, full_gate, full_up, full_down = gathered[:7]
    gain_mixer, gain_feed, gain_query, gain_key = [
        entry.astype(jnp.float32) for entry in gathered[7:]
    ]
    normed_in, scale_in = unit_norm(inputs)
    hidden_in = (normed_in * gain_mixer).astype(jnp.bfloat16)
    query_lin = jnp.dot(hidden_in, full_query, preferred_element_type=jnp.float32)
    key_lin = jnp.dot(hidden_in, full_key, preferred_element_type=jnp.float32)
    value_lin = jnp.dot(hidden_in, full_value, preferred_element_type=jnp.float32)
    query_normed, query_scale = unit_norm(query_lin.reshape(tokens, H, HD))
    key_normed, key_scale = unit_norm(key_lin.reshape(tokens, KVH, HD))
    query_att = (
        rotate_pairs(query_normed * gain_query, cosine, sine_part)
        .reshape(tokens, H * HD)
        .astype(jnp.bfloat16)
    )
    key_att = (
        rotate_pairs(key_normed * gain_key, cosine, sine_part)
        .reshape(tokens, kv_width)
        .astype(jnp.bfloat16)
    )
    value_att = value_lin.astype(jnp.bfloat16)
    query_four = query_att.reshape(tokens, KVH, repeat, HD)
    start_state = (
        jnp.full((KVH, repeat, tokens), FLOOR_SCORE, jnp.float32),
        jnp.zeros((KVH, repeat, tokens), jnp.float32),
        jnp.zeros((tokens, H * HD), jnp.float32),
    )
    key_part = lax.all_gather(key_att, "ctx", axis=0, tiled=True)
    value_part = lax.all_gather(value_att, "ctx", axis=0, tiled=True)
    rows = key_part.shape[0]
    width = math.gcd(math.gcd(rows, tokens // 2), 512)

    def forward_key_block(block_index, totals):
        offset = block_index * width
        key_rows = lax.dynamic_slice_in_dim(key_part, offset, width, 0).reshape(width, KVH, HD)
        value_rows = lax.dynamic_slice_in_dim(value_part, offset, width, 0).reshape(width, KVH, HD)
        key_at = place_rows(offset + jnp.arange(width, dtype=jnp.int32), tokens, ctx_count)

        def attend(totals):
            highest, total_mass, accum = totals
            visible = visible_pairs(where_at, begins, key_at, doc_begin(starts, key_at))
            scores = jnp.where(visible, score_block(query_four, key_rows, scaling), FLOOR_SCORE)
            new_high = jnp.maximum(highest, jnp.max(scores, axis=-1))
            rescale = jnp.exp(highest - new_high)
            probable = jnp.where(visible, jnp.exp(scores - new_high[..., None]), 0.0)
            total_mass = total_mass * rescale + jnp.sum(probable, axis=-1)
            part_out = jnp.einsum(
                "grij,jgd->igrd",
                probable.astype(jnp.bfloat16),
                value_rows,
                preferred_element_type=jnp.float32,
            )
            accum = (
                accum.reshape(tokens, KVH, repeat, HD)
                * jnp.transpose(rescale, (2, 0, 1))[..., None]
                + part_out
            )
            return (new_high, total_mass, accum.reshape(tokens, H * HD))

        return lax.cond(any_visible(where_at, begins, key_at), attend, keep_same, totals)

    highest, total_mass, accum = lax.fori_loop(0, rows // width, forward_key_block, start_state)
    lse_heads = highest + jnp.log(total_mass)
    attn_raw = (
        accum.reshape(tokens, KVH, repeat, HD) / jnp.transpose(total_mass, (2, 0, 1))[..., None]
    ).reshape(tokens, H * HD)
    attn_low = attn_raw.astype(jnp.bfloat16)
    mixed = inputs + jnp.dot(attn_low, full_proj, preferred_element_type=jnp.float32)
    normed_mid, scale_mid = unit_norm(mixed)
    hidden_mid = (normed_mid * gain_feed).astype(jnp.bfloat16)
    gate_lin = jnp.dot(hidden_mid, full_gate, preferred_element_type=jnp.float32)
    up_lin = jnp.dot(hidden_mid, full_up, preferred_element_type=jnp.float32)
    sigmoid_gate = jax.nn.sigmoid(gate_lin)
    activated = (gate_lin * sigmoid_gate * up_lin).astype(jnp.bfloat16)
    block_output = (
        mixed + jnp.dot(activated, full_down, preferred_element_type=jnp.float32)
    ).astype(jnp.bfloat16)
    regathered = (
        lax.all_gather(query_weight, "fsdp", axis=0, tiled=True),
        lax.all_gather(key_weight, "fsdp", axis=0, tiled=True),
        lax.all_gather(value_weight, "fsdp", axis=0, tiled=True),
        lax.all_gather(output_weight, "fsdp", axis=0, tiled=True),
        lax.all_gather(gate_weight, "fsdp", axis=0, tiled=True),
        lax.all_gather(up_weight, "fsdp", axis=0, tiled=True),
        lax.all_gather(down_weight, "fsdp", axis=0, tiled=True),
        lax.all_gather(mixer_gain, "fsdp", axis=0, tiled=True),
        lax.all_gather(feed_gain, "fsdp", axis=0, tiled=True),
        lax.all_gather(query_gain, "fsdp", axis=0, tiled=True),
        lax.all_gather(key_gain, "fsdp", axis=0, tiled=True),
    )
    full_query, full_key, full_value, full_proj, full_gate, full_up, full_down = regathered[:7]
    gain_mixer, gain_feed, gain_query, gain_key = [
        entry.astype(jnp.float32) for entry in regathered[7:]
    ]
    grad_top = out_grad[0].astype(jnp.float32)
    grad_top_low = grad_top.astype(jnp.bfloat16)
    grad_down = contract_rows(activated, grad_top_low)
    grad_act = contract_cols(grad_top_low, full_down)
    grad_gate_low = (
        grad_act * up_lin * sigmoid_gate * (1.0 + gate_lin * (1.0 - sigmoid_gate))
    ).astype(jnp.bfloat16)
    grad_up_low = (grad_act * gate_lin * sigmoid_gate).astype(jnp.bfloat16)
    grad_gate = contract_rows(hidden_mid, grad_gate_low)
    grad_up = contract_rows(hidden_mid, grad_up_low)
    grad_hidden_mid = contract_cols(grad_gate_low, full_gate) + contract_cols(grad_up_low, full_up)
    grad_normed_mid, grad_feed = norm_back(grad_hidden_mid, normed_mid, scale_mid, gain_feed)
    grad_mixed = grad_top + grad_normed_mid
    grad_mixed_low = grad_mixed.astype(jnp.bfloat16)
    grad_proj = contract_rows(attn_low, grad_mixed_low)
    grad_attn = contract_cols(grad_mixed_low, full_proj).astype(jnp.bfloat16)
    grad_four = grad_attn.reshape(tokens, KVH, repeat, HD)
    delta_heads = jnp.sum(
        grad_four.astype(jnp.float32) * attn_raw.reshape(tokens, KVH, repeat, HD), axis=-1
    )
    delta_grid = jnp.transpose(delta_heads, (1, 2, 0))
    lse_rows = jnp.transpose(lse_heads, (2, 0, 1)).reshape(tokens, H)
    delta_rows = delta_heads.reshape(tokens, H)
    query_key_part = lax.all_gather(key_att, "ctx", axis=0, tiled=True)
    query_value_part = lax.all_gather(value_att, "ctx", axis=0, tiled=True)
    rows = query_key_part.shape[0]
    query_width = math.gcd(math.gcd(rows, tokens // 2), 512)

    def query_key_block(block_index, grad_query_acc):
        offset = block_index * query_width
        key_rows = lax.dynamic_slice_in_dim(query_key_part, offset, query_width, 0).reshape(
            query_width, KVH, HD
        )
        value_rows = lax.dynamic_slice_in_dim(query_value_part, offset, query_width, 0).reshape(
            query_width, KVH, HD
        )
        key_at = place_rows(offset + jnp.arange(query_width, dtype=jnp.int32), tokens, ctx_count)

        def attend(grad_query_acc):
            visible = visible_pairs(where_at, begins, key_at, doc_begin(starts, key_at))
            scores = score_block(query_four, key_rows, scaling)
            probable = jnp.where(visible, jnp.exp(scores - lse_heads[..., None]), 0.0)
            grad_prob = jnp.einsum(
                "igrd,jgd->grij", grad_four, value_rows, preferred_element_type=jnp.float32
            )
            grad_score = (probable * (grad_prob - delta_grid[..., None])).astype(jnp.bfloat16)
            added = (
                jnp.einsum(
                    "grij,jgd->igrd", grad_score, key_rows, preferred_element_type=jnp.float32
                )
                * scaling
            )
            return grad_query_acc + added.reshape(tokens, H * HD)

        return lax.cond(any_visible(where_at, begins, key_at), attend, keep_same, grad_query_acc)

    grad_query_att = lax.fori_loop(
        0, rows // query_width, query_key_block, jnp.zeros((tokens, H * HD), jnp.float32)
    )
    lse_all, delta_all = (
        lax.all_gather(lse_rows.astype(jnp.bfloat16), "ctx", axis=0, tiled=True).astype(
            lse_rows.dtype
        ),
        lax.all_gather(delta_rows.astype(jnp.bfloat16), "ctx", axis=0, tiled=True).astype(
            delta_rows.dtype
        ),
    )
    key_three = key_att.reshape(tokens, KVH, HD)
    value_three = value_att.reshape(tokens, KVH, HD)
    empty_keys = jnp.zeros((tokens, kv_width), jnp.float32)
    query_part = lax.all_gather(query_att, "ctx", axis=0, tiled=True)
    grad_part = lax.all_gather(grad_attn, "ctx", axis=0, tiled=True)
    rows = query_part.shape[0]
    key_width = math.gcd(math.gcd(rows, tokens // 2), 512)

    def query_block(block_index, totals):
        offset = block_index * key_width
        query_rows = lax.dynamic_slice_in_dim(query_part, offset, key_width, 0).reshape(
            key_width, KVH, repeat, HD
        )
        grad_rows = lax.dynamic_slice_in_dim(grad_part, offset, key_width, 0).reshape(
            key_width, KVH, repeat, HD
        )
        query_at = place_rows(offset + jnp.arange(key_width, dtype=jnp.int32), tokens, ctx_count)
        query_doc = doc_begin(starts, query_at)
        lse_block = jnp.transpose(
            lax.dynamic_slice_in_dim(lse_all, offset, key_width, 0).reshape(key_width, KVH, repeat),
            (1, 2, 0),
        )
        delta_block = jnp.transpose(
            lax.dynamic_slice_in_dim(delta_all, offset, key_width, 0).reshape(
                key_width, KVH, repeat
            ),
            (1, 2, 0),
        )

        def attend(totals):
            grad_key_acc, grad_value_acc = totals
            visible = visible_pairs(query_at, query_doc, where_at, begins)
            scores = score_block(query_rows, key_three, scaling)
            probable = jnp.where(visible, jnp.exp(scores - lse_block[..., None]), 0.0)
            grad_prob = jnp.einsum(
                "igrd,jgd->grij", grad_rows, value_three, preferred_element_type=jnp.float32
            )
            grad_score = (probable * (grad_prob - delta_block[..., None])).astype(jnp.bfloat16)
            value_added = jnp.einsum(
                "grij,igrd->jgd",
                probable.astype(jnp.bfloat16),
                grad_rows,
                preferred_element_type=jnp.float32,
            )
            key_added = (
                jnp.einsum(
                    "grij,igrd->jgd", grad_score, query_rows, preferred_element_type=jnp.float32
                )
                * scaling
            )
            return (
                grad_key_acc + key_added.reshape(tokens, kv_width),
                grad_value_acc + value_added.reshape(tokens, kv_width),
            )

        return lax.cond(any_visible(query_at, query_doc, where_at), attend, keep_same, totals)

    grad_key_att, grad_value_att = lax.fori_loop(
        0, rows // key_width, query_block, (empty_keys, empty_keys)
    )
    grad_query_unit = rotate_back(grad_query_att.reshape(tokens, H, HD), cosine, sine_part)
    grad_query_lin, grad_qgain = norm_back(grad_query_unit, query_normed, query_scale, gain_query)
    grad_key_unit = rotate_back(grad_key_att.reshape(tokens, KVH, HD), cosine, sine_part)
    grad_key_lin, grad_kgain = norm_back(grad_key_unit, key_normed, key_scale, gain_key)
    grad_query_low = grad_query_lin.reshape(tokens, H * HD).astype(jnp.bfloat16)
    grad_key_low = grad_key_lin.reshape(tokens, kv_width).astype(jnp.bfloat16)
    grad_value_low = grad_value_att.astype(jnp.bfloat16)
    grad_query = contract_rows(hidden_in, grad_query_low)
    grad_key = contract_rows(hidden_in, grad_key_low)
    grad_value = contract_rows(hidden_in, grad_value_low)
    grad_hidden_in = (
        contract_cols(grad_query_low, full_query)
        + contract_cols(grad_key_low, full_key)
        + contract_cols(grad_value_low, full_value)
    )
    grad_normed_in, grad_mixer = norm_back(grad_hidden_in, normed_in, scale_in, gain_mixer)
    input_grad = grad_mixed + grad_normed_in
    parts = (
        lax.psum_scatter(
            grad_query.astype(jnp.bfloat16), "fsdp", scatter_dimension=0, tiled=True
        ).astype(jnp.float32),
        lax.psum_scatter(
            grad_key.astype(jnp.bfloat16), "fsdp", scatter_dimension=0, tiled=True
        ).astype(jnp.float32),
        lax.psum_scatter(
            grad_value.astype(jnp.bfloat16), "fsdp", scatter_dimension=0, tiled=True
        ).astype(jnp.float32),
        lax.psum_scatter(
            grad_proj.astype(jnp.bfloat16), "fsdp", scatter_dimension=0, tiled=True
        ).astype(jnp.float32),
        lax.psum_scatter(
            grad_gate.astype(jnp.bfloat16), "fsdp", scatter_dimension=0, tiled=True
        ).astype(jnp.float32),
        lax.psum_scatter(
            grad_up.astype(jnp.bfloat16), "fsdp", scatter_dimension=0, tiled=True
        ).astype(jnp.float32),
        lax.psum_scatter(
            grad_down.astype(jnp.bfloat16), "fsdp", scatter_dimension=0, tiled=True
        ).astype(jnp.float32),
        lax.psum_scatter(
            grad_mixer.astype(jnp.bfloat16), "fsdp", scatter_dimension=0, tiled=True
        ).astype(jnp.float32),
        lax.psum_scatter(
            grad_feed.astype(jnp.bfloat16), "fsdp", scatter_dimension=0, tiled=True
        ).astype(jnp.float32),
        lax.psum_scatter(
            grad_qgain.astype(jnp.bfloat16), "fsdp", scatter_dimension=0, tiled=True
        ).astype(jnp.float32),
        lax.psum_scatter(
            grad_kgain.astype(jnp.bfloat16), "fsdp", scatter_dimension=0, tiled=True
        ).astype(jnp.float32),
    )
    summed = (
        lax.psum(parts[0].astype(jnp.bfloat16), "ctx").astype(jnp.float32),
        lax.psum(parts[1].astype(jnp.bfloat16), "ctx").astype(jnp.float32),
        lax.psum(parts[2].astype(jnp.bfloat16), "ctx").astype(jnp.float32),
        lax.psum(parts[3].astype(jnp.bfloat16), "ctx").astype(jnp.float32),
        lax.psum(parts[4].astype(jnp.bfloat16), "ctx").astype(jnp.float32),
        lax.psum(parts[5].astype(jnp.bfloat16), "ctx").astype(jnp.float32),
        lax.psum(parts[6].astype(jnp.bfloat16), "ctx").astype(jnp.float32),
        lax.psum(parts[7].astype(jnp.bfloat16), "ctx").astype(jnp.float32),
        lax.psum(parts[8].astype(jnp.bfloat16), "ctx").astype(jnp.float32),
        lax.psum(parts[9].astype(jnp.bfloat16), "ctx").astype(jnp.float32),
        lax.psum(parts[10].astype(jnp.bfloat16), "ctx").astype(jnp.float32),
    )
    return (
        block_output[None],
        input_grad[None],
        summed[0],
        summed[1],
        summed[2],
        summed[3],
        summed[4],
        summed[5],
        summed[6],
        summed[7],
        summed[8],
        summed[9],
        summed[10],
    )


def flipped(bits, count):
    return [(index, index ^ bits) for index in range(count)]


def swap_ctx(values, bits, count):
    return lax.ppermute(values, "ctx", flipped(bits, count))


def behind(values, *ready):
    return lax.optimization_barrier((values,) + ready)[0]


def dot_nn(left, right):
    return lax.dot_general(
        left, right, (((1,), (0,)), ((), ())), preferred_element_type=jnp.float32
    )


def dot_nt(left, right):
    return lax.dot_general(
        left, right, (((1,), (1,)), ((), ())), preferred_element_type=jnp.float32
    )


def gather_plane(block, count):
    across = swap_ctx(block, 2, count)
    along = swap_ctx(block, 4, count)
    half = block.shape[0] // 2
    corner = jnp.concatenate(
        [swap_ctx(along[:half], 2, count), swap_ctx(across[half:], 4, count)], axis=0
    )
    near = jnp.concatenate([block, across, along], axis=0)
    far = swap_ctx(near, 1, count)
    same = jnp.concatenate([near, corner], axis=0)
    other = jnp.concatenate([far, swap_ctx(corner, 1, count)], axis=0)
    return same, other


def scatter_plane(same, other, count):
    size = same.shape[0] // 4
    partner = swap_ctx(other, 1, count)
    sums = same.astype(jnp.float32) + partner.astype(jnp.float32)
    away = sums[size:].astype(jnp.bfloat16)
    across = swap_ctx(away[:size], 2, count)
    along = swap_ctx(away[size : 2 * size], 4, count)
    corner = swap_ctx(away[2 * size :], 6, count)
    return sums[:size], across, along, corner


def exchange_plane(blocks, count):
    got = swap_ctx(blocks[4:], 1, count)
    outs = []
    for slot, bits in ((1, 2), (2, 4), (3, 6)):
        outs.append(swap_ctx(jnp.stack([blocks[slot], got[slot]]), bits, count))
    same = [blocks[0]] + [out[0] for out in outs]
    other = [got[0]] + [out[1] for out in outs]
    return jnp.stack(same + other)


def slot_of(bits):
    return lax.shift_right_logical(bits, 1) + 4 * lax.bitwise_and(bits, 1)


def row_of(place, here, tokens, count):
    half = tokens // 2
    device = jnp.where(place < count, place, 2 * count - 1 - place)
    late = jnp.where(place < count, 0, half)
    return slot_of(lax.bitwise_xor(device, here)) * tokens + late


def swap_half(values, low_lane):
    return jnp.where(low_lane, pltpu.roll(values, 96, 1), pltpu.roll(values, 32, 1))


def head_mean(values, first):
    lower = jnp.sum(jnp.where(first, values, 0.0), axis=1, keepdims=True)
    upper = jnp.sum(jnp.where(first, 0.0, values), axis=1, keepdims=True)
    return jnp.where(first, lower, upper) * (1.0 / HD)


def lane_masks(rows):
    lanes = lax.broadcasted_iota(jnp.int32, (rows, 2 * HD), 1)
    return lanes < HD, (lanes % HD) < (HD // 2)


def two_heads(values):
    first, _ = lane_masks(values.shape[0])
    zero = jnp.zeros_like(values)
    return jnp.concatenate(
        [jnp.where(first, values, zero), jnp.where(first, zero, values)], axis=0
    )


def begin_at(meta_ref, docs, where_at):
    begin = jnp.zeros_like(where_at)
    for doc in range(docs):
        begin = jnp.where(meta_ref[1 + doc] <= where_at, meta_ref[1 + doc], begin)
    return begin


def block_visible(meta_ref, docs, query_block, key_block, size):
    query_at = query_block * size + lax.broadcasted_iota(jnp.int32, (1, size), 1)
    begin = begin_at(meta_ref, docs, query_at)
    key_at = key_block * size + lax.broadcasted_iota(jnp.int32, (size, size), 0)
    return (key_at <= query_at) & (key_at >= begin)


def aligned(value, size):
    return pl.multiple_of(value, size)


def attention_kernel(
    tokens, count, docs,
    meta_ref, lin_ref, cos_ref, sin_ref, gains_ref,
    query_ref, key_ref, value_ref, attn_ref, lse_ref, low_ref,
    value_t, accum,
):
    here = meta_ref[0]
    half = tokens // 2
    size = tokens
    blocks = count

    def prepare(place, carry):
        first, low_lane = lane_masks(half)
        source = aligned(row_of(place, here, tokens, count), half)
        target = aligned(place * half, half)
        cosine = cos_ref[pl.ds(target, half), :]
        sine = sin_ref[pl.ds(target, half), :]
        query = lin_ref[pl.ds(source, half), : 2 * HD]
        unit = query * lax.rsqrt(head_mean(query * query, first) + EPSILON) * gains_ref[0:1, :]
        turned = unit * cosine + swap_half(unit, low_lane) * sine
        query_ref[pl.ds(target, half), :] = (
            turned.astype(jnp.bfloat16).astype(jnp.float32) * (HD**-0.5)
        ).astype(jnp.bfloat16)
        both = lin_ref[pl.ds(source, half), 2 * HD :]
        unit = both * lax.rsqrt(head_mean(both * both, first) + EPSILON) * gains_ref[1:2, :]
        turned = unit * cosine + swap_half(unit, low_lane) * sine
        key_ref[pl.ds(target, half), :] = jnp.where(
            first, turned, pltpu.roll(turned, HD, 1)
        ).astype(jnp.bfloat16)
        values = jnp.where(first, pltpu.roll(both, HD, 1), both)
        value_ref[pl.ds(target, half), :] = values.astype(jnp.bfloat16)
        return carry

    lax.fori_loop(0, 2 * count, prepare, 0)

    def turn_values(block, carry):
        values = value_ref[pl.ds(aligned(block * size, size), size), :].astype(jnp.float32)
        value_t[block, :HD, :] = values.T[:HD].astype(jnp.bfloat16)
        value_t[block, HD:, :] = jnp.ones((value_t.shape[1] - HD, size), jnp.bfloat16)
        return carry

    lax.fori_loop(0, blocks, turn_values, 0)

    def query_step(block, carry):
        query = two_heads(query_ref[pl.ds(aligned(block * size, size), size), :])
        accum[...] = jnp.zeros_like(accum)
        lowest = begin_at(meta_ref, docs, block * size) // size

        def key_step(other, carry):
            keys = key_ref[pl.ds(aligned(other * size, size), size), :]
            scores = dot_nt(keys, query)
            visible = block_visible(meta_ref, docs, block, other, size)
            probable = jnp.concatenate(
                [
                    jnp.where(visible, jnp.exp(scores[:, :size]), 0.0),
                    jnp.where(visible, jnp.exp(scores[:, size:]), 0.0),
                ],
                axis=1,
            ).astype(jnp.bfloat16)
            accum[...] += dot_nn(value_t[other], probable)
            return carry

        lax.fori_loop(lowest, block + 1, key_step, 0)
        mass = accum[HD : HD + 1, :]
        mixed = accum[:HD, :] / mass
        lse_ref[block] = jnp.log(mass)
        rows = jnp.concatenate([mixed[:, :size], mixed[:, size:]], axis=0).T
        attn_ref[pl.ds(aligned(block * size, size), size), :] = rows
        for part in range(2):
            target = aligned(row_of(2 * block + part, here, tokens, count), half)
            low_ref[pl.ds(target, half), :] = rows[part * half : (part + 1) * half].astype(
                jnp.bfloat16
            )
        return carry

    lax.fori_loop(0, blocks, query_step, 0)


def attention_back_kernel(
    tokens, count, docs,
    meta_ref, lin_ref, cos_ref, sin_ref, gains_ref,
    query_ref, key_ref, value_ref, attn_ref, lse_ref, grad_ref,
    out_ref, gain_ref,
    key_t, grad_query, grad_key, grad_value, accum,
):
    here = meta_ref[0]
    half = tokens // 2
    size = tokens
    blocks = count
    grad_key[...] = jnp.zeros_like(grad_key)
    grad_value[...] = jnp.zeros_like(grad_value)
    gain_ref[...] = jnp.zeros_like(gain_ref)

    def turn_keys(block, carry):
        keys = key_ref[pl.ds(aligned(block * size, size), size), :].astype(jnp.float32)
        key_t[block] = keys.T[:HD].astype(jnp.bfloat16)
        return carry

    lax.fori_loop(0, blocks, turn_keys, 0)

    def query_step(block, carry):
        here_rows = pl.ds(aligned(block * size, size), size)
        query = two_heads(query_ref[here_rows, :])
        parts = []
        for part in range(2):
            source = aligned(row_of(2 * block + part, here, tokens, count), half)
            parts.append(grad_ref[pl.ds(source, half), :])
        grads = jnp.concatenate(parts, axis=0)
        products = (grads.astype(jnp.float32) * attn_ref[here_rows, :]).T
        deltas = (
            jnp.sum(products[:HD], axis=0, keepdims=True),
            jnp.sum(products[HD:], axis=0, keepdims=True),
        )
        grads = two_heads(grads)
        lse = lse_ref[block]
        accum[...] = jnp.zeros_like(accum)
        lowest = begin_at(meta_ref, docs, block * size) // size

        def key_step(other, carry):
            rows = pl.ds(aligned(other * size, size), size)
            scores = dot_nt(key_ref[rows, :], query)
            grad_prob = dot_nt(value_ref[rows, :], grads)
            visible = block_visible(meta_ref, docs, block, other, size)
            probs, grad_scores = [], []
            for head in range(2):
                cols = slice(head * size, (head + 1) * size)
                prob = jnp.where(visible, jnp.exp(scores[:, cols] - lse[:, cols]), 0.0)
                probs.append(prob)
                grad_scores.append(prob * (grad_prob[:, cols] - deltas[head]))
            probs = jnp.concatenate(probs, axis=1).astype(jnp.bfloat16)
            grad_scores = jnp.concatenate(grad_scores, axis=1).astype(jnp.bfloat16)
            grad_value[rows, :] += dot_nn(probs, grads)
            grad_key[rows, :] += dot_nn(grad_scores, query)
            accum[...] += dot_nn(key_t[other], grad_scores)
            return carry

        lax.fori_loop(lowest, block + 1, key_step, 0)
        total = accum[...] * (HD**-0.5)
        grad_query[here_rows, :] = jnp.concatenate([total[:, :size], total[:, size:]], axis=0).T
        return carry

    lax.fori_loop(0, blocks, query_step, 0)

    def finish(place, carry):
        first, low_lane = lane_masks(half)
        source = aligned(row_of(place, here, tokens, count), half)
        target = pl.ds(aligned(place * half, half), half)
        cosine = cos_ref[target, :]
        sine = sin_ref[target, :]

        def through(linear, grads, gain):
            scale = lax.rsqrt(head_mean(linear * linear, first) + EPSILON)
            normed = linear * scale
            turned = grads * cosine + swap_half(grads * sine, low_lane)
            weighted = turned * gain
            grad_in = scale * (weighted - normed * head_mean(weighted * normed, first))
            return grad_in, jnp.sum(turned * normed, axis=0, keepdims=True)

        grad_in, gain_row = through(
            lin_ref[pl.ds(source, half), : 2 * HD], grad_query[target, :], gains_ref[0:1, :]
        )
        out_ref[pl.ds(source, half), : 2 * HD] = grad_in.astype(jnp.bfloat16)
        gain_ref[0:1, :] += gain_row
        keys = grad_key[target, :]
        grad_in, gain_row = through(
            lin_ref[pl.ds(source, half), 2 * HD :], keys + pltpu.roll(keys, HD, 1), gains_ref[1:2, :]
        )
        gain_ref[1:2, :] += gain_row
        values = grad_value[target, :]
        values = values + pltpu.roll(values, HD, 1)
        out_ref[pl.ds(source, half), 2 * HD :] = jnp.where(first, grad_in, values).astype(
            jnp.bfloat16
        )
        return carry

    lax.fori_loop(0, 2 * count, finish, 0)


def project_kernel(
    count, parts, meta_ref, attn_ref, weight_ref, input_ref, gain_ref,
    full_ref, attn_out_ref, mixed_ref, hidden_ref,
):
    here = meta_ref[0]
    rows = weight_ref.shape[1] // parts
    for owner in range(count):
        slot = slot_of(lax.bitwise_xor(jnp.int32(owner), here))
        for part in range(parts):
            start = (part * count + owner) * rows
            full_ref[start : start + rows, :] = weight_ref[slot, part * rows : (part + 1) * rows, :]
        attn_out_ref[:, owner * 2 * HD : (owner + 1) * 2 * HD] = attn_ref[slot]
    mixed = input_ref[...].astype(jnp.float32) + dot_nn(attn_out_ref[...], full_ref[...])
    mixed_ref[...] = mixed
    scale = lax.rsqrt(jnp.mean(mixed * mixed, axis=1, keepdims=True) + EPSILON)
    hidden_ref[...] = (mixed * scale * gain_ref[...]).astype(jnp.bfloat16)


def feed_kernel(
    hidden_ref, grad_ref, wide_ref, down_ref,
    act_ref, grad_wide_ref, out_ref, grad_hidden_ref,
):
    width = down_ref.shape[0]
    wide = dot_nn(hidden_ref[...], wide_ref[...])
    grad_act = dot_nt(grad_ref[...], down_ref[...])
    gate, up = wide[:, :width], wide[:, width:]
    sigmoid = 1.0 / (1.0 + jnp.exp(-gate))
    silu = gate * sigmoid
    act = (silu * up).astype(jnp.bfloat16)
    act_ref[...] = act
    grad_gate = grad_act * up * sigmoid * (1.0 + gate * (1.0 - sigmoid))
    grad_wide = jnp.concatenate([grad_gate, grad_act * silu], axis=1).astype(jnp.bfloat16)
    grad_wide_ref[...] = grad_wide
    grad_hidden_ref[...] = dot_nt(grad_wide, wide_ref[...]).astype(jnp.bfloat16)
    out_ref[...] = dot_nn(act, down_ref[...]).astype(jnp.bfloat16)


def feed_back_kernel(
    count, meta_ref, sum_ref, across_ref, along_ref, corner_ref, mixed_ref, grad_ref, full_ref,
    gain_ref, grad_mixed_ref, grad_low_ref, blocks_ref, grad_gain_ref,
):
    here = meta_ref[0]
    grad_hidden = (
        sum_ref[...]
        + across_ref[...].astype(jnp.float32)
        + along_ref[...].astype(jnp.float32)
        + corner_ref[...].astype(jnp.float32)
    )
    mixed = mixed_ref[...]
    scale = lax.rsqrt(jnp.mean(mixed * mixed, axis=1, keepdims=True) + EPSILON)
    normed = mixed * scale
    weighted = grad_hidden * gain_ref[...]
    grad_in = scale * (weighted - normed * jnp.mean(weighted * normed, axis=1, keepdims=True))
    grad_gain_ref[...] = jnp.sum(grad_hidden * normed, axis=0, keepdims=True)
    grad_mixed = grad_ref[...].astype(jnp.float32) + grad_in
    grad_mixed_ref[...] = grad_mixed
    grad_low_ref[...] = grad_mixed.astype(jnp.bfloat16)
    grad_attn = dot_nt(grad_low_ref[...], full_ref[...]).astype(jnp.bfloat16)
    for owner in range(count):
        slot = slot_of(lax.bitwise_xor(jnp.int32(owner), here))
        blocks_ref[slot] = grad_attn[:, owner * 2 * HD : (owner + 1) * 2 * HD]


def wide_out_kernel(count, parts, meta_ref, blocks_ref, gate_ref, up_ref):
    here = meta_ref[0]
    width = blocks_ref.shape[2] // 2
    piece = width // parts
    for part in range(parts):
        for start, out_ref in ((0, gate_ref), (width, up_ref)):
            columns = []
            for owner in range(count):
                slot = slot_of(lax.bitwise_xor(jnp.int32(owner), here))
                first = start + part * piece
                columns.append(blocks_ref[slot, :, first : first + piece].astype(jnp.float32))
            out_ref[:, part * count * piece : (part + 1) * count * piece] = jnp.concatenate(
                columns, axis=1
            )


def rows_out_kernel(meta_ref, block_ref, out_ref):
    out_ref[...] = block_ref[0].astype(jnp.float32)


def heads_out_kernel(count, meta_ref, blocks_ref, query_ref, key_ref, value_ref):
    here = meta_ref[0]
    queries, keys, values = [], [], []
    for owner in range(count):
        slot = slot_of(lax.bitwise_xor(jnp.int32(owner), here))
        block = blocks_ref[slot].astype(jnp.float32)
        queries.append(block[:, : 2 * HD])
        keys.append(block[:, 2 * HD : 3 * HD])
        values.append(block[:, 3 * HD :])
    query_ref[...] = jnp.concatenate(queries, axis=1)
    key_ref[...] = jnp.concatenate(keys, axis=1)
    value_ref[...] = jnp.concatenate(values, axis=1)


SCALARS = pl.BlockSpec(memory_space=pltpu.SMEM)
WHOLE = pl.BlockSpec(memory_space=pltpu.VMEM)


def shaped(shape, kind):
    return jax.ShapeDtypeStruct(shape, kind)


def whole_call(kernel, outs, ins, flops, scratch=(), name=None):
    moved = sum(math.prod(out.shape) * out.dtype.itemsize for out in outs)
    return pl.pallas_call(
        kernel,
        out_shape=outs,
        in_specs=[SCALARS] + [WHOLE] * ins,
        out_specs=[WHOLE] * len(outs),
        scratch_shapes=list(scratch),
        cost_estimate=pl.CostEstimate(
            flops=int(flops), bytes_accessed=int(2 * moved), transcendentals=0
        ),
        compiler_params=pltpu.CompilerParams(vmem_limit_bytes=60 * 2**20),
        name=name,
    )


def rows_out(meta, blocks, name):
    count, rows, width = blocks.shape
    return pl.pallas_call(
        rows_out_kernel,
        out_shape=shaped((count * rows, width), jnp.float32),
        grid_spec=pltpu.PrefetchScalarGridSpec(
            num_scalar_prefetch=1,
            grid=(count,),
            in_specs=[
                pl.BlockSpec(
                    (1, rows, width),
                    lambda owner, meta_ref: (
                        slot_of(lax.bitwise_xor(owner, meta_ref[0])), 0, 0,
                    ),
                )
            ],
            out_specs=pl.BlockSpec((rows, width), lambda owner, meta_ref: (owner, 0)),
        ),
        name=name,
    )(meta, blocks)


def feed_call(hidden, grads, wide, down, tile):
    rows, width = hidden.shape
    inner = down.shape[0]
    low = jnp.bfloat16
    moved = 2 * (4 * rows * width + 3 * rows * inner + 3 * width * inner)
    return pl.pallas_call(
        feed_kernel,
        grid=(rows // tile,),
        in_specs=[
            pl.BlockSpec((tile, width), lambda step: (step, 0)),
            pl.BlockSpec((tile, width), lambda step: (step, 0)),
            pl.BlockSpec((width, 2 * inner), lambda step: (0, 0)),
            pl.BlockSpec((inner, width), lambda step: (0, 0)),
        ],
        out_specs=[
            pl.BlockSpec((tile, inner), lambda step: (step, 0)),
            pl.BlockSpec((tile, 2 * inner), lambda step: (step, 0)),
            pl.BlockSpec((tile, width), lambda step: (step, 0)),
            pl.BlockSpec((tile, width), lambda step: (step, 0)),
        ],
        out_shape=[
            shaped((rows, inner), low),
            shaped((rows, 2 * inner), low),
            shaped((rows, width), low),
            shaped((rows, width), low),
        ],
        cost_estimate=pl.CostEstimate(
            flops=12 * rows * width * inner, bytes_accessed=moved, transcendentals=rows * inner
        ),
        compiler_params=pltpu.CompilerParams(vmem_limit_bytes=60 * 2**20),
        name="feed",
    )(hidden, grads, wide, down)


def local_heads(
    block_input, doc_starts, out_grad, query_weight, key_weight, value_weight, output_weight,
    gate_weight, up_weight, down_weight, mixer_gain, feed_gain, query_gain, key_gain,
):
    low = jnp.bfloat16
    tokens, width = block_input.shape[1:]
    count = lax.axis_size("ctx")
    shards = lax.axis_size("fsdp")
    here = lax.axis_index("ctx").astype(jnp.int32)
    stream = tokens * count
    docs = doc_starts.shape[1]
    pair = 2 * HD
    own_rows = width // shards
    meta = jnp.concatenate([here[None], doc_starts[0].astype(jnp.int32)])
    own_input = block_input[0]
    own_grad = out_grad[0]

    gains = jnp.zeros((16, 4 * HD), low)
    gains = gains.at[0].set(mixer_gain).at[1].set(feed_gain)
    gains = gains.at[2, : query_gain.shape[0]].set(query_gain)
    gains = gains.at[3, : key_gain.shape[0]].set(key_gain)
    head_part = jnp.concatenate(
        [
            lax.dynamic_slice_in_dim(query_weight, here * pair, pair, 1),
            lax.dynamic_slice_in_dim(key_weight, here * HD, HD, 1),
            lax.dynamic_slice_in_dim(value_weight, here * HD, HD, 1),
        ],
        axis=1,
    )
    first = lax.all_gather(jnp.concatenate([head_part, gains], axis=0), "fsdp", axis=0, tiled=False)
    heads_weight = first[:, :own_rows].reshape(width, 4 * HD)
    gain_rows = first[:, own_rows:].astype(jnp.float32)
    gain_mixer = gain_rows[:, 0].reshape(1, width)
    gain_feed = gain_rows[:, 1].reshape(1, width)
    gain_query = gain_rows[:, 2, : query_gain.shape[0]].reshape(1, HD)
    gain_key = gain_rows[:, 3, : key_gain.shape[0]].reshape(1, HD)
    gain_heads = jnp.concatenate(
        [jnp.tile(gain_query, (1, 2)), jnp.tile(gain_key, (1, 2))], axis=0
    )

    inner = down_weight.shape[0] // count
    wide_inner = inner * shards

    def columns_of(weight):
        split = weight.reshape(own_rows, shards, -1)
        return lax.dynamic_slice_in_dim(split, here * inner, inner, 2).reshape(own_rows, wide_inner)

    proj_rows = own_rows // count
    proj_part = lax.all_gather(
        lax.dynamic_slice_in_dim(output_weight, here * proj_rows, proj_rows, 0),
        "fsdp", axis=0, tiled=True,
    )
    wide_weight = lax.all_gather(
        jnp.concatenate([columns_of(gate_weight), columns_of(up_weight)], axis=1),
        "fsdp", axis=0, tiled=True,
    )
    down_part = lax.all_gather(
        lax.dynamic_slice_in_dim(down_weight, here * inner, inner, 0), "fsdp", axis=0, tiled=True
    )

    input_same, input_other = gather_plane(own_input, count)
    proj_same, proj_other = gather_plane(behind(proj_part, input_other), count)
    grad_same, grad_other = gather_plane(behind(own_grad, input_other), count)
    proj_weight = jnp.concatenate([proj_same, proj_other], axis=0).reshape(
        count, shards * proj_rows, width
    )

    where_at = jnp.arange(stream, dtype=jnp.int32)
    starts = doc_starts[0]
    begins = doc_begin(starts, where_at)
    lanes = jnp.arange(pair) % (HD // 2)
    frequency = ROPE_BASE ** (-(2.0 * lanes.astype(jnp.float32)) / HD)
    angles = (where_at - begins).astype(jnp.float32)[:, None] * frequency[None, :]
    cosine = jnp.cos(angles)
    sine = jnp.sin(angles) * jnp.where(jnp.arange(pair) % HD < HD // 2, -1.0, 1.0)[None, :]

    all_input = jnp.concatenate([input_same, input_other], axis=0)
    normed_in, _ = unit_norm(all_input.astype(jnp.float32))
    hidden_in = (normed_in * gain_mixer).astype(low)
    linear = jnp.dot(hidden_in, heads_weight, preferred_element_type=jnp.float32)

    pairs = stream * stream // 2
    query_att, key_att, value_att, attn, lse, attn_low = whole_call(
        functools.partial(attention_kernel, tokens, count, docs),
        [
            shaped((stream, pair), low),
            shaped((stream, pair), low),
            shaped((stream, pair), low),
            shaped((stream, pair), jnp.float32),
            shaped((count, 1, 2 * tokens), jnp.float32),
            shaped((stream, pair), low),
        ],
        4,
        8 * pairs * HD,
        [pltpu.VMEM((count, HD + 16, tokens), low), pltpu.VMEM((HD + 16, 2 * tokens), jnp.float32)],
        name="attention",
    )(meta, linear, cosine, sine, gain_heads)

    attn_blocks = exchange_plane(attn_low.reshape(count, tokens, pair), count)
    full_proj, attn_rows, mixed, hidden_mid = whole_call(
        functools.partial(project_kernel, count, shards),
        [
            shaped((width, width), low),
            shaped((tokens, width), low),
            shaped((tokens, width), jnp.float32),
            shaped((tokens, width), low),
        ],
        4,
        2 * tokens * width * width,
        name="project",
    )(meta, attn_blocks, proj_weight, own_input, gain_feed)

    hidden_same, hidden_other = gather_plane(hidden_mid, count)
    act_other, wide_other, out_other, back_other = feed_call(
        hidden_other, grad_other, wide_weight, down_part, tokens
    )
    act_same, wide_same, out_same, back_same = feed_call(
        hidden_same, grad_same, wide_weight, down_part, tokens
    )
    back_parts = scatter_plane(back_same, back_other, count)
    grad_mixed, grad_mixed_low, grad_blocks, grad_feed = whole_call(
        functools.partial(feed_back_kernel, count),
        [
            shaped((tokens, width), jnp.float32),
            shaped((tokens, width), low),
            shaped((count, tokens, pair), low),
            shaped((1, width), jnp.float32),
        ],
        8,
        2 * tokens * width * width,
        name="feed_back",
    )(meta, *back_parts, mixed, own_grad, full_proj, gain_feed)

    grad_wide = (
        contract_rows(hidden_same, wide_same) + contract_rows(hidden_other, wide_other)
    ).astype(low)
    grad_down = (contract_rows(act_same, grad_same) + contract_rows(act_other, grad_other)).astype(
        low
    )
    grad_down_part = lax.psum_scatter(grad_down, "fsdp", scatter_dimension=0, tiled=True)
    grad_wide_part = lax.psum_scatter(grad_wide, "fsdp", scatter_dimension=0, tiled=True)

    grad_attn = exchange_plane(grad_blocks, count).reshape(stream, pair)
    grad_linear, gain_sums = whole_call(
        functools.partial(attention_back_kernel, tokens, count, docs),
        [shaped((stream, 2 * pair), low), shaped((8, pair), jnp.float32)],
        10,
        20 * pairs * HD,
        [
            pltpu.VMEM((count, HD, tokens), low),
            pltpu.VMEM((stream, pair), jnp.float32),
            pltpu.VMEM((stream, pair), jnp.float32),
            pltpu.VMEM((stream, pair), jnp.float32),
            pltpu.VMEM((HD, 2 * tokens), jnp.float32),
        ],
        name="attention_back",
    )(meta, linear, cosine, sine, gain_heads, query_att, key_att, value_att, attn, lse, grad_attn)

    out_parts = scatter_plane(behind(out_same, grad_attn), behind(out_other, grad_attn), count)
    block_output = (mixed + sum(part.astype(jnp.float32) for part in out_parts)).astype(low)

    grad_proj = contract_rows(attn_rows, grad_mixed_low).astype(low)
    grad_proj = grad_proj.reshape(shards, count, proj_rows, width)
    order = [lax.bitwise_xor(here, jnp.int32(bits)) for bits in (0, 2, 4, 6, 1, 3, 5, 7)]
    grad_proj = [
        lax.dynamic_index_in_dim(grad_proj, index, 1, keepdims=False).reshape(-1, width)
        for index in order
    ]
    grad_proj = sum(
        part.astype(jnp.float32)
        for part in scatter_plane(
            jnp.concatenate(grad_proj[:4], axis=0), jnp.concatenate(grad_proj[4:], axis=0), count
        )
    ).astype(low)
    grad_proj_part = lax.psum_scatter(grad_proj, "fsdp", scatter_dimension=0, tiled=True)

    grad_hidden_in = contract_cols(grad_linear, heads_weight)
    grad_mixer = jnp.sum(grad_hidden_in * normed_in, axis=0, keepdims=True)
    grad_hidden_low = grad_hidden_in.astype(low)
    grad_in_parts = scatter_plane(grad_hidden_low[: stream // 2], grad_hidden_low[stream // 2 :], count)
    grad_heads = contract_rows(hidden_in, grad_linear).astype(low)
    sums = jnp.zeros((shards, 16, 4 * HD), low)
    sums = sums.at[:, 0].set(grad_mixer.reshape(shards, own_rows).astype(low))
    sums = sums.at[:, 1].set(grad_feed.reshape(shards, own_rows).astype(low))
    query_sums = (gain_sums[0, :HD] + gain_sums[0, HD:]).reshape(shards, -1)
    key_sums = gain_sums[1, :HD].reshape(shards, -1)
    sums = sums.at[:, 2, : query_sums.shape[1]].set(query_sums.astype(low))
    sums = sums.at[:, 3, : key_sums.shape[1]].set(key_sums.astype(low))
    grad_heads_part = lax.psum_scatter(
        jnp.concatenate([grad_heads.reshape(shards, own_rows, 4 * HD), sums], axis=1),
        "fsdp", scatter_dimension=0, tiled=False,
    )

    grad_hidden_own = sum(part.astype(jnp.float32) for part in grad_in_parts)
    own_normed, own_scale = unit_norm(own_input.astype(jnp.float32))
    grad_normed_in, _ = norm_back(grad_hidden_own, own_normed, own_scale, gain_mixer)
    input_grad = grad_mixed + grad_normed_in

    def everywhere(part):
        same, other = gather_plane(part, count)
        return jnp.concatenate([same, other], axis=0).reshape((count,) + part.shape)

    down_blocks = everywhere(behind(grad_down_part, grad_linear))
    wide_blocks = everywhere(behind(grad_wide_part, grad_linear))
    proj_blocks = everywhere(grad_proj_part)
    heads_blocks = everywhere(grad_heads_part)
    out_down = rows_out(meta, down_blocks, "down_out")
    out_proj = rows_out(meta, proj_blocks, "proj_out")
    tile = 64
    out_gate, out_up = pl.pallas_call(
        functools.partial(wide_out_kernel, count, shards),
        grid=(own_rows // tile,),
        in_specs=[
            SCALARS,
            pl.BlockSpec((count, tile, 2 * wide_inner), lambda step: (0, step, 0)),
        ],
        out_specs=[
            pl.BlockSpec((tile, wide_inner * count), lambda step: (step, 0)),
            pl.BlockSpec((tile, wide_inner * count), lambda step: (step, 0)),
        ],
        out_shape=[shaped((own_rows, wide_inner * count), jnp.float32)] * 2,
        name="wide_out",
    )(meta, wide_blocks)
    out_query, out_key, out_value = whole_call(
        functools.partial(heads_out_kernel, count),
        [
            shaped((own_rows, width), jnp.float32),
            shaped((own_rows, KVH * HD), jnp.float32),
            shaped((own_rows, KVH * HD), jnp.float32),
        ],
        1,
        0,
        name="heads_out",
    )(meta, heads_blocks[:, :own_rows])
    gain_out = jnp.sum(heads_blocks[:, own_rows:].astype(jnp.float32), axis=0)
    return (
        block_output[None],
        input_grad[None],
        out_query,
        out_key,
        out_value,
        out_proj,
        out_gate,
        out_up,
        out_down,
        gain_out[0],
        gain_out[1],
        gain_out[2, : query_gain.shape[0]],
        gain_out[3, : key_gain.shape[0]],
    )


def divides_heads(mesh, shapes=None):
    return mesh.shape["ctx"] == KVH and H == 2 * KVH


def solution(mesh):
    in_specs = (
        P("fsdp", "ctx", None),
        P("fsdp", None),
        P("fsdp", "ctx", None),
        P("fsdp", None),
        P("fsdp", None),
        P("fsdp", None),
        P("fsdp", None),
        P("fsdp", None),
        P("fsdp", None),
        P("fsdp", None),
        P("fsdp"),
        P("fsdp"),
        P("fsdp"),
        P("fsdp"),
    )
    out_specs = (
        P("fsdp", "ctx", None),
        P("fsdp", "ctx", None),
        P("fsdp", None),
        P("fsdp", None),
        P("fsdp", None),
        P("fsdp", None),
        P("fsdp", None),
        P("fsdp", None),
        P("fsdp", None),
        P("fsdp"),
        P("fsdp"),
        P("fsdp"),
        P("fsdp"),
    )
    chosen = local_heads if divides_heads(mesh) else local
    return jax.shard_map(chosen, mesh=mesh, in_specs=in_specs, out_specs=out_specs, check_vma=False)
```

```python
import functools
import math

import jax
import jax.numpy as jnp
from jax import lax
from jax.experimental import pallas as pl
from jax.experimental.pallas import tpu as pltpu
from jax.sharding import PartitionSpec as P

H = 16
KVH = 8
HD = 64


EPSILON = 1e-05
ROPE_BASE = 1000000.0
FLOOR_SCORE = -1e30


def place_rows(row_index, tokens, ctx_count):
    half_rows = tokens // 2
    device = row_index // tokens
    offset = row_index % tokens
    early = device * half_rows + offset
    late = (2 * ctx_count - 1 - device) * half_rows + offset - half_rows
    return jnp.where(offset < half_rows, early, late)


def doc_begin(starts, where_at):
    started = starts[None, :] <= where_at[:, None]
    return jnp.max(jnp.where(started, starts[None, :], 0), axis=1)


def rotary(positions):
    half_dim = HD // 2
    frequency = ROPE_BASE ** (-(2.0 * jnp.arange(half_dim, dtype=jnp.float32)) / HD)
    angles = positions.astype(jnp.float32)[:, None] * frequency[None, :]
    angles = jnp.concatenate([angles, angles], axis=1)
    return (jnp.cos(angles)[:, None, :], jnp.sin(angles)[:, None, :])


def rotate_pairs(values, cosine, sine_part):
    half_dim = values.shape[-1] // 2
    rolled = jnp.concatenate([-values[..., half_dim:], values[..., :half_dim]], axis=-1)
    return values * cosine + rolled * sine_part


def rotate_back(grads, cosine, sine_part):
    half_dim = grads.shape[-1] // 2
    moved = grads * sine_part
    rolled = jnp.concatenate([moved[..., half_dim:], -moved[..., :half_dim]], axis=-1)
    return grads * cosine + rolled


def unit_norm(values):
    scaling = lax.rsqrt(jnp.mean(values * values, axis=-1, keepdims=True) + EPSILON)
    return (values * scaling, scaling)


def norm_back(grad_out, normed, scaling, gain_row):
    weighted = grad_out * gain_row
    grad_in = scaling * (weighted - normed * jnp.mean(weighted * normed, axis=-1, keepdims=True))
    grad_gain = jnp.sum((grad_out * normed).reshape(-1, normed.shape[-1]), axis=0)
    return (grad_in, grad_gain)


def score_block(query_rows, key_rows, scaling):
    return (
        jnp.einsum("igrd,jgd->grij", query_rows, key_rows, preferred_element_type=jnp.float32)
        * scaling
    )


def visible_pairs(query_at, query_doc, key_at, key_doc):
    return (query_doc[:, None] == key_doc[None, :]) & (key_at[None, :] <= query_at[:, None])


def any_visible(query_at, query_doc, key_at):
    return (jnp.min(key_at) <= jnp.max(query_at)) & (jnp.max(key_at) >= jnp.min(query_doc))


def contract_rows(left, right):
    return lax.dot_general(
        left, right, (((0,), (0,)), ((), ())), preferred_element_type=jnp.float32
    )


def contract_cols(left, right):
    return lax.dot_general(
        left, right, (((1,), (1,)), ((), ())), preferred_element_type=jnp.float32
    )


def keep_same(totals):
    return totals


def local(
    block_input,
    doc_starts,
    out_grad,
    query_weight,
    key_weight,
    value_weight,
    output_weight,
    gate_weight,
    up_weight,
    down_weight,
    mixer_gain,
    feed_gain,
    query_gain,
    key_gain,
):
    tokens = block_input.shape[1]
    ctx_count = lax.axis_size("ctx")
    repeat = H // KVH
    kv_width = KVH * HD
    scaling = HD ** (-0.5)
    inputs = block_input[0].astype(jnp.float32)
    starts = doc_starts[0]
    where_at = place_rows(
        lax.axis_index("ctx") * tokens + jnp.arange(tokens, dtype=jnp.int32), tokens, ctx_count
    )
    begins = doc_begin(starts, where_at)
    cosine, sine_part = rotary(where_at - begins)
    gathered = (
        lax.all_gather(query_weight, "fsdp", axis=0, tiled=True),
        lax.all_gather(key_weight, "fsdp", axis=0, tiled=True),
        lax.all_gather(value_weight, "fsdp", axis=0, tiled=True),
        lax.all_gather(output_weight, "fsdp", axis=0, tiled=True),
        lax.all_gather(gate_weight, "fsdp", axis=0, tiled=True),
        lax.all_gather(up_weight, "fsdp", axis=0, tiled=True),
        lax.all_gather(down_weight, "fsdp", axis=0, tiled=True),
        lax.all_gather(mixer_gain, "fsdp", axis=0, tiled=True),
        lax.all_gather(feed_gain, "fsdp", axis=0, tiled=True),
        lax.all_gather(query_gain, "fsdp", axis=0, tiled=True),
        lax.all_gather(key_gain, "fsdp", axis=0, tiled=True),
    )
    full_query, full_key, full_value, full_proj, full_gate, full_up, full_down = gathered[:7]
    gain_mixer, gain_feed, gain_query, gain_key = [
        entry.astype(jnp.float32) for entry in gathered[7:]
    ]
    normed_in, scale_in = unit_norm(inputs)
    hidden_in = (normed_in * gain_mixer).astype(jnp.bfloat16)
    query_lin = jnp.dot(hidden_in, full_query, preferred_element_type=jnp.float32)
    key_lin = jnp.dot(hidden_in, full_key, preferred_element_type=jnp.float32)
    value_lin = jnp.dot(hidden_in, full_value, preferred_element_type=jnp.float32)
    query_normed, query_scale = unit_norm(query_lin.reshape(tokens, H, HD))
    key_normed, key_scale = unit_norm(key_lin.reshape(tokens, KVH, HD))
    query_att = (
        rotate_pairs(query_normed * gain_query, cosine, sine_part)
        .reshape(tokens, H * HD)
        .astype(jnp.bfloat16)
    )
    key_att = (
        rotate_pairs(key_normed * gain_key, cosine, sine_part)
        .reshape(tokens, kv_width)
        .astype(jnp.bfloat16)
    )
    value_att = value_lin.astype(jnp.bfloat16)
    query_four = query_att.reshape(tokens, KVH, repeat, HD)
    start_state = (
        jnp.full((KVH, repeat, tokens), FLOOR_SCORE, jnp.float32),
        jnp.zeros((KVH, repeat, tokens), jnp.float32),
        jnp.zeros((tokens, H * HD), jnp.float32),
    )
    key_part = lax.all_gather(key_att, "ctx", axis=0, tiled=True)
    value_part = lax.all_gather(value_att, "ctx", axis=0, tiled=True)
    rows = key_part.shape[0]
    width = math.gcd(math.gcd(rows, tokens // 2), 512)

    def forward_key_block(block_index, totals):
        offset = block_index * width
        key_rows = lax.dynamic_slice_in_dim(key_part, offset, width, 0).reshape(width, KVH, HD)
        value_rows = lax.dynamic_slice_in_dim(value_part, offset, width, 0).reshape(width, KVH, HD)
        key_at = place_rows(offset + jnp.arange(width, dtype=jnp.int32), tokens, ctx_count)

        def attend(totals):
            highest, total_mass, accum = totals
            visible = visible_pairs(where_at, begins, key_at, doc_begin(starts, key_at))
            scores = jnp.where(visible, score_block(query_four, key_rows, scaling), FLOOR_SCORE)
            new_high = jnp.maximum(highest, jnp.max(scores, axis=-1))
            rescale = jnp.exp(highest - new_high)
            probable = jnp.where(visible, jnp.exp(scores - new_high[..., None]), 0.0)
            total_mass = total_mass * rescale + jnp.sum(probable, axis=-1)
            part_out = jnp.einsum(
                "grij,jgd->igrd",
                probable.astype(jnp.bfloat16),
                value_rows,
                preferred_element_type=jnp.float32,
            )
            accum = (
                accum.reshape(tokens, KVH, repeat, HD)
                * jnp.transpose(rescale, (2, 0, 1))[..., None]
                + part_out
            )
            return (new_high, total_mass, accum.reshape(tokens, H * HD))

        return lax.cond(any_visible(where_at, begins, key_at), attend, keep_same, totals)

    highest, total_mass, accum = lax.fori_loop(0, rows // width, forward_key_block, start_state)
    lse_heads = highest + jnp.log(total_mass)
    attn_raw = (
        accum.reshape(tokens, KVH, repeat, HD) / jnp.transpose(total_mass, (2, 0, 1))[..., None]
    ).reshape(tokens, H * HD)
    attn_low = attn_raw.astype(jnp.bfloat16)
    mixed = inputs + jnp.dot(attn_low, full_proj, preferred_element_type=jnp.float32)
    normed_mid, scale_mid = unit_norm(mixed)
    hidden_mid = (normed_mid * gain_feed).astype(jnp.bfloat16)
    gate_lin = jnp.dot(hidden_mid, full_gate, preferred_element_type=jnp.float32)
    up_lin = jnp.dot(hidden_mid, full_up, preferred_element_type=jnp.float32)
    sigmoid_gate = jax.nn.sigmoid(gate_lin)
    activated = (gate_lin * sigmoid_gate * up_lin).astype(jnp.bfloat16)
    block_output = (
        mixed + jnp.dot(activated, full_down, preferred_element_type=jnp.float32)
    ).astype(jnp.bfloat16)
    regathered = (
        lax.all_gather(query_weight, "fsdp", axis=0, tiled=True),
        lax.all_gather(key_weight, "fsdp", axis=0, tiled=True),
        lax.all_gather(value_weight, "fsdp", axis=0, tiled=True),
        lax.all_gather(output_weight, "fsdp", axis=0, tiled=True),
        lax.all_gather(gate_weight, "fsdp", axis=0, tiled=True),
        lax.all_gather(up_weight, "fsdp", axis=0, tiled=True),
        lax.all_gather(down_weight, "fsdp", axis=0, tiled=True),
        lax.all_gather(mixer_gain, "fsdp", axis=0, tiled=True),
        lax.all_gather(feed_gain, "fsdp", axis=0, tiled=True),
        lax.all_gather(query_gain, "fsdp", axis=0, tiled=True),
        lax.all_gather(key_gain, "fsdp", axis=0, tiled=True),
    )
    full_query, full_key, full_value, full_proj, full_gate, full_up, full_down = regathered[:7]
    gain_mixer, gain_feed, gain_query, gain_key = [
        entry.astype(jnp.float32) for entry in regathered[7:]
    ]
    grad_top = out_grad[0].astype(jnp.float32)
    grad_top_low = grad_top.astype(jnp.bfloat16)
    grad_down = contract_rows(activated, grad_top_low)
    grad_act = contract_cols(grad_top_low, full_down)
    grad_gate_low = (
        grad_act * up_lin * sigmoid_gate * (1.0 + gate_lin * (1.0 - sigmoid_gate))
    ).astype(jnp.bfloat16)
    grad_up_low = (grad_act * gate_lin * sigmoid_gate).astype(jnp.bfloat16)
    grad_gate = contract_rows(hidden_mid, grad_gate_low)
    grad_up = contract_rows(hidden_mid, grad_up_low)
    grad_hidden_mid = contract_cols(grad_gate_low, full_gate) + contract_cols(grad_up_low, full_up)
    grad_normed_mid, grad_feed = norm_back(grad_hidden_mid, normed_mid, scale_mid, gain_feed)
    grad_mixed = grad_top + grad_normed_mid
    grad_mixed_low = grad_mixed.astype(jnp.bfloat16)
    grad_proj = contract_rows(attn_low, grad_mixed_low)
    grad_attn = contract_cols(grad_mixed_low, full_proj).astype(jnp.bfloat16)
    grad_four = grad_attn.reshape(tokens, KVH, repeat, HD)
    delta_heads = jnp.sum(
        grad_four.astype(jnp.float32) * attn_raw.reshape(tokens, KVH, repeat, HD), axis=-1
    )
    delta_grid = jnp.transpose(delta_heads, (1, 2, 0))
    lse_rows = jnp.transpose(lse_heads, (2, 0, 1)).reshape(tokens, H)
    delta_rows = delta_heads.reshape(tokens, H)
    query_key_part = lax.all_gather(key_att, "ctx", axis=0, tiled=True)
    query_value_part = lax.all_gather(value_att, "ctx", axis=0, tiled=True)
    rows = query_key_part.shape[0]
    query_width = math.gcd(math.gcd(rows, tokens // 2), 512)

    def query_key_block(block_index, grad_query_acc):
        offset = block_index * query_width
        key_rows = lax.dynamic_slice_in_dim(query_key_part, offset, query_width, 0).reshape(
            query_width, KVH, HD
        )
        value_rows = lax.dynamic_slice_in_dim(query_value_part, offset, query_width, 0).reshape(
            query_width, KVH, HD
        )
        key_at = place_rows(offset + jnp.arange(query_width, dtype=jnp.int32), tokens, ctx_count)

        def attend(grad_query_acc):
            visible = visible_pairs(where_at, begins, key_at, doc_begin(starts, key_at))
            scores = score_block(query_four, key_rows, scaling)
            probable = jnp.where(visible, jnp.exp(scores - lse_heads[..., None]), 0.0)
            grad_prob = jnp.einsum(
                "igrd,jgd->grij", grad_four, value_rows, preferred_element_type=jnp.float32
            )
            grad_score = (probable * (grad_prob - delta_grid[..., None])).astype(jnp.bfloat16)
            added = (
                jnp.einsum(
                    "grij,jgd->igrd", grad_score, key_rows, preferred_element_type=jnp.float32
                )
                * scaling
            )
            return grad_query_acc + added.reshape(tokens, H * HD)

        return lax.cond(any_visible(where_at, begins, key_at), attend, keep_same, grad_query_acc)

    grad_query_att = lax.fori_loop(
        0, rows // query_width, query_key_block, jnp.zeros((tokens, H * HD), jnp.float32)
    )
    lse_all, delta_all = (
        lax.all_gather(lse_rows.astype(jnp.bfloat16), "ctx", axis=0, tiled=True).astype(
            lse_rows.dtype
        ),
        lax.all_gather(delta_rows.astype(jnp.bfloat16), "ctx", axis=0, tiled=True).astype(
            delta_rows.dtype
        ),
    )
    key_three = key_att.reshape(tokens, KVH, HD)
    value_three = value_att.reshape(tokens, KVH, HD)
    empty_keys = jnp.zeros((tokens, kv_width), jnp.float32)
    query_part = lax.all_gather(query_att, "ctx", axis=0, tiled=True)
    grad_part = lax.all_gather(grad_attn, "ctx", axis=0, tiled=True)
    rows = query_part.shape[0]
    key_width = math.gcd(math.gcd(rows, tokens // 2), 512)

    def query_block(block_index, totals):
        offset = block_index * key_width
        query_rows = lax.dynamic_slice_in_dim(query_part, offset, key_width, 0).reshape(
            key_width, KVH, repeat, HD
        )
        grad_rows = lax.dynamic_slice_in_dim(grad_part, offset, key_width, 0).reshape(
            key_width, KVH, repeat, HD
        )
        query_at = place_rows(offset + jnp.arange(key_width, dtype=jnp.int32), tokens, ctx_count)
        query_doc = doc_begin(starts, query_at)
        lse_block = jnp.transpose(
            lax.dynamic_slice_in_dim(lse_all, offset, key_width, 0).reshape(key_width, KVH, repeat),
            (1, 2, 0),
        )
        delta_block = jnp.transpose(
            lax.dynamic_slice_in_dim(delta_all, offset, key_width, 0).reshape(
                key_width, KVH, repeat
            ),
            (1, 2, 0),
        )

        def attend(totals):
            grad_key_acc, grad_value_acc = totals
            visible = visible_pairs(query_at, query_doc, where_at, begins)
            scores = score_block(query_rows, key_three, scaling)
            probable = jnp.where(visible, jnp.exp(scores - lse_block[..., None]), 0.0)
            grad_prob = jnp.einsum(
                "igrd,jgd->grij", grad_rows, value_three, preferred_element_type=jnp.float32
            )
            grad_score = (probable * (grad_prob - delta_block[..., None])).astype(jnp.bfloat16)
            value_added = jnp.einsum(
                "grij,igrd->jgd",
                probable.astype(jnp.bfloat16),
                grad_rows,
                preferred_element_type=jnp.float32,
            )
            key_added = (
                jnp.einsum(
                    "grij,igrd->jgd", grad_score, query_rows, preferred_element_type=jnp.float32
                )
                * scaling
            )
            return (
                grad_key_acc + key_added.reshape(tokens, kv_width),
                grad_value_acc + value_added.reshape(tokens, kv_width),
            )

        return lax.cond(any_visible(query_at, query_doc, where_at), attend, keep_same, totals)

    grad_key_att, grad_value_att = lax.fori_loop(
        0, rows // key_width, query_block, (empty_keys, empty_keys)
    )
    grad_query_unit = rotate_back(grad_query_att.reshape(tokens, H, HD), cosine, sine_part)
    grad_query_lin, grad_qgain = norm_back(grad_query_unit, query_normed, query_scale, gain_query)
    grad_key_unit = rotate_back(grad_key_att.reshape(tokens, KVH, HD), cosine, sine_part)
    grad_key_lin, grad_kgain = norm_back(grad_key_unit, key_normed, key_scale, gain_key)
    grad_query_low = grad_query_lin.reshape(tokens, H * HD).astype(jnp.bfloat16)
    grad_key_low = grad_key_lin.reshape(tokens, kv_width).astype(jnp.bfloat16)
    grad_value_low = grad_value_att.astype(jnp.bfloat16)
    grad_query = contract_rows(hidden_in, grad_query_low)
    grad_key = contract_rows(hidden_in, grad_key_low)
    grad_value = contract_rows(hidden_in, grad_value_low)
    grad_hidden_in = (
        contract_cols(grad_query_low, full_query)
        + contract_cols(grad_key_low, full_key)
        + contract_cols(grad_value_low, full_value)
    )
    grad_normed_in, grad_mixer = norm_back(grad_hidden_in, normed_in, scale_in, gain_mixer)
    input_grad = grad_mixed + grad_normed_in
    parts = (
        lax.psum_scatter(
            grad_query.astype(jnp.bfloat16), "fsdp", scatter_dimension=0, tiled=True
        ).astype(jnp.float32),
        lax.psum_scatter(
            grad_key.astype(jnp.bfloat16), "fsdp", scatter_dimension=0, tiled=True
        ).astype(jnp.float32),
        lax.psum_scatter(
            grad_value.astype(jnp.bfloat16), "fsdp", scatter_dimension=0, tiled=True
        ).astype(jnp.float32),
        lax.psum_scatter(
            grad_proj.astype(jnp.bfloat16), "fsdp", scatter_dimension=0, tiled=True
        ).astype(jnp.float32),
        lax.psum_scatter(
            grad_gate.astype(jnp.bfloat16), "fsdp", scatter_dimension=0, tiled=True
        ).astype(jnp.float32),
        lax.psum_scatter(
            grad_up.astype(jnp.bfloat16), "fsdp", scatter_dimension=0, tiled=True
        ).astype(jnp.float32),
        lax.psum_scatter(
            grad_down.astype(jnp.bfloat16), "fsdp", scatter_dimension=0, tiled=True
        ).astype(jnp.float32),
        lax.psum_scatter(
            grad_mixer.astype(jnp.bfloat16), "fsdp", scatter_dimension=0, tiled=True
        ).astype(jnp.float32),
        lax.psum_scatter(
            grad_feed.astype(jnp.bfloat16), "fsdp", scatter_dimension=0, tiled=True
        ).astype(jnp.float32),
        lax.psum_scatter(
            grad_qgain.astype(jnp.bfloat16), "fsdp", scatter_dimension=0, tiled=True
        ).astype(jnp.float32),
        lax.psum_scatter(
            grad_kgain.astype(jnp.bfloat16), "fsdp", scatter_dimension=0, tiled=True
        ).astype(jnp.float32),
    )
    summed = (
        lax.psum(parts[0].astype(jnp.bfloat16), "ctx").astype(jnp.float32),
        lax.psum(parts[1].astype(jnp.bfloat16), "ctx").astype(jnp.float32),
        lax.psum(parts[2].astype(jnp.bfloat16), "ctx").astype(jnp.float32),
        lax.psum(parts[3].astype(jnp.bfloat16), "ctx").astype(jnp.float32),
        lax.psum(parts[4].astype(jnp.bfloat16), "ctx").astype(jnp.float32),
        lax.psum(parts[5].astype(jnp.bfloat16), "ctx").astype(jnp.float32),
        lax.psum(parts[6].astype(jnp.bfloat16), "ctx").astype(jnp.float32),
        lax.psum(parts[7].astype(jnp.bfloat16), "ctx").astype(jnp.float32),
        lax.psum(parts[8].astype(jnp.bfloat16), "ctx").astype(jnp.float32),
        lax.psum(parts[9].astype(jnp.bfloat16), "ctx").astype(jnp.float32),
        lax.psum(parts[10].astype(jnp.bfloat16), "ctx").astype(jnp.float32),
    )
    return (
        block_output[None],
        input_grad[None],
        summed[0],
        summed[1],
        summed[2],
        summed[3],
        summed[4],
        summed[5],
        summed[6],
        summed[7],
        summed[8],
        summed[9],
        summed[10],
    )


ORDER = (0, 1, 2, 4, 3, 5, 6, 7)


def flipped(bits, count):
    return [(index, index ^ bits) for index in range(count)]


def swap_ctx(values, bits):
    return lax.ppermute(values, "ctx", flipped(bits, lax.axis_size("ctx")))


def swap_fsdp(values, bits):
    return lax.ppermute(values, "fsdp", flipped(bits, lax.axis_size("fsdp")))


def behind(values, *ready):
    return lax.optimization_barrier((values,) + ready)[0]


def dot_nn(left, right):
    return lax.dot_general(
        left, right, (((1,), (0,)), ((), ())), preferred_element_type=jnp.float32
    )


def dot_nt(left, right):
    return lax.dot_general(
        left, right, (((1,), (1,)), ((), ())), preferred_element_type=jnp.float32
    )


def wide(values):
    return values.astype(jnp.float32)


def gather_plane(block):
    half = block.shape[0] // 2
    across = swap_ctx(block, 2)
    along = swap_ctx(block, 4)
    partner = swap_ctx(block, 1)
    corner_low = swap_ctx(along[:half], 2)
    corner_high = swap_ctx(across[half:], 4)
    across_other = swap_ctx(across, 1)
    along_other = swap_ctx(along, 1)
    corner = jnp.concatenate([corner_low, corner_high], axis=0)
    corner_other = swap_ctx(corner, 1)
    return [block, partner, across, across_other, along, along_other, corner, corner_other]


def scatter_plane(blocks):
    got = [swap_ctx(blocks[bits], 1) for bits in (3, 5, 7, 1)]
    sent = [
        swap_ctx((wide(blocks[bits]) + wide(other)).astype(jnp.bfloat16), bits)
        for bits, other in zip((2, 4, 6), got)
    ]
    return [blocks[0], got[3]] + sent


def exchange_plane(blocks):
    return [blocks[0]] + [swap_ctx(blocks[bits], bits) for bits in range(1, 8)]


def gather_fsdp(block):
    return [block] + [swap_fsdp(block, bits) for bits in (1, 2, 3)]


def slot_of(bits):
    return jnp.where(bits == 3, 4, jnp.where(bits == 4, 3, bits))


def row_of(place, here, tokens, count):
    half = tokens // 2
    device = jnp.where(place < count, place, 2 * count - 1 - place)
    late = jnp.where(place < count, 0, half)
    return slot_of(lax.bitwise_xor(device, here)) * tokens + late


def swap_half(values, low_lane):
    return jnp.where(low_lane, pltpu.roll(values, 96, 1), pltpu.roll(values, 32, 1))


def head_mean(values, first):
    lower = jnp.sum(jnp.where(first, values, 0.0), axis=1, keepdims=True)
    upper = jnp.sum(jnp.where(first, 0.0, values), axis=1, keepdims=True)
    return jnp.where(first, lower, upper) * (1.0 / HD)


def lane_masks(rows):
    lanes = lax.broadcasted_iota(jnp.int32, (rows, 2 * HD), 1)
    return lanes < HD, (lanes % HD) < (HD // 2)


def two_heads(values):
    first, _ = lane_masks(values.shape[0])
    zero = jnp.zeros_like(values)
    return jnp.concatenate(
        [jnp.where(first, values, zero), jnp.where(first, zero, values)], axis=0
    )


def begin_at(meta_ref, docs, where_at):
    begin = jnp.zeros_like(where_at)
    for doc in range(docs):
        begin = jnp.where(meta_ref[2 + doc] <= where_at, meta_ref[2 + doc], begin)
    return begin


def block_visible(meta_ref, docs, query_block, key_block, size):
    query_at = query_block * size + lax.broadcasted_iota(jnp.int32, (1, size), 1)
    begin = begin_at(meta_ref, docs, query_at)
    key_at = key_block * size + lax.broadcasted_iota(jnp.int32, (size, size), 0)
    return (key_at <= query_at) & (key_at >= begin)


def aligned(value, size):
    return pl.multiple_of(value, size)


def take_heads_kernel(
    meta_ref, query_ref, key_ref, value_ref, proj_ref, mixer_ref, feed_ref, query_gain_ref, key_gain_ref,
    out_ref, gains,
):
    here = meta_ref[0]
    rows = query_ref.shape[0]
    pair = 2 * HD
    out_ref[:rows, :pair] = query_ref[:, pl.ds(aligned(here * pair, pair), pair)]
    start = aligned(lax.shift_right_logical(here, 1) * pair, pair)
    odd = lax.bitwise_and(here, 1) == 1
    keys = wide(key_ref[:, pl.ds(start, pair)])
    values = wide(value_ref[:, pl.ds(start, pair)])
    first, _ = lane_masks(rows)
    keys = jnp.where(odd, pltpu.roll(keys, HD, 1), keys)
    values = jnp.where(odd, values, pltpu.roll(values, HD, 1))
    out_ref[:rows, pair:] = jnp.where(first, keys, values).astype(jnp.bfloat16)
    gains[...] = jnp.zeros_like(gains)
    gains[0:1, :] = wide(mixer_ref[...])
    gains[1:2, :] = wide(feed_ref[...])
    gains[2:3, : query_gain_ref.shape[1]] = wide(query_gain_ref[...])
    gains[3:4, : key_gain_ref.shape[1]] = wide(key_gain_ref[...])
    extra = gains.shape[0]
    out_ref[rows : rows + extra, :] = gains[...].astype(jnp.bfloat16)
    count = proj_ref.shape[1] // (2 * pair)
    part = (out_ref.shape[0] - rows - extra) // count
    for index in range(count):
        target = rows + extra + index * part
        out_ref[target : target + part, :] = proj_ref[
            pl.ds(aligned(here * part, part), part), index * 2 * pair : (index + 1) * 2 * pair
        ]


def arrange_heads_kernel(
    extra, meta_ref, *refs
):
    pieces, (weight_ref, mixer_ref, feed_ref, gains_ref, proj_ref) = refs[:4], refs[4:]
    shard = meta_ref[1]
    rows = weight_ref.shape[0] // 4
    pair = 2 * HD
    each = HD // 4
    gains = jnp.zeros((8, pair), jnp.float32)
    part = proj_ref.shape[0] // 4
    for bits, piece in enumerate(pieces):
        owner = lax.bitwise_xor(shard, bits)
        weight_ref[pl.ds(aligned(owner * rows, rows), rows), :] = piece[:rows, :]
        block = wide(piece[rows : rows + extra, :])
        lanes = pl.ds(aligned(owner * rows, rows), rows)
        mixer_ref[:, lanes] = block[0:1, :]
        feed_ref[:, lanes] = block[1:2, :]
        gains = gains + pltpu.roll(block[:8, :pair], owner * each, 1)
        for index in range(proj_ref.shape[1] // (2 * pair)):
            source = rows + extra + index * part
            proj_ref[
                pl.ds(aligned(owner * part, part), part), index * 2 * pair : (index + 1) * 2 * pair
            ] = piece[source : source + part, :]
    gains_ref[...] = gains + pltpu.roll(gains, HD, 1)


def wide_column(column, main, rest):
    late = (column >= 2 * main).astype(jnp.int32)
    late_up = (column >= 2 * main + rest).astype(jnp.int32)
    early_up = (column >= main).astype(jnp.int32) * (1 - late)
    is_up = late * late_up + early_up
    return is_up, column - early_up * main - late * (main + late_up * rest)


def take_wide_kernel(shards, meta_ref, gate_ref, up_ref, out_ref, window, sem):
    here = meta_ref[0]
    inner = out_ref.shape[1] // 2
    piece = inner // shards
    span = window.shape[2]
    shift = here * (piece - 128)
    copies = []
    for kind, source in enumerate((gate_ref, up_ref)):
        for part in range(shards):
            start = aligned(part * (source.shape[1] // shards) + here * 128, 128)
            copies.append(
                pltpu.make_async_copy(
                    source.at[:, pl.ds(start, span)],
                    window.at[kind * shards + part],
                    sem.at[kind * shards + part],
                )
            )
    for copy in copies:
        copy.start()
    columns = lax.broadcasted_iota(jnp.int32, (1, 2 * inner), 1)
    main = inner // 128 * 128
    is_up, unit = wide_column(columns, main, inner - main)
    owner = jnp.zeros_like(unit)
    for part in range(1, shards):
        owner = jnp.where(unit >= part * piece, part, owner)
    target = unit - owner * piece + shift
    owner = owner + is_up * shards
    rows = lax.broadcasted_iota(jnp.int32, (span, 2 * inner), 0)
    total = jnp.zeros(out_ref.shape, jnp.float32)
    for index, copy in enumerate(copies):
        copy.wait()
        place = jnp.where(owner == index, target, -1)
        chosen = jnp.where(rows == place, 1.0, 0.0).astype(jnp.bfloat16)
        total = total + dot_nn(window[index], chosen)
    out_ref[...] = total.astype(jnp.bfloat16)


def arrange_feed_kernel(meta_ref, *refs):
    wide_pieces, down_pieces, (wide_ref, down_ref) = refs[:4], refs[4:8], refs[8:]
    shard = meta_ref[1]
    rows = wide_pieces[0].shape[0]
    inner = down_pieces[0].shape[0]
    for bits in range(4):
        owner = lax.bitwise_xor(shard, bits)
        wide_ref[pl.ds(aligned(owner * rows, rows), rows), :] = wide_pieces[bits][...]
        down_ref[pl.ds(aligned(owner * inner, 16), inner), :] = down_pieces[bits][...]
    down_ref[4 * inner :, :] = jnp.zeros_like(down_ref[4 * inner :, :])


def head_linear_kernel(
    meta_ref, first_ref, second_ref, weight_ref, gain_ref, *refs
):
    hidden_ref, linear_ref = refs[-2:]
    rows = first_ref.shape[0]
    for index, source in enumerate((first_ref, second_ref)):
        values = wide(source[...])
        scale = lax.rsqrt(jnp.mean(values * values, axis=1, keepdims=True) + EPSILON)
        hidden = (values * scale * gain_ref[...]).astype(jnp.bfloat16)
        hidden_ref[index * rows : (index + 1) * rows, :] = hidden
        linear_ref[index * rows : (index + 1) * rows, :] = dot_nn(hidden, weight_ref[...])


def attention_kernel(
    tokens, count, docs,
    meta_ref, lin_ref, cos_ref, sin_ref, gains_ref,
    query_ref, key_ref, value_ref, attn_ref, lse_ref, *refs,
):
    low_refs, (value_t, accum, low) = refs[:count], refs[count:]
    here = meta_ref[0]
    half = tokens // 2
    size = tokens
    blocks = count

    def prepare(place, carry):
        first, low_lane = lane_masks(half)
        source = aligned(row_of(place, here, tokens, count), half)
        target = aligned(place * half, half)
        cosine = cos_ref[pl.ds(target, half), :]
        sine = sin_ref[pl.ds(target, half), :]
        query = lin_ref[pl.ds(source, half), : 2 * HD]
        unit = query * lax.rsqrt(head_mean(query * query, first) + EPSILON) * gains_ref[2:3, :]
        turned = unit * cosine + swap_half(unit, low_lane) * sine
        query_ref[pl.ds(target, half), :] = (
            turned.astype(jnp.bfloat16).astype(jnp.float32) * (HD**-0.5)
        ).astype(jnp.bfloat16)
        both = lin_ref[pl.ds(source, half), 2 * HD :]
        unit = both * lax.rsqrt(head_mean(both * both, first) + EPSILON) * gains_ref[3:4, :]
        turned = unit * cosine + swap_half(unit, low_lane) * sine
        key_ref[pl.ds(target, half), :] = jnp.where(
            first, turned, pltpu.roll(turned, HD, 1)
        ).astype(jnp.bfloat16)
        values = jnp.where(first, pltpu.roll(both, HD, 1), both)
        value_ref[pl.ds(target, half), :] = values.astype(jnp.bfloat16)
        return carry

    lax.fori_loop(0, 2 * count, prepare, 0)

    def turn_values(block, carry):
        values = wide(value_ref[pl.ds(aligned(block * size, size), size), :])
        value_t[block, :HD, :] = values.T[:HD].astype(jnp.bfloat16)
        value_t[block, HD:, :] = jnp.ones((value_t.shape[1] - HD, size), jnp.bfloat16)
        return carry

    lax.fori_loop(0, blocks, turn_values, 0)

    def query_step(block, carry):
        query = two_heads(query_ref[pl.ds(aligned(block * size, size), size), :])
        accum[...] = jnp.zeros_like(accum)
        lowest = begin_at(meta_ref, docs, block * size) // size

        def key_step(other, carry):
            keys = key_ref[pl.ds(aligned(other * size, size), size), :]
            scores = dot_nt(keys, query)
            visible = block_visible(meta_ref, docs, block, other, size)
            probable = jnp.concatenate(
                [
                    jnp.where(visible, jnp.exp(scores[:, :size]), 0.0),
                    jnp.where(visible, jnp.exp(scores[:, size:]), 0.0),
                ],
                axis=1,
            ).astype(jnp.bfloat16)
            accum[...] += dot_nn(value_t[other], probable)
            return carry

        lax.fori_loop(lowest, block + 1, key_step, 0)
        mass = accum[HD : HD + 1, :]
        mixed = accum[:HD, :] / mass
        lse_ref[block] = jnp.log(mass)
        rows = jnp.concatenate([mixed[:, :size], mixed[:, size:]], axis=0).T
        attn_ref[pl.ds(aligned(block * size, size), size), :] = rows
        for part in range(2):
            target = aligned(row_of(2 * block + part, here, tokens, count), half)
            low[pl.ds(target, half), :] = rows[part * half : (part + 1) * half].astype(jnp.bfloat16)
        return carry

    lax.fori_loop(0, blocks, query_step, 0)
    for slot, bits in enumerate(ORDER):
        low_refs[bits][...] = low[slot * tokens : (slot + 1) * tokens, :]


def attention_back_kernel(
    tokens, count, docs,
    meta_ref, lin_ref, cos_ref, sin_ref, gains_ref,
    query_ref, key_ref, value_ref, attn_ref, lse_ref, *refs,
):
    grad_refs = refs[:count]
    out_ref, gain_ref, key_t, grad_query, grad_key, grad_value, accum, grad_rows = refs[count:]
    here = meta_ref[0]
    half = tokens // 2
    size = tokens
    blocks = count
    grad_key[...] = jnp.zeros_like(grad_key)
    grad_value[...] = jnp.zeros_like(grad_value)
    gain_ref[...] = jnp.zeros_like(gain_ref)
    for slot, bits in enumerate(ORDER):
        grad_rows[slot * tokens : (slot + 1) * tokens, :] = grad_refs[bits][...]

    def turn_keys(block, carry):
        keys = wide(key_ref[pl.ds(aligned(block * size, size), size), :])
        key_t[block] = keys.T[:HD].astype(jnp.bfloat16)
        return carry

    lax.fori_loop(0, blocks, turn_keys, 0)

    def query_step(block, carry):
        here_rows = pl.ds(aligned(block * size, size), size)
        query = two_heads(query_ref[here_rows, :])
        parts = []
        for part in range(2):
            source = aligned(row_of(2 * block + part, here, tokens, count), half)
            parts.append(grad_rows[pl.ds(source, half), :])
        grads = jnp.concatenate(parts, axis=0)
        products = (wide(grads) * attn_ref[here_rows, :]).T
        deltas = (
            jnp.sum(products[:HD], axis=0, keepdims=True),
            jnp.sum(products[HD:], axis=0, keepdims=True),
        )
        grads = two_heads(grads)
        lse = lse_ref[block]
        accum[...] = jnp.zeros_like(accum)
        lowest = begin_at(meta_ref, docs, block * size) // size

        def key_step(other, carry):
            rows = pl.ds(aligned(other * size, size), size)
            scores = dot_nt(key_ref[rows, :], query)
            grad_prob = dot_nt(value_ref[rows, :], grads)
            visible = block_visible(meta_ref, docs, block, other, size)
            probs, grad_scores = [], []
            for head in range(2):
                cols = slice(head * size, (head + 1) * size)
                prob = jnp.where(visible, jnp.exp(scores[:, cols] - lse[:, cols]), 0.0)
                probs.append(prob)
                grad_scores.append(prob * (grad_prob[:, cols] - deltas[head]))
            probs = jnp.concatenate(probs, axis=1).astype(jnp.bfloat16)
            grad_scores = jnp.concatenate(grad_scores, axis=1).astype(jnp.bfloat16)
            grad_value[rows, :] += dot_nn(probs, grads)
            grad_key[rows, :] += dot_nn(grad_scores, query)
            accum[...] += dot_nn(key_t[other], grad_scores)
            return carry

        lax.fori_loop(lowest, block + 1, key_step, 0)
        total = accum[...] * (HD**-0.5)
        grad_query[here_rows, :] = jnp.concatenate([total[:, :size], total[:, size:]], axis=0).T
        return carry

    lax.fori_loop(0, blocks, query_step, 0)

    def finish(place, carry):
        first, low_lane = lane_masks(half)
        source = aligned(row_of(place, here, tokens, count), half)
        target = pl.ds(aligned(place * half, half), half)
        cosine = cos_ref[target, :]
        sine = sin_ref[target, :]

        def through(linear, grads, gain):
            scale = lax.rsqrt(head_mean(linear * linear, first) + EPSILON)
            normed = linear * scale
            turned = grads * cosine + swap_half(grads * sine, low_lane)
            weighted = turned * gain
            grad_in = scale * (weighted - normed * head_mean(weighted * normed, first))
            return grad_in, jnp.sum(turned * normed, axis=0, keepdims=True)

        grad_in, gain_row = through(
            lin_ref[pl.ds(source, half), : 2 * HD], grad_query[target, :], gains_ref[2:3, :]
        )
        out_ref[pl.ds(source, half), : 2 * HD] = grad_in.astype(jnp.bfloat16)
        gain_ref[0:1, :] += gain_row
        keys = grad_key[target, :]
        grad_in, gain_row = through(
            lin_ref[pl.ds(source, half), 2 * HD :], keys + pltpu.roll(keys, HD, 1), gains_ref[3:4, :]
        )
        gain_ref[1:2, :] += gain_row
        values = grad_value[target, :]
        values = values + pltpu.roll(values, HD, 1)
        out_ref[pl.ds(source, half), 2 * HD :] = jnp.where(first, grad_in, values).astype(
            jnp.bfloat16
        )
        return carry

    lax.fori_loop(0, 2 * count, finish, 0)


def project_kernel(count, parts, start, meta_ref, *refs):
    attn_refs, weight_refs, rest = refs[:count], refs[count : 2 * count], refs[2 * count :]
    input_ref, gain_ref, full_ref, attn_out_ref, mixed_ref, hidden_ref, attn = rest
    here = meta_ref[0]
    total = weight_refs[0].shape[0] - start
    rows = total // parts
    for bits in range(count):
        owner = lax.bitwise_xor(here, bits)
        for part in range(parts):
            target = aligned(part * count * rows + owner * rows, rows)
            source = start + part * rows
            full_ref[pl.ds(target, rows), :] = weight_refs[bits][source : source + rows, :]
        attn_out_ref[:, pl.ds(aligned(owner * 2 * HD, 2 * HD), 2 * HD)] = attn_refs[bits][...]
    mixed = wide(input_ref[...]) + dot_nn(attn_out_ref[...], full_ref[...])
    mixed_ref[...] = mixed
    scale = lax.rsqrt(jnp.mean(mixed * mixed, axis=1, keepdims=True) + EPSILON)
    hidden_ref[...] = (mixed * scale * gain_ref[...]).astype(jnp.bfloat16)


def feed_kernel(
    meta_ref, first_ref, second_ref, grad_first_ref, grad_second_ref, wide_ref, down_ref, *refs
):
    refs = refs[-10:]
    hidden_ref, grad_ref, act_ref, grad_wide_ref = refs[:4]
    out_refs, back_refs, (out_low, back_low) = refs[4:6], refs[6:8], refs[8:]
    tokens = first_ref.shape[0]
    inner = wide_ref.shape[1] // 2
    main = inner // 128 * 128
    hidden_ref[:tokens, :] = first_ref[...]
    hidden_ref[tokens:, :] = second_ref[...]
    grad_ref[:tokens, :] = grad_first_ref[:tokens, :]
    grad_ref[tokens:, :] = grad_second_ref[:tokens, :]
    first, _ = lane_masks(tokens)

    def activate(gate, up, grad_act):
        sigmoid = 1.0 / (1.0 + jnp.exp(-gate))
        silu = gate * sigmoid
        grad_gate = grad_act * up * sigmoid * (1.0 + gate * (1.0 - sigmoid))
        return silu * up, grad_gate, grad_act * silu

    def step(index, carry):
        rows = pl.ds(aligned(index * tokens, tokens), tokens)
        both = dot_nn(hidden_ref[rows, :], wide_ref[...])
        grad_act = dot_nt(grad_ref[rows, :], down_ref[...])
        act, grad_gate, grad_up = activate(
            both[:, :main], both[:, main : 2 * main], grad_act[:, :main]
        )
        act_ref[rows, :main] = act.astype(jnp.bfloat16)
        grad_wide_ref[rows, :main] = grad_gate.astype(jnp.bfloat16)
        grad_wide_ref[rows, main : 2 * main] = grad_up.astype(jnp.bfloat16)
        last = both[:, 2 * main :]
        act, grad_gate, grad_up = activate(last, pltpu.roll(last, HD, 1), grad_act[:, main:])
        act_ref[rows, main:] = jnp.where(first, act, 0.0).astype(jnp.bfloat16)
        grad_wide_ref[rows, 2 * main :] = jnp.where(
            first, grad_gate, pltpu.roll(grad_up, HD, 1)
        ).astype(jnp.bfloat16)
        back_low[index] = dot_nt(grad_wide_ref[rows, :], wide_ref[...]).astype(jnp.bfloat16)
        out_low[index] = dot_nn(act_ref[rows, :], down_ref[...]).astype(jnp.bfloat16)
        return carry

    lax.fori_loop(0, 2, step, 0)
    for index in range(2):
        out_refs[index][...] = out_low[index]
        back_refs[index][...] = back_low[index]


def feed_back_kernel(count, meta_ref, *refs):
    sums, rest = refs[:5], refs[5:]
    mixed_ref, grad_ref, full_ref, gain_ref, grad_mixed_ref, grad_low_ref, grad_gain_ref = rest[:7]
    block_refs, attn = rest[7 : 7 + count], rest[7 + count]
    here = meta_ref[0]
    grad_hidden = wide(sums[0][...])
    for part in sums[1:]:
        grad_hidden = grad_hidden + wide(part[...])
    mixed = mixed_ref[...]
    scale = lax.rsqrt(jnp.mean(mixed * mixed, axis=1, keepdims=True) + EPSILON)
    normed = mixed * scale
    weighted = grad_hidden * gain_ref[...]
    grad_in = scale * (weighted - normed * jnp.mean(weighted * normed, axis=1, keepdims=True))
    grad_gain_ref[...] = jnp.sum(grad_hidden * normed, axis=0, keepdims=True)
    grad_mixed = wide(grad_ref[...]) + grad_in
    grad_mixed_ref[...] = grad_mixed
    grad_low_ref[...] = grad_mixed.astype(jnp.bfloat16)
    attn[...] = dot_nt(grad_low_ref[...], full_ref[...]).astype(jnp.bfloat16)
    for bits in range(count):
        owner = lax.bitwise_xor(here, bits)
        block_refs[bits][...] = attn[:, pl.ds(aligned(owner * 2 * HD, 2 * HD), 2 * HD)]


def wide_out_kernel(count, parts, meta_ref, *refs):
    blocks, (gate_ref, up_ref, held) = refs[:count], refs[count:]
    here = meta_ref[0]
    for bits in range(count):
        held[lax.bitwise_xor(here, bits)] = wide(blocks[bits][...])
    inner = held.shape[2] // 2
    main = inner // 128 * 128
    piece = inner // parts
    for kind, out_ref in enumerate((gate_ref, up_ref)):
        for part in range(parts):
            columns = []
            for owner in range(count):
                start, stop = part * piece, (part + 1) * piece
                begin = kind * main
                if start < main:
                    columns.append(held[owner, :, begin + start : begin + min(stop, main)])
                if stop > main:
                    begin = main + kind * (inner - main)
                    columns.append(held[owner, :, begin + max(start, main) : begin + stop])
            out_ref[:, part * count * piece : (part + 1) * count * piece] = jnp.concatenate(
                columns, axis=1
            )


def rows_out_kernel(meta_ref, *refs):
    blocks, out_ref = refs[:-1], refs[-1]
    rows = blocks[0].shape[0]
    for bits, block in enumerate(blocks):
        owner = lax.bitwise_xor(meta_ref[0], bits)
        out_ref[pl.ds(aligned(owner * rows, 16), rows), :] = wide(block[...])


def heads_out_kernel(count, own, extra, meta_ref, *refs):
    blocks, rest = refs[:count], refs[count:]
    query_ref, key_ref, value_ref, proj_ref, gain_ref, held = rest
    here = meta_ref[0]
    pair = 2 * HD
    part = (blocks[0].shape[0] - own - extra) // 4
    gains = jnp.zeros(gain_ref.shape, jnp.float32)
    for bits in range(count):
        owner = lax.bitwise_xor(here, bits)
        block = wide(blocks[bits][...])
        query_ref[:, pl.ds(aligned(owner * pair, pair), pair)] = block[:own, :pair]
        held[owner] = block[:own, pair:]
        gains = gains + block[own : own + extra, :]
        for index in range(4):
            source = own + extra + index * part
            proj_ref[
                pl.ds(aligned(owner * part, part), part), index * 2 * pair : (index + 1) * 2 * pair
            ] = block[source : source + part, :]
    gain_ref[...] = gains
    first, _ = lane_masks(own)
    for index in range(count // 2):
        early, late = held[2 * index], held[2 * index + 1]
        lanes = slice(index * pair, (index + 1) * pair)
        key_ref[:, lanes] = jnp.where(first, early, pltpu.roll(late, HD, 1))
        value_ref[:, lanes] = jnp.where(first, pltpu.roll(early, HD, 1), late)


SCALARS = pl.BlockSpec(memory_space=pltpu.SMEM)
WHOLE = pl.BlockSpec(memory_space=pltpu.VMEM)
PLACED = pl.BlockSpec(memory_space=pl.ANY)


def shaped(shape, kind=jnp.bfloat16):
    return jax.ShapeDtypeStruct(shape, kind)


def whole_call(kernel, outs, ins, flops, scratch=(), name=None, grant=24, specs=None):
    moved = sum(math.prod(out.shape) * out.dtype.itemsize for out in outs)
    return pl.pallas_call(
        kernel,
        out_shape=outs,
        in_specs=[SCALARS] + (specs or [WHOLE] * ins),
        out_specs=[WHOLE] * len(outs),
        scratch_shapes=list(scratch),
        cost_estimate=pl.CostEstimate(
            flops=int(flops), bytes_accessed=int(2 * moved), transcendentals=0
        ),
        compiler_params=pltpu.CompilerParams(vmem_limit_bytes=grant * 2**20),
        name=name,
    )


def rows_call(kernel, arrays, kept, outs, shared, index, flops, scratch=(), name=None, grant=24):
    specs = [SCALARS] + [WHOLE] * (len(arrays) - 1) + [PLACED] * len(kept)
    out_specs, shapes = [], []
    for position, out in enumerate(outs):
        if position < shared:
            rows = out.shape[0] // 4
            out_specs.append(
                pl.BlockSpec((rows, out.shape[1]), lambda step, index=index: (index, 0))
            )
        else:
            out_specs.append(pl.BlockSpec(out.shape, lambda step: (0, 0)))
        shapes.append(out)
    moved = sum(math.prod(out.shape) * out.dtype.itemsize for out in outs)
    return pl.pallas_call(
        kernel,
        grid=(1,),
        out_shape=shapes,
        in_specs=specs,
        out_specs=out_specs,
        scratch_shapes=list(scratch),
        input_output_aliases={len(arrays) + place: place for place in range(len(kept))},
        cost_estimate=pl.CostEstimate(
            flops=int(flops), bytes_accessed=int(moved), transcendentals=0
        ),
        compiler_params=pltpu.CompilerParams(vmem_limit_bytes=grant * 2**20),
        name=name,
    )(*arrays, *kept)


def local_heads(
    block_input, doc_starts, out_grad, query_weight, key_weight, value_weight, output_weight,
    gate_weight, up_weight, down_weight, mixer_gain, feed_gain, query_gain, key_gain,
):
    low = jnp.bfloat16
    tokens, width = block_input.shape[1:]
    count = lax.axis_size("ctx")
    shards = lax.axis_size("fsdp")
    here = lax.axis_index("ctx").astype(jnp.int32)
    shard = lax.axis_index("fsdp").astype(jnp.int32)
    stream = tokens * count
    docs = doc_starts.shape[1]
    pair = 2 * HD
    own_rows = width // shards
    extra = 16
    meta = jnp.concatenate([here[None], shard[None], doc_starts[0].astype(jnp.int32)])
    own_input = block_input[0]
    own_grad = out_grad[0]
    inner = down_weight.shape[0] // count
    wide_inner = inner * shards
    padded = -(-wide_inner // 128) * 128
    proj_rows = own_rows // count

    piece_rows = own_rows + extra + 4 * proj_rows
    head_piece = whole_call(
        take_heads_kernel,
        [shaped((piece_rows, 2 * pair))],
        8,
        0,
        [pltpu.VMEM((extra, 2 * pair), jnp.float32)],
        name="take_heads",
        grant=8,
    )(
        meta, query_weight, key_weight, value_weight, output_weight,
        mixer_gain[None], feed_gain[None], query_gain[None], key_gain[None],
    )[0]
    head_pieces = gather_fsdp(head_piece)
    input_blocks = gather_plane(own_input)
    wide_piece = whole_call(
        functools.partial(take_wide_kernel, shards),
        [shaped((own_rows, 2 * wide_inner))],
        2,
        2 * own_rows * 2 * wide_inner * 2048,
        [pltpu.VMEM((2 * shards, own_rows, 256), low), pltpu.SemaphoreType.DMA((2 * shards,))],
        name="take_wide",
        grant=16,
        specs=[PLACED] * 2,
    )(meta, gate_weight, up_weight)[0]
    down_piece = lax.dynamic_slice_in_dim(down_weight, here * inner, inner, 0)
    ready = head_pieces[1:]
    wide_pieces = gather_fsdp(behind(wide_piece, *ready))
    down_pieces = gather_fsdp(behind(down_piece, *ready))
    heads_weight, gain_mixer, gain_feed, gain_heads, proj_part = whole_call(
        functools.partial(arrange_heads_kernel, extra),
        [
            shaped((width, 2 * pair)),
            shaped((1, width), jnp.float32),
            shaped((1, width), jnp.float32),
            shaped((8, pair), jnp.float32),
            shaped((shards * proj_rows, width)),
        ],
        4,
        0,
        name="arrange_heads",
        grant=8,
    )(meta, *head_pieces)
    extra_blocks = gather_plane(
        behind(jnp.concatenate([own_grad, proj_part], axis=0), input_blocks[6])
    )

    where_at = jnp.arange(stream, dtype=jnp.int32)
    begins = doc_begin(doc_starts[0], where_at)
    lanes = jnp.arange(pair) % (HD // 2)
    frequency = ROPE_BASE ** (-(2.0 * lanes.astype(jnp.float32)) / HD)
    angles = (where_at - begins).astype(jnp.float32)[:, None] * frequency[None, :]
    cosine = jnp.cos(angles)
    sine = jnp.sin(angles) * jnp.where(jnp.arange(pair) % HD < HD // 2, -1.0, 1.0)[None, :]

    hidden_in, linear = [], []
    kept = []
    for index in range(4):
        kept = rows_call(
            head_linear_kernel,
            [meta]
            + [input_blocks[bits] for bits in ORDER[2 * index : 2 * index + 2]]
            + [heads_weight, gain_mixer],
            kept,
            [shaped((stream, width)), shaped((stream, 2 * pair), jnp.float32)],
            2,
            index,
            4 * tokens * width * 2 * pair,
            name="head_linear",
            grant=12,
        )
    hidden_in, linear = kept

    pairs = stream * stream // 2
    query_att, key_att, value_att, attn, lse, *attn_low = whole_call(
        functools.partial(attention_kernel, tokens, count, docs),
        [
            shaped((stream, pair)),
            shaped((stream, pair)),
            shaped((stream, pair)),
            shaped((stream, pair), jnp.float32),
            shaped((count, 1, 2 * tokens), jnp.float32),
        ]
        + [shaped((tokens, pair))] * count,
        4,
        8 * pairs * HD,
        [
            pltpu.VMEM((count, HD + 16, tokens), low),
            pltpu.VMEM((HD + 16, 2 * tokens), jnp.float32),
            pltpu.VMEM((stream, pair), low),
        ],
        name="attention",
        grant=20,
    )(meta, linear, cosine, sine, gain_heads)

    attn_blocks = exchange_plane(attn_low)
    full_proj, attn_rows, mixed, hidden_mid = whole_call(
        functools.partial(project_kernel, count, shards, tokens),
        [
            shaped((width, width)),
            shaped((tokens, width)),
            shaped((tokens, width), jnp.float32),
            shaped((tokens, width)),
        ],
        2 * count + 2,
        2 * tokens * width * width,
        [pltpu.VMEM((tokens, width), low)],
        name="project",
        grant=20,
    )(meta, *attn_blocks, *extra_blocks, own_input, gain_feed)

    hidden_blocks = gather_plane(hidden_mid)
    wide_weight, down_part = whole_call(
        arrange_feed_kernel,
        [shaped((width, 2 * wide_inner)), shaped((padded, width))],
        8,
        0,
        name="arrange_feed",
        grant=12,
    )(meta, *wide_pieces, *down_pieces)
    out_parts, back_parts = [None] * count, [None] * count
    kept = []
    for index in range(4):
        chosen = ORDER[2 * index : 2 * index + 2]
        results = rows_call(
            feed_kernel,
            [meta]
            + [hidden_blocks[bits] for bits in chosen]
            + [extra_blocks[bits] for bits in chosen]
            + [wide_weight, down_part],
            kept,
            [
                shaped((stream, width)),
                shaped((stream, width)),
                shaped((stream, padded)),
                shaped((stream, 2 * wide_inner)),
            ]
            + [shaped((tokens, width))] * 4,
            4,
            index,
            24 * tokens * width * wide_inner,
            [pltpu.VMEM((2, tokens, width), low)] * 2,
            name="feed",
            grant=32,
        )
        kept = results[:4]
        for place, bits in enumerate(chosen):
            out_parts[bits] = results[4 + place]
            back_parts[bits] = results[6 + place]
    hidden_all, grad_all, act_all, grad_wide_all = kept
    back_sums = scatter_plane(back_parts)
    grad_mixed, grad_mixed_low, grad_feed, *grad_blocks = whole_call(
        functools.partial(feed_back_kernel, count),
        [
            shaped((tokens, width), jnp.float32),
            shaped((tokens, width)),
            shaped((1, width), jnp.float32),
        ]
        + [shaped((tokens, pair))] * count,
        9,
        2 * tokens * width * width,
        [pltpu.VMEM((tokens, width), low)],
        name="feed_back",
        grant=20,
    )(meta, *back_sums, mixed, own_grad, full_proj, gain_feed)
    grad_attn = exchange_plane(grad_blocks)

    grad_down = contract_rows(act_all, grad_all).astype(low)
    grad_wide = contract_rows(hidden_all, grad_wide_all).astype(low)

    def scatter_fsdp(whole, rows, *ready):
        pieces = [
            lax.dynamic_slice_in_dim(whole, lax.bitwise_xor(shard, bits) * rows, rows, 0)
            for bits in range(4)
        ]
        sent = [swap_fsdp(behind(pieces[bits], *ready), bits) for bits in (1, 2, 3)]
        return sum([wide(part) for part in sent], wide(pieces[0])).astype(low)

    grad_down_part = scatter_fsdp(grad_down, inner)
    grad_wide_part = scatter_fsdp(grad_wide, own_rows)

    grad_linear, gain_sums = whole_call(
        functools.partial(attention_back_kernel, tokens, count, docs),
        [shaped((stream, 2 * pair)), shaped((8, pair), jnp.float32)],
        9 + count,
        20 * pairs * HD,
        [
            pltpu.VMEM((count, HD, tokens), low),
            pltpu.VMEM((stream, pair), jnp.float32),
            pltpu.VMEM((stream, pair), jnp.float32),
            pltpu.VMEM((stream, pair), jnp.float32),
            pltpu.VMEM((HD, 2 * tokens), jnp.float32),
            pltpu.VMEM((stream, pair), low),
        ],
        name="attention_back",
        grant=24,
    )(meta, linear, cosine, sine, gain_heads, query_att, key_att, value_att, attn, lse, *grad_attn)

    grad_proj = contract_rows(attn_rows, grad_mixed_low).astype(low)
    grad_proj = grad_proj.reshape(shards, count, proj_rows, width)
    proj_parts = [
        lax.dynamic_index_in_dim(
            grad_proj, lax.bitwise_xor(here, jnp.int32(bits)), 1, keepdims=False
        ).reshape(-1, width)
        for bits in range(count)
    ]
    joined = [
        behind(jnp.concatenate([out, proj], axis=0), grad_attn[6])
        for out, proj in zip(out_parts, proj_parts)
    ]
    joined = sum(wide(part) for part in scatter_plane(joined))
    block_output = (mixed + joined[:tokens]).astype(low)
    grad_proj = joined[tokens:].astype(low).reshape(shards, proj_rows, 4, 2 * pair)
    grad_proj = grad_proj.transpose(0, 2, 1, 3).reshape(shards, 4 * proj_rows, 2 * pair)

    grad_hidden_in = contract_cols(grad_linear, heads_weight)
    grad_hidden_low = grad_hidden_in.astype(low).reshape(count, tokens, width)
    in_parts = [None] * count
    for slot, bits in enumerate(ORDER):
        in_parts[bits] = grad_hidden_low[slot]
    grad_in_parts = scatter_plane(in_parts)

    own_normed, own_scale = unit_norm(wide(own_input))
    grad_hidden_own = sum(wide(part) for part in grad_in_parts)
    grad_normed_in, _ = norm_back(grad_hidden_own, own_normed, own_scale, gain_mixer)
    input_grad = grad_mixed + grad_normed_in

    scale_rows = jnp.concatenate(
        [
            lax.rsqrt(jnp.mean(wide(input_blocks[bits]) ** 2, axis=1, keepdims=True) + EPSILON)
            for bits in ORDER
        ],
        axis=0,
    )
    all_input = jnp.concatenate([input_blocks[bits] for bits in ORDER], axis=0)
    grad_mixer = jnp.sum(grad_hidden_in * (wide(all_input) * scale_rows), axis=0)
    grad_heads = contract_rows(hidden_in, grad_linear).astype(low)
    sums = jnp.zeros((shards, extra, 2 * pair), low)
    sums = sums.at[:, 0].set(grad_mixer.reshape(shards, own_rows).astype(low))
    sums = sums.at[:, 1].set(grad_feed.reshape(shards, own_rows).astype(low))
    query_sums = (gain_sums[0, :HD] + gain_sums[0, HD:]).reshape(shards, -1)
    key_sums = gain_sums[1, :HD].reshape(shards, -1)
    sums = sums.at[:, 2, : query_sums.shape[1]].set(query_sums.astype(low))
    sums = sums.at[:, 3, : key_sums.shape[1]].set(key_sums.astype(low))
    grad_heads = jnp.concatenate(
        [grad_heads.reshape(shards, own_rows, 2 * pair), sums, grad_proj], axis=1
    ).reshape(shards * piece_rows, 2 * pair)
    grad_heads_part = scatter_fsdp(grad_heads, piece_rows)

    down_blocks = gather_plane(behind(grad_down_part, grad_attn[6]))
    wide_blocks = gather_plane(behind(grad_wide_part, grad_attn[6]))
    heads_blocks = gather_plane(grad_heads_part)
    out_down = whole_call(
        rows_out_kernel, [shaped((count * inner, width), jnp.float32)], count, 0, name="down_out"
    )(meta, *down_blocks)[0]
    tile = own_rows // 4
    out_gate, out_up = pl.pallas_call(
        functools.partial(wide_out_kernel, count, shards),
        grid=(4,),
        in_specs=[SCALARS]
        + [pl.BlockSpec((tile, 2 * wide_inner), lambda step: (step, 0))] * count,
        out_specs=[pl.BlockSpec((tile, wide_inner * count), lambda step: (step, 0))] * 2,
        out_shape=[shaped((own_rows, wide_inner * count), jnp.float32)] * 2,
        scratch_shapes=[pltpu.VMEM((count, tile, 2 * wide_inner), jnp.float32)],
        compiler_params=pltpu.CompilerParams(vmem_limit_bytes=24 * 2**20),
        name="wide_out",
    )(meta, *wide_blocks)
    out_query, out_key, out_value, out_proj, gain_out = whole_call(
        functools.partial(heads_out_kernel, count, own_rows, extra),
        [
            shaped((own_rows, width), jnp.float32),
            shaped((own_rows, KVH * HD), jnp.float32),
            shaped((own_rows, KVH * HD), jnp.float32),
            shaped((own_rows, width), jnp.float32),
            shaped((extra, 2 * pair), jnp.float32),
        ],
        count,
        0,
        [pltpu.VMEM((count, own_rows, pair), jnp.float32)],
        name="heads_out",
    )(meta, *heads_blocks)
    return (
        block_output[None],
        input_grad[None],
        out_query,
        out_key,
        out_value,
        out_proj,
        out_gate,
        out_up,
        out_down,
        gain_out[0],
        gain_out[1],
        gain_out[2, : query_gain.shape[0]],
        gain_out[3, : key_gain.shape[0]],
    )


def divides_heads(mesh):
    return mesh.shape["ctx"] == KVH and mesh.shape["fsdp"] == 4 and H == 2 * KVH


def solution(mesh):
    in_specs = (
        P("fsdp", "ctx", None),
        P("fsdp", None),
        P("fsdp", "ctx", None),
        P("fsdp", None),
        P("fsdp", None),
        P("fsdp", None),
        P("fsdp", None),
        P("fsdp", None),
        P("fsdp", None),
        P("fsdp", None),
        P("fsdp"),
        P("fsdp"),
        P("fsdp"),
        P("fsdp"),
    )
    out_specs = (
        P("fsdp", "ctx", None),
        P("fsdp", "ctx", None),
        P("fsdp", None),
        P("fsdp", None),
        P("fsdp", None),
        P("fsdp", None),
        P("fsdp", None),
        P("fsdp", None),
        P("fsdp", None),
        P("fsdp"),
        P("fsdp"),
        P("fsdp"),
        P("fsdp"),
    )
    chosen = local_heads if divides_heads(mesh) else local
    return jax.shard_map(chosen, mesh=mesh, in_specs=in_specs, out_specs=out_specs, check_vma=False)
```

```python
import functools
import math

import jax
import jax.numpy as jnp
from jax import lax
from jax.experimental import pallas as pl
from jax.experimental.pallas import tpu as pltpu
from jax.sharding import PartitionSpec as P

H = 16
KVH = 8
HD = 64


EPSILON = 1e-05
ROPE_BASE = 1000000.0
FLOOR_SCORE = -1e30


def place_rows(row_index, tokens, ctx_count):
    half_rows = tokens // 2
    device = row_index // tokens
    offset = row_index % tokens
    early = device * half_rows + offset
    late = (2 * ctx_count - 1 - device) * half_rows + offset - half_rows
    return jnp.where(offset < half_rows, early, late)


def doc_begin(starts, where_at):
    started = starts[None, :] <= where_at[:, None]
    return jnp.max(jnp.where(started, starts[None, :], 0), axis=1)


def rotary(positions):
    half_dim = HD // 2
    frequency = ROPE_BASE ** (-(2.0 * jnp.arange(half_dim, dtype=jnp.float32)) / HD)
    angles = positions.astype(jnp.float32)[:, None] * frequency[None, :]
    angles = jnp.concatenate([angles, angles], axis=1)
    return (jnp.cos(angles)[:, None, :], jnp.sin(angles)[:, None, :])


def rotate_pairs(values, cosine, sine_part):
    half_dim = values.shape[-1] // 2
    rolled = jnp.concatenate([-values[..., half_dim:], values[..., :half_dim]], axis=-1)
    return values * cosine + rolled * sine_part


def rotate_back(grads, cosine, sine_part):
    half_dim = grads.shape[-1] // 2
    moved = grads * sine_part
    rolled = jnp.concatenate([moved[..., half_dim:], -moved[..., :half_dim]], axis=-1)
    return grads * cosine + rolled


def unit_norm(values):
    scaling = lax.rsqrt(jnp.mean(values * values, axis=-1, keepdims=True) + EPSILON)
    return (values * scaling, scaling)


def norm_back(grad_out, normed, scaling, gain_row):
    weighted = grad_out * gain_row
    grad_in = scaling * (weighted - normed * jnp.mean(weighted * normed, axis=-1, keepdims=True))
    grad_gain = jnp.sum((grad_out * normed).reshape(-1, normed.shape[-1]), axis=0)
    return (grad_in, grad_gain)


def score_block(query_rows, key_rows, scaling):
    return (
        jnp.einsum("igrd,jgd->grij", query_rows, key_rows, preferred_element_type=jnp.float32)
        * scaling
    )


def visible_pairs(query_at, query_doc, key_at, key_doc):
    return (query_doc[:, None] == key_doc[None, :]) & (key_at[None, :] <= query_at[:, None])


def any_visible(query_at, query_doc, key_at):
    return (jnp.min(key_at) <= jnp.max(query_at)) & (jnp.max(key_at) >= jnp.min(query_doc))


def contract_rows(left, right):
    return lax.dot_general(
        left, right, (((0,), (0,)), ((), ())), preferred_element_type=jnp.float32
    )


def contract_cols(left, right):
    return lax.dot_general(
        left, right, (((1,), (1,)), ((), ())), preferred_element_type=jnp.float32
    )


def keep_same(totals):
    return totals


def local(
    block_input,
    doc_starts,
    out_grad,
    query_weight,
    key_weight,
    value_weight,
    output_weight,
    gate_weight,
    up_weight,
    down_weight,
    mixer_gain,
    feed_gain,
    query_gain,
    key_gain,
):
    tokens = block_input.shape[1]
    ctx_count = lax.axis_size("ctx")
    repeat = H // KVH
    kv_width = KVH * HD
    scaling = HD ** (-0.5)
    inputs = block_input[0].astype(jnp.float32)
    starts = doc_starts[0]
    where_at = place_rows(
        lax.axis_index("ctx") * tokens + jnp.arange(tokens, dtype=jnp.int32), tokens, ctx_count
    )
    begins = doc_begin(starts, where_at)
    cosine, sine_part = rotary(where_at - begins)
    gathered = (
        lax.all_gather(query_weight, "fsdp", axis=0, tiled=True),
        lax.all_gather(key_weight, "fsdp", axis=0, tiled=True),
        lax.all_gather(value_weight, "fsdp", axis=0, tiled=True),
        lax.all_gather(output_weight, "fsdp", axis=0, tiled=True),
        lax.all_gather(gate_weight, "fsdp", axis=0, tiled=True),
        lax.all_gather(up_weight, "fsdp", axis=0, tiled=True),
        lax.all_gather(down_weight, "fsdp", axis=0, tiled=True),
        lax.all_gather(mixer_gain, "fsdp", axis=0, tiled=True),
        lax.all_gather(feed_gain, "fsdp", axis=0, tiled=True),
        lax.all_gather(query_gain, "fsdp", axis=0, tiled=True),
        lax.all_gather(key_gain, "fsdp", axis=0, tiled=True),
    )
    full_query, full_key, full_value, full_proj, full_gate, full_up, full_down = gathered[:7]
    gain_mixer, gain_feed, gain_query, gain_key = [
        entry.astype(jnp.float32) for entry in gathered[7:]
    ]
    normed_in, scale_in = unit_norm(inputs)
    hidden_in = (normed_in * gain_mixer).astype(jnp.bfloat16)
    query_lin = jnp.dot(hidden_in, full_query, preferred_element_type=jnp.float32)
    key_lin = jnp.dot(hidden_in, full_key, preferred_element_type=jnp.float32)
    value_lin = jnp.dot(hidden_in, full_value, preferred_element_type=jnp.float32)
    query_normed, query_scale = unit_norm(query_lin.reshape(tokens, H, HD))
    key_normed, key_scale = unit_norm(key_lin.reshape(tokens, KVH, HD))
    query_att = (
        rotate_pairs(query_normed * gain_query, cosine, sine_part)
        .reshape(tokens, H * HD)
        .astype(jnp.bfloat16)
    )
    key_att = (
        rotate_pairs(key_normed * gain_key, cosine, sine_part)
        .reshape(tokens, kv_width)
        .astype(jnp.bfloat16)
    )
    value_att = value_lin.astype(jnp.bfloat16)
    query_four = query_att.reshape(tokens, KVH, repeat, HD)
    start_state = (
        jnp.full((KVH, repeat, tokens), FLOOR_SCORE, jnp.float32),
        jnp.zeros((KVH, repeat, tokens), jnp.float32),
        jnp.zeros((tokens, H * HD), jnp.float32),
    )
    key_part = lax.all_gather(key_att, "ctx", axis=0, tiled=True)
    value_part = lax.all_gather(value_att, "ctx", axis=0, tiled=True)
    rows = key_part.shape[0]
    width = math.gcd(math.gcd(rows, tokens // 2), 512)

    def forward_key_block(block_index, totals):
        offset = block_index * width
        key_rows = lax.dynamic_slice_in_dim(key_part, offset, width, 0).reshape(width, KVH, HD)
        value_rows = lax.dynamic_slice_in_dim(value_part, offset, width, 0).reshape(width, KVH, HD)
        key_at = place_rows(offset + jnp.arange(width, dtype=jnp.int32), tokens, ctx_count)

        def attend(totals):
            highest, total_mass, accum = totals
            visible = visible_pairs(where_at, begins, key_at, doc_begin(starts, key_at))
            scores = jnp.where(visible, score_block(query_four, key_rows, scaling), FLOOR_SCORE)
            new_high = jnp.maximum(highest, jnp.max(scores, axis=-1))
            rescale = jnp.exp(highest - new_high)
            probable = jnp.where(visible, jnp.exp(scores - new_high[..., None]), 0.0)
            total_mass = total_mass * rescale + jnp.sum(probable, axis=-1)
            part_out = jnp.einsum(
                "grij,jgd->igrd",
                probable.astype(jnp.bfloat16),
                value_rows,
                preferred_element_type=jnp.float32,
            )
            accum = (
                accum.reshape(tokens, KVH, repeat, HD)
                * jnp.transpose(rescale, (2, 0, 1))[..., None]
                + part_out
            )
            return (new_high, total_mass, accum.reshape(tokens, H * HD))

        return lax.cond(any_visible(where_at, begins, key_at), attend, keep_same, totals)

    highest, total_mass, accum = lax.fori_loop(0, rows // width, forward_key_block, start_state)
    lse_heads = highest + jnp.log(total_mass)
    attn_raw = (
        accum.reshape(tokens, KVH, repeat, HD) / jnp.transpose(total_mass, (2, 0, 1))[..., None]
    ).reshape(tokens, H * HD)
    attn_low = attn_raw.astype(jnp.bfloat16)
    mixed = inputs + jnp.dot(attn_low, full_proj, preferred_element_type=jnp.float32)
    normed_mid, scale_mid = unit_norm(mixed)
    hidden_mid = (normed_mid * gain_feed).astype(jnp.bfloat16)
    gate_lin = jnp.dot(hidden_mid, full_gate, preferred_element_type=jnp.float32)
    up_lin = jnp.dot(hidden_mid, full_up, preferred_element_type=jnp.float32)
    sigmoid_gate = jax.nn.sigmoid(gate_lin)
    activated = (gate_lin * sigmoid_gate * up_lin).astype(jnp.bfloat16)
    block_output = (
        mixed + jnp.dot(activated, full_down, preferred_element_type=jnp.float32)
    ).astype(jnp.bfloat16)
    regathered = (
        lax.all_gather(query_weight, "fsdp", axis=0, tiled=True),
        lax.all_gather(key_weight, "fsdp", axis=0, tiled=True),
        lax.all_gather(value_weight, "fsdp", axis=0, tiled=True),
        lax.all_gather(output_weight, "fsdp", axis=0, tiled=True),
        lax.all_gather(gate_weight, "fsdp", axis=0, tiled=True),
        lax.all_gather(up_weight, "fsdp", axis=0, tiled=True),
        lax.all_gather(down_weight, "fsdp", axis=0, tiled=True),
        lax.all_gather(mixer_gain, "fsdp", axis=0, tiled=True),
        lax.all_gather(feed_gain, "fsdp", axis=0, tiled=True),
        lax.all_gather(query_gain, "fsdp", axis=0, tiled=True),
        lax.all_gather(key_gain, "fsdp", axis=0, tiled=True),
    )
    full_query, full_key, full_value, full_proj, full_gate, full_up, full_down = regathered[:7]
    gain_mixer, gain_feed, gain_query, gain_key = [
        entry.astype(jnp.float32) for entry in regathered[7:]
    ]
    grad_top = out_grad[0].astype(jnp.float32)
    grad_top_low = grad_top.astype(jnp.bfloat16)
    grad_down = contract_rows(activated, grad_top_low)
    grad_act = contract_cols(grad_top_low, full_down)
    grad_gate_low = (
        grad_act * up_lin * sigmoid_gate * (1.0 + gate_lin * (1.0 - sigmoid_gate))
    ).astype(jnp.bfloat16)
    grad_up_low = (grad_act * gate_lin * sigmoid_gate).astype(jnp.bfloat16)
    grad_gate = contract_rows(hidden_mid, grad_gate_low)
    grad_up = contract_rows(hidden_mid, grad_up_low)
    grad_hidden_mid = contract_cols(grad_gate_low, full_gate) + contract_cols(grad_up_low, full_up)
    grad_normed_mid, grad_feed = norm_back(grad_hidden_mid, normed_mid, scale_mid, gain_feed)
    grad_mixed = grad_top + grad_normed_mid
    grad_mixed_low = grad_mixed.astype(jnp.bfloat16)
    grad_proj = contract_rows(attn_low, grad_mixed_low)
    grad_attn = contract_cols(grad_mixed_low, full_proj).astype(jnp.bfloat16)
    grad_four = grad_attn.reshape(tokens, KVH, repeat, HD)
    delta_heads = jnp.sum(
        grad_four.astype(jnp.float32) * attn_raw.reshape(tokens, KVH, repeat, HD), axis=-1
    )
    delta_grid = jnp.transpose(delta_heads, (1, 2, 0))
    lse_rows = jnp.transpose(lse_heads, (2, 0, 1)).reshape(tokens, H)
    delta_rows = delta_heads.reshape(tokens, H)
    query_key_part = lax.all_gather(key_att, "ctx", axis=0, tiled=True)
    query_value_part = lax.all_gather(value_att, "ctx", axis=0, tiled=True)
    rows = query_key_part.shape[0]
    query_width = math.gcd(math.gcd(rows, tokens // 2), 512)

    def query_key_block(block_index, grad_query_acc):
        offset = block_index * query_width
        key_rows = lax.dynamic_slice_in_dim(query_key_part, offset, query_width, 0).reshape(
            query_width, KVH, HD
        )
        value_rows = lax.dynamic_slice_in_dim(query_value_part, offset, query_width, 0).reshape(
            query_width, KVH, HD
        )
        key_at = place_rows(offset + jnp.arange(query_width, dtype=jnp.int32), tokens, ctx_count)

        def attend(grad_query_acc):
            visible = visible_pairs(where_at, begins, key_at, doc_begin(starts, key_at))
            scores = score_block(query_four, key_rows, scaling)
            probable = jnp.where(visible, jnp.exp(scores - lse_heads[..., None]), 0.0)
            grad_prob = jnp.einsum(
                "igrd,jgd->grij", grad_four, value_rows, preferred_element_type=jnp.float32
            )
            grad_score = (probable * (grad_prob - delta_grid[..., None])).astype(jnp.bfloat16)
            added = (
                jnp.einsum(
                    "grij,jgd->igrd", grad_score, key_rows, preferred_element_type=jnp.float32
                )
                * scaling
            )
            return grad_query_acc + added.reshape(tokens, H * HD)

        return lax.cond(any_visible(where_at, begins, key_at), attend, keep_same, grad_query_acc)

    grad_query_att = lax.fori_loop(
        0, rows // query_width, query_key_block, jnp.zeros((tokens, H * HD), jnp.float32)
    )
    lse_all, delta_all = (
        lax.all_gather(lse_rows.astype(jnp.bfloat16), "ctx", axis=0, tiled=True).astype(
            lse_rows.dtype
        ),
        lax.all_gather(delta_rows.astype(jnp.bfloat16), "ctx", axis=0, tiled=True).astype(
            delta_rows.dtype
        ),
    )
    key_three = key_att.reshape(tokens, KVH, HD)
    value_three = value_att.reshape(tokens, KVH, HD)
    empty_keys = jnp.zeros((tokens, kv_width), jnp.float32)
    query_part = lax.all_gather(query_att, "ctx", axis=0, tiled=True)
    grad_part = lax.all_gather(grad_attn, "ctx", axis=0, tiled=True)
    rows = query_part.shape[0]
    key_width = math.gcd(math.gcd(rows, tokens // 2), 512)

    def query_block(block_index, totals):
        offset = block_index * key_width
        query_rows = lax.dynamic_slice_in_dim(query_part, offset, key_width, 0).reshape(
            key_width, KVH, repeat, HD
        )
        grad_rows = lax.dynamic_slice_in_dim(grad_part, offset, key_width, 0).reshape(
            key_width, KVH, repeat, HD
        )
        query_at = place_rows(offset + jnp.arange(key_width, dtype=jnp.int32), tokens, ctx_count)
        query_doc = doc_begin(starts, query_at)
        lse_block = jnp.transpose(
            lax.dynamic_slice_in_dim(lse_all, offset, key_width, 0).reshape(key_width, KVH, repeat),
            (1, 2, 0),
        )
        delta_block = jnp.transpose(
            lax.dynamic_slice_in_dim(delta_all, offset, key_width, 0).reshape(
                key_width, KVH, repeat
            ),
            (1, 2, 0),
        )

        def attend(totals):
            grad_key_acc, grad_value_acc = totals
            visible = visible_pairs(query_at, query_doc, where_at, begins)
            scores = score_block(query_rows, key_three, scaling)
            probable = jnp.where(visible, jnp.exp(scores - lse_block[..., None]), 0.0)
            grad_prob = jnp.einsum(
                "igrd,jgd->grij", grad_rows, value_three, preferred_element_type=jnp.float32
            )
            grad_score = (probable * (grad_prob - delta_block[..., None])).astype(jnp.bfloat16)
            value_added = jnp.einsum(
                "grij,igrd->jgd",
                probable.astype(jnp.bfloat16),
                grad_rows,
                preferred_element_type=jnp.float32,
            )
            key_added = (
                jnp.einsum(
                    "grij,igrd->jgd", grad_score, query_rows, preferred_element_type=jnp.float32
                )
                * scaling
            )
            return (
                grad_key_acc + key_added.reshape(tokens, kv_width),
                grad_value_acc + value_added.reshape(tokens, kv_width),
            )

        return lax.cond(any_visible(query_at, query_doc, where_at), attend, keep_same, totals)

    grad_key_att, grad_value_att = lax.fori_loop(
        0, rows // key_width, query_block, (empty_keys, empty_keys)
    )
    grad_query_unit = rotate_back(grad_query_att.reshape(tokens, H, HD), cosine, sine_part)
    grad_query_lin, grad_qgain = norm_back(grad_query_unit, query_normed, query_scale, gain_query)
    grad_key_unit = rotate_back(grad_key_att.reshape(tokens, KVH, HD), cosine, sine_part)
    grad_key_lin, grad_kgain = norm_back(grad_key_unit, key_normed, key_scale, gain_key)
    grad_query_low = grad_query_lin.reshape(tokens, H * HD).astype(jnp.bfloat16)
    grad_key_low = grad_key_lin.reshape(tokens, kv_width).astype(jnp.bfloat16)
    grad_value_low = grad_value_att.astype(jnp.bfloat16)
    grad_query = contract_rows(hidden_in, grad_query_low)
    grad_key = contract_rows(hidden_in, grad_key_low)
    grad_value = contract_rows(hidden_in, grad_value_low)
    grad_hidden_in = (
        contract_cols(grad_query_low, full_query)
        + contract_cols(grad_key_low, full_key)
        + contract_cols(grad_value_low, full_value)
    )
    grad_normed_in, grad_mixer = norm_back(grad_hidden_in, normed_in, scale_in, gain_mixer)
    input_grad = grad_mixed + grad_normed_in
    parts = (
        lax.psum_scatter(
            grad_query.astype(jnp.bfloat16), "fsdp", scatter_dimension=0, tiled=True
        ).astype(jnp.float32),
        lax.psum_scatter(
            grad_key.astype(jnp.bfloat16), "fsdp", scatter_dimension=0, tiled=True
        ).astype(jnp.float32),
        lax.psum_scatter(
            grad_value.astype(jnp.bfloat16), "fsdp", scatter_dimension=0, tiled=True
        ).astype(jnp.float32),
        lax.psum_scatter(
            grad_proj.astype(jnp.bfloat16), "fsdp", scatter_dimension=0, tiled=True
        ).astype(jnp.float32),
        lax.psum_scatter(
            grad_gate.astype(jnp.bfloat16), "fsdp", scatter_dimension=0, tiled=True
        ).astype(jnp.float32),
        lax.psum_scatter(
            grad_up.astype(jnp.bfloat16), "fsdp", scatter_dimension=0, tiled=True
        ).astype(jnp.float32),
        lax.psum_scatter(
            grad_down.astype(jnp.bfloat16), "fsdp", scatter_dimension=0, tiled=True
        ).astype(jnp.float32),
        lax.psum_scatter(
            grad_mixer.astype(jnp.bfloat16), "fsdp", scatter_dimension=0, tiled=True
        ).astype(jnp.float32),
        lax.psum_scatter(
            grad_feed.astype(jnp.bfloat16), "fsdp", scatter_dimension=0, tiled=True
        ).astype(jnp.float32),
        lax.psum_scatter(
            grad_qgain.astype(jnp.bfloat16), "fsdp", scatter_dimension=0, tiled=True
        ).astype(jnp.float32),
        lax.psum_scatter(
            grad_kgain.astype(jnp.bfloat16), "fsdp", scatter_dimension=0, tiled=True
        ).astype(jnp.float32),
    )
    summed = (
        lax.psum(parts[0].astype(jnp.bfloat16), "ctx").astype(jnp.float32),
        lax.psum(parts[1].astype(jnp.bfloat16), "ctx").astype(jnp.float32),
        lax.psum(parts[2].astype(jnp.bfloat16), "ctx").astype(jnp.float32),
        lax.psum(parts[3].astype(jnp.bfloat16), "ctx").astype(jnp.float32),
        lax.psum(parts[4].astype(jnp.bfloat16), "ctx").astype(jnp.float32),
        lax.psum(parts[5].astype(jnp.bfloat16), "ctx").astype(jnp.float32),
        lax.psum(parts[6].astype(jnp.bfloat16), "ctx").astype(jnp.float32),
        lax.psum(parts[7].astype(jnp.bfloat16), "ctx").astype(jnp.float32),
        lax.psum(parts[8].astype(jnp.bfloat16), "ctx").astype(jnp.float32),
        lax.psum(parts[9].astype(jnp.bfloat16), "ctx").astype(jnp.float32),
        lax.psum(parts[10].astype(jnp.bfloat16), "ctx").astype(jnp.float32),
    )
    return (
        block_output[None],
        input_grad[None],
        summed[0],
        summed[1],
        summed[2],
        summed[3],
        summed[4],
        summed[5],
        summed[6],
        summed[7],
        summed[8],
        summed[9],
        summed[10],
    )


ORDER = (0, 1, 2, 4, 3, 5, 6, 7)


def flipped(bits, count):
    return [(index, index ^ bits) for index in range(count)]


def swap_ctx(values, bits):
    return lax.ppermute(values, "ctx", flipped(bits, lax.axis_size("ctx")))


def behind(values, *ready):
    return lax.optimization_barrier((values,) + ready)[0]


def dot_nn(left, right):
    return lax.dot_general(
        left, right, (((1,), (0,)), ((), ())), preferred_element_type=jnp.float32
    )


def dot_nt(left, right):
    return lax.dot_general(
        left, right, (((1,), (1,)), ((), ())), preferred_element_type=jnp.float32
    )


def wide(values):
    return values.astype(jnp.float32)


def gather_near(block):
    return swap_ctx(block, 2), swap_ctx(block, 4), swap_ctx(block, 1)


def gather_corner(across, along):
    half = across.shape[0] // 2
    first = swap_ctx(along[:half], 2)
    second = swap_ctx(across[half:], 4)
    return jnp.concatenate([first, second], axis=0)


def gather_far(across, along, corner, *ready):
    return [swap_ctx(behind(part, *ready), 1) for part in (across, along, corner)]


def gather_plane(block, *ready):
    across, along, partner = gather_near(block)
    corner = gather_corner(across, along)
    others = gather_far(across, along, corner, *ready)
    return [block, partner, across, others[0], along, others[1], corner, others[2]]


def scatter_pair(blocks):
    got = [swap_ctx(blocks[bits], 1) for bits in (3, 5, 7, 1)]
    sums = [
        (wide(blocks[bits]) + wide(other)).astype(jnp.bfloat16)
        for bits, other in zip((2, 4, 6), got)
    ]
    return [blocks[0], got[3]], sums


def scatter_links(sums):
    return [swap_ctx(part, bits) for bits, part in zip((2, 4, 6), sums)]


def exchange_plane(blocks):
    return [blocks[0]] + [swap_ctx(blocks[bits], bits) for bits in range(1, 8)]


def shift_fsdp(values, pairs):
    return lax.ppermute(values, "fsdp", pairs)


def slot_of(bits):
    return jnp.where(bits == 3, 4, jnp.where(bits == 4, 3, bits))


def row_of(place, here, tokens, count):
    half = tokens // 2
    device = jnp.where(place < count, place, 2 * count - 1 - place)
    late = jnp.where(place < count, 0, half)
    return slot_of(lax.bitwise_xor(device, here)) * tokens + late


def swap_half(values, low_lane):
    return jnp.where(low_lane, pltpu.roll(values, 96, 1), pltpu.roll(values, 32, 1))


def head_mean(values, first):
    lower = jnp.sum(jnp.where(first, values, 0.0), axis=1, keepdims=True)
    upper = jnp.sum(jnp.where(first, 0.0, values), axis=1, keepdims=True)
    return jnp.where(first, lower, upper) * (1.0 / HD)


def lane_masks(rows):
    lanes = lax.broadcasted_iota(jnp.int32, (rows, 2 * HD), 1)
    return lanes < HD, (lanes % HD) < (HD // 2)


def two_heads(values):
    first, _ = lane_masks(values.shape[0])
    zero = jnp.zeros_like(values)
    return jnp.concatenate(
        [jnp.where(first, values, zero), jnp.where(first, zero, values)], axis=0
    )


def begin_at(meta_ref, docs, where_at):
    begin = jnp.zeros_like(where_at)
    for doc in range(docs):
        begin = jnp.where(meta_ref[2 + doc] <= where_at, meta_ref[2 + doc], begin)
    return begin


def block_visible(meta_ref, docs, query_block, key_block, size):
    query_at = query_block * size + lax.broadcasted_iota(jnp.int32, (1, size), 1)
    begin = begin_at(meta_ref, docs, query_at)
    key_at = key_block * size + lax.broadcasted_iota(jnp.int32, (size, size), 0)
    return (key_at <= query_at) & (key_at >= begin)


def aligned(value, size):
    return pl.multiple_of(value, size)


def take_heads_kernel(
    meta_ref, query_ref, key_ref, value_ref, proj_ref, mixer_ref, feed_ref, query_gain_ref, key_gain_ref,
    out_ref, gains, windows, proj, sem,
):
    here = meta_ref[0]
    rows = query_ref.shape[0]
    pair = 2 * HD
    start = aligned(lax.shift_right_logical(here, 1) * pair, pair)
    part = proj.shape[0]
    copies = [
        pltpu.make_async_copy(
            query_ref.at[:, pl.ds(aligned(here * pair, pair), pair)], windows.at[0], sem.at[0]
        ),
        pltpu.make_async_copy(key_ref.at[:, pl.ds(start, pair)], windows.at[1], sem.at[1]),
        pltpu.make_async_copy(value_ref.at[:, pl.ds(start, pair)], windows.at[2], sem.at[2]),
        pltpu.make_async_copy(
            proj_ref.at[pl.ds(aligned(here * part, part), part), :], proj, sem.at[3]
        ),
    ]
    for copy in copies:
        copy.start()
    gains[...] = jnp.zeros_like(gains)
    gains[0:1, :] = wide(mixer_ref[...])
    gains[1:2, :] = wide(feed_ref[...])
    gains[2:3, : query_gain_ref.shape[1]] = wide(query_gain_ref[...])
    gains[3:4, : key_gain_ref.shape[1]] = wide(key_gain_ref[...])
    extra = gains.shape[0]
    out_ref[rows : rows + extra, :] = gains[...].astype(jnp.bfloat16)
    for copy in copies:
        copy.wait()
    out_ref[:rows, :pair] = windows[0]
    odd = lax.bitwise_and(here, 1) == 1
    keys = wide(windows[1])
    values = wide(windows[2])
    first, _ = lane_masks(rows)
    keys = jnp.where(odd, pltpu.roll(keys, HD, 1), keys)
    values = jnp.where(odd, values, pltpu.roll(values, HD, 1))
    out_ref[:rows, pair:] = jnp.where(first, keys, values).astype(jnp.bfloat16)
    for index in range(proj.shape[1] // (2 * pair)):
        target = rows + extra + index * part
        out_ref[target : target + part, :] = proj[:, index * 2 * pair : (index + 1) * 2 * pair]


def arrange_heads_kernel(
    extra, meta_ref, *refs
):
    pieces, (weight_ref, mixer_ref, feed_ref, gains_ref, proj_ref) = refs[:4], refs[4:]
    shard = meta_ref[1]
    rows = weight_ref.shape[0] // 4
    pair = 2 * HD
    each = HD // 4
    gains = jnp.zeros((8, pair), jnp.float32)
    part = proj_ref.shape[0] // 4
    for bits, piece in enumerate(pieces):
        owner = lax.bitwise_xor(shard, bits)
        weight_ref[pl.ds(aligned(owner * rows, rows), rows), :] = piece[:rows, :]
        block = wide(piece[rows : rows + extra, :])
        lanes = pl.ds(aligned(owner * rows, rows), rows)
        mixer_ref[:, lanes] = block[0:1, :]
        feed_ref[:, lanes] = block[1:2, :]
        gains = gains + pltpu.roll(block[:8, :pair], owner * each, 1)
        for index in range(proj_ref.shape[1] // (2 * pair)):
            source = rows + extra + index * part
            proj_ref[
                pl.ds(aligned(owner * part, part), part), index * 2 * pair : (index + 1) * 2 * pair
            ] = piece[source : source + part, :]
    gains_ref[...] = gains + pltpu.roll(gains, HD, 1)


def wide_column(column, main, rest):
    late = (column >= 2 * main).astype(jnp.int32)
    late_up = (column >= 2 * main + rest).astype(jnp.int32)
    early_up = (column >= main).astype(jnp.int32) * (1 - late)
    is_up = late * late_up + early_up
    return is_up, column - early_up * main - late * (main + late_up * rest)


def take_wide_kernel(shards, meta_ref, gate_ref, up_ref, down_ref, out_ref, window, sem, rows, down_sem, total):
    here = meta_ref[0]
    own_rows = window.shape[1]
    inner = out_ref.shape[1] // 2
    piece = inner // shards
    span = window.shape[2]
    shift = here * (piece - 128)
    copies = []
    for kind, source in enumerate((gate_ref, up_ref)):
        for part in range(shards):
            start = aligned(part * (source.shape[1] // shards) + here * 128, 128)
            copies.append(
                pltpu.make_async_copy(
                    source.at[:, pl.ds(start, span)],
                    window.at[kind * shards + part],
                    sem.at[kind * shards + part],
                )
            )
    down = pltpu.make_async_copy(
        down_ref.at[pl.ds(aligned(here * rows.shape[0], 16), rows.shape[0]), :], rows, down_sem
    )
    for copy in copies:
        copy.start()
    down.start()
    columns = lax.broadcasted_iota(jnp.int32, (1, 2 * inner), 1)
    main = inner // 128 * 128
    is_up, unit = wide_column(columns, main, inner - main)
    owner = jnp.zeros_like(unit)
    for part in range(1, shards):
        owner = jnp.where(unit >= part * piece, part, owner)
    target = unit - owner * piece + shift
    owner = owner + is_up * shards
    places = lax.broadcasted_iota(jnp.int32, (span, 2 * inner), 0)
    for copy in copies:
        copy.wait()
    total[...] = jnp.zeros_like(total)

    def add(index, carry):
        place = jnp.where(owner == index, target, -1)
        chosen = jnp.where(places == place, 1.0, 0.0).astype(jnp.bfloat16)
        total[...] += dot_nn(window[index], chosen)
        return carry

    lax.fori_loop(0, len(copies), add, 0)
    out_ref[:own_rows, :] = total[...].astype(jnp.bfloat16)
    down.wait()
    out_ref[own_rows:, : rows.shape[1]] = rows[...]
    out_ref[own_rows:, rows.shape[1] :] = jnp.zeros_like(out_ref[own_rows:, rows.shape[1] :])


def arrange_feed_kernel(meta_ref, own_ref, near_ref, far_ref, middle_ref, relay_ref, wide_ref, down_ref):
    shard = meta_ref[1]
    rows = wide_ref.shape[0] // 4
    inner = own_ref.shape[0] - rows
    width = down_ref.shape[1]
    for bits, piece in enumerate((own_ref, near_ref, far_ref, None)):
        owner = lax.bitwise_xor(shard, bits)
        if piece is None:
            piece = middle_ref[...] + relay_ref[...]
        wide_ref[pl.ds(aligned(owner * rows, rows), rows), :] = piece[:rows, :]
        down_ref[pl.ds(aligned(owner * inner, 16), inner), :] = piece[rows:, :width]
    down_ref[4 * inner :, :] = jnp.zeros_like(down_ref[4 * inner :, :])


def head_linear_kernel(
    meta_ref, first_ref, second_ref, weight_ref, gain_ref, *refs
):
    hidden_ref, linear_ref = refs[-2:]
    rows = first_ref.shape[0]
    for index, source in enumerate((first_ref, second_ref)):
        values = wide(source[...])
        scale = lax.rsqrt(jnp.mean(values * values, axis=1, keepdims=True) + EPSILON)
        hidden = (values * scale * gain_ref[...]).astype(jnp.bfloat16)
        hidden_ref[index * rows : (index + 1) * rows, :] = hidden
        linear_ref[index * rows : (index + 1) * rows, :] = dot_nn(hidden, weight_ref[...])


def attention_kernel(
    tokens, count, docs,
    meta_ref, lin_ref, cos_ref, sin_ref, gains_ref,
    query_ref, key_ref, value_ref, attn_ref, lse_ref, *refs,
):
    low_refs, (value_t, accum, low) = refs[:count], refs[count:]
    here = meta_ref[0]
    half = tokens // 2
    size = tokens
    blocks = count

    def prepare(place, carry):
        first, low_lane = lane_masks(half)
        source = aligned(row_of(place, here, tokens, count), half)
        target = aligned(place * half, half)
        cosine = cos_ref[pl.ds(target, half), :]
        sine = sin_ref[pl.ds(target, half), :]
        query = lin_ref[pl.ds(source, half), : 2 * HD]
        unit = query * lax.rsqrt(head_mean(query * query, first) + EPSILON) * gains_ref[2:3, :]
        turned = unit * cosine + swap_half(unit, low_lane) * sine
        query_ref[pl.ds(target, half), :] = (
            turned.astype(jnp.bfloat16).astype(jnp.float32) * (HD**-0.5)
        ).astype(jnp.bfloat16)
        both = lin_ref[pl.ds(source, half), 2 * HD :]
        unit = both * lax.rsqrt(head_mean(both * both, first) + EPSILON) * gains_ref[3:4, :]
        turned = unit * cosine + swap_half(unit, low_lane) * sine
        key_ref[pl.ds(target, half), :] = jnp.where(
            first, turned, pltpu.roll(turned, HD, 1)
        ).astype(jnp.bfloat16)
        values = jnp.where(first, pltpu.roll(both, HD, 1), both)
        value_ref[pl.ds(target, half), :] = values.astype(jnp.bfloat16)
        return carry

    lax.fori_loop(0, 2 * count, prepare, 0)

    def turn_values(block, carry):
        values = wide(value_ref[pl.ds(aligned(block * size, size), size), :])
        value_t[block, :HD, :] = values.T[:HD].astype(jnp.bfloat16)
        value_t[block, HD:, :] = jnp.ones((value_t.shape[1] - HD, size), jnp.bfloat16)
        return carry

    lax.fori_loop(0, blocks, turn_values, 0)

    def query_step(block, carry):
        query = two_heads(query_ref[pl.ds(aligned(block * size, size), size), :])
        accum[...] = jnp.zeros_like(accum)
        lowest = begin_at(meta_ref, docs, block * size) // size

        def key_step(other, carry):
            keys = key_ref[pl.ds(aligned(other * size, size), size), :]
            scores = dot_nt(keys, query)
            visible = block_visible(meta_ref, docs, block, other, size)
            probable = jnp.concatenate(
                [
                    jnp.where(visible, jnp.exp(scores[:, :size]), 0.0),
                    jnp.where(visible, jnp.exp(scores[:, size:]), 0.0),
                ],
                axis=1,
            ).astype(jnp.bfloat16)
            accum[...] += dot_nn(value_t[other], probable)
            return carry

        lax.fori_loop(lowest, block + 1, key_step, 0)
        mass = accum[HD : HD + 1, :]
        mixed = accum[:HD, :] / mass
        lse_ref[block] = jnp.log(mass)
        rows = jnp.concatenate([mixed[:, :size], mixed[:, size:]], axis=0).T
        attn_ref[pl.ds(aligned(block * size, size), size), :] = rows
        for part in range(2):
            target = aligned(row_of(2 * block + part, here, tokens, count), half)
            low[pl.ds(target, half), :] = rows[part * half : (part + 1) * half].astype(jnp.bfloat16)
        return carry

    lax.fori_loop(0, blocks, query_step, 0)
    for slot, bits in enumerate(ORDER):
        low_refs[bits][...] = low[slot * tokens : (slot + 1) * tokens, :]


def attention_back_kernel(
    tokens, count, docs,
    meta_ref, lin_ref, cos_ref, sin_ref, gains_ref,
    query_ref, key_ref, value_ref, attn_ref, lse_ref, *refs,
):
    grad_refs = refs[:count]
    out_ref, gain_ref = refs[count : count + 2]
    block_refs = refs[count + 2 : 2 * count + 2]
    key_t, grad_query, grad_key, grad_value, accum, grad_rows = refs[2 * count + 2 :]
    here = meta_ref[0]
    half = tokens // 2
    size = tokens
    blocks = count
    grad_key[...] = jnp.zeros_like(grad_key)
    grad_value[...] = jnp.zeros_like(grad_value)
    gain_ref[...] = jnp.zeros_like(gain_ref)
    for slot, bits in enumerate(ORDER):
        grad_rows[slot * tokens : (slot + 1) * tokens, :] = grad_refs[bits][...]

    def turn_keys(block, carry):
        keys = wide(key_ref[pl.ds(aligned(block * size, size), size), :])
        key_t[block] = keys.T[:HD].astype(jnp.bfloat16)
        return carry

    lax.fori_loop(0, blocks, turn_keys, 0)

    def query_step(block, carry):
        here_rows = pl.ds(aligned(block * size, size), size)
        query = two_heads(query_ref[here_rows, :])
        parts = []
        for part in range(2):
            source = aligned(row_of(2 * block + part, here, tokens, count), half)
            parts.append(grad_rows[pl.ds(source, half), :])
        grads = jnp.concatenate(parts, axis=0)
        products = (wide(grads) * attn_ref[here_rows, :]).T
        deltas = (
            jnp.sum(products[:HD], axis=0, keepdims=True),
            jnp.sum(products[HD:], axis=0, keepdims=True),
        )
        grads = two_heads(grads)
        lse = lse_ref[block]
        accum[...] = jnp.zeros_like(accum)
        lowest = begin_at(meta_ref, docs, block * size) // size

        def key_step(other, carry):
            rows = pl.ds(aligned(other * size, size), size)
            scores = dot_nt(key_ref[rows, :], query)
            grad_prob = dot_nt(value_ref[rows, :], grads)
            visible = block_visible(meta_ref, docs, block, other, size)
            probs, grad_scores = [], []
            for head in range(2):
                cols = slice(head * size, (head + 1) * size)
                prob = jnp.where(visible, jnp.exp(scores[:, cols] - lse[:, cols]), 0.0)
                probs.append(prob)
                grad_scores.append(prob * (grad_prob[:, cols] - deltas[head]))
            probs = jnp.concatenate(probs, axis=1).astype(jnp.bfloat16)
            grad_scores = jnp.concatenate(grad_scores, axis=1).astype(jnp.bfloat16)
            grad_value[rows, :] += dot_nn(probs, grads)
            grad_key[rows, :] += dot_nn(grad_scores, query)
            accum[...] += dot_nn(key_t[other], grad_scores)
            return carry

        lax.fori_loop(lowest, block + 1, key_step, 0)
        total = accum[...] * (HD**-0.5)
        grad_query[here_rows, :] = jnp.concatenate([total[:, :size], total[:, size:]], axis=0).T
        return carry

    lax.fori_loop(0, blocks, query_step, 0)

    def finish(place, carry):
        first, low_lane = lane_masks(half)
        source = aligned(row_of(place, here, tokens, count), half)
        target = pl.ds(aligned(place * half, half), half)
        cosine = cos_ref[target, :]
        sine = sin_ref[target, :]

        def through(linear, grads, gain):
            scale = lax.rsqrt(head_mean(linear * linear, first) + EPSILON)
            normed = linear * scale
            turned = grads * cosine + swap_half(grads * sine, low_lane)
            weighted = turned * gain
            grad_in = scale * (weighted - normed * head_mean(weighted * normed, first))
            return grad_in, jnp.sum(turned * normed, axis=0, keepdims=True)

        grad_in, gain_row = through(
            lin_ref[pl.ds(source, half), : 2 * HD], grad_query[target, :], gains_ref[2:3, :]
        )
        out_ref[pl.ds(source, half), : 2 * HD] = grad_in.astype(jnp.bfloat16)
        gain_ref[0:1, :] += gain_row
        keys = grad_key[target, :]
        grad_in, gain_row = through(
            lin_ref[pl.ds(source, half), 2 * HD :], keys + pltpu.roll(keys, HD, 1), gains_ref[3:4, :]
        )
        gain_ref[1:2, :] += gain_row
        values = grad_value[target, :]
        values = values + pltpu.roll(values, HD, 1)
        out_ref[pl.ds(source, half), 2 * HD :] = jnp.where(first, grad_in, values).astype(
            jnp.bfloat16
        )
        return carry

    lax.fori_loop(0, 2 * count, finish, 0)
    for slot, bits in enumerate(ORDER):
        block_refs[bits][...] = out_ref[slot * tokens : (slot + 1) * tokens, :]


def proj_grad_kernel(parts, meta_ref, attn_ref, grad_ref, *refs):
    blocks, full = refs[:-1], refs[-1]
    count = len(blocks)
    here = meta_ref[0]
    full[...] = contract_rows(attn_ref[...], grad_ref[...]).astype(jnp.bfloat16)
    rows = blocks[0].shape[0] // parts
    for bits, block in enumerate(blocks):
        owner = lax.bitwise_xor(here, bits)
        for part in range(parts):
            source = aligned(part * count * rows + owner * rows, rows)
            block[part * rows : (part + 1) * rows, :] = full[pl.ds(source, rows), :]


def pack_heads_kernel(
    extra, meta_ref, heads_ref, mixer_ref, gain_ref, feed_ref, sums_ref, *refs
):
    proj_refs, pieces = refs[:5], refs[5:]
    shard = meta_ref[1]
    rows = heads_ref.shape[0] // 4
    pair = 2 * HD
    proj = wide(proj_refs[0][...])
    for other in proj_refs[1:]:
        proj = proj + wide(other[...])
    proj_low, mixer, _, gains = pieces[4:]
    pieces = pieces[:4]
    part = proj.shape[0] // 4
    proj_low[...] = proj.astype(jnp.bfloat16)
    mixer[...] = mixer_ref[...] / gain_ref[...]
    values = sums_ref[...]
    lower = lax.broadcasted_iota(jnp.int32, values.shape, 0) == 0
    values = values + jnp.where(lower, pltpu.roll(values, HD, 1), 0.0)
    each = HD // 4
    lanes = lax.broadcasted_iota(jnp.int32, values.shape, 1)
    for bits, piece in enumerate(pieces):
        owner = lax.bitwise_xor(shard, bits)
        piece[:rows, :] = heads_ref[pl.ds(aligned(owner * rows, rows), rows), :]
        gains[...] = jnp.zeros_like(gains)
        own = pl.ds(aligned(owner * rows, rows), rows)
        gains[0:1, :] = mixer[:, own]
        gains[1:2, :] = feed_ref[:, own]
        moved = pltpu.roll(values, pair - owner * each, 1)
        moved = jnp.where(lanes < each, moved, 0.0)
        gains[2:4, :pair] = moved[0:2, :]
        piece[rows : rows + extra, :] = gains[...].astype(jnp.bfloat16)
        for index in range(proj.shape[1] // (2 * pair)):
            target = rows + extra + index * part
            piece[target : target + part, :] = proj_low[
                pl.ds(aligned(owner * part, part), part), index * 2 * pair : (index + 1) * 2 * pair
            ]


def pack_feed_kernel(meta_ref, wide_ref, down_ref, *pieces):
    shard = meta_ref[1]
    rows = wide_ref.shape[0] // 4
    inner = pieces[0].shape[0] - rows
    width = down_ref.shape[1]
    for bits, piece in enumerate(pieces):
        owner = lax.bitwise_xor(shard, bits)
        piece[:rows, :] = wide_ref[pl.ds(aligned(owner * rows, 16), rows), :]
        piece[rows:, :width] = down_ref[pl.ds(aligned(owner * inner, 16), inner), :]
        piece[rows:, width:] = jnp.zeros_like(piece[rows:, width:])


def input_grad_kernel(count, meta_ref, *refs):
    grads, weights = refs[:count], refs[count : 2 * count]
    input_ref, grad_ref, gain_ref, out_ref = refs[2 * count :]
    total = dot_nt(grads[0][...], weights[0][...])
    for left, right in zip(grads[1:], weights[1:]):
        total = total + dot_nt(left[...], right[...])
    values = wide(input_ref[...])
    scale = lax.rsqrt(jnp.mean(values * values, axis=1, keepdims=True) + EPSILON)
    normed = values * scale
    weighted = total * gain_ref[...]
    grad_in = scale * (weighted - normed * jnp.mean(weighted * normed, axis=1, keepdims=True))
    out_ref[...] = grad_ref[...] + grad_in


def project_kernel(count, parts, start, meta_ref, *refs):
    attn_refs, weight_refs, rest = refs[:count], refs[count : 2 * count], refs[2 * count :]
    input_ref, gain_ref, full_ref, attn_out_ref, mixed_ref, hidden_ref, _ = rest
    here = meta_ref[0]
    total = weight_refs[0].shape[0] - start
    rows = total // parts
    for bits in range(count):
        owner = lax.bitwise_xor(here, bits)
        for part in range(parts):
            target = aligned(part * count * rows + owner * rows, rows)
            source = start + part * rows
            full_ref[pl.ds(target, rows), :] = weight_refs[bits][source : source + rows, :]
        attn_out_ref[:, pl.ds(aligned(owner * 2 * HD, 2 * HD), 2 * HD)] = attn_refs[bits][...]
    mixed = wide(input_ref[...]) + dot_nn(attn_out_ref[...], full_ref[...])
    mixed_ref[...] = mixed
    scale = lax.rsqrt(jnp.mean(mixed * mixed, axis=1, keepdims=True) + EPSILON)
    hidden_ref[...] = (mixed * scale * gain_ref[...]).astype(jnp.bfloat16)


def feed_kernel(
    meta_ref, first_ref, second_ref, grad_first_ref, grad_second_ref, wide_ref, down_ref, *refs
):
    refs = refs[-10:]
    hidden_ref, grad_ref, act_ref, grad_wide_ref = refs[:4]
    out_refs, back_refs, (out_low, back_low) = refs[4:6], refs[6:8], refs[8:]
    tokens = first_ref.shape[0]
    inner = wide_ref.shape[1] // 2
    main = inner // 128 * 128
    hidden_ref[:tokens, :] = first_ref[...]
    hidden_ref[tokens:, :] = second_ref[...]
    grad_ref[:tokens, :] = grad_first_ref[:tokens, :]
    grad_ref[tokens:, :] = grad_second_ref[:tokens, :]
    first, _ = lane_masks(tokens)

    def activate(gate, up, grad_act):
        sigmoid = 1.0 / (1.0 + jnp.exp(-gate))
        silu = gate * sigmoid
        grad_gate = grad_act * up * sigmoid * (1.0 + gate * (1.0 - sigmoid))
        return silu * up, grad_gate, grad_act * silu

    def step(index, carry):
        rows = pl.ds(aligned(index * tokens, tokens), tokens)
        both = dot_nn(hidden_ref[rows, :], wide_ref[...])
        grad_act = dot_nt(grad_ref[rows, :], down_ref[...])
        act, grad_gate, grad_up = activate(
            both[:, :main], both[:, main : 2 * main], grad_act[:, :main]
        )
        act_ref[rows, :main] = act.astype(jnp.bfloat16)
        grad_wide_ref[rows, :main] = grad_gate.astype(jnp.bfloat16)
        grad_wide_ref[rows, main : 2 * main] = grad_up.astype(jnp.bfloat16)
        last = both[:, 2 * main :]
        act, grad_gate, grad_up = activate(last, pltpu.roll(last, HD, 1), grad_act[:, main:])
        act_ref[rows, main:] = jnp.where(first, act, 0.0).astype(jnp.bfloat16)
        grad_wide_ref[rows, 2 * main :] = jnp.where(
            first, grad_gate, pltpu.roll(grad_up, HD, 1)
        ).astype(jnp.bfloat16)
        back_low[index] = dot_nt(grad_wide_ref[rows, :], wide_ref[...]).astype(jnp.bfloat16)
        out_low[index] = dot_nn(act_ref[rows, :], down_ref[...]).astype(jnp.bfloat16)
        return carry

    lax.fori_loop(0, 2, step, 0)
    for index in range(2):
        out_refs[index][...] = out_low[index]
        back_refs[index][...] = back_low[index]


def feed_back_kernel(count, meta_ref, *refs):
    sums, rest = refs[:5], refs[5:]
    mixed_ref, grad_ref, full_ref, gain_ref, grad_mixed_ref, grad_low_ref, grad_gain_ref = rest[:7]
    block_refs, attn = rest[7 : 7 + count], rest[7 + count]
    here = meta_ref[0]
    grad_hidden = wide(sums[0][...])
    for part in sums[1:]:
        grad_hidden = grad_hidden + wide(part[...])
    mixed = mixed_ref[...]
    scale = lax.rsqrt(jnp.mean(mixed * mixed, axis=1, keepdims=True) + EPSILON)
    normed = mixed * scale
    weighted = grad_hidden * gain_ref[...]
    grad_in = scale * (weighted - normed * jnp.mean(weighted * normed, axis=1, keepdims=True))
    grad_gain_ref[...] = jnp.sum(grad_hidden * normed, axis=0, keepdims=True)
    grad_mixed = wide(grad_ref[...]) + grad_in
    grad_mixed_ref[...] = grad_mixed
    grad_low_ref[...] = grad_mixed.astype(jnp.bfloat16)
    attn[...] = dot_nt(grad_low_ref[...], full_ref[...]).astype(jnp.bfloat16)
    for bits in range(count):
        owner = lax.bitwise_xor(here, bits)
        block_refs[bits][...] = attn[:, pl.ds(aligned(owner * 2 * HD, 2 * HD), 2 * HD)]


def wide_out_kernel(count, parts, meta_ref, *refs):
    blocks, (gate_ref, up_ref, held) = refs[:count], refs[count:]
    here = meta_ref[0]
    for bits in range(count):
        held[lax.bitwise_xor(here, bits)] = wide(blocks[bits][...])
    inner = held.shape[2] // 2
    main = inner // 128 * 128
    piece = inner // parts
    for kind, out_ref in enumerate((gate_ref, up_ref)):
        for part in range(parts):
            columns = []
            for owner in range(count):
                start, stop = part * piece, (part + 1) * piece
                begin = kind * main
                if start < main:
                    columns.append(held[owner, :, begin + start : begin + min(stop, main)])
                if stop > main:
                    begin = main + kind * (inner - main)
                    columns.append(held[owner, :, begin + max(start, main) : begin + stop])
            out_ref[:, part * count * piece : (part + 1) * count * piece] = jnp.concatenate(
                columns, axis=1
            )


def rows_out_kernel(meta_ref, *refs):
    blocks, out_ref = refs[:-1], refs[-1]
    rows = out_ref.shape[0] // len(blocks)
    start = blocks[0].shape[0] - rows
    for bits, block in enumerate(blocks):
        owner = lax.bitwise_xor(meta_ref[0], bits)
        out_ref[pl.ds(aligned(owner * rows, 16), rows), :] = wide(
            block[start:, : out_ref.shape[1]]
        )


def heads_out_kernel(count, own, extra, meta_ref, *refs):
    blocks, rest = refs[:count], refs[count:]
    query_ref, key_ref, value_ref, proj_ref, gain_ref, held = rest
    here = meta_ref[0]
    pair = 2 * HD
    part = (blocks[0].shape[0] - own - extra) // 4
    gains = jnp.zeros(gain_ref.shape, jnp.float32)
    for bits in range(count):
        owner = lax.bitwise_xor(here, bits)
        block = wide(blocks[bits][...])
        query_ref[:, pl.ds(aligned(owner * pair, pair), pair)] = block[:own, :pair]
        held[owner] = block[:own, pair:]
        gains = gains + block[own : own + extra, :]
        for index in range(4):
            source = own + extra + index * part
            proj_ref[
                pl.ds(aligned(owner * part, part), part), index * 2 * pair : (index + 1) * 2 * pair
            ] = block[source : source + part, :]
    gain_ref[...] = gains
    first, _ = lane_masks(own)
    for index in range(count // 2):
        early, late = held[2 * index], held[2 * index + 1]
        lanes = slice(index * pair, (index + 1) * pair)
        key_ref[:, lanes] = jnp.where(first, early, pltpu.roll(late, HD, 1))
        value_ref[:, lanes] = jnp.where(first, pltpu.roll(early, HD, 1), late)


SCALARS = pl.BlockSpec(memory_space=pltpu.SMEM)
WHOLE = pl.BlockSpec(memory_space=pltpu.VMEM)
PLACED = pl.BlockSpec(memory_space=pl.ANY)
FAR = pl.BlockSpec(memory_space=pltpu.HBM)


def shaped(shape, kind=jnp.bfloat16):
    return jax.ShapeDtypeStruct(shape, kind)


def whole_call(kernel, outs, ins, flops, scratch=(), grant=24, specs=None):
    moved = sum(math.prod(out.shape) * out.dtype.itemsize for out in outs)
    return pl.pallas_call(
        kernel,
        out_shape=outs,
        in_specs=[SCALARS] + (specs or [WHOLE] * ins),
        out_specs=[WHOLE] * len(outs),
        scratch_shapes=list(scratch),
        cost_estimate=pl.CostEstimate(
            flops=int(flops), bytes_accessed=int(2 * moved), transcendentals=0
        ),
        compiler_params=pltpu.CompilerParams(vmem_limit_bytes=grant * 2**20),
    )


def rows_call(kernel, arrays, kept, outs, shared, index, flops, scratch=(), grant=24):
    specs = [SCALARS] + [WHOLE] * (len(arrays) - 1) + [PLACED] * len(kept)
    out_specs, shapes = [], []
    for position, out in enumerate(outs):
        if position < shared:
            rows = out.shape[0] // 4
            out_specs.append(
                pl.BlockSpec((rows, out.shape[1]), lambda step, index=index: (index, 0))
            )
        else:
            out_specs.append(pl.BlockSpec(out.shape, lambda step: (0, 0)))
        shapes.append(out)
    moved = sum(math.prod(out.shape) * out.dtype.itemsize for out in outs)
    return pl.pallas_call(
        kernel,
        grid=(1,),
        out_shape=shapes,
        in_specs=specs,
        out_specs=out_specs,
        scratch_shapes=list(scratch),
        input_output_aliases={len(arrays) + place: place for place in range(len(kept))},
        cost_estimate=pl.CostEstimate(
            flops=int(flops), bytes_accessed=int(moved), transcendentals=0
        ),
        compiler_params=pltpu.CompilerParams(vmem_limit_bytes=grant * 2**20),
    )(*arrays, *kept)


def local_heads(
    block_input, doc_starts, out_grad, query_weight, key_weight, value_weight, output_weight,
    gate_weight, up_weight, down_weight, mixer_gain, feed_gain, query_gain, key_gain,
):
    low = jnp.bfloat16
    tokens, width = block_input.shape[1:]
    count = lax.axis_size("ctx")
    shards = lax.axis_size("fsdp")
    here = lax.axis_index("ctx").astype(jnp.int32)
    shard = lax.axis_index("fsdp").astype(jnp.int32)
    stream = tokens * count
    docs = doc_starts.shape[1]
    pair = 2 * HD
    own_rows = width // shards
    extra = 16
    meta = jnp.concatenate([here[None], shard[None], doc_starts[0].astype(jnp.int32)])
    own_input = block_input[0]
    own_grad = out_grad[0]
    inner = down_weight.shape[0] // count
    wide_inner = inner * shards
    padded = -(-wide_inner // 128) * 128
    proj_rows = own_rows // count
    edges = [(0, 1), (3, 2)]
    middle = [(1, 2), (2, 1)]
    relay = [(1, 0), (2, 3)]

    def near(piece, bits):
        return shift_fsdp(piece, flipped(bits, shards))

    across, along, partner = gather_near(own_input)
    piece_rows = own_rows + extra + 4 * proj_rows
    head_piece = whole_call(
        take_heads_kernel,
        [shaped((piece_rows, 2 * pair))],
        8,
        0,
        [
            pltpu.VMEM((extra, 2 * pair), jnp.float32),
            pltpu.VMEM((3, own_rows, pair), low),
            pltpu.VMEM((proj_rows, width), low),
            pltpu.SemaphoreType.DMA((4,)),
        ],
        grant=8,
        specs=[FAR] * 4 + [WHOLE] * 4,
    )(
        meta, query_weight, key_weight, value_weight, output_weight,
        mixer_gain[None], feed_gain[None], query_gain[None], key_gain[None],
    )[0]
    head_pieces = [head_piece] + [near(head_piece, bits) for bits in (1, 2, 3)]
    feed_rows = own_rows + inner
    feed_piece = whole_call(
        functools.partial(take_wide_kernel, shards),
        [shaped((feed_rows, 2 * wide_inner))],
        3,
        2 * own_rows * 2 * wide_inner * 2048,
        [
            pltpu.VMEM((2 * shards, own_rows, 256), low),
            pltpu.SemaphoreType.DMA((2 * shards,)),
            pltpu.VMEM((inner, width), low),
            pltpu.SemaphoreType.DMA(()),
            pltpu.VMEM((own_rows, 2 * wide_inner), jnp.float32),
        ],
        grant=16,
        specs=[FAR] * 3,
    )(behind(meta, head_piece), gate_weight, up_weight, down_weight)[0]
    feed_first = behind(feed_piece, *head_pieces[1:])
    feed_far = near(feed_first, 2)
    feed_near = near(feed_first, 1)
    corner = gather_corner(across, along)
    others = gather_far(across, along, corner)
    input_blocks = [own_input, partner, across, others[0], along, others[1], corner, others[2]]

    where_at = jnp.arange(stream, dtype=jnp.int32)
    begins = doc_begin(doc_starts[0], where_at)
    lanes = jnp.arange(pair) % (HD // 2)
    frequency = ROPE_BASE ** (-(2.0 * lanes.astype(jnp.float32)) / HD)
    angles = (where_at - begins).astype(jnp.float32)[:, None] * frequency[None, :]
    cosine = jnp.cos(angles)
    sine = jnp.sin(angles) * jnp.where(jnp.arange(pair) % HD < HD // 2, -1.0, 1.0)[None, :]

    heads_weight, gain_mixer, gain_feed, gain_heads, proj_part = whole_call(
        functools.partial(arrange_heads_kernel, extra),
        [
            shaped((width, 2 * pair)),
            shaped((1, width), jnp.float32),
            shaped((1, width), jnp.float32),
            shaped((8, pair), jnp.float32),
            shaped((shards * proj_rows, width)),
        ],
        4,
        0,
        grant=8,
    )(behind(meta, cosine, sine), *head_pieces)

    kept = []
    for index in range(4):
        kept = rows_call(
            head_linear_kernel,
            [meta]
            + [input_blocks[bits] for bits in ORDER[2 * index : 2 * index + 2]]
            + [heads_weight, gain_mixer],
            kept,
            [shaped((stream, width)), shaped((stream, 2 * pair), jnp.float32)],
            2,
            index,
            4 * tokens * width * 2 * pair,
            grant=12,
        )
    hidden_in, linear = kept

    pairs = stream * stream // 2
    extra_piece = behind(jnp.concatenate([own_grad, proj_part], axis=0), corner)
    extra_across, extra_along, extra_partner = gather_near(extra_piece)
    extra_corner = swap_ctx(extra_piece, 6)
    query_att, key_att, value_att, attn, lse, *attn_low = whole_call(
        functools.partial(attention_kernel, tokens, count, docs),
        [
            shaped((stream, pair)),
            shaped((stream, pair)),
            shaped((stream, pair)),
            shaped((stream, pair), jnp.float32),
            shaped((count, 1, 2 * tokens), jnp.float32),
        ]
        + [shaped((tokens, pair))] * count,
        4,
        8 * pairs * HD,
        [
            pltpu.VMEM((count, HD + 16, tokens), low),
            pltpu.VMEM((HD + 16, 2 * tokens), jnp.float32),
            pltpu.VMEM((stream, pair), low),
        ],
        grant=20,
    )(meta, linear, cosine, sine, gain_heads)

    attn_blocks = exchange_plane(attn_low)
    feed_middle = shift_fsdp(behind(feed_piece, attn_blocks[1]), middle)
    feed_relay = shift_fsdp(behind(feed_far, attn_blocks[1]), relay)
    extra_others = gather_far(extra_across, extra_along, extra_corner, attn_blocks[1])
    extra_blocks = [
        extra_piece, extra_partner, extra_across, extra_others[0],
        extra_along, extra_others[1], extra_corner, extra_others[2],
    ]
    full_proj, attn_rows, mixed, hidden_mid = whole_call(
        functools.partial(project_kernel, count, shards, tokens),
        [
            shaped((width, width)),
            shaped((tokens, width)),
            shaped((tokens, width), jnp.float32),
            shaped((tokens, width)),
        ],
        2 * count + 2,
        2 * tokens * width * width,
        [pltpu.VMEM((tokens, width), low)],
        grant=20,
    )(meta, *attn_blocks, *extra_blocks, own_input, gain_feed)

    hidden_across, hidden_along, hidden_partner = gather_near(hidden_mid)
    hidden_corner = swap_ctx(hidden_mid, 6)
    wide_weight, down_part = whole_call(
        arrange_feed_kernel,
        [shaped((width, 2 * wide_inner)), shaped((padded, width))],
        5,
        0,
        grant=16,
    )(behind(meta, hidden_mid), feed_piece, feed_near, feed_far, feed_middle, feed_relay)
    hidden_blocks = {0: hidden_mid, 1: hidden_partner, 2: hidden_across, 4: hidden_along}
    out_parts, back_parts = [None] * count, [None] * count
    kept = []
    for index in range(4):
        chosen = ORDER[2 * index : 2 * index + 2]
        results = rows_call(
            feed_kernel,
            [meta]
            + [hidden_blocks[bits] for bits in chosen]
            + [extra_blocks[bits] for bits in chosen]
            + [wide_weight, down_part],
            kept,
            [
                shaped((stream, width)),
                shaped((stream, width)),
                shaped((stream, padded)),
                shaped((stream, 2 * wide_inner)),
            ]
            + [shaped((tokens, width))] * 4,
            4,
            index,
            24 * tokens * width * wide_inner,
            [pltpu.VMEM((2, tokens, width), low)] * 2,
            grant=32,
        )
        kept = results[:4]
        for place, bits in enumerate(chosen):
            out_parts[bits] = results[4 + place]
            back_parts[bits] = results[6 + place]
        if index == 0:
            far = gather_far(hidden_across, hidden_along, hidden_corner, results[6])
            hidden_blocks.update({3: far[0], 5: far[1], 6: hidden_corner, 7: far[2]})
            weight_piece = behind(heads_weight, far[2])
            weight_near = gather_near(weight_piece)
            weight_corner = swap_ctx(weight_piece, 6)
    hidden_all, grad_all, act_all, grad_wide_all = kept
    back_own, back_pairs = scatter_pair(back_parts)
    back_sums = back_own + scatter_links(back_pairs)

    def scatter_early(pieces):
        return shift_fsdp(pieces[3], edges), shift_fsdp(pieces[3], middle)

    def scatter_late(pieces, early, *ready):
        second = behind((wide(pieces[2]) + wide(early)).astype(low), *ready)
        return near(second, 2), near(behind(pieces[1], *ready), 1)

    grad_down = contract_rows(behind(act_all, *back_pairs), grad_all).astype(low)
    grad_wide = contract_rows(behind(hidden_all, grad_down), grad_wide_all).astype(low)
    feed_pieces = whole_call(
        pack_feed_kernel, [shaped((feed_rows, 2 * wide_inner))] * shards, 2, 0, grant=16
    )(meta, grad_wide, grad_down)
    wide_edge, wide_middle = scatter_early(feed_pieces)
    out_own, out_pairs = scatter_pair([behind(part, grad_wide) for part in out_parts])

    grad_mixed, grad_mixed_low, grad_feed, *grad_blocks = whole_call(
        functools.partial(feed_back_kernel, count),
        [
            shaped((tokens, width), jnp.float32),
            shaped((tokens, width)),
            shaped((1, width), jnp.float32),
        ]
        + [shaped((tokens, pair))] * count,
        9,
        2 * tokens * width * width,
        [pltpu.VMEM((tokens, width), low)],
        grant=20,
    )(meta, *back_sums, mixed, own_grad, full_proj, gain_feed)
    grad_attn = exchange_plane(grad_blocks)
    wide_late = scatter_late(feed_pieces, wide_edge, grad_blocks[0])
    proj_blocks = whole_call(
        functools.partial(proj_grad_kernel, shards),
        [shaped((shards * proj_rows, width))] * count,
        2,
        2 * tokens * width * width,
        [pltpu.VMEM((width, width), low)],
        grant=16,
    )(meta, attn_rows, grad_mixed_low)
    proj_own, proj_pairs = scatter_pair(proj_blocks)
    proj_parts = proj_own + scatter_links(proj_pairs)
    out_sums = out_own + scatter_links([behind(part, grad_blocks[0]) for part in out_pairs])

    back_outs = whole_call(
        functools.partial(attention_back_kernel, tokens, count, docs),
        [shaped((stream, 2 * pair)), shaped((8, pair), jnp.float32)]
        + [shaped((tokens, 2 * pair))] * count,
        9 + count,
        20 * pairs * HD,
        [
            pltpu.VMEM((count, HD, tokens), low),
            pltpu.VMEM((stream, pair), jnp.float32),
            pltpu.VMEM((stream, pair), jnp.float32),
            pltpu.VMEM((stream, pair), jnp.float32),
            pltpu.VMEM((HD, 2 * tokens), jnp.float32),
            pltpu.VMEM((stream, pair), low),
        ],
        grant=24,
    )(meta, linear, cosine, sine, gain_heads, query_att, key_att, value_att, attn, lse, *grad_attn)
    grad_linear, gain_sums, *token_blocks = back_outs

    token_grads = exchange_plane(token_blocks)
    late_linear = behind(grad_linear, token_grads[1])
    weight_far = gather_far(weight_near[0], weight_near[1], weight_corner, late_linear)
    weight_all = [
        weight_piece, weight_near[2], weight_near[0], weight_far[0],
        weight_near[1], weight_far[1], weight_corner, weight_far[2],
    ]
    grad_heads = contract_rows(hidden_in, late_linear).astype(low)
    grad_mixer = jnp.sum(
        contract_cols(late_linear, heads_weight) * wide(hidden_in), axis=0, keepdims=True
    )
    packed = whole_call(
        functools.partial(pack_heads_kernel, extra),
        [shaped((piece_rows, 2 * pair))] * shards,
        10,
        0,
        [
            pltpu.VMEM((shards * proj_rows, width), low),
            pltpu.VMEM((1, width), jnp.float32),
            pltpu.VMEM((8, pair), jnp.float32),
            pltpu.VMEM((extra, 2 * pair), jnp.float32),
        ],
        grant=12,
    )(meta, grad_heads, grad_mixer, gain_mixer, grad_feed, gain_sums, *proj_parts)
    heads_sent = [near(packed[bits], bits) for bits in (1, 2, 3)]

    def total_of(first, *parts):
        return sum([wide(part) for part in parts], wide(first)).astype(low)

    def total_late(pieces, parts, *ready):
        return total_of(pieces[0], *[behind(part, *ready) for part in parts])

    wide_total = total_late(feed_pieces, (wide_middle,) + wide_late, packed[0])
    wide_blocks = gather_plane(wide_total)
    input_grad = whole_call(
        functools.partial(input_grad_kernel, count),
        [shaped((tokens, width), jnp.float32)],
        2 * count + 3,
        2 * tokens * width * 2 * width,
        grant=20,
    )(meta, *token_grads, *weight_all, own_input, grad_mixed, gain_mixer)[0]
    heads_total = total_of(packed[0], *heads_sent)
    heads_blocks = gather_plane(heads_total)
    block_output = (
        mixed + sum(wide(behind(part, packed[0])) for part in out_sums)
    ).astype(low)

    out_down = whole_call(
        rows_out_kernel, [shaped((count * inner, width), jnp.float32)], count, 0
    )(meta, *wide_blocks)[0]
    tile = own_rows // 4
    out_gate, out_up = pl.pallas_call(
        functools.partial(wide_out_kernel, count, shards),
        grid=(4,),
        in_specs=[SCALARS]
        + [pl.BlockSpec((tile, 2 * wide_inner), lambda step: (step, 0))] * count,
        out_specs=[pl.BlockSpec((tile, wide_inner * count), lambda step: (step, 0))] * 2,
        out_shape=[shaped((own_rows, wide_inner * count), jnp.float32)] * 2,
        scratch_shapes=[pltpu.VMEM((count, tile, 2 * wide_inner), jnp.float32)],
        compiler_params=pltpu.CompilerParams(vmem_limit_bytes=24 * 2**20),
        name="wide_out",
    )(meta, *wide_blocks)
    out_query, out_key, out_value, out_proj, gain_out = whole_call(
        functools.partial(heads_out_kernel, count, own_rows, extra),
        [
            shaped((own_rows, width), jnp.float32),
            shaped((own_rows, KVH * HD), jnp.float32),
            shaped((own_rows, KVH * HD), jnp.float32),
            shaped((own_rows, width), jnp.float32),
            shaped((extra, 2 * pair), jnp.float32),
        ],
        count,
        0,
        [pltpu.VMEM((count, own_rows, pair), jnp.float32)],
    )(meta, *heads_blocks)
    return (
        block_output[None],
        input_grad[None],
        out_query,
        out_key,
        out_value,
        out_proj,
        out_gate,
        out_up,
        out_down,
        gain_out[0],
        gain_out[1],
        gain_out[2, : query_gain.shape[0]],
        gain_out[3, : key_gain.shape[0]],
    )


def divides_heads(mesh):
    return mesh.shape["ctx"] == KVH and mesh.shape["fsdp"] == 4 and H == 2 * KVH


def solution(mesh):
    in_specs = (
        P("fsdp", "ctx", None),
        P("fsdp", None),
        P("fsdp", "ctx", None),
        P("fsdp", None),
        P("fsdp", None),
        P("fsdp", None),
        P("fsdp", None),
        P("fsdp", None),
        P("fsdp", None),
        P("fsdp", None),
        P("fsdp"),
        P("fsdp"),
        P("fsdp"),
        P("fsdp"),
    )
    out_specs = (
        P("fsdp", "ctx", None),
        P("fsdp", "ctx", None),
        P("fsdp", None),
        P("fsdp", None),
        P("fsdp", None),
        P("fsdp", None),
        P("fsdp", None),
        P("fsdp", None),
        P("fsdp", None),
        P("fsdp"),
        P("fsdp"),
        P("fsdp"),
        P("fsdp"),
    )
    if not divides_heads(mesh):
        return jax.shard_map(
            local, mesh=mesh, in_specs=in_specs, out_specs=out_specs, check_vma=False
        )

    return jax.shard_map(local_heads, mesh=mesh, in_specs=in_specs, out_specs=out_specs, check_vma=False)
```

```python
import functools
import math

import jax
import jax.numpy as jnp
from jax import lax
from jax.experimental import pallas as pl
from jax.experimental.pallas import tpu as pltpu
from jax.sharding import PartitionSpec as P

H = 16
KVH = 8
HD = 64


EPSILON = 1e-05
ROPE_BASE = 1000000.0
FLOOR_SCORE = -1e30


def place_rows(row_index, tokens, ctx_count):
    half_rows = tokens // 2
    device = row_index // tokens
    offset = row_index % tokens
    early = device * half_rows + offset
    late = (2 * ctx_count - 1 - device) * half_rows + offset - half_rows
    return jnp.where(offset < half_rows, early, late)


def doc_begin(starts, where_at):
    started = starts[None, :] <= where_at[:, None]
    return jnp.max(jnp.where(started, starts[None, :], 0), axis=1)


def rotary(positions):
    half_dim = HD // 2
    frequency = ROPE_BASE ** (-(2.0 * jnp.arange(half_dim, dtype=jnp.float32)) / HD)
    angles = positions.astype(jnp.float32)[:, None] * frequency[None, :]
    angles = jnp.concatenate([angles, angles], axis=1)
    return (jnp.cos(angles)[:, None, :], jnp.sin(angles)[:, None, :])


def rotate_pairs(values, cosine, sine_part):
    half_dim = values.shape[-1] // 2
    rolled = jnp.concatenate([-values[..., half_dim:], values[..., :half_dim]], axis=-1)
    return values * cosine + rolled * sine_part


def rotate_back(grads, cosine, sine_part):
    half_dim = grads.shape[-1] // 2
    moved = grads * sine_part
    rolled = jnp.concatenate([moved[..., half_dim:], -moved[..., :half_dim]], axis=-1)
    return grads * cosine + rolled


def unit_norm(values):
    scaling = lax.rsqrt(jnp.mean(values * values, axis=-1, keepdims=True) + EPSILON)
    return (values * scaling, scaling)


def norm_back(grad_out, normed, scaling, gain_row):
    weighted = grad_out * gain_row
    grad_in = scaling * (weighted - normed * jnp.mean(weighted * normed, axis=-1, keepdims=True))
    grad_gain = jnp.sum((grad_out * normed).reshape(-1, normed.shape[-1]), axis=0)
    return (grad_in, grad_gain)


def score_block(query_rows, key_rows, scaling):
    return (
        jnp.einsum("igrd,jgd->grij", query_rows, key_rows, preferred_element_type=jnp.float32)
        * scaling
    )


def visible_pairs(query_at, query_doc, key_at, key_doc):
    return (query_doc[:, None] == key_doc[None, :]) & (key_at[None, :] <= query_at[:, None])


def any_visible(query_at, query_doc, key_at):
    return (jnp.min(key_at) <= jnp.max(query_at)) & (jnp.max(key_at) >= jnp.min(query_doc))


def contract_rows(left, right):
    return lax.dot_general(
        left, right, (((0,), (0,)), ((), ())), preferred_element_type=jnp.float32
    )


def contract_cols(left, right):
    return lax.dot_general(
        left, right, (((1,), (1,)), ((), ())), preferred_element_type=jnp.float32
    )


def keep_same(totals):
    return totals


def local(
    block_input,
    doc_starts,
    out_grad,
    query_weight,
    key_weight,
    value_weight,
    output_weight,
    gate_weight,
    up_weight,
    down_weight,
    mixer_gain,
    feed_gain,
    query_gain,
    key_gain,
):
    tokens = block_input.shape[1]
    ctx_count = lax.axis_size("ctx")
    repeat = H // KVH
    kv_width = KVH * HD
    scaling = HD ** (-0.5)
    inputs = block_input[0].astype(jnp.float32)
    starts = doc_starts[0]
    where_at = place_rows(
        lax.axis_index("ctx") * tokens + jnp.arange(tokens, dtype=jnp.int32), tokens, ctx_count
    )
    begins = doc_begin(starts, where_at)
    cosine, sine_part = rotary(where_at - begins)
    gathered = (
        lax.all_gather(query_weight, "fsdp", axis=0, tiled=True),
        lax.all_gather(key_weight, "fsdp", axis=0, tiled=True),
        lax.all_gather(value_weight, "fsdp", axis=0, tiled=True),
        lax.all_gather(output_weight, "fsdp", axis=0, tiled=True),
        lax.all_gather(gate_weight, "fsdp", axis=0, tiled=True),
        lax.all_gather(up_weight, "fsdp", axis=0, tiled=True),
        lax.all_gather(down_weight, "fsdp", axis=0, tiled=True),
        lax.all_gather(mixer_gain, "fsdp", axis=0, tiled=True),
        lax.all_gather(feed_gain, "fsdp", axis=0, tiled=True),
        lax.all_gather(query_gain, "fsdp", axis=0, tiled=True),
        lax.all_gather(key_gain, "fsdp", axis=0, tiled=True),
    )
    full_query, full_key, full_value, full_proj, full_gate, full_up, full_down = gathered[:7]
    gain_mixer, gain_feed, gain_query, gain_key = [
        entry.astype(jnp.float32) for entry in gathered[7:]
    ]
    normed_in, scale_in = unit_norm(inputs)
    hidden_in = (normed_in * gain_mixer).astype(jnp.bfloat16)
    query_lin = jnp.dot(hidden_in, full_query, preferred_element_type=jnp.float32)
    key_lin = jnp.dot(hidden_in, full_key, preferred_element_type=jnp.float32)
    value_lin = jnp.dot(hidden_in, full_value, preferred_element_type=jnp.float32)
    query_normed, query_scale = unit_norm(query_lin.reshape(tokens, H, HD))
    key_normed, key_scale = unit_norm(key_lin.reshape(tokens, KVH, HD))
    query_att = (
        rotate_pairs(query_normed * gain_query, cosine, sine_part)
        .reshape(tokens, H * HD)
        .astype(jnp.bfloat16)
    )
    key_att = (
        rotate_pairs(key_normed * gain_key, cosine, sine_part)
        .reshape(tokens, kv_width)
        .astype(jnp.bfloat16)
    )
    value_att = value_lin.astype(jnp.bfloat16)
    query_four = query_att.reshape(tokens, KVH, repeat, HD)
    start_state = (
        jnp.full((KVH, repeat, tokens), FLOOR_SCORE, jnp.float32),
        jnp.zeros((KVH, repeat, tokens), jnp.float32),
        jnp.zeros((tokens, H * HD), jnp.float32),
    )
    key_part = lax.all_gather(key_att, "ctx", axis=0, tiled=True)
    value_part = lax.all_gather(value_att, "ctx", axis=0, tiled=True)
    rows = key_part.shape[0]
    width = math.gcd(math.gcd(rows, tokens // 2), 512)

    def forward_key_block(block_index, totals):
        offset = block_index * width
        key_rows = lax.dynamic_slice_in_dim(key_part, offset, width, 0).reshape(width, KVH, HD)
        value_rows = lax.dynamic_slice_in_dim(value_part, offset, width, 0).reshape(width, KVH, HD)
        key_at = place_rows(offset + jnp.arange(width, dtype=jnp.int32), tokens, ctx_count)

        def attend(totals):
            highest, total_mass, accum = totals
            visible = visible_pairs(where_at, begins, key_at, doc_begin(starts, key_at))
            scores = jnp.where(visible, score_block(query_four, key_rows, scaling), FLOOR_SCORE)
            new_high = jnp.maximum(highest, jnp.max(scores, axis=-1))
            rescale = jnp.exp(highest - new_high)
            probable = jnp.where(visible, jnp.exp(scores - new_high[..., None]), 0.0)
            total_mass = total_mass * rescale + jnp.sum(probable, axis=-1)
            part_out = jnp.einsum(
                "grij,jgd->igrd",
                probable.astype(jnp.bfloat16),
                value_rows,
                preferred_element_type=jnp.float32,
            )
            accum = (
                accum.reshape(tokens, KVH, repeat, HD)
                * jnp.transpose(rescale, (2, 0, 1))[..., None]
                + part_out
            )
            return (new_high, total_mass, accum.reshape(tokens, H * HD))

        return lax.cond(any_visible(where_at, begins, key_at), attend, keep_same, totals)

    highest, total_mass, accum = lax.fori_loop(0, rows // width, forward_key_block, start_state)
    lse_heads = highest + jnp.log(total_mass)
    attn_raw = (
        accum.reshape(tokens, KVH, repeat, HD) / jnp.transpose(total_mass, (2, 0, 1))[..., None]
    ).reshape(tokens, H * HD)
    attn_low = attn_raw.astype(jnp.bfloat16)
    mixed = inputs + jnp.dot(attn_low, full_proj, preferred_element_type=jnp.float32)
    normed_mid, scale_mid = unit_norm(mixed)
    hidden_mid = (normed_mid * gain_feed).astype(jnp.bfloat16)
    gate_lin = jnp.dot(hidden_mid, full_gate, preferred_element_type=jnp.float32)
    up_lin = jnp.dot(hidden_mid, full_up, preferred_element_type=jnp.float32)
    sigmoid_gate = jax.nn.sigmoid(gate_lin)
    activated = (gate_lin * sigmoid_gate * up_lin).astype(jnp.bfloat16)
    block_output = (
        mixed + jnp.dot(activated, full_down, preferred_element_type=jnp.float32)
    ).astype(jnp.bfloat16)
    regathered = (
        lax.all_gather(query_weight, "fsdp", axis=0, tiled=True),
        lax.all_gather(key_weight, "fsdp", axis=0, tiled=True),
        lax.all_gather(value_weight, "fsdp", axis=0, tiled=True),
        lax.all_gather(output_weight, "fsdp", axis=0, tiled=True),
        lax.all_gather(gate_weight, "fsdp", axis=0, tiled=True),
        lax.all_gather(up_weight, "fsdp", axis=0, tiled=True),
        lax.all_gather(down_weight, "fsdp", axis=0, tiled=True),
        lax.all_gather(mixer_gain, "fsdp", axis=0, tiled=True),
        lax.all_gather(feed_gain, "fsdp", axis=0, tiled=True),
        lax.all_gather(query_gain, "fsdp", axis=0, tiled=True),
        lax.all_gather(key_gain, "fsdp", axis=0, tiled=True),
    )
    full_query, full_key, full_value, full_proj, full_gate, full_up, full_down = regathered[:7]
    gain_mixer, gain_feed, gain_query, gain_key = [
        entry.astype(jnp.float32) for entry in regathered[7:]
    ]
    grad_top = out_grad[0].astype(jnp.float32)
    grad_top_low = grad_top.astype(jnp.bfloat16)
    grad_down = contract_rows(activated, grad_top_low)
    grad_act = contract_cols(grad_top_low, full_down)
    grad_gate_low = (
        grad_act * up_lin * sigmoid_gate * (1.0 + gate_lin * (1.0 - sigmoid_gate))
    ).astype(jnp.bfloat16)
    grad_up_low = (grad_act * gate_lin * sigmoid_gate).astype(jnp.bfloat16)
    grad_gate = contract_rows(hidden_mid, grad_gate_low)
    grad_up = contract_rows(hidden_mid, grad_up_low)
    grad_hidden_mid = contract_cols(grad_gate_low, full_gate) + contract_cols(grad_up_low, full_up)
    grad_normed_mid, grad_feed = norm_back(grad_hidden_mid, normed_mid, scale_mid, gain_feed)
    grad_mixed = grad_top + grad_normed_mid
    grad_mixed_low = grad_mixed.astype(jnp.bfloat16)
    grad_proj = contract_rows(attn_low, grad_mixed_low)
    grad_attn = contract_cols(grad_mixed_low, full_proj).astype(jnp.bfloat16)
    grad_four = grad_attn.reshape(tokens, KVH, repeat, HD)
    delta_heads = jnp.sum(
        grad_four.astype(jnp.float32) * attn_raw.reshape(tokens, KVH, repeat, HD), axis=-1
    )
    delta_grid = jnp.transpose(delta_heads, (1, 2, 0))
    lse_rows = jnp.transpose(lse_heads, (2, 0, 1)).reshape(tokens, H)
    delta_rows = delta_heads.reshape(tokens, H)
    query_key_part = lax.all_gather(key_att, "ctx", axis=0, tiled=True)
    query_value_part = lax.all_gather(value_att, "ctx", axis=0, tiled=True)
    rows = query_key_part.shape[0]
    query_width = math.gcd(math.gcd(rows, tokens // 2), 512)

    def query_key_block(block_index, grad_query_acc):
        offset = block_index * query_width
        key_rows = lax.dynamic_slice_in_dim(query_key_part, offset, query_width, 0).reshape(
            query_width, KVH, HD
        )
        value_rows = lax.dynamic_slice_in_dim(query_value_part, offset, query_width, 0).reshape(
            query_width, KVH, HD
        )
        key_at = place_rows(offset + jnp.arange(query_width, dtype=jnp.int32), tokens, ctx_count)

        def attend(grad_query_acc):
            visible = visible_pairs(where_at, begins, key_at, doc_begin(starts, key_at))
            scores = score_block(query_four, key_rows, scaling)
            probable = jnp.where(visible, jnp.exp(scores - lse_heads[..., None]), 0.0)
            grad_prob = jnp.einsum(
                "igrd,jgd->grij", grad_four, value_rows, preferred_element_type=jnp.float32
            )
            grad_score = (probable * (grad_prob - delta_grid[..., None])).astype(jnp.bfloat16)
            added = (
                jnp.einsum(
                    "grij,jgd->igrd", grad_score, key_rows, preferred_element_type=jnp.float32
                )
                * scaling
            )
            return grad_query_acc + added.reshape(tokens, H * HD)

        return lax.cond(any_visible(where_at, begins, key_at), attend, keep_same, grad_query_acc)

    grad_query_att = lax.fori_loop(
        0, rows // query_width, query_key_block, jnp.zeros((tokens, H * HD), jnp.float32)
    )
    lse_all, delta_all = (
        lax.all_gather(lse_rows.astype(jnp.bfloat16), "ctx", axis=0, tiled=True).astype(
            lse_rows.dtype
        ),
        lax.all_gather(delta_rows.astype(jnp.bfloat16), "ctx", axis=0, tiled=True).astype(
            delta_rows.dtype
        ),
    )
    key_three = key_att.reshape(tokens, KVH, HD)
    value_three = value_att.reshape(tokens, KVH, HD)
    empty_keys = jnp.zeros((tokens, kv_width), jnp.float32)
    query_part = lax.all_gather(query_att, "ctx", axis=0, tiled=True)
    grad_part = lax.all_gather(grad_attn, "ctx", axis=0, tiled=True)
    rows = query_part.shape[0]
    key_width = math.gcd(math.gcd(rows, tokens // 2), 512)

    def query_block(block_index, totals):
        offset = block_index * key_width
        query_rows = lax.dynamic_slice_in_dim(query_part, offset, key_width, 0).reshape(
            key_width, KVH, repeat, HD
        )
        grad_rows = lax.dynamic_slice_in_dim(grad_part, offset, key_width, 0).reshape(
            key_width, KVH, repeat, HD
        )
        query_at = place_rows(offset + jnp.arange(key_width, dtype=jnp.int32), tokens, ctx_count)
        query_doc = doc_begin(starts, query_at)
        lse_block = jnp.transpose(
            lax.dynamic_slice_in_dim(lse_all, offset, key_width, 0).reshape(key_width, KVH, repeat),
            (1, 2, 0),
        )
        delta_block = jnp.transpose(
            lax.dynamic_slice_in_dim(delta_all, offset, key_width, 0).reshape(
                key_width, KVH, repeat
            ),
            (1, 2, 0),
        )

        def attend(totals):
            grad_key_acc, grad_value_acc = totals
            visible = visible_pairs(query_at, query_doc, where_at, begins)
            scores = score_block(query_rows, key_three, scaling)
            probable = jnp.where(visible, jnp.exp(scores - lse_block[..., None]), 0.0)
            grad_prob = jnp.einsum(
                "igrd,jgd->grij", grad_rows, value_three, preferred_element_type=jnp.float32
            )
            grad_score = (probable * (grad_prob - delta_block[..., None])).astype(jnp.bfloat16)
            value_added = jnp.einsum(
                "grij,igrd->jgd",
                probable.astype(jnp.bfloat16),
                grad_rows,
                preferred_element_type=jnp.float32,
            )
            key_added = (
                jnp.einsum(
                    "grij,igrd->jgd", grad_score, query_rows, preferred_element_type=jnp.float32
                )
                * scaling
            )
            return (
                grad_key_acc + key_added.reshape(tokens, kv_width),
                grad_value_acc + value_added.reshape(tokens, kv_width),
            )

        return lax.cond(any_visible(query_at, query_doc, where_at), attend, keep_same, totals)

    grad_key_att, grad_value_att = lax.fori_loop(
        0, rows // key_width, query_block, (empty_keys, empty_keys)
    )
    grad_query_unit = rotate_back(grad_query_att.reshape(tokens, H, HD), cosine, sine_part)
    grad_query_lin, grad_qgain = norm_back(grad_query_unit, query_normed, query_scale, gain_query)
    grad_key_unit = rotate_back(grad_key_att.reshape(tokens, KVH, HD), cosine, sine_part)
    grad_key_lin, grad_kgain = norm_back(grad_key_unit, key_normed, key_scale, gain_key)
    grad_query_low = grad_query_lin.reshape(tokens, H * HD).astype(jnp.bfloat16)
    grad_key_low = grad_key_lin.reshape(tokens, kv_width).astype(jnp.bfloat16)
    grad_value_low = grad_value_att.astype(jnp.bfloat16)
    grad_query = contract_rows(hidden_in, grad_query_low)
    grad_key = contract_rows(hidden_in, grad_key_low)
    grad_value = contract_rows(hidden_in, grad_value_low)
    grad_hidden_in = (
        contract_cols(grad_query_low, full_query)
        + contract_cols(grad_key_low, full_key)
        + contract_cols(grad_value_low, full_value)
    )
    grad_normed_in, grad_mixer = norm_back(grad_hidden_in, normed_in, scale_in, gain_mixer)
    input_grad = grad_mixed + grad_normed_in
    parts = (
        lax.psum_scatter(
            grad_query.astype(jnp.bfloat16), "fsdp", scatter_dimension=0, tiled=True
        ).astype(jnp.float32),
        lax.psum_scatter(
            grad_key.astype(jnp.bfloat16), "fsdp", scatter_dimension=0, tiled=True
        ).astype(jnp.float32),
        lax.psum_scatter(
            grad_value.astype(jnp.bfloat16), "fsdp", scatter_dimension=0, tiled=True
        ).astype(jnp.float32),
        lax.psum_scatter(
            grad_proj.astype(jnp.bfloat16), "fsdp", scatter_dimension=0, tiled=True
        ).astype(jnp.float32),
        lax.psum_scatter(
            grad_gate.astype(jnp.bfloat16), "fsdp", scatter_dimension=0, tiled=True
        ).astype(jnp.float32),
        lax.psum_scatter(
            grad_up.astype(jnp.bfloat16), "fsdp", scatter_dimension=0, tiled=True
        ).astype(jnp.float32),
        lax.psum_scatter(
            grad_down.astype(jnp.bfloat16), "fsdp", scatter_dimension=0, tiled=True
        ).astype(jnp.float32),
        lax.psum_scatter(
            grad_mixer.astype(jnp.bfloat16), "fsdp", scatter_dimension=0, tiled=True
        ).astype(jnp.float32),
        lax.psum_scatter(
            grad_feed.astype(jnp.bfloat16), "fsdp", scatter_dimension=0, tiled=True
        ).astype(jnp.float32),
        lax.psum_scatter(
            grad_qgain.astype(jnp.bfloat16), "fsdp", scatter_dimension=0, tiled=True
        ).astype(jnp.float32),
        lax.psum_scatter(
            grad_kgain.astype(jnp.bfloat16), "fsdp", scatter_dimension=0, tiled=True
        ).astype(jnp.float32),
    )
    summed = (
        lax.psum(parts[0].astype(jnp.bfloat16), "ctx").astype(jnp.float32),
        lax.psum(parts[1].astype(jnp.bfloat16), "ctx").astype(jnp.float32),
        lax.psum(parts[2].astype(jnp.bfloat16), "ctx").astype(jnp.float32),
        lax.psum(parts[3].astype(jnp.bfloat16), "ctx").astype(jnp.float32),
        lax.psum(parts[4].astype(jnp.bfloat16), "ctx").astype(jnp.float32),
        lax.psum(parts[5].astype(jnp.bfloat16), "ctx").astype(jnp.float32),
        lax.psum(parts[6].astype(jnp.bfloat16), "ctx").astype(jnp.float32),
        lax.psum(parts[7].astype(jnp.bfloat16), "ctx").astype(jnp.float32),
        lax.psum(parts[8].astype(jnp.bfloat16), "ctx").astype(jnp.float32),
        lax.psum(parts[9].astype(jnp.bfloat16), "ctx").astype(jnp.float32),
        lax.psum(parts[10].astype(jnp.bfloat16), "ctx").astype(jnp.float32),
    )
    return (
        block_output[None],
        input_grad[None],
        summed[0],
        summed[1],
        summed[2],
        summed[3],
        summed[4],
        summed[5],
        summed[6],
        summed[7],
        summed[8],
        summed[9],
        summed[10],
    )


ORDER = (0, 1, 2, 4, 3, 5, 6, 7)


def flipped(bits, count):
    return [(index, index ^ bits) for index in range(count)]


def swap_ctx(values, bits):
    return lax.ppermute(values, "ctx", flipped(bits, lax.axis_size("ctx")))


def behind(values, *ready):
    return lax.optimization_barrier((values,) + ready)[0]


def dot_nn(left, right):
    return lax.dot_general(
        left, right, (((1,), (0,)), ((), ())), preferred_element_type=jnp.float32
    )


def dot_nt(left, right):
    return lax.dot_general(
        left, right, (((1,), (1,)), ((), ())), preferred_element_type=jnp.float32
    )


def wide(values):
    return values.astype(jnp.float32)


def gather_near(block):
    return swap_ctx(block, 2), swap_ctx(block, 4), swap_ctx(block, 1)


def gather_corner(across, along):
    half = across.shape[0] // 2
    first = swap_ctx(along[:half], 2)
    second = swap_ctx(across[half:], 4)
    return jnp.concatenate([first, second], axis=0)


def gather_far(across, along, corner, *ready):
    return [swap_ctx(behind(part, *ready), 1) for part in (across, along, corner)]


def gather_plane(block, *ready):
    across, along, partner = gather_near(block)
    corner = gather_corner(across, along)
    others = gather_far(across, along, corner, *ready)
    return [block, partner, across, others[0], along, others[1], corner, others[2]]


def scatter_pair(blocks):
    got = [swap_ctx(blocks[bits], 1) for bits in (3, 5, 7, 1)]
    sums = [
        (wide(blocks[bits]) + wide(other)).astype(jnp.bfloat16)
        for bits, other in zip((2, 4, 6), got)
    ]
    return [blocks[0], got[3]], sums


def scatter_links(sums):
    return [swap_ctx(part, bits) for bits, part in zip((2, 4, 6), sums)]


def exchange_plane(blocks):
    return [blocks[0]] + [swap_ctx(blocks[bits], bits) for bits in range(1, 8)]


def shift_fsdp(values, pairs):
    return lax.ppermute(values, "fsdp", pairs)


def slot_of(bits):
    return jnp.where(bits == 3, 4, jnp.where(bits == 4, 3, bits))


def row_of(place, here, tokens, count):
    half = tokens // 2
    device = jnp.where(place < count, place, 2 * count - 1 - place)
    late = jnp.where(place < count, 0, half)
    return slot_of(lax.bitwise_xor(device, here)) * tokens + late


def swap_half(values, low_lane):
    return jnp.where(low_lane, pltpu.roll(values, 96, 1), pltpu.roll(values, 32, 1))


def head_mean(values, first):
    lower = jnp.sum(jnp.where(first, values, 0.0), axis=1, keepdims=True)
    upper = jnp.sum(jnp.where(first, 0.0, values), axis=1, keepdims=True)
    return jnp.where(first, lower, upper) * (1.0 / HD)


def lane_masks(rows):
    lanes = lax.broadcasted_iota(jnp.int32, (rows, 2 * HD), 1)
    return lanes < HD, (lanes % HD) < (HD // 2)


def two_heads(values):
    first, _ = lane_masks(values.shape[0])
    zero = jnp.zeros_like(values)
    return jnp.concatenate(
        [jnp.where(first, values, zero), jnp.where(first, zero, values)], axis=0
    )


def begin_at(meta_ref, docs, where_at):
    begin = jnp.zeros_like(where_at)
    for doc in range(docs):
        begin = jnp.where(meta_ref[2 + doc] <= where_at, meta_ref[2 + doc], begin)
    return begin


def block_visible(meta_ref, docs, query_block, key_block, size):
    query_at = query_block * size + lax.broadcasted_iota(jnp.int32, (1, size), 1)
    begin = begin_at(meta_ref, docs, query_at)
    key_at = key_block * size + lax.broadcasted_iota(jnp.int32, (size, size), 0)
    return (key_at <= query_at) & (key_at >= begin)


def aligned(value, size):
    return pl.multiple_of(value, size)


def take_heads_kernel(
    meta_ref, query_ref, key_ref, value_ref, proj_ref, mixer_ref, feed_ref, query_gain_ref, key_gain_ref,
    out_ref, gains, windows, proj, sem,
):
    here = meta_ref[0]
    rows = query_ref.shape[0]
    pair = 2 * HD
    start = aligned(lax.shift_right_logical(here, 1) * pair, pair)
    part = proj.shape[0]
    copies = [
        pltpu.make_async_copy(
            query_ref.at[:, pl.ds(aligned(here * pair, pair), pair)], windows.at[0], sem.at[0]
        ),
        pltpu.make_async_copy(key_ref.at[:, pl.ds(start, pair)], windows.at[1], sem.at[1]),
        pltpu.make_async_copy(value_ref.at[:, pl.ds(start, pair)], windows.at[2], sem.at[2]),
        pltpu.make_async_copy(
            proj_ref.at[pl.ds(aligned(here * part, part), part), :], proj, sem.at[3]
        ),
    ]
    for copy in copies:
        copy.start()
    gains[...] = jnp.zeros_like(gains)
    gains[0:1, :] = wide(mixer_ref[...])
    gains[1:2, :] = wide(feed_ref[...])
    gains[2:3, : query_gain_ref.shape[1]] = wide(query_gain_ref[...])
    gains[3:4, : key_gain_ref.shape[1]] = wide(key_gain_ref[...])
    extra = gains.shape[0]
    out_ref[rows : rows + extra, :] = gains[...].astype(jnp.bfloat16)
    for copy in copies:
        copy.wait()
    out_ref[:rows, :pair] = windows[0]
    odd = lax.bitwise_and(here, 1) == 1
    keys = wide(windows[1])
    values = wide(windows[2])
    first, _ = lane_masks(rows)
    keys = jnp.where(odd, pltpu.roll(keys, HD, 1), keys)
    values = jnp.where(odd, values, pltpu.roll(values, HD, 1))
    out_ref[:rows, pair:] = jnp.where(first, keys, values).astype(jnp.bfloat16)
    for index in range(proj.shape[1] // (2 * pair)):
        target = rows + extra + index * part
        out_ref[target : target + part, :] = proj[:, index * 2 * pair : (index + 1) * 2 * pair]


def arrange_heads_kernel(
    extra, meta_ref, *refs
):
    pieces, (weight_ref, mixer_ref, feed_ref, gains_ref, proj_ref) = refs[:4], refs[4:]
    shard = meta_ref[1]
    rows = weight_ref.shape[0] // 4
    pair = 2 * HD
    each = HD // 4
    gains = jnp.zeros((8, pair), jnp.float32)
    part = proj_ref.shape[0] // 4
    for bits, piece in enumerate(pieces):
        owner = lax.bitwise_xor(shard, bits)
        weight_ref[pl.ds(aligned(owner * rows, rows), rows), :] = piece[:rows, :]
        block = wide(piece[rows : rows + extra, :])
        lanes = pl.ds(aligned(owner * rows, rows), rows)
        mixer_ref[:, lanes] = block[0:1, :]
        feed_ref[:, lanes] = block[1:2, :]
        gains = gains + pltpu.roll(block[:8, :pair], owner * each, 1)
        for index in range(proj_ref.shape[1] // (2 * pair)):
            source = rows + extra + index * part
            proj_ref[
                pl.ds(aligned(owner * part, part), part), index * 2 * pair : (index + 1) * 2 * pair
            ] = piece[source : source + part, :]
    gains_ref[...] = gains + pltpu.roll(gains, HD, 1)


def wide_column(column, main, rest):
    late = (column >= 2 * main).astype(jnp.int32)
    late_up = (column >= 2 * main + rest).astype(jnp.int32)
    early_up = (column >= main).astype(jnp.int32) * (1 - late)
    is_up = late * late_up + early_up
    return is_up, column - early_up * main - late * (main + late_up * rest)


def take_wide_kernel(shards, meta_ref, gate_ref, up_ref, down_ref, out_ref, window, sem, rows, down_sem, total):
    here = meta_ref[0]
    own_rows = window.shape[1]
    inner = out_ref.shape[1] // 2
    piece = inner // shards
    span = window.shape[2]
    shift = here * (piece - 128)
    copies = []
    for kind, source in enumerate((gate_ref, up_ref)):
        for part in range(shards):
            start = aligned(part * (source.shape[1] // shards) + here * 128, 128)
            copies.append(
                pltpu.make_async_copy(
                    source.at[:, pl.ds(start, span)],
                    window.at[kind * shards + part],
                    sem.at[kind * shards + part],
                )
            )
    down = pltpu.make_async_copy(
        down_ref.at[pl.ds(aligned(here * rows.shape[0], 16), rows.shape[0]), :], rows, down_sem
    )
    for copy in copies:
        copy.start()
    down.start()
    columns = lax.broadcasted_iota(jnp.int32, (1, 2 * inner), 1)
    main = inner // 128 * 128
    is_up, unit = wide_column(columns, main, inner - main)
    owner = jnp.zeros_like(unit)
    for part in range(1, shards):
        owner = jnp.where(unit >= part * piece, part, owner)
    target = unit - owner * piece + shift
    owner = owner + is_up * shards
    places = lax.broadcasted_iota(jnp.int32, (span, 2 * inner), 0)
    for copy in copies:
        copy.wait()
    total[...] = jnp.zeros_like(total)

    def add(index, carry):
        place = jnp.where(owner == index, target, -1)
        chosen = jnp.where(places == place, 1.0, 0.0).astype(jnp.bfloat16)
        total[...] += dot_nn(window[index], chosen)
        return carry

    lax.fori_loop(0, len(copies), add, 0)
    out_ref[:own_rows, :] = total[...].astype(jnp.bfloat16)
    down.wait()
    out_ref[own_rows:, : rows.shape[1]] = rows[...]
    out_ref[own_rows:, rows.shape[1] :] = jnp.zeros_like(out_ref[own_rows:, rows.shape[1] :])


def arrange_feed_kernel(meta_ref, own_ref, near_ref, far_ref, middle_ref, relay_ref, wide_ref, down_ref):
    shard = meta_ref[1]
    rows = wide_ref.shape[0] // 4
    inner = own_ref.shape[0] - rows
    width = down_ref.shape[1]
    for bits, piece in enumerate((own_ref, near_ref, far_ref, None)):
        owner = lax.bitwise_xor(shard, bits)
        if piece is None:
            piece = middle_ref[...] + relay_ref[...]
        wide_ref[pl.ds(aligned(owner * rows, rows), rows), :] = piece[:rows, :]
        down_ref[pl.ds(aligned(owner * inner, 16), inner), :] = piece[rows:, :width]
    down_ref[4 * inner :, :] = jnp.zeros_like(down_ref[4 * inner :, :])


def head_linear_kernel(
    meta_ref, first_ref, second_ref, weight_ref, gain_ref, *refs
):
    hidden_ref, linear_ref = refs[-2:]
    rows = first_ref.shape[0]
    for index, source in enumerate((first_ref, second_ref)):
        values = wide(source[...])
        scale = lax.rsqrt(jnp.mean(values * values, axis=1, keepdims=True) + EPSILON)
        hidden = (values * scale * gain_ref[...]).astype(jnp.bfloat16)
        hidden_ref[index * rows : (index + 1) * rows, :] = hidden
        linear_ref[index * rows : (index + 1) * rows, :] = dot_nn(hidden, weight_ref[...])


def attention_kernel(
    tokens, count, docs,
    meta_ref, lin_ref, cos_ref, sin_ref, gains_ref,
    query_ref, key_ref, value_ref, attn_ref, lse_ref, *refs,
):
    low_refs, (value_t, accum, low) = refs[:count], refs[count:]
    here = meta_ref[0]
    half = tokens // 2
    size = tokens
    blocks = count

    def prepare(place, carry):
        first, low_lane = lane_masks(half)
        source = aligned(row_of(place, here, tokens, count), half)
        target = aligned(place * half, half)
        cosine = cos_ref[pl.ds(target, half), :]
        sine = sin_ref[pl.ds(target, half), :]
        query = lin_ref[pl.ds(source, half), : 2 * HD]
        unit = query * lax.rsqrt(head_mean(query * query, first) + EPSILON) * gains_ref[2:3, :]
        turned = unit * cosine + swap_half(unit, low_lane) * sine
        query_ref[pl.ds(target, half), :] = (
            turned.astype(jnp.bfloat16).astype(jnp.float32) * (HD**-0.5)
        ).astype(jnp.bfloat16)
        both = lin_ref[pl.ds(source, half), 2 * HD :]
        unit = both * lax.rsqrt(head_mean(both * both, first) + EPSILON) * gains_ref[3:4, :]
        turned = unit * cosine + swap_half(unit, low_lane) * sine
        key_ref[pl.ds(target, half), :] = jnp.where(
            first, turned, pltpu.roll(turned, HD, 1)
        ).astype(jnp.bfloat16)
        values = jnp.where(first, pltpu.roll(both, HD, 1), both)
        value_ref[pl.ds(target, half), :] = values.astype(jnp.bfloat16)
        return carry

    lax.fori_loop(0, 2 * count, prepare, 0)

    def turn_values(block, carry):
        values = wide(value_ref[pl.ds(aligned(block * size, size), size), :])
        value_t[block, :HD, :] = values.T[:HD].astype(jnp.bfloat16)
        value_t[block, HD:, :] = jnp.ones((value_t.shape[1] - HD, size), jnp.bfloat16)
        return carry

    lax.fori_loop(0, blocks, turn_values, 0)

    def query_step(block, carry):
        query = two_heads(query_ref[pl.ds(aligned(block * size, size), size), :])
        accum[...] = jnp.zeros_like(accum)
        lowest = begin_at(meta_ref, docs, block * size) // size

        def key_step(other, carry):
            keys = key_ref[pl.ds(aligned(other * size, size), size), :]
            scores = dot_nt(keys, query)
            visible = block_visible(meta_ref, docs, block, other, size)
            probable = jnp.concatenate(
                [
                    jnp.where(visible, jnp.exp(scores[:, :size]), 0.0),
                    jnp.where(visible, jnp.exp(scores[:, size:]), 0.0),
                ],
                axis=1,
            ).astype(jnp.bfloat16)
            accum[...] += dot_nn(value_t[other], probable)
            return carry

        lax.fori_loop(lowest, block + 1, key_step, 0)
        mass = accum[HD : HD + 1, :]
        mixed = accum[:HD, :] / mass
        lse_ref[block] = jnp.log(mass)
        rows = jnp.concatenate([mixed[:, :size], mixed[:, size:]], axis=0).T
        attn_ref[pl.ds(aligned(block * size, size), size), :] = rows
        for part in range(2):
            target = aligned(row_of(2 * block + part, here, tokens, count), half)
            low[pl.ds(target, half), :] = rows[part * half : (part + 1) * half].astype(jnp.bfloat16)
        return carry

    lax.fori_loop(0, blocks, query_step, 0)
    for slot, bits in enumerate(ORDER):
        low_refs[bits][...] = low[slot * tokens : (slot + 1) * tokens, :]


def attention_back_kernel(
    tokens, count, docs,
    meta_ref, lin_ref, cos_ref, sin_ref, gains_ref,
    query_ref, key_ref, value_ref, attn_ref, lse_ref, *refs,
):
    grad_refs = refs[:count]
    out_ref, gain_ref = refs[count : count + 2]
    block_refs = refs[count + 2 : 2 * count + 2]
    key_t, grad_query, grad_key, grad_value, accum, grad_rows = refs[2 * count + 2 :]
    here = meta_ref[0]
    half = tokens // 2
    size = tokens
    blocks = count
    grad_key[...] = jnp.zeros_like(grad_key)
    grad_value[...] = jnp.zeros_like(grad_value)
    gain_ref[...] = jnp.zeros_like(gain_ref)
    for slot, bits in enumerate(ORDER):
        grad_rows[slot * tokens : (slot + 1) * tokens, :] = grad_refs[bits][...]

    def turn_keys(block, carry):
        keys = wide(key_ref[pl.ds(aligned(block * size, size), size), :])
        key_t[block] = keys.T[:HD].astype(jnp.bfloat16)
        return carry

    lax.fori_loop(0, blocks, turn_keys, 0)

    def query_step(block, carry):
        here_rows = pl.ds(aligned(block * size, size), size)
        query = two_heads(query_ref[here_rows, :])
        parts = []
        for part in range(2):
            source = aligned(row_of(2 * block + part, here, tokens, count), half)
            parts.append(grad_rows[pl.ds(source, half), :])
        grads = jnp.concatenate(parts, axis=0)
        products = (wide(grads) * attn_ref[here_rows, :]).T
        deltas = (
            jnp.sum(products[:HD], axis=0, keepdims=True),
            jnp.sum(products[HD:], axis=0, keepdims=True),
        )
        grads = two_heads(grads)
        lse = lse_ref[block]
        accum[...] = jnp.zeros_like(accum)
        lowest = begin_at(meta_ref, docs, block * size) // size

        def key_step(other, carry):
            rows = pl.ds(aligned(other * size, size), size)
            scores = dot_nt(key_ref[rows, :], query)
            grad_prob = dot_nt(value_ref[rows, :], grads)
            visible = block_visible(meta_ref, docs, block, other, size)
            probs, grad_scores = [], []
            for head in range(2):
                cols = slice(head * size, (head + 1) * size)
                prob = jnp.where(visible, jnp.exp(scores[:, cols] - lse[:, cols]), 0.0)
                probs.append(prob)
                grad_scores.append(prob * (grad_prob[:, cols] - deltas[head]))
            probs = jnp.concatenate(probs, axis=1).astype(jnp.bfloat16)
            grad_scores = jnp.concatenate(grad_scores, axis=1).astype(jnp.bfloat16)
            grad_value[rows, :] += dot_nn(probs, grads)
            grad_key[rows, :] += dot_nn(grad_scores, query)
            accum[...] += dot_nn(key_t[other], grad_scores)
            return carry

        lax.fori_loop(lowest, block + 1, key_step, 0)
        total = accum[...] * (HD**-0.5)
        grad_query[here_rows, :] = jnp.concatenate([total[:, :size], total[:, size:]], axis=0).T
        return carry

    lax.fori_loop(0, blocks, query_step, 0)

    def finish(place, carry):
        first, low_lane = lane_masks(half)
        source = aligned(row_of(place, here, tokens, count), half)
        target = pl.ds(aligned(place * half, half), half)
        cosine = cos_ref[target, :]
        sine = sin_ref[target, :]

        def through(linear, grads, gain):
            scale = lax.rsqrt(head_mean(linear * linear, first) + EPSILON)
            normed = linear * scale
            turned = grads * cosine + swap_half(grads * sine, low_lane)
            weighted = turned * gain
            grad_in = scale * (weighted - normed * head_mean(weighted * normed, first))
            return grad_in, jnp.sum(turned * normed, axis=0, keepdims=True)

        grad_in, gain_row = through(
            lin_ref[pl.ds(source, half), : 2 * HD], grad_query[target, :], gains_ref[2:3, :]
        )
        out_ref[pl.ds(source, half), : 2 * HD] = grad_in.astype(jnp.bfloat16)
        gain_ref[0:1, :] += gain_row
        keys = grad_key[target, :]
        grad_in, gain_row = through(
            lin_ref[pl.ds(source, half), 2 * HD :], keys + pltpu.roll(keys, HD, 1), gains_ref[3:4, :]
        )
        gain_ref[1:2, :] += gain_row
        values = grad_value[target, :]
        values = values + pltpu.roll(values, HD, 1)
        out_ref[pl.ds(source, half), 2 * HD :] = jnp.where(first, grad_in, values).astype(
            jnp.bfloat16
        )
        return carry

    lax.fori_loop(0, 2 * count, finish, 0)
    for slot, bits in enumerate(ORDER):
        block_refs[bits][...] = out_ref[slot * tokens : (slot + 1) * tokens, :]


def proj_grad_kernel(parts, meta_ref, attn_ref, grad_ref, *refs):
    blocks, full = refs[:-1], refs[-1]
    count = len(blocks)
    here = meta_ref[0]
    full[...] = contract_rows(attn_ref[...], grad_ref[...]).astype(jnp.bfloat16)
    rows = blocks[0].shape[0] // parts
    for bits, block in enumerate(blocks):
        owner = lax.bitwise_xor(here, bits)
        for part in range(parts):
            source = aligned(part * count * rows + owner * rows, rows)
            block[part * rows : (part + 1) * rows, :] = full[pl.ds(source, rows), :]


def pack_heads_kernel(
    extra, meta_ref, heads_ref, mixer_ref, gain_ref, feed_ref, sums_ref, *refs
):
    proj_refs, pieces = refs[:5], refs[5:]
    shard = meta_ref[1]
    rows = heads_ref.shape[0] // 4
    pair = 2 * HD
    proj = wide(proj_refs[0][...])
    for other in proj_refs[1:]:
        proj = proj + wide(other[...])
    proj_low, mixer, _, gains = pieces[4:]
    pieces = pieces[:4]
    part = proj.shape[0] // 4
    proj_low[...] = proj.astype(jnp.bfloat16)
    mixer[...] = mixer_ref[...] / gain_ref[...]
    values = sums_ref[...]
    lower = lax.broadcasted_iota(jnp.int32, values.shape, 0) == 0
    values = values + jnp.where(lower, pltpu.roll(values, HD, 1), 0.0)
    each = HD // 4
    lanes = lax.broadcasted_iota(jnp.int32, values.shape, 1)
    for bits, piece in enumerate(pieces):
        owner = lax.bitwise_xor(shard, bits)
        piece[:rows, :] = heads_ref[pl.ds(aligned(owner * rows, rows), rows), :]
        gains[...] = jnp.zeros_like(gains)
        own = pl.ds(aligned(owner * rows, rows), rows)
        gains[0:1, :] = mixer[:, own]
        gains[1:2, :] = feed_ref[:, own]
        moved = pltpu.roll(values, pair - owner * each, 1)
        moved = jnp.where(lanes < each, moved, 0.0)
        gains[2:4, :pair] = moved[0:2, :]
        piece[rows : rows + extra, :] = gains[...].astype(jnp.bfloat16)
        for index in range(proj.shape[1] // (2 * pair)):
            target = rows + extra + index * part
            piece[target : target + part, :] = proj_low[
                pl.ds(aligned(owner * part, part), part), index * 2 * pair : (index + 1) * 2 * pair
            ]


def pack_feed_kernel(meta_ref, wide_ref, down_ref, *pieces):
    shard = meta_ref[1]
    rows = wide_ref.shape[0] // 4
    inner = pieces[0].shape[0] - rows
    width = down_ref.shape[1]
    for bits, piece in enumerate(pieces):
        owner = lax.bitwise_xor(shard, bits)
        piece[:rows, :] = wide_ref[pl.ds(aligned(owner * rows, 16), rows), :]
        piece[rows:, :width] = down_ref[pl.ds(aligned(owner * inner, 16), inner), :]
        piece[rows:, width:] = jnp.zeros_like(piece[rows:, width:])


def input_grad_kernel(count, meta_ref, *refs):
    grads, weights = refs[:count], refs[count : 2 * count]
    input_ref, grad_ref, gain_ref, out_ref = refs[2 * count :]
    total = dot_nt(grads[0][...], weights[0][...])
    for left, right in zip(grads[1:], weights[1:]):
        total = total + dot_nt(left[...], right[...])
    values = wide(input_ref[...])
    scale = lax.rsqrt(jnp.mean(values * values, axis=1, keepdims=True) + EPSILON)
    normed = values * scale
    weighted = total * gain_ref[...]
    grad_in = scale * (weighted - normed * jnp.mean(weighted * normed, axis=1, keepdims=True))
    out_ref[...] = grad_ref[...] + grad_in


def project_kernel(count, parts, start, meta_ref, *refs):
    attn_refs, weight_refs, rest = refs[:count], refs[count : 2 * count], refs[2 * count :]
    input_ref, gain_ref, full_ref, attn_out_ref, mixed_ref, hidden_ref, _ = rest
    here = meta_ref[0]
    total = weight_refs[0].shape[0] - start
    rows = total // parts
    for bits in range(count):
        owner = lax.bitwise_xor(here, bits)
        for part in range(parts):
            target = aligned(part * count * rows + owner * rows, rows)
            source = start + part * rows
            full_ref[pl.ds(target, rows), :] = weight_refs[bits][source : source + rows, :]
        attn_out_ref[:, pl.ds(aligned(owner * 2 * HD, 2 * HD), 2 * HD)] = attn_refs[bits][...]
    mixed = wide(input_ref[...]) + dot_nn(attn_out_ref[...], full_ref[...])
    mixed_ref[...] = mixed
    scale = lax.rsqrt(jnp.mean(mixed * mixed, axis=1, keepdims=True) + EPSILON)
    hidden_ref[...] = (mixed * scale * gain_ref[...]).astype(jnp.bfloat16)


def feed_kernel(
    meta_ref, first_ref, second_ref, grad_first_ref, grad_second_ref, wide_ref, down_ref, *refs
):
    refs = refs[-10:]
    hidden_ref, grad_ref, act_ref, grad_wide_ref = refs[:4]
    out_refs, back_refs, (out_low, back_low) = refs[4:6], refs[6:8], refs[8:]
    tokens = first_ref.shape[0]
    inner = wide_ref.shape[1] // 2
    main = inner // 128 * 128
    hidden_ref[:tokens, :] = first_ref[...]
    hidden_ref[tokens:, :] = second_ref[...]
    grad_ref[:tokens, :] = grad_first_ref[:tokens, :]
    grad_ref[tokens:, :] = grad_second_ref[:tokens, :]
    first, _ = lane_masks(tokens)

    def activate(gate, up, grad_act):
        sigmoid = 1.0 / (1.0 + jnp.exp(-gate))
        silu = gate * sigmoid
        grad_gate = grad_act * up * sigmoid * (1.0 + gate * (1.0 - sigmoid))
        return silu * up, grad_gate, grad_act * silu

    def step(index, carry):
        rows = pl.ds(aligned(index * tokens, tokens), tokens)
        both = dot_nn(hidden_ref[rows, :], wide_ref[...])
        grad_act = dot_nt(grad_ref[rows, :], down_ref[...])
        act, grad_gate, grad_up = activate(
            both[:, :main], both[:, main : 2 * main], grad_act[:, :main]
        )
        act_ref[rows, :main] = act.astype(jnp.bfloat16)
        grad_wide_ref[rows, :main] = grad_gate.astype(jnp.bfloat16)
        grad_wide_ref[rows, main : 2 * main] = grad_up.astype(jnp.bfloat16)
        last = both[:, 2 * main :]
        act, grad_gate, grad_up = activate(last, pltpu.roll(last, HD, 1), grad_act[:, main:])
        act_ref[rows, main:] = jnp.where(first, act, 0.0).astype(jnp.bfloat16)
        grad_wide_ref[rows, 2 * main :] = jnp.where(
            first, grad_gate, pltpu.roll(grad_up, HD, 1)
        ).astype(jnp.bfloat16)
        back_low[index] = dot_nt(grad_wide_ref[rows, :], wide_ref[...]).astype(jnp.bfloat16)
        out_low[index] = dot_nn(act_ref[rows, :], down_ref[...]).astype(jnp.bfloat16)
        return carry

    lax.fori_loop(0, 2, step, 0)
    for index in range(2):
        out_refs[index][...] = out_low[index]
        back_refs[index][...] = back_low[index]


def feed_back_kernel(count, meta_ref, *refs):
    sums, rest = refs[:5], refs[5:]
    mixed_ref, grad_ref, full_ref, gain_ref, grad_mixed_ref, grad_low_ref, grad_gain_ref = rest[:7]
    block_refs, attn = rest[7 : 7 + count], rest[7 + count]
    here = meta_ref[0]
    grad_hidden = wide(sums[0][...])
    for part in sums[1:]:
        grad_hidden = grad_hidden + wide(part[...])
    mixed = mixed_ref[...]
    scale = lax.rsqrt(jnp.mean(mixed * mixed, axis=1, keepdims=True) + EPSILON)
    normed = mixed * scale
    weighted = grad_hidden * gain_ref[...]
    grad_in = scale * (weighted - normed * jnp.mean(weighted * normed, axis=1, keepdims=True))
    grad_gain_ref[...] = jnp.sum(grad_hidden * normed, axis=0, keepdims=True)
    grad_mixed = wide(grad_ref[...]) + grad_in
    grad_mixed_ref[...] = grad_mixed
    grad_low_ref[...] = grad_mixed.astype(jnp.bfloat16)
    attn[...] = dot_nt(grad_low_ref[...], full_ref[...]).astype(jnp.bfloat16)
    for bits in range(count):
        owner = lax.bitwise_xor(here, bits)
        block_refs[bits][...] = attn[:, pl.ds(aligned(owner * 2 * HD, 2 * HD), 2 * HD)]


def wide_out_kernel(count, parts, meta_ref, *refs):
    blocks, (gate_ref, up_ref, held) = refs[:count], refs[count:]
    here = meta_ref[0]
    for bits in range(count):
        held[lax.bitwise_xor(here, bits)] = wide(blocks[bits][...])
    inner = held.shape[2] // 2
    main = inner // 128 * 128
    piece = inner // parts
    for kind, out_ref in enumerate((gate_ref, up_ref)):
        for part in range(parts):
            columns = []
            for owner in range(count):
                start, stop = part * piece, (part + 1) * piece
                begin = kind * main
                if start < main:
                    columns.append(held[owner, :, begin + start : begin + min(stop, main)])
                if stop > main:
                    begin = main + kind * (inner - main)
                    columns.append(held[owner, :, begin + max(start, main) : begin + stop])
            out_ref[:, part * count * piece : (part + 1) * count * piece] = jnp.concatenate(
                columns, axis=1
            )


def rows_out_kernel(meta_ref, *refs):
    blocks, out_ref = refs[:-1], refs[-1]
    rows = out_ref.shape[0] // len(blocks)
    start = blocks[0].shape[0] - rows
    for bits, block in enumerate(blocks):
        owner = lax.bitwise_xor(meta_ref[0], bits)
        out_ref[pl.ds(aligned(owner * rows, 16), rows), :] = wide(
            block[start:, : out_ref.shape[1]]
        )


def heads_out_kernel(count, own, extra, meta_ref, *refs):
    blocks, rest = refs[:count], refs[count:]
    query_ref, key_ref, value_ref, proj_ref, gain_ref, held = rest
    here = meta_ref[0]
    pair = 2 * HD
    part = (blocks[0].shape[0] - own - extra) // 4
    gains = jnp.zeros(gain_ref.shape, jnp.float32)
    for bits in range(count):
        owner = lax.bitwise_xor(here, bits)
        block = wide(blocks[bits][...])
        query_ref[:, pl.ds(aligned(owner * pair, pair), pair)] = block[:own, :pair]
        held[owner] = block[:own, pair:]
        gains = gains + block[own : own + extra, :]
        for index in range(4):
            source = own + extra + index * part
            proj_ref[
                pl.ds(aligned(owner * part, part), part), index * 2 * pair : (index + 1) * 2 * pair
            ] = block[source : source + part, :]
    gain_ref[...] = gains
    first, _ = lane_masks(own)
    for index in range(count // 2):
        early, late = held[2 * index], held[2 * index + 1]
        lanes = slice(index * pair, (index + 1) * pair)
        key_ref[:, lanes] = jnp.where(first, early, pltpu.roll(late, HD, 1))
        value_ref[:, lanes] = jnp.where(first, pltpu.roll(early, HD, 1), late)


SCALARS = pl.BlockSpec(memory_space=pltpu.SMEM)
WHOLE = pl.BlockSpec(memory_space=pltpu.VMEM)
PLACED = pl.BlockSpec(memory_space=pl.ANY)
FAR = pl.BlockSpec(memory_space=pltpu.HBM)


def shaped(shape, kind=jnp.bfloat16):
    return jax.ShapeDtypeStruct(shape, kind)


def whole_call(kernel, outs, ins, flops, scratch=(), grant=24, specs=None):
    moved = sum(math.prod(out.shape) * out.dtype.itemsize for out in outs)
    return pl.pallas_call(
        kernel,
        out_shape=outs,
        in_specs=[SCALARS] + (specs or [WHOLE] * ins),
        out_specs=[WHOLE] * len(outs),
        scratch_shapes=list(scratch),
        cost_estimate=pl.CostEstimate(
            flops=int(flops), bytes_accessed=int(2 * moved), transcendentals=0
        ),
        compiler_params=pltpu.CompilerParams(vmem_limit_bytes=grant * 2**20),
    )


def rows_call(kernel, arrays, kept, outs, shared, index, flops, scratch=(), grant=24):
    specs = [SCALARS] + [WHOLE] * (len(arrays) - 1) + [PLACED] * len(kept)
    out_specs, shapes = [], []
    for position, out in enumerate(outs):
        if position < shared:
            rows = out.shape[0] // 4
            out_specs.append(
                pl.BlockSpec((rows, out.shape[1]), lambda step, index=index: (index, 0))
            )
        else:
            out_specs.append(pl.BlockSpec(out.shape, lambda step: (0, 0)))
        shapes.append(out)
    moved = sum(math.prod(out.shape) * out.dtype.itemsize for out in outs)
    return pl.pallas_call(
        kernel,
        grid=(1,),
        out_shape=shapes,
        in_specs=specs,
        out_specs=out_specs,
        scratch_shapes=list(scratch),
        input_output_aliases={len(arrays) + place: place for place in range(len(kept))},
        cost_estimate=pl.CostEstimate(
            flops=int(flops), bytes_accessed=int(moved), transcendentals=0
        ),
        compiler_params=pltpu.CompilerParams(vmem_limit_bytes=grant * 2**20),
    )(*arrays, *kept)


def local_heads(
    block_input, doc_starts, out_grad, query_weight, key_weight, value_weight, output_weight,
    gate_weight, up_weight, down_weight, mixer_gain, feed_gain, query_gain, key_gain,
):
    low = jnp.bfloat16
    tokens, width = block_input.shape[1:]
    count = lax.axis_size("ctx")
    shards = lax.axis_size("fsdp")
    here = lax.axis_index("ctx").astype(jnp.int32)
    shard = lax.axis_index("fsdp").astype(jnp.int32)
    stream = tokens * count
    docs = doc_starts.shape[1]
    pair = 2 * HD
    own_rows = width // shards
    extra = 16
    meta = jnp.concatenate([here[None], shard[None], doc_starts[0].astype(jnp.int32)])
    own_input = block_input[0]
    own_grad = out_grad[0]
    inner = down_weight.shape[0] // count
    wide_inner = inner * shards
    padded = -(-wide_inner // 128) * 128
    proj_rows = own_rows // count
    edges = [(0, 1), (3, 2)]
    middle = [(1, 2), (2, 1)]
    relay = [(1, 0), (2, 3)]

    def near(piece, bits):
        return shift_fsdp(piece, flipped(bits, shards))

    across, along, partner = gather_near(own_input)
    piece_rows = own_rows + extra + 4 * proj_rows
    head_piece = whole_call(
        take_heads_kernel,
        [shaped((piece_rows, 2 * pair))],
        8,
        0,
        [
            pltpu.VMEM((extra, 2 * pair), jnp.float32),
            pltpu.VMEM((3, own_rows, pair), low),
            pltpu.VMEM((proj_rows, width), low),
            pltpu.SemaphoreType.DMA((4,)),
        ],
        grant=60,
        specs=[FAR] * 4 + [WHOLE] * 4,
    )(
        meta, query_weight, key_weight, value_weight, output_weight,
        mixer_gain[None], feed_gain[None], query_gain[None], key_gain[None],
    )[0]
    head_pieces = [head_piece] + [near(head_piece, bits) for bits in (1, 2, 3)]
    feed_rows = own_rows + inner
    feed_piece = whole_call(
        functools.partial(take_wide_kernel, shards),
        [shaped((feed_rows, 2 * wide_inner))],
        3,
        2 * own_rows * 2 * wide_inner * 2048,
        [
            pltpu.VMEM((2 * shards, own_rows, 256), low),
            pltpu.SemaphoreType.DMA((2 * shards,)),
            pltpu.VMEM((inner, width), low),
            pltpu.SemaphoreType.DMA(()),
            pltpu.VMEM((own_rows, 2 * wide_inner), jnp.float32),
        ],
        grant=60,
        specs=[FAR] * 3,
    )(behind(meta, head_piece), gate_weight, up_weight, down_weight)[0]
    feed_first = behind(feed_piece, *head_pieces[1:])
    feed_far = near(feed_first, 2)
    feed_near = near(feed_first, 1)
    corner = gather_corner(across, along)
    others = gather_far(across, along, corner)
    input_blocks = [own_input, partner, across, others[0], along, others[1], corner, others[2]]

    where_at = jnp.arange(stream, dtype=jnp.int32)
    begins = doc_begin(doc_starts[0], where_at)
    lanes = jnp.arange(pair) % (HD // 2)
    frequency = ROPE_BASE ** (-(2.0 * lanes.astype(jnp.float32)) / HD)
    angles = (where_at - begins).astype(jnp.float32)[:, None] * frequency[None, :]
    cosine = jnp.cos(angles)
    sine = jnp.sin(angles) * jnp.where(jnp.arange(pair) % HD < HD // 2, -1.0, 1.0)[None, :]

    heads_weight, gain_mixer, gain_feed, gain_heads, proj_part = whole_call(
        functools.partial(arrange_heads_kernel, extra),
        [
            shaped((width, 2 * pair)),
            shaped((1, width), jnp.float32),
            shaped((1, width), jnp.float32),
            shaped((8, pair), jnp.float32),
            shaped((shards * proj_rows, width)),
        ],
        4,
        0,
        grant=8,
    )(behind(meta, cosine, sine), *head_pieces)

    kept = []
    for index in range(4):
        kept = rows_call(
            head_linear_kernel,
            [meta]
            + [input_blocks[bits] for bits in ORDER[2 * index : 2 * index + 2]]
            + [heads_weight, gain_mixer],
            kept,
            [shaped((stream, width)), shaped((stream, 2 * pair), jnp.float32)],
            2,
            index,
            4 * tokens * width * 2 * pair,
            grant=6,
        )
    hidden_in, linear = kept

    pairs = stream * stream // 2
    extra_piece = behind(jnp.concatenate([own_grad, proj_part], axis=0), corner)
    extra_across, extra_along, extra_partner = gather_near(extra_piece)
    extra_corner = swap_ctx(extra_piece, 6)
    query_att, key_att, value_att, attn, lse, *attn_low = whole_call(
        functools.partial(attention_kernel, tokens, count, docs),
        [
            shaped((stream, pair)),
            shaped((stream, pair)),
            shaped((stream, pair)),
            shaped((stream, pair), jnp.float32),
            shaped((count, 1, 2 * tokens), jnp.float32),
        ]
        + [shaped((tokens, pair))] * count,
        4,
        8 * pairs * HD,
        [
            pltpu.VMEM((count, HD + 16, tokens), low),
            pltpu.VMEM((HD + 16, 2 * tokens), jnp.float32),
            pltpu.VMEM((stream, pair), low),
        ],
        grant=10,
    )(meta, linear, cosine, sine, gain_heads)

    attn_blocks = exchange_plane(attn_low)
    extra_others = gather_far(extra_across, extra_along, extra_corner, attn_blocks[1])
    extra_blocks = [
        extra_piece, extra_partner, extra_across, extra_others[0],
        extra_along, extra_others[1], extra_corner, extra_others[2],
    ]
    full_proj, attn_rows, mixed, hidden_mid = whole_call(
        functools.partial(project_kernel, count, shards, tokens),
        [
            shaped((width, width)),
            shaped((tokens, width)),
            shaped((tokens, width), jnp.float32),
            shaped((tokens, width)),
        ],
        2 * count + 2,
        2 * tokens * width * width,
        [pltpu.VMEM((tokens, width), low)],
        grant=8,
    )(meta, *attn_blocks, *extra_blocks, own_input, gain_feed)

    hidden_across, hidden_along, hidden_partner = gather_near(hidden_mid)
    hidden_corner = swap_ctx(hidden_mid, 6)
    feed_middle = shift_fsdp(behind(feed_piece, hidden_mid), middle)
    feed_relay = shift_fsdp(behind(feed_far, hidden_mid), relay)
    wide_weight, down_part = whole_call(
        arrange_feed_kernel,
        [shaped((width, 2 * wide_inner)), shaped((padded, width))],
        5,
        0,
        grant=8,
    )(behind(meta, hidden_mid), feed_piece, feed_near, feed_far, feed_middle, feed_relay)
    hidden_blocks = {0: hidden_mid, 1: hidden_partner, 2: hidden_across, 4: hidden_along}
    out_parts, back_parts = [None] * count, [None] * count
    kept = []
    for index in range(4):
        chosen = ORDER[2 * index : 2 * index + 2]
        results = rows_call(
            feed_kernel,
            [meta]
            + [hidden_blocks[bits] for bits in chosen]
            + [extra_blocks[bits] for bits in chosen]
            + [wide_weight, down_part],
            kept,
            [
                shaped((stream, width)),
                shaped((stream, width)),
                shaped((stream, padded)),
                shaped((stream, 2 * wide_inner)),
            ]
            + [shaped((tokens, width))] * 4,
            4,
            index,
            24 * tokens * width * wide_inner,
            [pltpu.VMEM((2, tokens, width), low)] * 2,
            grant=14,
        )
        kept = results[:4]
        for place, bits in enumerate(chosen):
            out_parts[bits] = results[4 + place]
            back_parts[bits] = results[6 + place]
        if index == 0:
            far = gather_far(hidden_across, hidden_along, hidden_corner, results[6])
            hidden_blocks.update({3: far[0], 5: far[1], 6: hidden_corner, 7: far[2]})
            weight_piece = behind(heads_weight, far[2])
            weight_near = gather_near(weight_piece)
            weight_corner = swap_ctx(weight_piece, 6)
    hidden_all, grad_all, act_all, grad_wide_all = kept
    back_own, back_pairs = scatter_pair(back_parts)
    back_sums = back_own + scatter_links(back_pairs)

    def scatter_early(pieces):
        return shift_fsdp(pieces[3], edges), shift_fsdp(pieces[3], middle)

    def scatter_late(pieces, early, *ready):
        second = behind((wide(pieces[2]) + wide(early)).astype(low), *ready)
        return near(second, 2), near(behind(pieces[1], *ready), 1)

    grad_down = contract_rows(behind(act_all, *back_pairs), grad_all).astype(low)
    grad_wide = contract_rows(behind(hidden_all, grad_down), grad_wide_all).astype(low)
    feed_pieces = whole_call(
        pack_feed_kernel, [shaped((feed_rows, 2 * wide_inner))] * shards, 2, 0, grant=10
    )(meta, grad_wide, grad_down)
    wide_edge, wide_middle = scatter_early(feed_pieces)
    out_own, out_pairs = scatter_pair([behind(part, grad_wide) for part in out_parts])

    grad_mixed, grad_mixed_low, grad_feed, *grad_blocks = whole_call(
        functools.partial(feed_back_kernel, count),
        [
            shaped((tokens, width), jnp.float32),
            shaped((tokens, width)),
            shaped((1, width), jnp.float32),
        ]
        + [shaped((tokens, pair))] * count,
        9,
        2 * tokens * width * width,
        [pltpu.VMEM((tokens, width), low)],
        grant=8,
    )(meta, *back_sums, mixed, own_grad, full_proj, gain_feed)
    grad_attn = exchange_plane(grad_blocks)
    wide_late = scatter_late(feed_pieces, wide_edge, grad_blocks[0])
    proj_blocks = whole_call(
        functools.partial(proj_grad_kernel, shards),
        [shaped((shards * proj_rows, width))] * count,
        2,
        2 * tokens * width * width,
        [pltpu.VMEM((width, width), low)],
        grant=8,
    )(meta, attn_rows, grad_mixed_low)
    proj_own, proj_pairs = scatter_pair(proj_blocks)
    proj_parts = proj_own + scatter_links(proj_pairs)
    out_sums = out_own + scatter_links([behind(part, grad_blocks[0]) for part in out_pairs])

    back_outs = whole_call(
        functools.partial(attention_back_kernel, tokens, count, docs),
        [shaped((stream, 2 * pair)), shaped((8, pair), jnp.float32)]
        + [shaped((tokens, 2 * pair))] * count,
        9 + count,
        20 * pairs * HD,
        [
            pltpu.VMEM((count, HD, tokens), low),
            pltpu.VMEM((stream, pair), jnp.float32),
            pltpu.VMEM((stream, pair), jnp.float32),
            pltpu.VMEM((stream, pair), jnp.float32),
            pltpu.VMEM((HD, 2 * tokens), jnp.float32),
            pltpu.VMEM((stream, pair), low),
        ],
        grant=14,
    )(meta, linear, cosine, sine, gain_heads, query_att, key_att, value_att, attn, lse, *grad_attn)
    grad_linear, gain_sums, *token_blocks = back_outs

    token_grads = exchange_plane(token_blocks)
    late_linear = behind(grad_linear, token_grads[1])
    weight_far = gather_far(weight_near[0], weight_near[1], weight_corner, late_linear)
    weight_all = [
        weight_piece, weight_near[2], weight_near[0], weight_far[0],
        weight_near[1], weight_far[1], weight_corner, weight_far[2],
    ]
    grad_heads = contract_rows(hidden_in, late_linear).astype(low)
    grad_mixer = jnp.sum(
        contract_cols(late_linear, heads_weight) * wide(hidden_in), axis=0, keepdims=True
    )
    packed = whole_call(
        functools.partial(pack_heads_kernel, extra),
        [shaped((piece_rows, 2 * pair))] * shards,
        10,
        0,
        [
            pltpu.VMEM((shards * proj_rows, width), low),
            pltpu.VMEM((1, width), jnp.float32),
            pltpu.VMEM((8, pair), jnp.float32),
            pltpu.VMEM((extra, 2 * pair), jnp.float32),
        ],
        grant=6,
    )(meta, grad_heads, grad_mixer, gain_mixer, grad_feed, gain_sums, *proj_parts)
    heads_sent = [near(packed[bits], bits) for bits in (1, 2, 3)]

    def total_of(first, *parts):
        return sum([wide(part) for part in parts], wide(first)).astype(low)

    def total_late(pieces, parts, *ready):
        return total_of(pieces[0], *[behind(part, *ready) for part in parts])

    wide_total = total_late(feed_pieces, (wide_middle,) + wide_late, packed[0])
    wide_blocks = gather_plane(wide_total)
    input_grad = whole_call(
        functools.partial(input_grad_kernel, count),
        [shaped((tokens, width), jnp.float32)],
        2 * count + 3,
        2 * tokens * width * 2 * width,
        grant=10,
    )(meta, *token_grads, *weight_all, own_input, grad_mixed, gain_mixer)[0]
    heads_total = total_of(packed[0], *heads_sent)
    heads_blocks = gather_plane(heads_total)
    block_output = (
        mixed + sum(wide(behind(part, packed[0])) for part in out_sums)
    ).astype(low)

    out_down = whole_call(
        rows_out_kernel, [shaped((count * inner, width), jnp.float32)], count, 0
    )(meta, *wide_blocks)[0]
    tile = own_rows // 4
    out_gate, out_up = pl.pallas_call(
        functools.partial(wide_out_kernel, count, shards),
        grid=(4,),
        in_specs=[SCALARS]
        + [pl.BlockSpec((tile, 2 * wide_inner), lambda step: (step, 0))] * count,
        out_specs=[pl.BlockSpec((tile, wide_inner * count), lambda step: (step, 0))] * 2,
        out_shape=[shaped((own_rows, wide_inner * count), jnp.float32)] * 2,
        scratch_shapes=[pltpu.VMEM((count, tile, 2 * wide_inner), jnp.float32)],
        compiler_params=pltpu.CompilerParams(vmem_limit_bytes=24 * 2**20),
        name="wide_out",
    )(meta, *wide_blocks)
    out_query, out_key, out_value, out_proj, gain_out = whole_call(
        functools.partial(heads_out_kernel, count, own_rows, extra),
        [
            shaped((own_rows, width), jnp.float32),
            shaped((own_rows, KVH * HD), jnp.float32),
            shaped((own_rows, KVH * HD), jnp.float32),
            shaped((own_rows, width), jnp.float32),
            shaped((extra, 2 * pair), jnp.float32),
        ],
        count,
        0,
        [pltpu.VMEM((count, own_rows, pair), jnp.float32)],
    )(meta, *heads_blocks)
    return (
        block_output[None],
        input_grad[None],
        out_query,
        out_key,
        out_value,
        out_proj,
        out_gate,
        out_up,
        out_down,
        gain_out[0],
        gain_out[1],
        gain_out[2, : query_gain.shape[0]],
        gain_out[3, : key_gain.shape[0]],
    )


def divides_heads(mesh):
    return mesh.shape["ctx"] == KVH and mesh.shape["fsdp"] == 4 and H == 2 * KVH


def solution(mesh):
    in_specs = (
        P("fsdp", "ctx", None),
        P("fsdp", None),
        P("fsdp", "ctx", None),
        P("fsdp", None),
        P("fsdp", None),
        P("fsdp", None),
        P("fsdp", None),
        P("fsdp", None),
        P("fsdp", None),
        P("fsdp", None),
        P("fsdp"),
        P("fsdp"),
        P("fsdp"),
        P("fsdp"),
    )
    out_specs = (
        P("fsdp", "ctx", None),
        P("fsdp", "ctx", None),
        P("fsdp", None),
        P("fsdp", None),
        P("fsdp", None),
        P("fsdp", None),
        P("fsdp", None),
        P("fsdp", None),
        P("fsdp", None),
        P("fsdp"),
        P("fsdp"),
        P("fsdp"),
        P("fsdp"),
    )
    if not divides_heads(mesh):
        return jax.shard_map(
            local, mesh=mesh, in_specs=in_specs, out_specs=out_specs, check_vma=False
        )

    return jax.shard_map(local_heads, mesh=mesh, in_specs=in_specs, out_specs=out_specs, check_vma=False)
```

```python
import functools
import math

import jax
import jax.numpy as jnp
from jax import lax
from jax.experimental import pallas as pl
from jax.experimental.pallas import tpu as pltpu
from jax.sharding import PartitionSpec as P

H = 16
KVH = 8
HD = 64


EPSILON = 1e-05
ROPE_BASE = 1000000.0
FLOOR_SCORE = -1e30


def place_rows(row_index, tokens, ctx_count):
    half_rows = tokens // 2
    device = row_index // tokens
    offset = row_index % tokens
    early = device * half_rows + offset
    late = (2 * ctx_count - 1 - device) * half_rows + offset - half_rows
    return jnp.where(offset < half_rows, early, late)


def doc_begin(starts, where_at):
    started = starts[None, :] <= where_at[:, None]
    return jnp.max(jnp.where(started, starts[None, :], 0), axis=1)


def rotary(positions):
    half_dim = HD // 2
    frequency = ROPE_BASE ** (-(2.0 * jnp.arange(half_dim, dtype=jnp.float32)) / HD)
    angles = positions.astype(jnp.float32)[:, None] * frequency[None, :]
    angles = jnp.concatenate([angles, angles], axis=1)
    return (jnp.cos(angles)[:, None, :], jnp.sin(angles)[:, None, :])


def rotate_pairs(values, cosine, sine_part):
    half_dim = values.shape[-1] // 2
    rolled = jnp.concatenate([-values[..., half_dim:], values[..., :half_dim]], axis=-1)
    return values * cosine + rolled * sine_part


def rotate_back(grads, cosine, sine_part):
    half_dim = grads.shape[-1] // 2
    moved = grads * sine_part
    rolled = jnp.concatenate([moved[..., half_dim:], -moved[..., :half_dim]], axis=-1)
    return grads * cosine + rolled


def unit_norm(values):
    scaling = lax.rsqrt(jnp.mean(values * values, axis=-1, keepdims=True) + EPSILON)
    return (values * scaling, scaling)


def norm_back(grad_out, normed, scaling, gain_row):
    weighted = grad_out * gain_row
    grad_in = scaling * (weighted - normed * jnp.mean(weighted * normed, axis=-1, keepdims=True))
    grad_gain = jnp.sum((grad_out * normed).reshape(-1, normed.shape[-1]), axis=0)
    return (grad_in, grad_gain)


def score_block(query_rows, key_rows, scaling):
    return (
        jnp.einsum("igrd,jgd->grij", query_rows, key_rows, preferred_element_type=jnp.float32)
        * scaling
    )


def visible_pairs(query_at, query_doc, key_at, key_doc):
    return (query_doc[:, None] == key_doc[None, :]) & (key_at[None, :] <= query_at[:, None])


def any_visible(query_at, query_doc, key_at):
    return (jnp.min(key_at) <= jnp.max(query_at)) & (jnp.max(key_at) >= jnp.min(query_doc))


def contract_rows(left, right):
    return lax.dot_general(
        left, right, (((0,), (0,)), ((), ())), preferred_element_type=jnp.float32
    )


def contract_cols(left, right):
    return lax.dot_general(
        left, right, (((1,), (1,)), ((), ())), preferred_element_type=jnp.float32
    )


def keep_same(totals):
    return totals


def local(
    block_input,
    doc_starts,
    out_grad,
    query_weight,
    key_weight,
    value_weight,
    output_weight,
    gate_weight,
    up_weight,
    down_weight,
    mixer_gain,
    feed_gain,
    query_gain,
    key_gain,
):
    tokens = block_input.shape[1]
    ctx_count = lax.axis_size("ctx")
    repeat = H // KVH
    kv_width = KVH * HD
    scaling = HD ** (-0.5)
    inputs = block_input[0].astype(jnp.float32)
    starts = doc_starts[0]
    where_at = place_rows(
        lax.axis_index("ctx") * tokens + jnp.arange(tokens, dtype=jnp.int32), tokens, ctx_count
    )
    begins = doc_begin(starts, where_at)
    cosine, sine_part = rotary(where_at - begins)
    gathered = (
        lax.all_gather(query_weight, "fsdp", axis=0, tiled=True),
        lax.all_gather(key_weight, "fsdp", axis=0, tiled=True),
        lax.all_gather(value_weight, "fsdp", axis=0, tiled=True),
        lax.all_gather(output_weight, "fsdp", axis=0, tiled=True),
        lax.all_gather(gate_weight, "fsdp", axis=0, tiled=True),
        lax.all_gather(up_weight, "fsdp", axis=0, tiled=True),
        lax.all_gather(down_weight, "fsdp", axis=0, tiled=True),
        lax.all_gather(mixer_gain, "fsdp", axis=0, tiled=True),
        lax.all_gather(feed_gain, "fsdp", axis=0, tiled=True),
        lax.all_gather(query_gain, "fsdp", axis=0, tiled=True),
        lax.all_gather(key_gain, "fsdp", axis=0, tiled=True),
    )
    full_query, full_key, full_value, full_proj, full_gate, full_up, full_down = gathered[:7]
    gain_mixer, gain_feed, gain_query, gain_key = [
        entry.astype(jnp.float32) for entry in gathered[7:]
    ]
    normed_in, scale_in = unit_norm(inputs)
    hidden_in = (normed_in * gain_mixer).astype(jnp.bfloat16)
    query_lin = jnp.dot(hidden_in, full_query, preferred_element_type=jnp.float32)
    key_lin = jnp.dot(hidden_in, full_key, preferred_element_type=jnp.float32)
    value_lin = jnp.dot(hidden_in, full_value, preferred_element_type=jnp.float32)
    query_normed, query_scale = unit_norm(query_lin.reshape(tokens, H, HD))
    key_normed, key_scale = unit_norm(key_lin.reshape(tokens, KVH, HD))
    query_att = (
        rotate_pairs(query_normed * gain_query, cosine, sine_part)
        .reshape(tokens, H * HD)
        .astype(jnp.bfloat16)
    )
    key_att = (
        rotate_pairs(key_normed * gain_key, cosine, sine_part)
        .reshape(tokens, kv_width)
        .astype(jnp.bfloat16)
    )
    value_att = value_lin.astype(jnp.bfloat16)
    query_four = query_att.reshape(tokens, KVH, repeat, HD)
    start_state = (
        jnp.full((KVH, repeat, tokens), FLOOR_SCORE, jnp.float32),
        jnp.zeros((KVH, repeat, tokens), jnp.float32),
        jnp.zeros((tokens, H * HD), jnp.float32),
    )
    key_part = lax.all_gather(key_att, "ctx", axis=0, tiled=True)
    value_part = lax.all_gather(value_att, "ctx", axis=0, tiled=True)
    rows = key_part.shape[0]
    width = math.gcd(math.gcd(rows, tokens // 2), 512)

    def forward_key_block(block_index, totals):
        offset = block_index * width
        key_rows = lax.dynamic_slice_in_dim(key_part, offset, width, 0).reshape(width, KVH, HD)
        value_rows = lax.dynamic_slice_in_dim(value_part, offset, width, 0).reshape(width, KVH, HD)
        key_at = place_rows(offset + jnp.arange(width, dtype=jnp.int32), tokens, ctx_count)

        def attend(totals):
            highest, total_mass, accum = totals
            visible = visible_pairs(where_at, begins, key_at, doc_begin(starts, key_at))
            scores = jnp.where(visible, score_block(query_four, key_rows, scaling), FLOOR_SCORE)
            new_high = jnp.maximum(highest, jnp.max(scores, axis=-1))
            rescale = jnp.exp(highest - new_high)
            probable = jnp.where(visible, jnp.exp(scores - new_high[..., None]), 0.0)
            total_mass = total_mass * rescale + jnp.sum(probable, axis=-1)
            part_out = jnp.einsum(
                "grij,jgd->igrd",
                probable.astype(jnp.bfloat16),
                value_rows,
                preferred_element_type=jnp.float32,
            )
            accum = (
                accum.reshape(tokens, KVH, repeat, HD)
                * jnp.transpose(rescale, (2, 0, 1))[..., None]
                + part_out
            )
            return (new_high, total_mass, accum.reshape(tokens, H * HD))

        return lax.cond(any_visible(where_at, begins, key_at), attend, keep_same, totals)

    highest, total_mass, accum = lax.fori_loop(0, rows // width, forward_key_block, start_state)
    lse_heads = highest + jnp.log(total_mass)
    attn_raw = (
        accum.reshape(tokens, KVH, repeat, HD) / jnp.transpose(total_mass, (2, 0, 1))[..., None]
    ).reshape(tokens, H * HD)
    attn_low = attn_raw.astype(jnp.bfloat16)
    mixed = inputs + jnp.dot(attn_low, full_proj, preferred_element_type=jnp.float32)
    normed_mid, scale_mid = unit_norm(mixed)
    hidden_mid = (normed_mid * gain_feed).astype(jnp.bfloat16)
    gate_lin = jnp.dot(hidden_mid, full_gate, preferred_element_type=jnp.float32)
    up_lin = jnp.dot(hidden_mid, full_up, preferred_element_type=jnp.float32)
    sigmoid_gate = jax.nn.sigmoid(gate_lin)
    activated = (gate_lin * sigmoid_gate * up_lin).astype(jnp.bfloat16)
    block_output = (
        mixed + jnp.dot(activated, full_down, preferred_element_type=jnp.float32)
    ).astype(jnp.bfloat16)
    regathered = (
        lax.all_gather(query_weight, "fsdp", axis=0, tiled=True),
        lax.all_gather(key_weight, "fsdp", axis=0, tiled=True),
        lax.all_gather(value_weight, "fsdp", axis=0, tiled=True),
        lax.all_gather(output_weight, "fsdp", axis=0, tiled=True),
        lax.all_gather(gate_weight, "fsdp", axis=0, tiled=True),
        lax.all_gather(up_weight, "fsdp", axis=0, tiled=True),
        lax.all_gather(down_weight, "fsdp", axis=0, tiled=True),
        lax.all_gather(mixer_gain, "fsdp", axis=0, tiled=True),
        lax.all_gather(feed_gain, "fsdp", axis=0, tiled=True),
        lax.all_gather(query_gain, "fsdp", axis=0, tiled=True),
        lax.all_gather(key_gain, "fsdp", axis=0, tiled=True),
    )
    full_query, full_key, full_value, full_proj, full_gate, full_up, full_down = regathered[:7]
    gain_mixer, gain_feed, gain_query, gain_key = [
        entry.astype(jnp.float32) for entry in regathered[7:]
    ]
    grad_top = out_grad[0].astype(jnp.float32)
    grad_top_low = grad_top.astype(jnp.bfloat16)
    grad_down = contract_rows(activated, grad_top_low)
    grad_act = contract_cols(grad_top_low, full_down)
    grad_gate_low = (
        grad_act * up_lin * sigmoid_gate * (1.0 + gate_lin * (1.0 - sigmoid_gate))
    ).astype(jnp.bfloat16)
    grad_up_low = (grad_act * gate_lin * sigmoid_gate).astype(jnp.bfloat16)
    grad_gate = contract_rows(hidden_mid, grad_gate_low)
    grad_up = contract_rows(hidden_mid, grad_up_low)
    grad_hidden_mid = contract_cols(grad_gate_low, full_gate) + contract_cols(grad_up_low, full_up)
    grad_normed_mid, grad_feed = norm_back(grad_hidden_mid, normed_mid, scale_mid, gain_feed)
    grad_mixed = grad_top + grad_normed_mid
    grad_mixed_low = grad_mixed.astype(jnp.bfloat16)
    grad_proj = contract_rows(attn_low, grad_mixed_low)
    grad_attn = contract_cols(grad_mixed_low, full_proj).astype(jnp.bfloat16)
    grad_four = grad_attn.reshape(tokens, KVH, repeat, HD)
    delta_heads = jnp.sum(
        grad_four.astype(jnp.float32) * attn_raw.reshape(tokens, KVH, repeat, HD), axis=-1
    )
    delta_grid = jnp.transpose(delta_heads, (1, 2, 0))
    lse_rows = jnp.transpose(lse_heads, (2, 0, 1)).reshape(tokens, H)
    delta_rows = delta_heads.reshape(tokens, H)
    query_key_part = lax.all_gather(key_att, "ctx", axis=0, tiled=True)
    query_value_part = lax.all_gather(value_att, "ctx", axis=0, tiled=True)
    rows = query_key_part.shape[0]
    query_width = math.gcd(math.gcd(rows, tokens // 2), 512)

    def query_key_block(block_index, grad_query_acc):
        offset = block_index * query_width
        key_rows = lax.dynamic_slice_in_dim(query_key_part, offset, query_width, 0).reshape(
            query_width, KVH, HD
        )
        value_rows = lax.dynamic_slice_in_dim(query_value_part, offset, query_width, 0).reshape(
            query_width, KVH, HD
        )
        key_at = place_rows(offset + jnp.arange(query_width, dtype=jnp.int32), tokens, ctx_count)

        def attend(grad_query_acc):
            visible = visible_pairs(where_at, begins, key_at, doc_begin(starts, key_at))
            scores = score_block(query_four, key_rows, scaling)
            probable = jnp.where(visible, jnp.exp(scores - lse_heads[..., None]), 0.0)
            grad_prob = jnp.einsum(
                "igrd,jgd->grij", grad_four, value_rows, preferred_element_type=jnp.float32
            )
            grad_score = (probable * (grad_prob - delta_grid[..., None])).astype(jnp.bfloat16)
            added = (
                jnp.einsum(
                    "grij,jgd->igrd", grad_score, key_rows, preferred_element_type=jnp.float32
                )
                * scaling
            )
            return grad_query_acc + added.reshape(tokens, H * HD)

        return lax.cond(any_visible(where_at, begins, key_at), attend, keep_same, grad_query_acc)

    grad_query_att = lax.fori_loop(
        0, rows // query_width, query_key_block, jnp.zeros((tokens, H * HD), jnp.float32)
    )
    lse_all, delta_all = (
        lax.all_gather(lse_rows.astype(jnp.bfloat16), "ctx", axis=0, tiled=True).astype(
            lse_rows.dtype
        ),
        lax.all_gather(delta_rows.astype(jnp.bfloat16), "ctx", axis=0, tiled=True).astype(
            delta_rows.dtype
        ),
    )
    key_three = key_att.reshape(tokens, KVH, HD)
    value_three = value_att.reshape(tokens, KVH, HD)
    empty_keys = jnp.zeros((tokens, kv_width), jnp.float32)
    query_part = lax.all_gather(query_att, "ctx", axis=0, tiled=True)
    grad_part = lax.all_gather(grad_attn, "ctx", axis=0, tiled=True)
    rows = query_part.shape[0]
    key_width = math.gcd(math.gcd(rows, tokens // 2), 512)

    def query_block(block_index, totals):
        offset = block_index * key_width
        query_rows = lax.dynamic_slice_in_dim(query_part, offset, key_width, 0).reshape(
            key_width, KVH, repeat, HD
        )
        grad_rows = lax.dynamic_slice_in_dim(grad_part, offset, key_width, 0).reshape(
            key_width, KVH, repeat, HD
        )
        query_at = place_rows(offset + jnp.arange(key_width, dtype=jnp.int32), tokens, ctx_count)
        query_doc = doc_begin(starts, query_at)
        lse_block = jnp.transpose(
            lax.dynamic_slice_in_dim(lse_all, offset, key_width, 0).reshape(key_width, KVH, repeat),
            (1, 2, 0),
        )
        delta_block = jnp.transpose(
            lax.dynamic_slice_in_dim(delta_all, offset, key_width, 0).reshape(
                key_width, KVH, repeat
            ),
            (1, 2, 0),
        )

        def attend(totals):
            grad_key_acc, grad_value_acc = totals
            visible = visible_pairs(query_at, query_doc, where_at, begins)
            scores = score_block(query_rows, key_three, scaling)
            probable = jnp.where(visible, jnp.exp(scores - lse_block[..., None]), 0.0)
            grad_prob = jnp.einsum(
                "igrd,jgd->grij", grad_rows, value_three, preferred_element_type=jnp.float32
            )
            grad_score = (probable * (grad_prob - delta_block[..., None])).astype(jnp.bfloat16)
            value_added = jnp.einsum(
                "grij,igrd->jgd",
                probable.astype(jnp.bfloat16),
                grad_rows,
                preferred_element_type=jnp.float32,
            )
            key_added = (
                jnp.einsum(
                    "grij,igrd->jgd", grad_score, query_rows, preferred_element_type=jnp.float32
                )
                * scaling
            )
            return (
                grad_key_acc + key_added.reshape(tokens, kv_width),
                grad_value_acc + value_added.reshape(tokens, kv_width),
            )

        return lax.cond(any_visible(query_at, query_doc, where_at), attend, keep_same, totals)

    grad_key_att, grad_value_att = lax.fori_loop(
        0, rows // key_width, query_block, (empty_keys, empty_keys)
    )
    grad_query_unit = rotate_back(grad_query_att.reshape(tokens, H, HD), cosine, sine_part)
    grad_query_lin, grad_qgain = norm_back(grad_query_unit, query_normed, query_scale, gain_query)
    grad_key_unit = rotate_back(grad_key_att.reshape(tokens, KVH, HD), cosine, sine_part)
    grad_key_lin, grad_kgain = norm_back(grad_key_unit, key_normed, key_scale, gain_key)
    grad_query_low = grad_query_lin.reshape(tokens, H * HD).astype(jnp.bfloat16)
    grad_key_low = grad_key_lin.reshape(tokens, kv_width).astype(jnp.bfloat16)
    grad_value_low = grad_value_att.astype(jnp.bfloat16)
    grad_query = contract_rows(hidden_in, grad_query_low)
    grad_key = contract_rows(hidden_in, grad_key_low)
    grad_value = contract_rows(hidden_in, grad_value_low)
    grad_hidden_in = (
        contract_cols(grad_query_low, full_query)
        + contract_cols(grad_key_low, full_key)
        + contract_cols(grad_value_low, full_value)
    )
    grad_normed_in, grad_mixer = norm_back(grad_hidden_in, normed_in, scale_in, gain_mixer)
    input_grad = grad_mixed + grad_normed_in
    parts = (
        lax.psum_scatter(
            grad_query.astype(jnp.bfloat16), "fsdp", scatter_dimension=0, tiled=True
        ).astype(jnp.float32),
        lax.psum_scatter(
            grad_key.astype(jnp.bfloat16), "fsdp", scatter_dimension=0, tiled=True
        ).astype(jnp.float32),
        lax.psum_scatter(
            grad_value.astype(jnp.bfloat16), "fsdp", scatter_dimension=0, tiled=True
        ).astype(jnp.float32),
        lax.psum_scatter(
            grad_proj.astype(jnp.bfloat16), "fsdp", scatter_dimension=0, tiled=True
        ).astype(jnp.float32),
        lax.psum_scatter(
            grad_gate.astype(jnp.bfloat16), "fsdp", scatter_dimension=0, tiled=True
        ).astype(jnp.float32),
        lax.psum_scatter(
            grad_up.astype(jnp.bfloat16), "fsdp", scatter_dimension=0, tiled=True
        ).astype(jnp.float32),
        lax.psum_scatter(
            grad_down.astype(jnp.bfloat16), "fsdp", scatter_dimension=0, tiled=True
        ).astype(jnp.float32),
        lax.psum_scatter(
            grad_mixer.astype(jnp.bfloat16), "fsdp", scatter_dimension=0, tiled=True
        ).astype(jnp.float32),
        lax.psum_scatter(
            grad_feed.astype(jnp.bfloat16), "fsdp", scatter_dimension=0, tiled=True
        ).astype(jnp.float32),
        lax.psum_scatter(
            grad_qgain.astype(jnp.bfloat16), "fsdp", scatter_dimension=0, tiled=True
        ).astype(jnp.float32),
        lax.psum_scatter(
            grad_kgain.astype(jnp.bfloat16), "fsdp", scatter_dimension=0, tiled=True
        ).astype(jnp.float32),
    )
    summed = (
        lax.psum(parts[0].astype(jnp.bfloat16), "ctx").astype(jnp.float32),
        lax.psum(parts[1].astype(jnp.bfloat16), "ctx").astype(jnp.float32),
        lax.psum(parts[2].astype(jnp.bfloat16), "ctx").astype(jnp.float32),
        lax.psum(parts[3].astype(jnp.bfloat16), "ctx").astype(jnp.float32),
        lax.psum(parts[4].astype(jnp.bfloat16), "ctx").astype(jnp.float32),
        lax.psum(parts[5].astype(jnp.bfloat16), "ctx").astype(jnp.float32),
        lax.psum(parts[6].astype(jnp.bfloat16), "ctx").astype(jnp.float32),
        lax.psum(parts[7].astype(jnp.bfloat16), "ctx").astype(jnp.float32),
        lax.psum(parts[8].astype(jnp.bfloat16), "ctx").astype(jnp.float32),
        lax.psum(parts[9].astype(jnp.bfloat16), "ctx").astype(jnp.float32),
        lax.psum(parts[10].astype(jnp.bfloat16), "ctx").astype(jnp.float32),
    )
    return (
        block_output[None],
        input_grad[None],
        summed[0],
        summed[1],
        summed[2],
        summed[3],
        summed[4],
        summed[5],
        summed[6],
        summed[7],
        summed[8],
        summed[9],
        summed[10],
    )


ORDER = (0, 1, 2, 4, 3, 5, 6, 7)


def flipped(bits, count):
    return [(index, index ^ bits) for index in range(count)]


def swap_ctx(values, bits):
    return lax.ppermute(values, "ctx", flipped(bits, lax.axis_size("ctx")))


def behind(values, *ready):
    return lax.optimization_barrier((values,) + ready)[0]


def dot_nn(left, right):
    return lax.dot_general(
        left, right, (((1,), (0,)), ((), ())), preferred_element_type=jnp.float32
    )


def dot_nt(left, right):
    return lax.dot_general(
        left, right, (((1,), (1,)), ((), ())), preferred_element_type=jnp.float32
    )


def wide(values):
    return values.astype(jnp.float32)


def gather_near(block):
    return swap_ctx(block, 2), swap_ctx(block, 4), swap_ctx(block, 1)


def gather_corner(across, along):
    half = across.shape[0] // 2
    first = swap_ctx(along[:half], 2)
    second = swap_ctx(across[half:], 4)
    return jnp.concatenate([first, second], axis=0)


def gather_far(across, along, corner, *ready):
    return [swap_ctx(behind(part, *ready), 1) for part in (across, along, corner)]


def gather_plane(block, *ready):
    across, along, partner = gather_near(block)
    corner = gather_corner(across, along)
    others = gather_far(across, along, corner, *ready)
    return [block, partner, across, others[0], along, others[1], corner, others[2]]


def gather_direct(block, *ready):
    across, along, partner = gather_near(block)
    corner = swap_ctx(block, 6)
    others = gather_far(across, along, corner, *ready)
    return [block, partner, across, others[0], along, others[1], corner, others[2]]


def scatter_pair(blocks):
    got = [swap_ctx(blocks[bits], 1) for bits in (3, 5, 7, 1)]
    sums = [
        (wide(blocks[bits]) + wide(other)).astype(jnp.bfloat16)
        for bits, other in zip((2, 4, 6), got)
    ]
    return [blocks[0], got[3]], sums


def scatter_links(sums):
    return [swap_ctx(part, bits) for bits, part in zip((2, 4, 6), sums)]


def exchange_plane(blocks):
    return [blocks[0]] + [swap_ctx(blocks[bits], bits) for bits in range(1, 8)]


def shift_fsdp(values, pairs):
    return lax.ppermute(values, "fsdp", pairs)


def slot_of(bits):
    return jnp.where(bits == 3, 4, jnp.where(bits == 4, 3, bits))


def row_of(place, here, tokens, count):
    half = tokens // 2
    device = jnp.where(place < count, place, 2 * count - 1 - place)
    late = jnp.where(place < count, 0, half)
    return slot_of(lax.bitwise_xor(device, here)) * tokens + late


def swap_half(values, low_lane):
    return jnp.where(low_lane, pltpu.roll(values, 96, 1), pltpu.roll(values, 32, 1))


def head_blocks():
    shape = (2 * HD, 2 * HD)
    row = lax.broadcasted_iota(jnp.int32, shape, 0) < HD
    column = lax.broadcasted_iota(jnp.int32, shape, 1) < HD
    return jnp.where(row == column, 1.0 / HD, 0.0).astype(jnp.bfloat16)


def head_mean(values, blocks):
    high = values.astype(jnp.bfloat16)
    rest = (values - wide(high)).astype(jnp.bfloat16)
    return dot_nn(high, blocks) + dot_nn(rest, blocks)


def lane_masks(rows):
    lanes = lax.broadcasted_iota(jnp.int32, (rows, 2 * HD), 1)
    return lanes < HD, (lanes % HD) < (HD // 2)


def two_heads(values):
    first, _ = lane_masks(values.shape[0])
    zero = jnp.zeros_like(values)
    return jnp.concatenate(
        [jnp.where(first, values, zero), jnp.where(first, zero, values)], axis=0
    )


def begin_at(meta_ref, docs, where_at):
    begin = jnp.zeros_like(where_at)
    for doc in range(docs):
        begin = jnp.where(meta_ref[2 + doc] <= where_at, meta_ref[2 + doc], begin)
    return begin


def block_visible(meta_ref, docs, query_block, key_block, size):
    query_at = query_block * size + lax.broadcasted_iota(jnp.int32, (1, size), 1)
    begin = begin_at(meta_ref, docs, query_at)
    key_at = key_block * size + lax.broadcasted_iota(jnp.int32, (size, size), 0)
    return (key_at <= query_at) & (key_at >= begin)


def pair_tile(ref):
    return 2 * HD if ref.shape[0] % (4 * HD) == 0 else ref.shape[0] // 2


def aligned(value, size):
    return pl.multiple_of(value, size)


def take_heads_kernel(
    meta_ref, query_ref, key_ref, value_ref, proj_ref, mixer_ref, feed_ref, query_gain_ref, key_gain_ref,
    out_ref, gains, windows, proj, sem,
):
    here = meta_ref[0]
    rows = query_ref.shape[0]
    pair = 2 * HD
    start = aligned(lax.shift_right_logical(here, 1) * pair, pair)
    part = proj.shape[0]
    copies = [
        pltpu.make_async_copy(
            query_ref.at[:, pl.ds(aligned(here * pair, pair), pair)], windows.at[0], sem.at[0]
        ),
        pltpu.make_async_copy(key_ref.at[:, pl.ds(start, pair)], windows.at[1], sem.at[1]),
        pltpu.make_async_copy(value_ref.at[:, pl.ds(start, pair)], windows.at[2], sem.at[2]),
        pltpu.make_async_copy(
            proj_ref.at[pl.ds(aligned(here * part, part), part), :], proj, sem.at[3]
        ),
    ]
    for copy in copies:
        copy.start()
    gains[...] = jnp.zeros_like(gains)
    gains[0:1, :] = wide(mixer_ref[...])
    gains[1:2, :] = wide(feed_ref[...])
    gains[2:3, : query_gain_ref.shape[1]] = wide(query_gain_ref[...])
    gains[3:4, : key_gain_ref.shape[1]] = wide(key_gain_ref[...])
    extra = gains.shape[0]
    out_ref[rows : rows + extra, :] = gains[...].astype(jnp.bfloat16)
    for copy in copies:
        copy.wait()
    out_ref[:rows, :pair] = windows[0]
    odd = lax.bitwise_and(here, 1) == 1
    keys = wide(windows[1])
    values = wide(windows[2])
    first, _ = lane_masks(rows)
    keys = jnp.where(odd, pltpu.roll(keys, HD, 1), keys)
    values = jnp.where(odd, values, pltpu.roll(values, HD, 1))
    out_ref[:rows, pair:] = jnp.where(first, keys, values).astype(jnp.bfloat16)
    for index in range(proj.shape[1] // (2 * pair)):
        target = rows + extra + index * part
        out_ref[target : target + part, :] = proj[:, index * 2 * pair : (index + 1) * 2 * pair]


def arrange_heads_kernel(
    extra, meta_ref, *refs
):
    pieces, (weight_ref, mixer_ref, feed_ref, gains_ref, proj_ref) = refs[:4], refs[4:]
    shard = meta_ref[1]
    rows = weight_ref.shape[0] // 4
    pair = 2 * HD
    each = HD // 4
    gains = jnp.zeros((8, pair), jnp.float32)
    part = proj_ref.shape[0] // 4
    for bits, piece in enumerate(pieces):
        owner = lax.bitwise_xor(shard, bits)
        weight_ref[pl.ds(aligned(owner * rows, rows), rows), :] = piece[:rows, :]
        block = wide(piece[rows : rows + extra, :])
        lanes = pl.ds(aligned(owner * rows, rows), rows)
        mixer_ref[:, lanes] = block[0:1, :]
        feed_ref[:, lanes] = block[1:2, :]
        gains = gains + pltpu.roll(block[:8, :pair], owner * each, 1)
        for index in range(proj_ref.shape[1] // (2 * pair)):
            source = rows + extra + index * part
            proj_ref[
                pl.ds(aligned(owner * part, part), part), index * 2 * pair : (index + 1) * 2 * pair
            ] = piece[source : source + part, :]
    gains_ref[...] = gains + pltpu.roll(gains, HD, 1)


def wide_column(column, main, rest):
    late = (column >= 2 * main).astype(jnp.int32)
    late_up = (column >= 2 * main + rest).astype(jnp.int32)
    early_up = (column >= main).astype(jnp.int32) * (1 - late)
    is_up = late * late_up + early_up
    return is_up, column - early_up * main - late * (main + late_up * rest)


def take_wide_kernel(shards, meta_ref, gate_ref, up_ref, down_ref, out_ref, window, sem, rows, down_sem, total):
    here = meta_ref[0]
    own_rows = window.shape[1]
    inner = out_ref.shape[1] // 2
    piece = inner // shards
    span = window.shape[2]
    shift = here * (piece - 128)
    copies = []
    for kind, source in enumerate((gate_ref, up_ref)):
        for part in range(shards):
            start = aligned(part * (source.shape[1] // shards) + here * 128, 128)
            copies.append(
                pltpu.make_async_copy(
                    source.at[:, pl.ds(start, span)],
                    window.at[kind * shards + part],
                    sem.at[kind * shards + part],
                )
            )
    down = pltpu.make_async_copy(
        down_ref.at[pl.ds(aligned(here * rows.shape[0], 16), rows.shape[0]), :], rows, down_sem
    )
    for copy in copies:
        copy.start()
    down.start()
    columns = lax.broadcasted_iota(jnp.int32, (1, 2 * inner), 1)
    main = inner // 128 * 128
    is_up, unit = wide_column(columns, main, inner - main)
    owner = jnp.zeros_like(unit)
    for part in range(1, shards):
        owner = jnp.where(unit >= part * piece, part, owner)
    target = unit - owner * piece + shift
    owner = owner + is_up * shards
    places = lax.broadcasted_iota(jnp.int32, (span, 2 * inner), 0)
    for copy in copies:
        copy.wait()
    total[...] = jnp.zeros_like(total)

    def add(index, carry):
        place = jnp.where(owner == index, target, -1)
        chosen = jnp.where(places == place, 1.0, 0.0).astype(jnp.bfloat16)
        total[...] += dot_nn(window[index], chosen)
        return carry

    lax.fori_loop(0, len(copies), add, 0)
    out_ref[:own_rows, :] = total[...].astype(jnp.bfloat16)
    down.wait()
    out_ref[own_rows:, : rows.shape[1]] = rows[...]
    out_ref[own_rows:, rows.shape[1] :] = jnp.zeros_like(out_ref[own_rows:, rows.shape[1] :])


def arrange_feed_kernel(meta_ref, own_ref, near_ref, far_ref, middle_ref, relay_ref, wide_ref, down_ref):
    shard = meta_ref[1]
    rows = wide_ref.shape[0] // 4
    inner = own_ref.shape[0] - rows
    width = down_ref.shape[1]
    for bits, piece in enumerate((own_ref, near_ref, far_ref, None)):
        owner = lax.bitwise_xor(shard, bits)
        if piece is None:
            piece = middle_ref[...] + relay_ref[...]
        wide_ref[pl.ds(aligned(owner * rows, rows), rows), :] = piece[:rows, :]
        down_ref[pl.ds(aligned(owner * inner, 16), inner), :] = piece[rows:, :width]
    down_ref[4 * inner :, :] = jnp.zeros_like(down_ref[4 * inner :, :])


def head_linear_kernel(
    meta_ref, first_ref, second_ref, weight_ref, gain_ref, *refs
):
    hidden_ref, linear_ref = refs[-2:]
    rows = first_ref.shape[0]
    hidden_ref[:rows, :] = first_ref[...]
    hidden_ref[rows:, :] = second_ref[...]

    def step(index, carry):
        part = pl.ds(aligned(index * rows, rows), rows)
        values = wide(hidden_ref[part, :])
        scale = lax.rsqrt(jnp.mean(values * values, axis=1, keepdims=True) + EPSILON)
        hidden_ref[part, :] = (values * scale * gain_ref[...]).astype(jnp.bfloat16)
        linear_ref[part, :] = dot_nn(hidden_ref[part, :], weight_ref[...])
        return carry

    lax.fori_loop(0, 2, step, 0)


def attention_kernel(
    tokens, count, docs,
    meta_ref, lin_ref, cos_ref, sin_ref, gains_ref,
    query_ref, key_ref, value_ref, attn_ref, lse_ref, *refs,
):
    low_refs, (value_t, accum, low, blocks_ref) = refs[:count], refs[count:]
    blocks_ref[...] = head_blocks()
    here = meta_ref[0]
    half = tokens // 2
    size = tokens
    blocks = count

    def prepare(place, carry):
        first, low_lane = lane_masks(half)
        source = aligned(row_of(place, here, tokens, count), half)
        target = aligned(place * half, half)
        cosine = cos_ref[pl.ds(target, half), :]
        sine = sin_ref[pl.ds(target, half), :]
        query = lin_ref[pl.ds(source, half), : 2 * HD]
        unit = query * lax.rsqrt(head_mean(query * query, blocks_ref[...]) + EPSILON) * gains_ref[2:3, :]
        turned = unit * cosine + swap_half(unit, low_lane) * sine
        query_ref[pl.ds(target, half), :] = (
            turned.astype(jnp.bfloat16).astype(jnp.float32) * (HD**-0.5)
        ).astype(jnp.bfloat16)
        both = lin_ref[pl.ds(source, half), 2 * HD :]
        unit = both * lax.rsqrt(head_mean(both * both, blocks_ref[...]) + EPSILON) * gains_ref[3:4, :]
        turned = unit * cosine + swap_half(unit, low_lane) * sine
        key_ref[pl.ds(target, half), :] = jnp.where(
            first, turned, pltpu.roll(turned, HD, 1)
        ).astype(jnp.bfloat16)
        values = jnp.where(first, pltpu.roll(both, HD, 1), both)
        value_ref[pl.ds(target, half), :] = values.astype(jnp.bfloat16)
        return carry

    lax.fori_loop(0, 2 * count, prepare, 0)

    def turn_values(block, carry):
        values = wide(value_ref[pl.ds(aligned(block * size, size), size), :])
        value_t[block, :HD, :] = values.T[:HD].astype(jnp.bfloat16)
        value_t[block, HD:, :] = jnp.ones((value_t.shape[1] - HD, size), jnp.bfloat16)
        return carry

    lax.fori_loop(0, blocks, turn_values, 0)

    def query_step(block, carry):
        query = two_heads(query_ref[pl.ds(aligned(block * size, size), size), :])
        accum[...] = jnp.zeros_like(accum)
        lowest = begin_at(meta_ref, docs, block * size) // size

        def key_step(other, carry):
            keys = key_ref[pl.ds(aligned(other * size, size), size), :]
            scores = dot_nt(keys, query)
            visible = block_visible(meta_ref, docs, block, other, size)
            probable = jnp.concatenate(
                [
                    jnp.where(visible, jnp.exp(scores[:, :size]), 0.0),
                    jnp.where(visible, jnp.exp(scores[:, size:]), 0.0),
                ],
                axis=1,
            ).astype(jnp.bfloat16)
            accum[...] += dot_nn(value_t[other], probable)
            return carry

        lax.fori_loop(lowest, block + 1, key_step, 0)
        mass = accum[HD : HD + 1, :]
        mixed = accum[:HD, :] / mass
        lse_ref[block] = jnp.log(mass)
        rows = jnp.concatenate([mixed[:, :size], mixed[:, size:]], axis=0).T
        attn_ref[pl.ds(aligned(block * size, size), size), :] = rows
        for part in range(2):
            target = aligned(row_of(2 * block + part, here, tokens, count), half)
            low[pl.ds(target, half), :] = rows[part * half : (part + 1) * half].astype(jnp.bfloat16)
        return carry

    lax.fori_loop(0, blocks, query_step, 0)
    for slot, bits in enumerate(ORDER):
        low_refs[bits][...] = low[slot * tokens : (slot + 1) * tokens, :]


def attention_back_kernel(
    tokens, count, docs,
    meta_ref, lin_ref, cos_ref, sin_ref, gains_ref,
    query_ref, key_ref, value_ref, attn_ref, lse_ref, *refs,
):
    grad_refs = refs[:count]
    out_ref, gain_ref = refs[count : count + 2]
    block_refs = refs[count + 2 : 2 * count + 2]
    key_t, grad_query, grad_key, grad_value, accum, grad_rows, blocks_ref = refs[2 * count + 2 :]
    blocks_ref[...] = head_blocks()
    here = meta_ref[0]
    half = tokens // 2
    size = tokens
    blocks = count
    grad_key[...] = jnp.zeros_like(grad_key)
    grad_value[...] = jnp.zeros_like(grad_value)
    gain_ref[...] = jnp.zeros_like(gain_ref)
    for slot, bits in enumerate(ORDER):
        grad_rows[slot * tokens : (slot + 1) * tokens, :] = grad_refs[bits][...]

    def turn_keys(block, carry):
        keys = wide(key_ref[pl.ds(aligned(block * size, size), size), :])
        key_t[block] = keys.T[:HD].astype(jnp.bfloat16)
        return carry

    lax.fori_loop(0, blocks, turn_keys, 0)

    def query_step(block, carry):
        here_rows = pl.ds(aligned(block * size, size), size)
        query = two_heads(query_ref[here_rows, :])
        parts = []
        for part in range(2):
            source = aligned(row_of(2 * block + part, here, tokens, count), half)
            parts.append(grad_rows[pl.ds(source, half), :])
        grads = jnp.concatenate(parts, axis=0)
        products = (wide(grads) * attn_ref[here_rows, :]).T
        deltas = (
            jnp.sum(products[:HD], axis=0, keepdims=True),
            jnp.sum(products[HD:], axis=0, keepdims=True),
        )
        grads = two_heads(grads)
        lse = lse_ref[block]
        accum[...] = jnp.zeros_like(accum)
        lowest = begin_at(meta_ref, docs, block * size) // size

        def key_step(other, carry):
            rows = pl.ds(aligned(other * size, size), size)
            scores = dot_nt(key_ref[rows, :], query)
            grad_prob = dot_nt(value_ref[rows, :], grads)
            visible = block_visible(meta_ref, docs, block, other, size)
            probs, grad_scores = [], []
            for head in range(2):
                cols = slice(head * size, (head + 1) * size)
                prob = jnp.where(visible, jnp.exp(scores[:, cols] - lse[:, cols]), 0.0)
                probs.append(prob)
                grad_scores.append(prob * (grad_prob[:, cols] - deltas[head]))
            probs = jnp.concatenate(probs, axis=1).astype(jnp.bfloat16)
            grad_scores = jnp.concatenate(grad_scores, axis=1).astype(jnp.bfloat16)
            grad_value[rows, :] += dot_nn(probs, grads)
            grad_key[rows, :] += dot_nn(grad_scores, query)
            accum[...] += dot_nn(key_t[other], grad_scores)
            return carry

        lax.fori_loop(lowest, block + 1, key_step, 0)
        total = accum[...] * (HD**-0.5)
        grad_query[here_rows, :] = jnp.concatenate([total[:, :size], total[:, size:]], axis=0).T
        return carry

    lax.fori_loop(0, blocks, query_step, 0)

    def finish(place, carry):
        first, low_lane = lane_masks(half)
        source = aligned(row_of(place, here, tokens, count), half)
        target = pl.ds(aligned(place * half, half), half)
        cosine = cos_ref[target, :]
        sine = sin_ref[target, :]

        def through(linear, grads, gain):
            scale = lax.rsqrt(head_mean(linear * linear, blocks_ref[...]) + EPSILON)
            normed = linear * scale
            turned = grads * cosine + swap_half(grads * sine, low_lane)
            weighted = turned * gain
            grad_in = scale * (weighted - normed * head_mean(weighted * normed, blocks_ref[...]))
            return grad_in, jnp.sum(turned * normed, axis=0, keepdims=True)

        grad_in, gain_row = through(
            lin_ref[pl.ds(source, half), : 2 * HD], grad_query[target, :], gains_ref[2:3, :]
        )
        out_ref[pl.ds(source, half), : 2 * HD] = grad_in.astype(jnp.bfloat16)
        gain_ref[0:1, :] += gain_row
        keys = grad_key[target, :]
        grad_in, gain_row = through(
            lin_ref[pl.ds(source, half), 2 * HD :], keys + pltpu.roll(keys, HD, 1), gains_ref[3:4, :]
        )
        gain_ref[1:2, :] += gain_row
        values = grad_value[target, :]
        values = values + pltpu.roll(values, HD, 1)
        out_ref[pl.ds(source, half), 2 * HD :] = jnp.where(first, grad_in, values).astype(
            jnp.bfloat16
        )
        return carry

    lax.fori_loop(0, 2 * count, finish, 0)
    for slot, bits in enumerate(ORDER):
        block_refs[bits][...] = out_ref[slot * tokens : (slot + 1) * tokens, :]


def proj_grad_kernel(parts, meta_ref, attn_ref, grad_ref, *refs):
    blocks, full = refs[:-1], refs[-1]
    count = len(blocks)
    here = meta_ref[0]
    tile = 2 * pair_tile(full)

    def outer(index, carry):
        part = pl.ds(aligned(index * tile, tile), tile)
        full[part, :] = contract_rows(attn_ref[:, part], grad_ref[...]).astype(jnp.bfloat16)
        return carry

    lax.fori_loop(0, full.shape[0] // tile, outer, 0)
    rows = blocks[0].shape[0] // parts
    for bits, block in enumerate(blocks):
        owner = lax.bitwise_xor(here, bits)
        for part in range(parts):
            source = aligned(part * count * rows + owner * rows, rows)
            block[part * rows : (part + 1) * rows, :] = full[pl.ds(source, rows), :]


def pack_heads_kernel(
    extra, meta_ref, heads_ref, mixer_ref, gain_ref, feed_ref, sums_ref, *refs
):
    proj_refs, pieces = refs[:5], refs[5:]
    shard = meta_ref[1]
    rows = heads_ref.shape[0] // 4
    pair = 2 * HD
    proj = wide(proj_refs[0][...])
    for other in proj_refs[1:]:
        proj = proj + wide(other[...])
    proj_low, mixer, _, gains = pieces[4:]
    pieces = pieces[:4]
    part = proj.shape[0] // 4
    proj_low[...] = proj.astype(jnp.bfloat16)
    mixer[...] = mixer_ref[...] / gain_ref[...]
    values = sums_ref[...]
    lower = lax.broadcasted_iota(jnp.int32, values.shape, 0) == 0
    values = values + jnp.where(lower, pltpu.roll(values, HD, 1), 0.0)
    each = HD // 4
    lanes = lax.broadcasted_iota(jnp.int32, values.shape, 1)
    for bits, piece in enumerate(pieces):
        owner = lax.bitwise_xor(shard, bits)
        piece[:rows, :] = heads_ref[pl.ds(aligned(owner * rows, rows), rows), :]
        gains[...] = jnp.zeros_like(gains)
        own = pl.ds(aligned(owner * rows, rows), rows)
        gains[0:1, :] = mixer[:, own]
        gains[1:2, :] = feed_ref[:, own]
        moved = pltpu.roll(values, pair - owner * each, 1)
        moved = jnp.where(lanes < each, moved, 0.0)
        gains[2:4, :pair] = moved[0:2, :]
        piece[rows : rows + extra, :] = gains[...].astype(jnp.bfloat16)
        for index in range(proj.shape[1] // (2 * pair)):
            target = rows + extra + index * part
            piece[target : target + part, :] = proj_low[
                pl.ds(aligned(owner * part, part), part), index * 2 * pair : (index + 1) * 2 * pair
            ]


def pack_feed_kernel(meta_ref, wide_ref, down_ref, *pieces):
    shard = meta_ref[1]
    rows = wide_ref.shape[0] // 4
    inner = pieces[0].shape[0] - rows
    width = down_ref.shape[1]
    for bits, piece in enumerate(pieces):
        owner = lax.bitwise_xor(shard, bits)
        piece[:rows, :] = wide_ref[pl.ds(aligned(owner * rows, 16), rows), :]
        piece[rows:, :width] = down_ref[pl.ds(aligned(owner * inner, 16), inner), :]
        piece[rows:, width:] = jnp.zeros_like(piece[rows:, width:])


def input_grad_kernel(count, meta_ref, *refs):
    grads, weights = refs[:count], refs[count : 2 * count]
    input_ref, grad_ref, gain_ref, out_ref = refs[2 * count :]
    total = dot_nt(grads[0][...], weights[0][...])
    for left, right in zip(grads[1:], weights[1:]):
        total = total + dot_nt(left[...], right[...])
    values = wide(input_ref[...])
    scale = lax.rsqrt(jnp.mean(values * values, axis=1, keepdims=True) + EPSILON)
    normed = values * scale
    weighted = total * gain_ref[...]
    grad_in = scale * (weighted - normed * jnp.mean(weighted * normed, axis=1, keepdims=True))
    out_ref[...] = grad_ref[...] + grad_in


def project_kernel(count, parts, start, meta_ref, *refs):
    attn_refs, weight_refs, rest = refs[:count], refs[count : 2 * count], refs[2 * count :]
    input_ref, gain_ref, full_ref, attn_out_ref, mixed_ref, hidden_ref, _ = rest
    here = meta_ref[0]
    total = weight_refs[0].shape[0] - start
    rows = total // parts
    for bits in range(count):
        owner = lax.bitwise_xor(here, bits)
        for part in range(parts):
            target = aligned(part * count * rows + owner * rows, rows)
            source = start + part * rows
            full_ref[pl.ds(target, rows), :] = weight_refs[bits][source : source + rows, :]
        attn_out_ref[:, pl.ds(aligned(owner * 2 * HD, 2 * HD), 2 * HD)] = attn_refs[bits][...]
    tile = 2 * pair_tile(full_ref)

    def project(index, carry):
        part = pl.ds(aligned(index * tile, tile), tile)
        mixed_ref[:, part] = wide(input_ref[:, part]) + dot_nn(attn_out_ref[...], full_ref[:, part])
        return carry

    lax.fori_loop(0, full_ref.shape[1] // tile, project, 0)
    mixed = mixed_ref[...]
    scale = lax.rsqrt(jnp.mean(mixed * mixed, axis=1, keepdims=True) + EPSILON)
    hidden_ref[...] = (mixed * scale * gain_ref[...]).astype(jnp.bfloat16)


def feed_block(hidden_ref, grad_ref, wide_ref, down_ref, act_ref, grad_wide_ref, out_ref, back_ref):
    tokens = hidden_ref.shape[0]
    inner = wide_ref.shape[1] // 2
    main = inner // 128 * 128
    first, _ = lane_masks(tokens)

    def activate(gate, up, grad_act):
        sigmoid = 1.0 / (1.0 + jnp.exp(-gate))
        silu = gate * sigmoid
        grad_gate = grad_act * up * sigmoid * (1.0 + gate * (1.0 - sigmoid))
        return silu * up, grad_gate, grad_act * silu

    both = dot_nn(hidden_ref[...], wide_ref[...])
    grad_act = dot_nt(grad_ref[...], down_ref[...])
    act, grad_gate, grad_up = activate(
        both[:, :main], both[:, main : 2 * main], grad_act[:, :main]
    )
    act_ref[:, :main] = act.astype(jnp.bfloat16)
    grad_wide_ref[:, :main] = grad_gate.astype(jnp.bfloat16)
    grad_wide_ref[:, main : 2 * main] = grad_up.astype(jnp.bfloat16)
    last = both[:, 2 * main :]
    act, grad_gate, grad_up = activate(last, pltpu.roll(last, HD, 1), grad_act[:, main:])
    act_ref[:, main:] = jnp.where(first, act, 0.0).astype(jnp.bfloat16)
    grad_wide_ref[:, 2 * main :] = jnp.where(
        first, grad_gate, pltpu.roll(grad_up, HD, 1)
    ).astype(jnp.bfloat16)
    back_ref[...] = dot_nt(grad_wide_ref[...], wide_ref[...]).astype(jnp.bfloat16)
    out_ref[...] = dot_nn(act_ref[...], down_ref[...]).astype(jnp.bfloat16)


def feed_kernel(number, done, meta_ref, *refs):
    firsts, grads = refs[:number], refs[number : 2 * number]
    refs = refs[2 * number :]
    (wide_ref, down_ref), refs = refs[:2], refs[2:]
    filed, refs = refs[: 2 * done + 2 * (done > 0)], refs[2 * done + 2 * (done > 0) :]
    shared = 4 if done else 2
    shared_refs, refs = refs[:shared], refs[shared:]
    out_refs, back_refs, refs = refs[:number], refs[number : 2 * number], refs[2 * number :]
    hidden, grad, out_low, back_low, hidden_sem, grad_sem, out_sem, back_sem = refs[:8]
    act_ref, grad_wide_ref = shared_refs[-2:]
    tokens = hidden.shape[1]
    step = pl.program_id(0)

    def moves(index):
        return (
            pltpu.make_async_copy(firsts[index], hidden.at[index], hidden_sem.at[index]),
            pltpu.make_async_copy(
                grads[index].at[pl.ds(0, tokens), :], grad.at[index], grad_sem.at[index]
            ),
            pltpu.make_async_copy(out_low.at[index], out_refs[index], out_sem.at[index]),
            pltpu.make_async_copy(back_low.at[index], back_refs[index], back_sem.at[index]),
        )

    @pl.when(step == 0)
    def _():
        for index in range(number):
            for move in moves(index)[:2]:
                move.start()

    for index in range(number):

        @pl.when(step == index)
        def _(index=index):
            for move in moves(index)[:2]:
                move.wait()

    @pl.when(step < number)
    def _():
        if done:
            shared_refs[0][...] = hidden[step]
            shared_refs[1][...] = grad[step]
        feed_block(
            hidden.at[step], grad.at[step], wide_ref, down_ref,
            act_ref, grad_wide_ref, out_low.at[step], back_low.at[step],
        )

    for index in range(number):

        @pl.when(step == index)
        def _(index=index):
            for move in moves(index)[2:]:
                move.start()

    if done:
        file_sem = refs[8]
        for index in range(done):

            @pl.when(step == number + index)
            def _(index=index):
                rows = pl.ds(index * tokens, tokens)
                copies = [
                    pltpu.make_async_copy(source, target, file_sem.at[place])
                    for place, (source, target) in enumerate(
                        (
                            (filed[index], shared_refs[0]),
                            (filed[done + index].at[pl.ds(0, tokens), :], shared_refs[1]),
                            (filed[2 * done].at[rows, :], act_ref),
                            (filed[2 * done + 1].at[rows, :], grad_wide_ref),
                        )
                    )
                ]
                for copy in copies:
                    copy.start()
                for copy in copies:
                    copy.wait()

    @pl.when(step == number + done - 1)
    def _():
        for index in range(number):
            for move in moves(index)[2:]:
                move.wait()


def feed_call(meta, hidden, grads, weights, earlier, grant):
    number = len(hidden)
    done = len(earlier[0]) if earlier else 0
    tokens, width = hidden[0].shape
    steps = number + done
    padded, inner = weights[1].shape[0], weights[0].shape[1]
    shared = [shaped((steps * tokens, columns)) for columns in (width, width, padded, inner)]
    shared = shared if done else shared[2:]
    filed = [*earlier[0], *earlier[1], *earlier[2]] if earlier else []
    scratch = [pltpu.VMEM((number, tokens, width), jnp.bfloat16)] * 4
    scratch += [pltpu.SemaphoreType.DMA((number,))] * 4
    scratch += [pltpu.SemaphoreType.DMA((4,))] if done else []
    return pl.pallas_call(
        functools.partial(feed_kernel, number, done),
        grid=(steps,),
        out_shape=shared + [shaped((tokens, width))] * (2 * number),
        in_specs=[SCALARS] + [PLACED] * (2 * number) + [WHOLE] * 2 + [PLACED] * len(filed),
        out_specs=[pl.BlockSpec((tokens, out.shape[1]), lambda step: (step, 0)) for out in shared]
        + [PLACED] * (2 * number),
        scratch_shapes=scratch,
        cost_estimate=pl.CostEstimate(
            flops=6 * number * tokens * width * inner,
            bytes_accessed=16 * number * tokens * width,
            transcendentals=0,
        ),
        compiler_params=pltpu.CompilerParams(vmem_limit_bytes=grant * 2**20),
        name="feed",
    )(meta, *hidden, *grads, *weights, *filed)


def feed_back_kernel(count, meta_ref, *refs):
    sums, rest = refs[:5], refs[5:]
    mixed_ref, grad_ref, full_ref, gain_ref, grad_mixed_ref, grad_low_ref, grad_gain_ref = rest[:7]
    block_refs, attn = rest[7 : 7 + count], rest[7 + count]
    here = meta_ref[0]
    grad_hidden = wide(sums[0][...])
    for part in sums[1:]:
        grad_hidden = grad_hidden + wide(part[...])
    mixed = mixed_ref[...]
    scale = lax.rsqrt(jnp.mean(mixed * mixed, axis=1, keepdims=True) + EPSILON)
    normed = mixed * scale
    weighted = grad_hidden * gain_ref[...]
    grad_in = scale * (weighted - normed * jnp.mean(weighted * normed, axis=1, keepdims=True))
    grad_gain_ref[...] = jnp.sum(grad_hidden * normed, axis=0, keepdims=True)
    grad_mixed = wide(grad_ref[...]) + grad_in
    grad_mixed_ref[...] = grad_mixed
    grad_low_ref[...] = grad_mixed.astype(jnp.bfloat16)
    tile = 2 * pair_tile(full_ref)

    def project_back(index, carry):
        part = pl.ds(aligned(index * tile, tile), tile)
        attn[:, part] = dot_nt(grad_low_ref[...], full_ref[part, :]).astype(jnp.bfloat16)
        return carry

    lax.fori_loop(0, full_ref.shape[0] // tile, project_back, 0)
    for bits in range(count):
        owner = lax.bitwise_xor(here, bits)
        block_refs[bits][...] = attn[:, pl.ds(aligned(owner * 2 * HD, 2 * HD), 2 * HD)]


def wide_out_kernel(count, parts, meta_ref, *refs):
    blocks, (gate_ref, up_ref, held) = refs[:count], refs[count:]
    here = meta_ref[0]
    for bits in range(count):
        held[lax.bitwise_xor(here, bits)] = wide(blocks[bits][...])
    inner = held.shape[2] // 2
    main = inner // 128 * 128
    piece = inner // parts
    for kind, out_ref in enumerate((gate_ref, up_ref)):
        for part in range(parts):
            columns = []
            for owner in range(count):
                start, stop = part * piece, (part + 1) * piece
                begin = kind * main
                if start < main:
                    columns.append(held[owner, :, begin + start : begin + min(stop, main)])
                if stop > main:
                    begin = main + kind * (inner - main)
                    columns.append(held[owner, :, begin + max(start, main) : begin + stop])
            out_ref[:, part * count * piece : (part + 1) * count * piece] = jnp.concatenate(
                columns, axis=1
            )


def rows_out_kernel(meta_ref, *refs):
    blocks, out_ref = refs[:-1], refs[-1]
    rows = out_ref.shape[0] // len(blocks)
    start = blocks[0].shape[0] - rows
    for bits, block in enumerate(blocks):
        owner = lax.bitwise_xor(meta_ref[0], bits)
        out_ref[pl.ds(aligned(owner * rows, 16), rows), :] = wide(
            block[start:, : out_ref.shape[1]]
        )


def heads_out_kernel(count, own, extra, meta_ref, *refs):
    blocks, rest = refs[:count], refs[count:]
    query_ref, key_ref, value_ref, proj_ref, gain_ref, held = rest
    here = meta_ref[0]
    pair = 2 * HD
    part = (blocks[0].shape[0] - own - extra) // 4
    gains = jnp.zeros(gain_ref.shape, jnp.float32)
    for bits in range(count):
        owner = lax.bitwise_xor(here, bits)
        block = wide(blocks[bits][...])
        query_ref[:, pl.ds(aligned(owner * pair, pair), pair)] = block[:own, :pair]
        held[owner] = block[:own, pair:]
        gains = gains + block[own : own + extra, :]
        for index in range(4):
            source = own + extra + index * part
            proj_ref[
                pl.ds(aligned(owner * part, part), part), index * 2 * pair : (index + 1) * 2 * pair
            ] = block[source : source + part, :]
    gain_ref[...] = gains
    first, _ = lane_masks(own)
    for index in range(count // 2):
        early, late = held[2 * index], held[2 * index + 1]
        lanes = slice(index * pair, (index + 1) * pair)
        key_ref[:, lanes] = jnp.where(first, early, pltpu.roll(late, HD, 1))
        value_ref[:, lanes] = jnp.where(first, pltpu.roll(early, HD, 1), late)


SCALARS = pl.BlockSpec(memory_space=pltpu.SMEM)
WHOLE = pl.BlockSpec(memory_space=pltpu.VMEM)
PLACED = pl.BlockSpec(memory_space=pl.ANY)
FAR = pl.BlockSpec(memory_space=pltpu.HBM)


def shaped(shape, kind=jnp.bfloat16):
    return jax.ShapeDtypeStruct(shape, kind)


def whole_call(kernel, outs, ins, flops, scratch=(), grant=24, specs=None):
    moved = sum(math.prod(out.shape) * out.dtype.itemsize for out in outs)
    return pl.pallas_call(
        kernel,
        out_shape=outs,
        in_specs=[SCALARS] + (specs or [WHOLE] * ins),
        out_specs=[WHOLE] * len(outs),
        scratch_shapes=list(scratch),
        cost_estimate=pl.CostEstimate(
            flops=int(flops), bytes_accessed=int(2 * moved), transcendentals=0
        ),
        compiler_params=pltpu.CompilerParams(vmem_limit_bytes=grant * 2**20),
    )


def rows_call(kernel, arrays, kept, outs, shared, rows, start, steps, flops, scratch=(), grant=24):
    specs = [SCALARS] + [WHOLE] * (len(arrays) - 1) + [PLACED] * len(kept)
    out_specs = [
        pl.BlockSpec((rows, out.shape[1]), lambda step: (start + step, 0)) for out in outs[:shared]
    ] + [WHOLE] * (len(outs) - shared)
    moved = sum(math.prod(out.shape) * out.dtype.itemsize for out in outs)
    return pl.pallas_call(
        kernel,
        grid=(steps,),
        out_shape=outs,
        in_specs=specs,
        out_specs=out_specs,
        scratch_shapes=list(scratch),
        input_output_aliases={len(arrays) + place: place for place in range(len(kept))},
        cost_estimate=pl.CostEstimate(
            flops=int(flops), bytes_accessed=int(moved), transcendentals=0
        ),
        compiler_params=pltpu.CompilerParams(vmem_limit_bytes=grant * 2**20),
    )(*arrays, *kept)


def local_heads(
    block_input, doc_starts, out_grad, query_weight, key_weight, value_weight, output_weight,
    gate_weight, up_weight, down_weight, mixer_gain, feed_gain, query_gain, key_gain,
):
    low = jnp.bfloat16
    tokens, width = block_input.shape[1:]
    count = lax.axis_size("ctx")
    shards = lax.axis_size("fsdp")
    here = lax.axis_index("ctx").astype(jnp.int32)
    shard = lax.axis_index("fsdp").astype(jnp.int32)
    stream = tokens * count
    docs = doc_starts.shape[1]
    pair = 2 * HD
    own_rows = width // shards
    extra = 16
    meta = jnp.concatenate([here[None], shard[None], doc_starts[0].astype(jnp.int32)])
    own_input = block_input[0]
    own_grad = out_grad[0]
    inner = down_weight.shape[0] // count
    wide_inner = inner * shards
    padded = -(-wide_inner // 128) * 128
    proj_rows = own_rows // count
    edges = [(0, 1), (3, 2)]
    middle = [(1, 2), (2, 1)]
    relay = [(1, 0), (2, 3)]

    def near(piece, bits):
        return shift_fsdp(piece, flipped(bits, shards))

    across, along, partner = gather_near(own_input)
    piece_rows = own_rows + extra + 4 * proj_rows
    head_piece = whole_call(
        take_heads_kernel,
        [shaped((piece_rows, 2 * pair))],
        8,
        0,
        [
            pltpu.VMEM((extra, 2 * pair), jnp.float32),
            pltpu.VMEM((3, own_rows, pair), low),
            pltpu.VMEM((proj_rows, width), low),
            pltpu.SemaphoreType.DMA((4,)),
        ],
        grant=60,
        specs=[FAR] * 4 + [WHOLE] * 4,
    )(
        meta, query_weight, key_weight, value_weight, output_weight,
        mixer_gain[None], feed_gain[None], query_gain[None], key_gain[None],
    )[0]
    head_pieces = [head_piece] + [near(head_piece, bits) for bits in (1, 2, 3)]
    feed_rows = own_rows + inner
    feed_piece = whole_call(
        functools.partial(take_wide_kernel, shards),
        [shaped((feed_rows, 2 * wide_inner))],
        3,
        2 * own_rows * 2 * wide_inner * 2048,
        [
            pltpu.VMEM((2 * shards, own_rows, 256), low),
            pltpu.SemaphoreType.DMA((2 * shards,)),
            pltpu.VMEM((inner, width), low),
            pltpu.SemaphoreType.DMA(()),
            pltpu.VMEM((own_rows, 2 * wide_inner), jnp.float32),
        ],
        grant=60,
        specs=[FAR] * 3,
    )(behind(meta, head_piece), gate_weight, up_weight, down_weight)[0]
    feed_near = near(feed_piece, 1)
    feed_far = near(behind(feed_piece, *head_pieces[1:]), 2)
    corner = gather_corner(across, along)
    others = gather_far(across, along, corner)
    input_blocks = [own_input, partner, across, others[0], along, others[1], corner, others[2]]

    where_at = jnp.arange(stream, dtype=jnp.int32)
    begins = doc_begin(doc_starts[0], where_at)
    lanes = jnp.arange(pair) % (HD // 2)
    frequency = ROPE_BASE ** (-(2.0 * lanes.astype(jnp.float32)) / HD)
    angles = (where_at - begins).astype(jnp.float32)[:, None] * frequency[None, :]
    cosine = jnp.cos(angles)
    sine = jnp.sin(angles) * jnp.where(jnp.arange(pair) % HD < HD // 2, -1.0, 1.0)[None, :]

    heads_weight, gain_mixer, gain_feed, gain_heads, proj_part = whole_call(
        functools.partial(arrange_heads_kernel, extra),
        [
            shaped((width, 2 * pair)),
            shaped((1, width), jnp.float32),
            shaped((1, width), jnp.float32),
            shaped((8, pair), jnp.float32),
            shaped((shards * proj_rows, width)),
        ],
        4,
        0,
        grant=8,
    )(behind(meta, cosine, sine), *head_pieces)

    kept = []
    for index in range(4):
        kept = rows_call(
            head_linear_kernel,
            [meta]
            + [input_blocks[bits] for bits in ORDER[2 * index : 2 * index + 2]]
            + [heads_weight, gain_mixer],
            kept,
            [shaped((stream, width)), shaped((stream, 2 * pair), jnp.float32)],
            2,
            2 * tokens,
            index,
            1,
            4 * tokens * width * 2 * pair,
            grant=6,
        )
    hidden_in, linear = kept

    pairs = stream * stream // 2
    extra_piece = behind(jnp.concatenate([own_grad, proj_part], axis=0), corner)
    extra_across, extra_along, extra_partner = gather_near(extra_piece)
    extra_corner = swap_ctx(extra_piece, 6)
    query_att, key_att, value_att, attn, lse, *attn_low = whole_call(
        functools.partial(attention_kernel, tokens, count, docs),
        [
            shaped((stream, pair)),
            shaped((stream, pair)),
            shaped((stream, pair)),
            shaped((stream, pair), jnp.float32),
            shaped((count, 1, 2 * tokens), jnp.float32),
        ]
        + [shaped((tokens, pair))] * count,
        4,
        8 * pairs * HD,
        [
            pltpu.VMEM((count, HD + 16, tokens), low),
            pltpu.VMEM((HD + 16, 2 * tokens), jnp.float32),
            pltpu.VMEM((stream, pair), low),
            pltpu.VMEM((pair, pair), low),
        ],
        grant=10,
    )(meta, linear, cosine, sine, gain_heads)

    attn_blocks = exchange_plane(attn_low)
    feed_middle = shift_fsdp(behind(feed_piece, attn_blocks[1]), middle)
    feed_relay = shift_fsdp(behind(feed_far, attn_blocks[1]), relay)
    extra_others = gather_far(extra_across, extra_along, extra_corner, attn_blocks[1])
    extra_blocks = [
        extra_piece, extra_partner, extra_across, extra_others[0],
        extra_along, extra_others[1], extra_corner, extra_others[2],
    ]
    full_proj, attn_rows, mixed, hidden_mid = whole_call(
        functools.partial(project_kernel, count, shards, tokens),
        [
            shaped((width, width)),
            shaped((tokens, width)),
            shaped((tokens, width), jnp.float32),
            shaped((tokens, width)),
        ],
        2 * count + 2,
        2 * tokens * width * width,
        [pltpu.VMEM((tokens, width), low)],
        grant=8,
    )(meta, *attn_blocks, *extra_blocks, own_input, gain_feed)

    hidden_across, hidden_along, hidden_partner = gather_near(hidden_mid)
    hidden_corner = swap_ctx(hidden_mid, 6)
    wide_weight, down_part = whole_call(
        arrange_feed_kernel,
        [shaped((width, 2 * wide_inner)), shaped((padded, width))],
        5,
        0,
        grant=8,
    )(behind(meta, hidden_mid), feed_piece, feed_near, feed_far, feed_middle, feed_relay)
    hidden_blocks = {0: hidden_mid, 1: hidden_partner, 2: hidden_across, 4: hidden_along}
    out_parts, back_parts = [None] * count, [None] * count
    earlier = None
    for index, chosen in enumerate(((0, 1), (2, 4, 6, 3, 5, 7))):
        number = len(chosen)
        results = feed_call(
            meta,
            [hidden_blocks[bits] for bits in chosen],
            [extra_blocks[bits] for bits in chosen],
            (wide_weight, down_part),
            earlier,
            (60, 60)[index],
        )
        results, parts = results[: -2 * number], results[-2 * number :]
        for place, bits in enumerate(chosen):
            out_parts[bits] = parts[place]
            back_parts[bits] = parts[number + place]
        if index == 0:
            earlier = (
                [hidden_blocks[bits] for bits in chosen],
                [extra_blocks[bits] for bits in chosen],
                results,
            )
            far = gather_far(hidden_across, hidden_along, hidden_corner, parts[0])
            hidden_blocks.update({3: far[0], 5: far[1], 6: hidden_corner, 7: far[2]})
            weight_piece = behind(heads_weight, far[2])
            weight_near = gather_near(weight_piece)
            weight_corner = swap_ctx(weight_piece, 6)
    hidden_all, grad_all, act_all, grad_wide_all = results
    back_own, back_pairs = scatter_pair(back_parts)
    back_sums = back_own + scatter_links(back_pairs)

    def scatter_early(pieces):
        return shift_fsdp(pieces[3], edges), shift_fsdp(pieces[3], middle)

    def scatter_late(pieces, early, *ready):
        second = behind((wide(pieces[2]) + wide(early)).astype(low), *ready)
        return near(second, 2), near(behind(pieces[1], *ready), 1)

    grad_down = contract_rows(behind(act_all, *back_pairs), grad_all).astype(low)
    grad_wide = contract_rows(behind(hidden_all, grad_down), grad_wide_all).astype(low)
    feed_pieces = whole_call(
        pack_feed_kernel, [shaped((feed_rows, 2 * wide_inner))] * shards, 2, 0, grant=10
    )(meta, grad_wide, grad_down)
    wide_edge, wide_middle = scatter_early(feed_pieces)
    out_own, out_pairs = scatter_pair([behind(part, grad_wide) for part in out_parts])

    grad_mixed, grad_mixed_low, grad_feed, *grad_blocks = whole_call(
        functools.partial(feed_back_kernel, count),
        [
            shaped((tokens, width), jnp.float32),
            shaped((tokens, width)),
            shaped((1, width), jnp.float32),
        ]
        + [shaped((tokens, pair))] * count,
        9,
        2 * tokens * width * width,
        [pltpu.VMEM((tokens, width), low)],
        grant=8,
    )(meta, *back_sums, mixed, own_grad, full_proj, gain_feed)
    grad_attn = exchange_plane(grad_blocks)
    wide_late = scatter_late(feed_pieces, wide_edge, grad_blocks[0])
    proj_blocks = whole_call(
        functools.partial(proj_grad_kernel, shards),
        [shaped((shards * proj_rows, width))] * count,
        2,
        2 * tokens * width * width,
        [pltpu.VMEM((width, width), low)],
        grant=8,
    )(meta, attn_rows, grad_mixed_low)
    proj_own, proj_pairs = scatter_pair(proj_blocks)
    proj_parts = proj_own + scatter_links(proj_pairs)
    out_sums = out_own + scatter_links([behind(part, grad_blocks[0]) for part in out_pairs])

    back_outs = whole_call(
        functools.partial(attention_back_kernel, tokens, count, docs),
        [shaped((stream, 2 * pair)), shaped((8, pair), jnp.float32)]
        + [shaped((tokens, 2 * pair))] * count,
        9 + count,
        20 * pairs * HD,
        [
            pltpu.VMEM((count, HD, tokens), low),
            pltpu.VMEM((stream, pair), jnp.float32),
            pltpu.VMEM((stream, pair), jnp.float32),
            pltpu.VMEM((stream, pair), jnp.float32),
            pltpu.VMEM((HD, 2 * tokens), jnp.float32),
            pltpu.VMEM((stream, pair), low),
            pltpu.VMEM((pair, pair), low),
        ],
        grant=14,
    )(meta, linear, cosine, sine, gain_heads, query_att, key_att, value_att, attn, lse, *grad_attn)
    grad_linear, gain_sums, *token_blocks = back_outs

    token_grads = exchange_plane(token_blocks)
    late_linear = behind(grad_linear, token_grads[1])
    weight_far = gather_far(weight_near[0], weight_near[1], weight_corner, late_linear)
    weight_all = [
        weight_piece, weight_near[2], weight_near[0], weight_far[0],
        weight_near[1], weight_far[1], weight_corner, weight_far[2],
    ]
    grad_heads = contract_rows(hidden_in, late_linear).astype(low)
    grad_mixer = jnp.sum(
        contract_cols(late_linear, heads_weight) * wide(hidden_in), axis=0, keepdims=True
    )
    packed = whole_call(
        functools.partial(pack_heads_kernel, extra),
        [shaped((piece_rows, 2 * pair))] * shards,
        10,
        0,
        [
            pltpu.VMEM((shards * proj_rows, width), low),
            pltpu.VMEM((1, width), jnp.float32),
            pltpu.VMEM((8, pair), jnp.float32),
            pltpu.VMEM((extra, 2 * pair), jnp.float32),
        ],
        grant=6,
    )(meta, grad_heads, grad_mixer, gain_mixer, grad_feed, gain_sums, *proj_parts)
    heads_sent = [near(packed[bits], bits) for bits in (1, 2, 3)]

    def total_of(first, *parts):
        return sum([wide(part) for part in parts], wide(first)).astype(low)

    def total_late(pieces, parts, *ready):
        return total_of(pieces[0], *[behind(part, *ready) for part in parts])

    wide_total = total_late(feed_pieces, (wide_middle,) + wide_late, grad_linear)
    wide_blocks = gather_plane(wide_total)
    input_grad = whole_call(
        functools.partial(input_grad_kernel, count),
        [shaped((tokens, width), jnp.float32)],
        2 * count + 3,
        2 * tokens * width * 2 * width,
        grant=10,
    )(meta, *token_grads, *weight_all, own_input, grad_mixed, gain_mixer)[0]
    heads_total = total_of(packed[0], *heads_sent)
    heads_blocks = gather_direct(heads_total)
    block_output = (
        mixed + sum(wide(behind(part, packed[0])) for part in out_sums)
    ).astype(low)

    out_down = whole_call(
        rows_out_kernel, [shaped((count * inner, width), jnp.float32)], count, 0
    )(meta, *wide_blocks)[0]
    tile = own_rows // 4
    out_gate, out_up = pl.pallas_call(
        functools.partial(wide_out_kernel, count, shards),
        grid=(4,),
        in_specs=[SCALARS]
        + [pl.BlockSpec((tile, 2 * wide_inner), lambda step: (step, 0))] * count,
        out_specs=[pl.BlockSpec((tile, wide_inner * count), lambda step: (step, 0))] * 2,
        out_shape=[shaped((own_rows, wide_inner * count), jnp.float32)] * 2,
        scratch_shapes=[pltpu.VMEM((count, tile, 2 * wide_inner), jnp.float32)],
        compiler_params=pltpu.CompilerParams(vmem_limit_bytes=24 * 2**20),
        name="wide_out",
    )(meta, *wide_blocks)
    out_query, out_key, out_value, out_proj, gain_out = whole_call(
        functools.partial(heads_out_kernel, count, own_rows, extra),
        [
            shaped((own_rows, width), jnp.float32),
            shaped((own_rows, KVH * HD), jnp.float32),
            shaped((own_rows, KVH * HD), jnp.float32),
            shaped((own_rows, width), jnp.float32),
            shaped((extra, 2 * pair), jnp.float32),
        ],
        count,
        0,
        [pltpu.VMEM((count, own_rows, pair), jnp.float32)],
    )(meta, *heads_blocks)
    return (
        block_output[None],
        input_grad[None],
        out_query,
        out_key,
        out_value,
        out_proj,
        out_gate,
        out_up,
        out_down,
        gain_out[0],
        gain_out[1],
        gain_out[2, : query_gain.shape[0]],
        gain_out[3, : key_gain.shape[0]],
    )


def divides_heads(mesh):
    return mesh.shape["ctx"] == KVH and mesh.shape["fsdp"] == 4 and H == 2 * KVH


def solution(mesh):
    in_specs = (
        P("fsdp", "ctx", None),
        P("fsdp", None),
        P("fsdp", "ctx", None),
        P("fsdp", None),
        P("fsdp", None),
        P("fsdp", None),
        P("fsdp", None),
        P("fsdp", None),
        P("fsdp", None),
        P("fsdp", None),
        P("fsdp"),
        P("fsdp"),
        P("fsdp"),
        P("fsdp"),
    )
    out_specs = (
        P("fsdp", "ctx", None),
        P("fsdp", "ctx", None),
        P("fsdp", None),
        P("fsdp", None),
        P("fsdp", None),
        P("fsdp", None),
        P("fsdp", None),
        P("fsdp", None),
        P("fsdp", None),
        P("fsdp"),
        P("fsdp"),
        P("fsdp"),
        P("fsdp"),
    )
    if not divides_heads(mesh):
        return jax.shard_map(
            local, mesh=mesh, in_specs=in_specs, out_specs=out_specs, check_vma=False
        )

    return jax.shard_map(local_heads, mesh=mesh, in_specs=in_specs, out_specs=out_specs, check_vma=False)
```

```python
import functools
import math

import jax
import jax.numpy as jnp
from jax import lax
from jax.experimental import pallas as pl
from jax.experimental.pallas import tpu as pltpu
from jax.sharding import PartitionSpec as P

H = 16
KVH = 8
HD = 64


EPSILON = 1e-05
ROPE_BASE = 1000000.0
FLOOR_SCORE = -1e30


def place_rows(row_index, tokens, ctx_count):
    half_rows = tokens // 2
    device = row_index // tokens
    offset = row_index % tokens
    early = device * half_rows + offset
    late = (2 * ctx_count - 1 - device) * half_rows + offset - half_rows
    return jnp.where(offset < half_rows, early, late)


def doc_begin(starts, where_at):
    started = starts[None, :] <= where_at[:, None]
    return jnp.max(jnp.where(started, starts[None, :], 0), axis=1)


def rotary(positions):
    half_dim = HD // 2
    frequency = ROPE_BASE ** (-(2.0 * jnp.arange(half_dim, dtype=jnp.float32)) / HD)
    angles = positions.astype(jnp.float32)[:, None] * frequency[None, :]
    angles = jnp.concatenate([angles, angles], axis=1)
    return (jnp.cos(angles)[:, None, :], jnp.sin(angles)[:, None, :])


def rotate_pairs(values, cosine, sine_part):
    half_dim = values.shape[-1] // 2
    rolled = jnp.concatenate([-values[..., half_dim:], values[..., :half_dim]], axis=-1)
    return values * cosine + rolled * sine_part


def rotate_back(grads, cosine, sine_part):
    half_dim = grads.shape[-1] // 2
    moved = grads * sine_part
    rolled = jnp.concatenate([moved[..., half_dim:], -moved[..., :half_dim]], axis=-1)
    return grads * cosine + rolled


def unit_norm(values):
    scaling = lax.rsqrt(jnp.mean(values * values, axis=-1, keepdims=True) + EPSILON)
    return (values * scaling, scaling)


def norm_back(grad_out, normed, scaling, gain_row):
    weighted = grad_out * gain_row
    grad_in = scaling * (weighted - normed * jnp.mean(weighted * normed, axis=-1, keepdims=True))
    grad_gain = jnp.sum((grad_out * normed).reshape(-1, normed.shape[-1]), axis=0)
    return (grad_in, grad_gain)


def score_block(query_rows, key_rows, scaling):
    return (
        jnp.einsum("igrd,jgd->grij", query_rows, key_rows, preferred_element_type=jnp.float32)
        * scaling
    )


def visible_pairs(query_at, query_doc, key_at, key_doc):
    return (query_doc[:, None] == key_doc[None, :]) & (key_at[None, :] <= query_at[:, None])


def any_visible(query_at, query_doc, key_at):
    return (jnp.min(key_at) <= jnp.max(query_at)) & (jnp.max(key_at) >= jnp.min(query_doc))


def contract_rows(left, right):
    return lax.dot_general(
        left, right, (((0,), (0,)), ((), ())), preferred_element_type=jnp.float32
    )


def contract_cols(left, right):
    return lax.dot_general(
        left, right, (((1,), (1,)), ((), ())), preferred_element_type=jnp.float32
    )


def keep_same(totals):
    return totals


def local(
    block_input,
    doc_starts,
    out_grad,
    query_weight,
    key_weight,
    value_weight,
    output_weight,
    gate_weight,
    up_weight,
    down_weight,
    mixer_gain,
    feed_gain,
    query_gain,
    key_gain,
):
    tokens = block_input.shape[1]
    ctx_count = lax.axis_size("ctx")
    repeat = H // KVH
    kv_width = KVH * HD
    scaling = HD ** (-0.5)
    inputs = block_input[0].astype(jnp.float32)
    starts = doc_starts[0]
    where_at = place_rows(
        lax.axis_index("ctx") * tokens + jnp.arange(tokens, dtype=jnp.int32), tokens, ctx_count
    )
    begins = doc_begin(starts, where_at)
    cosine, sine_part = rotary(where_at - begins)
    gathered = (
        lax.all_gather(query_weight, "fsdp", axis=0, tiled=True),
        lax.all_gather(key_weight, "fsdp", axis=0, tiled=True),
        lax.all_gather(value_weight, "fsdp", axis=0, tiled=True),
        lax.all_gather(output_weight, "fsdp", axis=0, tiled=True),
        lax.all_gather(gate_weight, "fsdp", axis=0, tiled=True),
        lax.all_gather(up_weight, "fsdp", axis=0, tiled=True),
        lax.all_gather(down_weight, "fsdp", axis=0, tiled=True),
        lax.all_gather(mixer_gain, "fsdp", axis=0, tiled=True),
        lax.all_gather(feed_gain, "fsdp", axis=0, tiled=True),
        lax.all_gather(query_gain, "fsdp", axis=0, tiled=True),
        lax.all_gather(key_gain, "fsdp", axis=0, tiled=True),
    )
    full_query, full_key, full_value, full_proj, full_gate, full_up, full_down = gathered[:7]
    gain_mixer, gain_feed, gain_query, gain_key = [
        entry.astype(jnp.float32) for entry in gathered[7:]
    ]
    normed_in, scale_in = unit_norm(inputs)
    hidden_in = (normed_in * gain_mixer).astype(jnp.bfloat16)
    query_lin = jnp.dot(hidden_in, full_query, preferred_element_type=jnp.float32)
    key_lin = jnp.dot(hidden_in, full_key, preferred_element_type=jnp.float32)
    value_lin = jnp.dot(hidden_in, full_value, preferred_element_type=jnp.float32)
    query_normed, query_scale = unit_norm(query_lin.reshape(tokens, H, HD))
    key_normed, key_scale = unit_norm(key_lin.reshape(tokens, KVH, HD))
    query_att = (
        rotate_pairs(query_normed * gain_query, cosine, sine_part)
        .reshape(tokens, H * HD)
        .astype(jnp.bfloat16)
    )
    key_att = (
        rotate_pairs(key_normed * gain_key, cosine, sine_part)
        .reshape(tokens, kv_width)
        .astype(jnp.bfloat16)
    )
    value_att = value_lin.astype(jnp.bfloat16)
    query_four = query_att.reshape(tokens, KVH, repeat, HD)
    start_state = (
        jnp.full((KVH, repeat, tokens), FLOOR_SCORE, jnp.float32),
        jnp.zeros((KVH, repeat, tokens), jnp.float32),
        jnp.zeros((tokens, H * HD), jnp.float32),
    )
    key_part = lax.all_gather(key_att, "ctx", axis=0, tiled=True)
    value_part = lax.all_gather(value_att, "ctx", axis=0, tiled=True)
    rows = key_part.shape[0]
    width = math.gcd(math.gcd(rows, tokens // 2), 512)

    def forward_key_block(block_index, totals):
        offset = block_index * width
        key_rows = lax.dynamic_slice_in_dim(key_part, offset, width, 0).reshape(width, KVH, HD)
        value_rows = lax.dynamic_slice_in_dim(value_part, offset, width, 0).reshape(width, KVH, HD)
        key_at = place_rows(offset + jnp.arange(width, dtype=jnp.int32), tokens, ctx_count)

        def attend(totals):
            highest, total_mass, accum = totals
            visible = visible_pairs(where_at, begins, key_at, doc_begin(starts, key_at))
            scores = jnp.where(visible, score_block(query_four, key_rows, scaling), FLOOR_SCORE)
            new_high = jnp.maximum(highest, jnp.max(scores, axis=-1))
            rescale = jnp.exp(highest - new_high)
            probable = jnp.where(visible, jnp.exp(scores - new_high[..., None]), 0.0)
            total_mass = total_mass * rescale + jnp.sum(probable, axis=-1)
            part_out = jnp.einsum(
                "grij,jgd->igrd",
                probable.astype(jnp.bfloat16),
                value_rows,
                preferred_element_type=jnp.float32,
            )
            accum = (
                accum.reshape(tokens, KVH, repeat, HD)
                * jnp.transpose(rescale, (2, 0, 1))[..., None]
                + part_out
            )
            return (new_high, total_mass, accum.reshape(tokens, H * HD))

        return lax.cond(any_visible(where_at, begins, key_at), attend, keep_same, totals)

    highest, total_mass, accum = lax.fori_loop(0, rows // width, forward_key_block, start_state)
    lse_heads = highest + jnp.log(total_mass)
    attn_raw = (
        accum.reshape(tokens, KVH, repeat, HD) / jnp.transpose(total_mass, (2, 0, 1))[..., None]
    ).reshape(tokens, H * HD)
    attn_low = attn_raw.astype(jnp.bfloat16)
    mixed = inputs + jnp.dot(attn_low, full_proj, preferred_element_type=jnp.float32)
    normed_mid, scale_mid = unit_norm(mixed)
    hidden_mid = (normed_mid * gain_feed).astype(jnp.bfloat16)
    gate_lin = jnp.dot(hidden_mid, full_gate, preferred_element_type=jnp.float32)
    up_lin = jnp.dot(hidden_mid, full_up, preferred_element_type=jnp.float32)
    sigmoid_gate = jax.nn.sigmoid(gate_lin)
    activated = (gate_lin * sigmoid_gate * up_lin).astype(jnp.bfloat16)
    block_output = (
        mixed + jnp.dot(activated, full_down, preferred_element_type=jnp.float32)
    ).astype(jnp.bfloat16)
    regathered = (
        lax.all_gather(query_weight, "fsdp", axis=0, tiled=True),
        lax.all_gather(key_weight, "fsdp", axis=0, tiled=True),
        lax.all_gather(value_weight, "fsdp", axis=0, tiled=True),
        lax.all_gather(output_weight, "fsdp", axis=0, tiled=True),
        lax.all_gather(gate_weight, "fsdp", axis=0, tiled=True),
        lax.all_gather(up_weight, "fsdp", axis=0, tiled=True),
        lax.all_gather(down_weight, "fsdp", axis=0, tiled=True),
        lax.all_gather(mixer_gain, "fsdp", axis=0, tiled=True),
        lax.all_gather(feed_gain, "fsdp", axis=0, tiled=True),
        lax.all_gather(query_gain, "fsdp", axis=0, tiled=True),
        lax.all_gather(key_gain, "fsdp", axis=0, tiled=True),
    )
    full_query, full_key, full_value, full_proj, full_gate, full_up, full_down = regathered[:7]
    gain_mixer, gain_feed, gain_query, gain_key = [
        entry.astype(jnp.float32) for entry in regathered[7:]
    ]
    grad_top = out_grad[0].astype(jnp.float32)
    grad_top_low = grad_top.astype(jnp.bfloat16)
    grad_down = contract_rows(activated, grad_top_low)
    grad_act = contract_cols(grad_top_low, full_down)
    grad_gate_low = (
        grad_act * up_lin * sigmoid_gate * (1.0 + gate_lin * (1.0 - sigmoid_gate))
    ).astype(jnp.bfloat16)
    grad_up_low = (grad_act * gate_lin * sigmoid_gate).astype(jnp.bfloat16)
    grad_gate = contract_rows(hidden_mid, grad_gate_low)
    grad_up = contract_rows(hidden_mid, grad_up_low)
    grad_hidden_mid = contract_cols(grad_gate_low, full_gate) + contract_cols(grad_up_low, full_up)
    grad_normed_mid, grad_feed = norm_back(grad_hidden_mid, normed_mid, scale_mid, gain_feed)
    grad_mixed = grad_top + grad_normed_mid
    grad_mixed_low = grad_mixed.astype(jnp.bfloat16)
    grad_proj = contract_rows(attn_low, grad_mixed_low)
    grad_attn = contract_cols(grad_mixed_low, full_proj).astype(jnp.bfloat16)
    grad_four = grad_attn.reshape(tokens, KVH, repeat, HD)
    delta_heads = jnp.sum(
        grad_four.astype(jnp.float32) * attn_raw.reshape(tokens, KVH, repeat, HD), axis=-1
    )
    delta_grid = jnp.transpose(delta_heads, (1, 2, 0))
    lse_rows = jnp.transpose(lse_heads, (2, 0, 1)).reshape(tokens, H)
    delta_rows = delta_heads.reshape(tokens, H)
    query_key_part = lax.all_gather(key_att, "ctx", axis=0, tiled=True)
    query_value_part = lax.all_gather(value_att, "ctx", axis=0, tiled=True)
    rows = query_key_part.shape[0]
    query_width = math.gcd(math.gcd(rows, tokens // 2), 512)

    def query_key_block(block_index, grad_query_acc):
        offset = block_index * query_width
        key_rows = lax.dynamic_slice_in_dim(query_key_part, offset, query_width, 0).reshape(
            query_width, KVH, HD
        )
        value_rows = lax.dynamic_slice_in_dim(query_value_part, offset, query_width, 0).reshape(
            query_width, KVH, HD
        )
        key_at = place_rows(offset + jnp.arange(query_width, dtype=jnp.int32), tokens, ctx_count)

        def attend(grad_query_acc):
            visible = visible_pairs(where_at, begins, key_at, doc_begin(starts, key_at))
            scores = score_block(query_four, key_rows, scaling)
            probable = jnp.where(visible, jnp.exp(scores - lse_heads[..., None]), 0.0)
            grad_prob = jnp.einsum(
                "igrd,jgd->grij", grad_four, value_rows, preferred_element_type=jnp.float32
            )
            grad_score = (probable * (grad_prob - delta_grid[..., None])).astype(jnp.bfloat16)
            added = (
                jnp.einsum(
                    "grij,jgd->igrd", grad_score, key_rows, preferred_element_type=jnp.float32
                )
                * scaling
            )
            return grad_query_acc + added.reshape(tokens, H * HD)

        return lax.cond(any_visible(where_at, begins, key_at), attend, keep_same, grad_query_acc)

    grad_query_att = lax.fori_loop(
        0, rows // query_width, query_key_block, jnp.zeros((tokens, H * HD), jnp.float32)
    )
    lse_all, delta_all = (
        lax.all_gather(lse_rows.astype(jnp.bfloat16), "ctx", axis=0, tiled=True).astype(
            lse_rows.dtype
        ),
        lax.all_gather(delta_rows.astype(jnp.bfloat16), "ctx", axis=0, tiled=True).astype(
            delta_rows.dtype
        ),
    )
    key_three = key_att.reshape(tokens, KVH, HD)
    value_three = value_att.reshape(tokens, KVH, HD)
    empty_keys = jnp.zeros((tokens, kv_width), jnp.float32)
    query_part = lax.all_gather(query_att, "ctx", axis=0, tiled=True)
    grad_part = lax.all_gather(grad_attn, "ctx", axis=0, tiled=True)
    rows = query_part.shape[0]
    key_width = math.gcd(math.gcd(rows, tokens // 2), 512)

    def query_block(block_index, totals):
        offset = block_index * key_width
        query_rows = lax.dynamic_slice_in_dim(query_part, offset, key_width, 0).reshape(
            key_width, KVH, repeat, HD
        )
        grad_rows = lax.dynamic_slice_in_dim(grad_part, offset, key_width, 0).reshape(
            key_width, KVH, repeat, HD
        )
        query_at = place_rows(offset + jnp.arange(key_width, dtype=jnp.int32), tokens, ctx_count)
        query_doc = doc_begin(starts, query_at)
        lse_block = jnp.transpose(
            lax.dynamic_slice_in_dim(lse_all, offset, key_width, 0).reshape(key_width, KVH, repeat),
            (1, 2, 0),
        )
        delta_block = jnp.transpose(
            lax.dynamic_slice_in_dim(delta_all, offset, key_width, 0).reshape(
                key_width, KVH, repeat
            ),
            (1, 2, 0),
        )

        def attend(totals):
            grad_key_acc, grad_value_acc = totals
            visible = visible_pairs(query_at, query_doc, where_at, begins)
            scores = score_block(query_rows, key_three, scaling)
            probable = jnp.where(visible, jnp.exp(scores - lse_block[..., None]), 0.0)
            grad_prob = jnp.einsum(
                "igrd,jgd->grij", grad_rows, value_three, preferred_element_type=jnp.float32
            )
            grad_score = (probable * (grad_prob - delta_block[..., None])).astype(jnp.bfloat16)
            value_added = jnp.einsum(
                "grij,igrd->jgd",
                probable.astype(jnp.bfloat16),
                grad_rows,
                preferred_element_type=jnp.float32,
            )
            key_added = (
                jnp.einsum(
                    "grij,igrd->jgd", grad_score, query_rows, preferred_element_type=jnp.float32
                )
                * scaling
            )
            return (
                grad_key_acc + key_added.reshape(tokens, kv_width),
                grad_value_acc + value_added.reshape(tokens, kv_width),
            )

        return lax.cond(any_visible(query_at, query_doc, where_at), attend, keep_same, totals)

    grad_key_att, grad_value_att = lax.fori_loop(
        0, rows // key_width, query_block, (empty_keys, empty_keys)
    )
    grad_query_unit = rotate_back(grad_query_att.reshape(tokens, H, HD), cosine, sine_part)
    grad_query_lin, grad_qgain = norm_back(grad_query_unit, query_normed, query_scale, gain_query)
    grad_key_unit = rotate_back(grad_key_att.reshape(tokens, KVH, HD), cosine, sine_part)
    grad_key_lin, grad_kgain = norm_back(grad_key_unit, key_normed, key_scale, gain_key)
    grad_query_low = grad_query_lin.reshape(tokens, H * HD).astype(jnp.bfloat16)
    grad_key_low = grad_key_lin.reshape(tokens, kv_width).astype(jnp.bfloat16)
    grad_value_low = grad_value_att.astype(jnp.bfloat16)
    grad_query = contract_rows(hidden_in, grad_query_low)
    grad_key = contract_rows(hidden_in, grad_key_low)
    grad_value = contract_rows(hidden_in, grad_value_low)
    grad_hidden_in = (
        contract_cols(grad_query_low, full_query)
        + contract_cols(grad_key_low, full_key)
        + contract_cols(grad_value_low, full_value)
    )
    grad_normed_in, grad_mixer = norm_back(grad_hidden_in, normed_in, scale_in, gain_mixer)
    input_grad = grad_mixed + grad_normed_in
    parts = (
        lax.psum_scatter(
            grad_query.astype(jnp.bfloat16), "fsdp", scatter_dimension=0, tiled=True
        ).astype(jnp.float32),
        lax.psum_scatter(
            grad_key.astype(jnp.bfloat16), "fsdp", scatter_dimension=0, tiled=True
        ).astype(jnp.float32),
        lax.psum_scatter(
            grad_value.astype(jnp.bfloat16), "fsdp", scatter_dimension=0, tiled=True
        ).astype(jnp.float32),
        lax.psum_scatter(
            grad_proj.astype(jnp.bfloat16), "fsdp", scatter_dimension=0, tiled=True
        ).astype(jnp.float32),
        lax.psum_scatter(
            grad_gate.astype(jnp.bfloat16), "fsdp", scatter_dimension=0, tiled=True
        ).astype(jnp.float32),
        lax.psum_scatter(
            grad_up.astype(jnp.bfloat16), "fsdp", scatter_dimension=0, tiled=True
        ).astype(jnp.float32),
        lax.psum_scatter(
            grad_down.astype(jnp.bfloat16), "fsdp", scatter_dimension=0, tiled=True
        ).astype(jnp.float32),
        lax.psum_scatter(
            grad_mixer.astype(jnp.bfloat16), "fsdp", scatter_dimension=0, tiled=True
        ).astype(jnp.float32),
        lax.psum_scatter(
            grad_feed.astype(jnp.bfloat16), "fsdp", scatter_dimension=0, tiled=True
        ).astype(jnp.float32),
        lax.psum_scatter(
            grad_qgain.astype(jnp.bfloat16), "fsdp", scatter_dimension=0, tiled=True
        ).astype(jnp.float32),
        lax.psum_scatter(
            grad_kgain.astype(jnp.bfloat16), "fsdp", scatter_dimension=0, tiled=True
        ).astype(jnp.float32),
    )
    summed = (
        lax.psum(parts[0].astype(jnp.bfloat16), "ctx").astype(jnp.float32),
        lax.psum(parts[1].astype(jnp.bfloat16), "ctx").astype(jnp.float32),
        lax.psum(parts[2].astype(jnp.bfloat16), "ctx").astype(jnp.float32),
        lax.psum(parts[3].astype(jnp.bfloat16), "ctx").astype(jnp.float32),
        lax.psum(parts[4].astype(jnp.bfloat16), "ctx").astype(jnp.float32),
        lax.psum(parts[5].astype(jnp.bfloat16), "ctx").astype(jnp.float32),
        lax.psum(parts[6].astype(jnp.bfloat16), "ctx").astype(jnp.float32),
        lax.psum(parts[7].astype(jnp.bfloat16), "ctx").astype(jnp.float32),
        lax.psum(parts[8].astype(jnp.bfloat16), "ctx").astype(jnp.float32),
        lax.psum(parts[9].astype(jnp.bfloat16), "ctx").astype(jnp.float32),
        lax.psum(parts[10].astype(jnp.bfloat16), "ctx").astype(jnp.float32),
    )
    return (
        block_output[None],
        input_grad[None],
        summed[0],
        summed[1],
        summed[2],
        summed[3],
        summed[4],
        summed[5],
        summed[6],
        summed[7],
        summed[8],
        summed[9],
        summed[10],
    )


ORDER = (0, 1, 2, 4, 3, 5, 6, 7)


def flipped(bits, count):
    return [(index, index ^ bits) for index in range(count)]


def swap_ctx(values, bits):
    return lax.ppermute(values, "ctx", flipped(bits, lax.axis_size("ctx")))


def behind(values, *ready):
    return lax.optimization_barrier((values,) + ready)[0]


def dot_nn(left, right):
    return lax.dot_general(
        left, right, (((1,), (0,)), ((), ())), preferred_element_type=jnp.float32
    )


def dot_nt(left, right):
    return lax.dot_general(
        left, right, (((1,), (1,)), ((), ())), preferred_element_type=jnp.float32
    )


def wide(values):
    return values.astype(jnp.float32)


def gather_near(block):
    return swap_ctx(block, 2), swap_ctx(block, 4), swap_ctx(block, 1)


def gather_corner(across, along):
    half = across.shape[0] // 2
    first = swap_ctx(along[:half], 2)
    second = swap_ctx(across[half:], 4)
    return jnp.concatenate([first, second], axis=0)


def gather_far(across, along, corner, *ready):
    return [swap_ctx(behind(part, *ready), 1) for part in (across, along, corner)]


def gather_plane(block, *ready):
    across, along, partner = gather_near(block)
    corner = gather_corner(across, along)
    others = gather_far(across, along, corner, *ready)
    return [block, partner, across, others[0], along, others[1], corner, others[2]]


def gather_direct(block, *ready):
    across, along, partner = gather_near(block)
    corner = swap_ctx(block, 6)
    others = gather_far(across, along, corner, *ready)
    return [block, partner, across, others[0], along, others[1], corner, others[2]]


def scatter_pair(blocks):
    got = [swap_ctx(blocks[bits], 1) for bits in (3, 5, 7, 1)]
    sums = [
        (wide(blocks[bits]) + wide(other)).astype(jnp.bfloat16)
        for bits, other in zip((2, 4, 6), got)
    ]
    return [blocks[0], got[3]], sums


def scatter_links(sums):
    return [swap_ctx(part, bits) for bits, part in zip((2, 4, 6), sums)]


def exchange_plane(blocks):
    return [blocks[0]] + [swap_ctx(blocks[bits], bits) for bits in range(1, 8)]


def shift_fsdp(values, pairs):
    return lax.ppermute(values, "fsdp", pairs)


def slot_of(bits):
    return jnp.where(bits == 3, 4, jnp.where(bits == 4, 3, bits))


def row_of(place, here, tokens, count):
    half = tokens // 2
    device = jnp.where(place < count, place, 2 * count - 1 - place)
    late = jnp.where(place < count, 0, half)
    return slot_of(lax.bitwise_xor(device, here)) * tokens + late


def swap_half(values, low_lane):
    return jnp.where(low_lane, pltpu.roll(values, 96, 1), pltpu.roll(values, 32, 1))


def head_blocks():
    shape = (2 * HD, 2 * HD)
    row = lax.broadcasted_iota(jnp.int32, shape, 0) < HD
    column = lax.broadcasted_iota(jnp.int32, shape, 1) < HD
    return jnp.where(row == column, 1.0 / HD, 0.0).astype(jnp.bfloat16)


def head_mean(values, blocks):
    high = values.astype(jnp.bfloat16)
    rest = (values - wide(high)).astype(jnp.bfloat16)
    return dot_nn(high, blocks) + dot_nn(rest, blocks)


def lane_masks(rows):
    lanes = lax.broadcasted_iota(jnp.int32, (rows, 2 * HD), 1)
    return lanes < HD, (lanes % HD) < (HD // 2)


def two_heads(values):
    first, _ = lane_masks(values.shape[0])
    zero = jnp.zeros_like(values)
    return jnp.concatenate(
        [jnp.where(first, values, zero), jnp.where(first, zero, values)], axis=0
    )


def begin_at(meta_ref, docs, where_at):
    begin = jnp.zeros_like(where_at)
    for doc in range(docs):
        begin = jnp.where(meta_ref[2 + doc] <= where_at, meta_ref[2 + doc], begin)
    return begin


def block_visible(meta_ref, docs, query_block, key_block, size):
    query_at = query_block * size + lax.broadcasted_iota(jnp.int32, (1, size), 1)
    begin = begin_at(meta_ref, docs, query_at)
    key_at = key_block * size + lax.broadcasted_iota(jnp.int32, (size, size), 0)
    return (key_at <= query_at) & (key_at >= begin)


def pair_tile(ref):
    return 2 * HD if ref.shape[0] % (4 * HD) == 0 else ref.shape[0] // 2


def aligned(value, size):
    return pl.multiple_of(value, size)


def take_heads_kernel(
    meta_ref, query_ref, key_ref, value_ref, proj_ref, mixer_ref, feed_ref, query_gain_ref, key_gain_ref,
    out_ref, gains, windows, proj, sem,
):
    here = meta_ref[0]
    rows = query_ref.shape[0]
    pair = 2 * HD
    start = aligned(lax.shift_right_logical(here, 1) * pair, pair)
    part = proj.shape[0]
    copies = [
        pltpu.make_async_copy(
            query_ref.at[:, pl.ds(aligned(here * pair, pair), pair)], windows.at[0], sem.at[0]
        ),
        pltpu.make_async_copy(key_ref.at[:, pl.ds(start, pair)], windows.at[1], sem.at[1]),
        pltpu.make_async_copy(value_ref.at[:, pl.ds(start, pair)], windows.at[2], sem.at[2]),
        pltpu.make_async_copy(
            proj_ref.at[pl.ds(aligned(here * part, part), part), :], proj, sem.at[3]
        ),
    ]
    for copy in copies:
        copy.start()
    gains[...] = jnp.zeros_like(gains)
    gains[0:1, :] = wide(mixer_ref[...])
    gains[1:2, :] = wide(feed_ref[...])
    gains[2:3, : query_gain_ref.shape[1]] = wide(query_gain_ref[...])
    gains[3:4, : key_gain_ref.shape[1]] = wide(key_gain_ref[...])
    extra = gains.shape[0]
    out_ref[rows : rows + extra, :] = gains[...].astype(jnp.bfloat16)
    for copy in copies:
        copy.wait()
    out_ref[:rows, :pair] = windows[0]
    odd = lax.bitwise_and(here, 1) == 1
    keys = wide(windows[1])
    values = wide(windows[2])
    first, _ = lane_masks(rows)
    keys = jnp.where(odd, pltpu.roll(keys, HD, 1), keys)
    values = jnp.where(odd, values, pltpu.roll(values, HD, 1))
    out_ref[:rows, pair:] = jnp.where(first, keys, values).astype(jnp.bfloat16)
    for index in range(proj.shape[1] // (2 * pair)):
        target = rows + extra + index * part
        out_ref[target : target + part, :] = proj[:, index * 2 * pair : (index + 1) * 2 * pair]


def arrange_heads_kernel(
    extra, meta_ref, *refs
):
    pieces, (weight_ref, mixer_ref, feed_ref, gains_ref, proj_ref) = refs[:4], refs[4:]
    shard = meta_ref[1]
    rows = weight_ref.shape[0] // 4
    pair = 2 * HD
    each = HD // 4
    gains = jnp.zeros((8, pair), jnp.float32)
    part = proj_ref.shape[0] // 4
    for bits, piece in enumerate(pieces):
        owner = lax.bitwise_xor(shard, bits)
        weight_ref[pl.ds(aligned(owner * rows, rows), rows), :] = piece[:rows, :]
        block = wide(piece[rows : rows + extra, :])
        lanes = pl.ds(aligned(owner * rows, rows), rows)
        mixer_ref[:, lanes] = block[0:1, :]
        feed_ref[:, lanes] = block[1:2, :]
        gains = gains + pltpu.roll(block[:8, :pair], owner * each, 1)
        for index in range(proj_ref.shape[1] // (2 * pair)):
            source = rows + extra + index * part
            proj_ref[
                pl.ds(aligned(owner * part, part), part), index * 2 * pair : (index + 1) * 2 * pair
            ] = piece[source : source + part, :]
    gains_ref[...] = gains + pltpu.roll(gains, HD, 1)


def take_wide_kernel(
    shards, meta_ref, gate_ref, up_ref, down_ref, out_ref, window, sem, rows, down_sem,
):
    here = meta_ref[0]
    own_rows = window.shape[1]
    inner = out_ref.shape[1] // 2
    piece = inner // shards
    span = window.shape[2]
    copies = []
    for kind, source in enumerate((gate_ref, up_ref)):
        for part in range(shards):
            start = aligned(part * (source.shape[1] // shards) + here * 128, 128)
            copies.append(
                pltpu.make_async_copy(
                    source.at[:, pl.ds(start, span)],
                    window.at[kind * shards + part],
                    sem.at[kind * shards + part],
                )
            )
    down = pltpu.make_async_copy(
        down_ref.at[pl.ds(aligned(here * rows.shape[0], 16), rows.shape[0]), :], rows, down_sem
    )
    for copy in copies:
        copy.start()
    down.start()
    main = inner // 128 * 128
    shift = span - here * (piece - 128)
    lasts = []
    for kind in range(2):
        parts = []
        for part in range(shards):
            copies[kind * shards + part].wait()
            moved = pltpu.roll(wide(window[kind * shards + part]), shift, 1)
            parts.append(moved[:, :piece])
        joined = jnp.concatenate(parts, axis=1)
        out_ref[:own_rows, kind * main : (kind + 1) * main] = joined[:, :main].astype(jnp.bfloat16)
        lasts.append(joined[:, main:])
    out_ref[:own_rows, 2 * main :] = jnp.concatenate(lasts, axis=1).astype(jnp.bfloat16)
    down.wait()
    out_ref[own_rows:, : rows.shape[1]] = rows[...]
    out_ref[own_rows:, rows.shape[1] :] = jnp.zeros_like(out_ref[own_rows:, rows.shape[1] :])


def head_linear_kernel(
    meta_ref, first_ref, second_ref, weight_ref, gain_ref, *refs
):
    hidden_ref, linear_ref = refs[-2:]
    rows = first_ref.shape[0]
    hidden_ref[:rows, :] = first_ref[...]
    hidden_ref[rows:, :] = second_ref[...]

    def step(index, carry):
        part = pl.ds(aligned(index * rows, rows), rows)
        values = wide(hidden_ref[part, :])
        scale = lax.rsqrt(jnp.mean(values * values, axis=1, keepdims=True) + EPSILON)
        hidden_ref[part, :] = (values * scale * gain_ref[...]).astype(jnp.bfloat16)
        linear_ref[part, :] = dot_nn(hidden_ref[part, :], weight_ref[...])
        return carry

    lax.fori_loop(0, 2, step, 0)


def attention_kernel(
    tokens, count, docs,
    meta_ref, lin_ref, cos_ref, sin_ref, gains_ref,
    query_ref, key_ref, value_ref, attn_ref, lse_ref, *refs,
):
    low_refs, (value_t, accum, low, blocks_ref) = refs[:count], refs[count:]
    blocks_ref[...] = head_blocks()
    here = meta_ref[0]
    half = tokens // 2
    size = tokens
    blocks = count

    def prepare(place, carry):
        first, low_lane = lane_masks(half)
        source = aligned(row_of(place, here, tokens, count), half)
        target = aligned(place * half, half)
        cosine = cos_ref[pl.ds(target, half), :]
        sine = sin_ref[pl.ds(target, half), :]
        query = lin_ref[pl.ds(source, half), : 2 * HD]
        unit = query * lax.rsqrt(head_mean(query * query, blocks_ref[...]) + EPSILON) * gains_ref[2:3, :]
        turned = unit * cosine + swap_half(unit, low_lane) * sine
        query_ref[pl.ds(target, half), :] = (
            turned.astype(jnp.bfloat16).astype(jnp.float32) * (HD**-0.5)
        ).astype(jnp.bfloat16)
        both = lin_ref[pl.ds(source, half), 2 * HD :]
        unit = both * lax.rsqrt(head_mean(both * both, blocks_ref[...]) + EPSILON) * gains_ref[3:4, :]
        turned = unit * cosine + swap_half(unit, low_lane) * sine
        key_ref[pl.ds(target, half), :] = jnp.where(
            first, turned, pltpu.roll(turned, HD, 1)
        ).astype(jnp.bfloat16)
        values = jnp.where(first, pltpu.roll(both, HD, 1), both)
        value_ref[pl.ds(target, half), :] = values.astype(jnp.bfloat16)
        return carry

    lax.fori_loop(0, 2 * count, prepare, 0)

    def turn_values(block, carry):
        values = wide(value_ref[pl.ds(aligned(block * size, size), size), :])
        value_t[block, :HD, :] = values.T[:HD].astype(jnp.bfloat16)
        value_t[block, HD:, :] = jnp.ones((value_t.shape[1] - HD, size), jnp.bfloat16)
        return carry

    lax.fori_loop(0, blocks, turn_values, 0)

    def query_step(block, carry):
        query = two_heads(query_ref[pl.ds(aligned(block * size, size), size), :])
        accum[...] = jnp.zeros_like(accum)
        lowest = begin_at(meta_ref, docs, block * size) // size

        def key_step(other, carry):
            keys = key_ref[pl.ds(aligned(other * size, size), size), :]
            scores = dot_nt(keys, query)
            visible = block_visible(meta_ref, docs, block, other, size)
            probable = jnp.concatenate(
                [
                    jnp.where(visible, jnp.exp(scores[:, :size]), 0.0),
                    jnp.where(visible, jnp.exp(scores[:, size:]), 0.0),
                ],
                axis=1,
            ).astype(jnp.bfloat16)
            accum[...] += dot_nn(value_t[other], probable)
            return carry

        lax.fori_loop(lowest, block + 1, key_step, 0)
        mass = accum[HD : HD + 1, :]
        mixed = accum[:HD, :] / mass
        lse_ref[block] = jnp.log(mass)
        rows = jnp.concatenate([mixed[:, :size], mixed[:, size:]], axis=0).T
        attn_ref[pl.ds(aligned(block * size, size), size), :] = rows
        for part in range(2):
            target = aligned(row_of(2 * block + part, here, tokens, count), half)
            low[pl.ds(target, half), :] = rows[part * half : (part + 1) * half].astype(jnp.bfloat16)
        return carry

    lax.fori_loop(0, blocks, query_step, 0)
    for slot, bits in enumerate(ORDER):
        low_refs[bits][...] = low[slot * tokens : (slot + 1) * tokens, :]


def attention_back_kernel(
    tokens, count, docs,
    meta_ref, lin_ref, cos_ref, sin_ref, gains_ref,
    query_ref, key_ref, value_ref, attn_ref, lse_ref, *refs,
):
    grad_refs = refs[:count]
    out_ref, gain_ref = refs[count : count + 2]
    block_refs = refs[count + 2 : 2 * count + 2]
    key_t, grad_query, grad_key, grad_value, accum, grad_rows, blocks_ref = refs[2 * count + 2 :]
    blocks_ref[...] = head_blocks()
    here = meta_ref[0]
    half = tokens // 2
    size = tokens
    blocks = count
    grad_key[...] = jnp.zeros_like(grad_key)
    grad_value[...] = jnp.zeros_like(grad_value)
    gain_ref[...] = jnp.zeros_like(gain_ref)
    for slot, bits in enumerate(ORDER):
        grad_rows[slot * tokens : (slot + 1) * tokens, :] = grad_refs[bits][...]

    def turn_keys(block, carry):
        keys = wide(key_ref[pl.ds(aligned(block * size, size), size), :])
        key_t[block] = keys.T[:HD].astype(jnp.bfloat16)
        return carry

    lax.fori_loop(0, blocks, turn_keys, 0)

    def query_step(block, carry):
        here_rows = pl.ds(aligned(block * size, size), size)
        query = two_heads(query_ref[here_rows, :])
        parts = []
        for part in range(2):
            source = aligned(row_of(2 * block + part, here, tokens, count), half)
            parts.append(grad_rows[pl.ds(source, half), :])
        grads = jnp.concatenate(parts, axis=0)
        products = (wide(grads) * attn_ref[here_rows, :]).T
        deltas = (
            jnp.sum(products[:HD], axis=0, keepdims=True),
            jnp.sum(products[HD:], axis=0, keepdims=True),
        )
        grads = two_heads(grads)
        lse = lse_ref[block]
        accum[...] = jnp.zeros_like(accum)
        lowest = begin_at(meta_ref, docs, block * size) // size

        def key_step(other, carry):
            rows = pl.ds(aligned(other * size, size), size)
            scores = dot_nt(key_ref[rows, :], query)
            grad_prob = dot_nt(value_ref[rows, :], grads)
            visible = block_visible(meta_ref, docs, block, other, size)
            probs, grad_scores = [], []
            for head in range(2):
                cols = slice(head * size, (head + 1) * size)
                prob = jnp.where(visible, jnp.exp(scores[:, cols] - lse[:, cols]), 0.0)
                probs.append(prob)
                grad_scores.append(prob * (grad_prob[:, cols] - deltas[head]))
            probs = jnp.concatenate(probs, axis=1).astype(jnp.bfloat16)
            grad_scores = jnp.concatenate(grad_scores, axis=1).astype(jnp.bfloat16)
            grad_value[rows, :] += dot_nn(probs, grads)
            grad_key[rows, :] += dot_nn(grad_scores, query)
            accum[...] += dot_nn(key_t[other], grad_scores)
            return carry

        lax.fori_loop(lowest, block + 1, key_step, 0)
        total = accum[...] * (HD**-0.5)
        grad_query[here_rows, :] = jnp.concatenate([total[:, :size], total[:, size:]], axis=0).T
        return carry

    lax.fori_loop(0, blocks, query_step, 0)

    def finish(place, carry):
        first, low_lane = lane_masks(half)
        source = aligned(row_of(place, here, tokens, count), half)
        target = pl.ds(aligned(place * half, half), half)
        cosine = cos_ref[target, :]
        sine = sin_ref[target, :]

        def through(linear, grads, gain):
            scale = lax.rsqrt(head_mean(linear * linear, blocks_ref[...]) + EPSILON)
            normed = linear * scale
            turned = grads * cosine + swap_half(grads * sine, low_lane)
            weighted = turned * gain
            grad_in = scale * (weighted - normed * head_mean(weighted * normed, blocks_ref[...]))
            return grad_in, jnp.sum(turned * normed, axis=0, keepdims=True)

        grad_in, gain_row = through(
            lin_ref[pl.ds(source, half), : 2 * HD], grad_query[target, :], gains_ref[2:3, :]
        )
        out_ref[pl.ds(source, half), : 2 * HD] = grad_in.astype(jnp.bfloat16)
        gain_ref[0:1, :] += gain_row
        keys = grad_key[target, :]
        grad_in, gain_row = through(
            lin_ref[pl.ds(source, half), 2 * HD :], keys + pltpu.roll(keys, HD, 1), gains_ref[3:4, :]
        )
        gain_ref[1:2, :] += gain_row
        values = grad_value[target, :]
        values = values + pltpu.roll(values, HD, 1)
        out_ref[pl.ds(source, half), 2 * HD :] = jnp.where(first, grad_in, values).astype(
            jnp.bfloat16
        )
        return carry

    lax.fori_loop(0, 2 * count, finish, 0)
    for slot, bits in enumerate(ORDER):
        block_refs[bits][...] = out_ref[slot * tokens : (slot + 1) * tokens, :]


def proj_grad_kernel(parts, meta_ref, attn_ref, grad_ref, *refs):
    blocks, full = refs[:-1], refs[-1]
    count = len(blocks)
    here = meta_ref[0]
    tile = 2 * pair_tile(full)

    def outer(index, carry):
        part = pl.ds(aligned(index * tile, tile), tile)
        full[part, :] = contract_rows(attn_ref[:, part], grad_ref[...]).astype(jnp.bfloat16)
        return carry

    lax.fori_loop(0, full.shape[0] // tile, outer, 0)
    rows = blocks[0].shape[0] // parts
    for bits, block in enumerate(blocks):
        owner = lax.bitwise_xor(here, bits)
        for part in range(parts):
            source = aligned(part * count * rows + owner * rows, rows)
            block[part * rows : (part + 1) * rows, :] = full[pl.ds(source, rows), :]


def head_grads_kernel(meta_ref, hidden_ref, grad_ref, weight_ref, out_ref, mixer_ref, total):
    step = pl.program_id(0)
    tile = weight_ref.shape[1]

    @pl.when(step == 0)
    def _():
        total[...] = jnp.zeros_like(total)
        mixer_ref[...] = jnp.zeros_like(mixer_ref)

    def part(index, carry):
        rows = pl.ds(aligned(index * tile, tile), tile)
        hidden = hidden_ref[:, rows]
        total[rows, :] += contract_rows(hidden, grad_ref[...])
        back = dot_nt(grad_ref[...], weight_ref[rows, :])
        mixer_ref[:, rows] += jnp.sum(back * wide(hidden), axis=0, keepdims=True)
        return carry

    lax.fori_loop(0, total.shape[0] // tile, part, 0)

    @pl.when(step == pl.num_programs(0) - 1)
    def _():
        out_ref[...] = total[...].astype(jnp.bfloat16)


def pack_heads_kernel(
    extra, meta_ref, heads_ref, mixer_ref, gain_ref, feed_ref, sums_ref, *refs
):
    proj_refs, pieces = refs[:5], refs[5:]
    shard = meta_ref[1]
    rows = heads_ref.shape[0] // 4
    pair = 2 * HD
    proj = wide(proj_refs[0][...])
    for other in proj_refs[1:]:
        proj = proj + wide(other[...])
    proj_low, mixer, _, gains = pieces[4:]
    pieces = pieces[:4]
    part = proj.shape[0] // 4
    proj_low[...] = proj.astype(jnp.bfloat16)
    mixer[...] = mixer_ref[...] / gain_ref[...]
    values = sums_ref[...]
    lower = lax.broadcasted_iota(jnp.int32, values.shape, 0) == 0
    values = values + jnp.where(lower, pltpu.roll(values, HD, 1), 0.0)
    each = HD // 4
    lanes = lax.broadcasted_iota(jnp.int32, values.shape, 1)
    for bits, piece in enumerate(pieces):
        owner = lax.bitwise_xor(shard, bits)
        piece[:rows, :] = heads_ref[pl.ds(aligned(owner * rows, rows), rows), :]
        gains[...] = jnp.zeros_like(gains)
        own = pl.ds(aligned(owner * rows, rows), rows)
        gains[0:1, :] = mixer[:, own]
        gains[1:2, :] = feed_ref[:, own]
        moved = pltpu.roll(values, pair - owner * each, 1)
        moved = jnp.where(lanes < each, moved, 0.0)
        gains[2:4, :pair] = moved[0:2, :]
        piece[rows : rows + extra, :] = gains[...].astype(jnp.bfloat16)
        for index in range(proj.shape[1] // (2 * pair)):
            target = rows + extra + index * part
            piece[target : target + part, :] = proj_low[
                pl.ds(aligned(owner * part, part), part), index * 2 * pair : (index + 1) * 2 * pair
            ]


def pack_feed_kernel(meta_ref, wide_ref, down_ref, *pieces):
    shard = meta_ref[1]
    rows = wide_ref.shape[0] // 4
    inner = pieces[0].shape[0] - rows
    width = down_ref.shape[1]
    for bits, piece in enumerate(pieces):
        owner = lax.bitwise_xor(shard, bits)
        piece[:rows, :] = wide_ref[pl.ds(aligned(owner * rows, 16), rows), :]
        piece[rows:, :width] = down_ref[pl.ds(aligned(owner * inner, 16), inner), :]
        piece[rows:, width:] = jnp.zeros_like(piece[rows:, width:])


def input_grad_kernel(count, meta_ref, *refs):
    grads, weights = refs[:count], refs[count : 2 * count]
    input_ref, grad_ref, gain_ref, out_ref = refs[2 * count :]
    total = dot_nt(grads[0][...], weights[0][...])
    for left, right in zip(grads[1:], weights[1:]):
        total = total + dot_nt(left[...], right[...])
    values = wide(input_ref[...])
    scale = lax.rsqrt(jnp.mean(values * values, axis=1, keepdims=True) + EPSILON)
    normed = values * scale
    weighted = total * gain_ref[...]
    grad_in = scale * (weighted - normed * jnp.mean(weighted * normed, axis=1, keepdims=True))
    out_ref[...] = grad_ref[...] + grad_in


def project_kernel(count, parts, start, meta_ref, *refs):
    attn_refs, weight_refs, rest = refs[:count], refs[count : 2 * count], refs[2 * count :]
    input_ref, gain_ref, full_ref, attn_out_ref, mixed_ref, hidden_ref, _ = rest
    here = meta_ref[0]
    total = weight_refs[0].shape[0] - start
    rows = total // parts
    for bits in range(count):
        owner = lax.bitwise_xor(here, bits)
        for part in range(parts):
            target = aligned(part * count * rows + owner * rows, rows)
            source = start + part * rows
            full_ref[pl.ds(target, rows), :] = weight_refs[bits][source : source + rows, :]
        attn_out_ref[:, pl.ds(aligned(owner * 2 * HD, 2 * HD), 2 * HD)] = attn_refs[bits][...]
    tile = 2 * pair_tile(full_ref)

    def project(index, carry):
        part = pl.ds(aligned(index * tile, tile), tile)
        mixed_ref[:, part] = wide(input_ref[:, part]) + dot_nn(attn_out_ref[...], full_ref[:, part])
        return carry

    lax.fori_loop(0, full_ref.shape[1] // tile, project, 0)
    mixed = mixed_ref[...]
    scale = lax.rsqrt(jnp.mean(mixed * mixed, axis=1, keepdims=True) + EPSILON)
    hidden_ref[...] = (mixed * scale * gain_ref[...]).astype(jnp.bfloat16)


def feed_block(hidden_ref, grad_ref, wide_ref, down_ref, act_ref, grad_wide_ref, out_ref, back_ref):
    tokens = hidden_ref.shape[0]
    inner = wide_ref.shape[1] // 2
    main = inner // 128 * 128
    first, _ = lane_masks(tokens)

    def activate(gate, up, grad_act):
        sigmoid = 1.0 / (1.0 + jnp.exp(-gate))
        silu = gate * sigmoid
        grad_gate = grad_act * up * sigmoid * (1.0 + gate * (1.0 - sigmoid))
        return silu * up, grad_gate, grad_act * silu

    both = dot_nn(hidden_ref[...], wide_ref[...])
    grad_act = dot_nt(grad_ref[...], down_ref[...])
    act, grad_gate, grad_up = activate(
        both[:, :main], both[:, main : 2 * main], grad_act[:, :main]
    )
    act_ref[:, :main] = act.astype(jnp.bfloat16)
    grad_wide_ref[:, :main] = grad_gate.astype(jnp.bfloat16)
    grad_wide_ref[:, main : 2 * main] = grad_up.astype(jnp.bfloat16)
    last = both[:, 2 * main :]
    act, grad_gate, grad_up = activate(last, pltpu.roll(last, HD, 1), grad_act[:, main:])
    act_ref[:, main:] = jnp.where(first, act, 0.0).astype(jnp.bfloat16)
    grad_wide_ref[:, 2 * main :] = jnp.where(
        first, grad_gate, pltpu.roll(grad_up, HD, 1)
    ).astype(jnp.bfloat16)
    back_ref[...] = dot_nt(grad_wide_ref[...], wide_ref[...]).astype(jnp.bfloat16)
    out_ref[...] = dot_nn(act_ref[...], down_ref[...]).astype(jnp.bfloat16)


def feed_kernel(number, meta_ref, *refs):
    firsts, grads, pieces = refs[:number], refs[number : 2 * number], refs[2 * number : 2 * number + 5]
    refs = refs[2 * number + 5 :]
    act_ref, grad_wide_ref, hidden_all, grad_all = refs[:4]
    out_refs, back_refs = refs[4 : 4 + number], refs[4 + number : 4 + 2 * number]
    hidden, grad, out_low, back_low, wide_ref, down_ref, joined = refs[4 + 2 * number :][:7]
    in_sem, grad_sem, all_sem, grad_all_sem, out_sem, back_sem, piece_sem = refs[11 + 2 * number :]
    tokens, width = hidden.shape[1:]
    shard = meta_ref[1]
    rows = wide_ref.shape[0] // 4
    inner = joined.shape[1] - rows
    step = pl.program_id(0)

    def moves(index):
        filed = pl.ds(index * tokens, tokens)
        return (
            pltpu.make_async_copy(firsts[index], hidden.at[index], in_sem.at[index]),
            pltpu.make_async_copy(
                grads[index].at[pl.ds(0, tokens), :], grad.at[index], grad_sem.at[index]
            ),
            pltpu.make_async_copy(hidden.at[index], hidden_all.at[filed, :], all_sem.at[index]),
            pltpu.make_async_copy(grad.at[index], grad_all.at[filed, :], grad_all_sem.at[index]),
            pltpu.make_async_copy(out_low.at[index], out_refs[index], out_sem.at[index]),
            pltpu.make_async_copy(back_low.at[index], back_refs[index], back_sem.at[index]),
        )

    def places(bits):
        owner = lax.bitwise_xor(shard, bits)
        return (
            pl.ds(aligned(owner * rows, rows), rows),
            pl.ds(aligned(owner * inner, 16), inner),
        )

    @pl.when(step == 0)
    def _():
        copies = []
        for bits in range(3):
            upper, lower = places(bits)
            copies.append(
                pltpu.make_async_copy(
                    pieces[bits].at[pl.ds(0, rows), :], wide_ref.at[upper, :], piece_sem.at[2 * bits]
                )
            )
            copies.append(
                pltpu.make_async_copy(
                    pieces[bits].at[pl.ds(rows, inner), pl.ds(0, width)],
                    down_ref.at[lower, :],
                    piece_sem.at[2 * bits + 1],
                )
            )
        for index in range(2):
            copies.append(
                pltpu.make_async_copy(pieces[3 + index], joined.at[index], piece_sem.at[6 + index])
            )
        for copy in copies:
            copy.start()
        for index in range(number):
            for move in moves(index)[:2]:
                move.start()
        down_ref[4 * inner :, :] = jnp.zeros_like(down_ref[4 * inner :, :])
        for copy in copies:
            copy.wait()
        upper, lower = places(3)
        wide_ref[upper, :] = joined[0, :rows, :] + joined[1, :rows, :]
        down_ref[lower, :] = joined[0, rows:, :width] + joined[1, rows:, :width]

    for index in range(number):

        @pl.when(step == index)
        def _(index=index):
            for move in moves(index)[:2]:
                move.wait()
            for move in moves(index)[2:4]:
                move.start()

    feed_block(
        hidden.at[step], grad.at[step], wide_ref, down_ref,
        act_ref, grad_wide_ref, out_low.at[step], back_low.at[step],
    )

    for index in range(number):

        @pl.when(step == index)
        def _(index=index):
            for move in moves(index)[4:]:
                move.start()

    @pl.when(step == number - 1)
    def _():
        for index in range(number):
            for move in moves(index)[2:]:
                move.wait()


def feed_call(meta, hidden, grads, pieces, padded, grant):
    number = len(hidden)
    tokens, width = hidden[0].shape
    rows, inner = pieces[0].shape
    low = jnp.bfloat16
    outs = [shaped((number * tokens, columns)) for columns in (padded, inner, width, width)]
    outs += [shaped((tokens, width))] * (2 * number)
    return pl.pallas_call(
        functools.partial(feed_kernel, number),
        grid=(number,),
        out_shape=outs,
        in_specs=[SCALARS] + [PLACED] * (2 * number + 5),
        out_specs=[
            pl.BlockSpec((tokens, padded), lambda step: (step, 0)),
            pl.BlockSpec((tokens, inner), lambda step: (step, 0)),
        ]
        + [PLACED] * (2 + 2 * number),
        scratch_shapes=[pltpu.VMEM((number, tokens, width), low)] * 4
        + [
            pltpu.VMEM((width, inner), low),
            pltpu.VMEM((padded, width), low),
            pltpu.VMEM((2, rows, inner), low),
        ]
        + [pltpu.SemaphoreType.DMA((number,))] * 6
        + [pltpu.SemaphoreType.DMA((8,))],
        cost_estimate=pl.CostEstimate(
            flops=6 * number * tokens * width * inner,
            bytes_accessed=16 * number * tokens * width,
            transcendentals=0,
        ),
        compiler_params=pltpu.CompilerParams(vmem_limit_bytes=grant * 2**20),
        name="feed",
    )(meta, *hidden, *grads, *pieces)


def feed_back_kernel(count, meta_ref, *refs):
    sums, rest = refs[:5], refs[5:]
    mixed_ref, grad_ref, full_ref, gain_ref, grad_mixed_ref, grad_low_ref, grad_gain_ref = rest[:7]
    block_refs, attn = rest[7 : 7 + count], rest[7 + count]
    here = meta_ref[0]
    grad_hidden = wide(sums[0][...])
    for part in sums[1:]:
        grad_hidden = grad_hidden + wide(part[...])
    mixed = mixed_ref[...]
    scale = lax.rsqrt(jnp.mean(mixed * mixed, axis=1, keepdims=True) + EPSILON)
    normed = mixed * scale
    weighted = grad_hidden * gain_ref[...]
    grad_in = scale * (weighted - normed * jnp.mean(weighted * normed, axis=1, keepdims=True))
    grad_gain_ref[...] = jnp.sum(grad_hidden * normed, axis=0, keepdims=True)
    grad_mixed = wide(grad_ref[...]) + grad_in
    grad_mixed_ref[...] = grad_mixed
    grad_low_ref[...] = grad_mixed.astype(jnp.bfloat16)
    tile = 2 * pair_tile(full_ref)

    def project_back(index, carry):
        part = pl.ds(aligned(index * tile, tile), tile)
        attn[:, part] = dot_nt(grad_low_ref[...], full_ref[part, :]).astype(jnp.bfloat16)
        return carry

    lax.fori_loop(0, full_ref.shape[0] // tile, project_back, 0)
    for bits in range(count):
        owner = lax.bitwise_xor(here, bits)
        block_refs[bits][...] = attn[:, pl.ds(aligned(owner * 2 * HD, 2 * HD), 2 * HD)]


def wide_out_kernel(count, parts, meta_ref, *refs):
    blocks, (gate_ref, up_ref, held) = refs[:count], refs[count:]
    here = meta_ref[0]
    for bits in range(count):
        held[lax.bitwise_xor(here, bits)] = wide(blocks[bits][...])
    inner = held.shape[2] // 2
    main = inner // 128 * 128
    piece = inner // parts
    for kind, out_ref in enumerate((gate_ref, up_ref)):
        for part in range(parts):
            columns = []
            for owner in range(count):
                start, stop = part * piece, (part + 1) * piece
                begin = kind * main
                if start < main:
                    columns.append(held[owner, :, begin + start : begin + min(stop, main)])
                if stop > main:
                    begin = main + kind * (inner - main)
                    columns.append(held[owner, :, begin + max(start, main) : begin + stop])
            out_ref[:, part * count * piece : (part + 1) * count * piece] = jnp.concatenate(
                columns, axis=1
            )


def rows_out_kernel(meta_ref, *refs):
    blocks, out_ref = refs[:-1], refs[-1]
    rows = out_ref.shape[0] // len(blocks)
    start = blocks[0].shape[0] - rows
    for bits, block in enumerate(blocks):
        owner = lax.bitwise_xor(meta_ref[0], bits)
        out_ref[pl.ds(aligned(owner * rows, 16), rows), :] = wide(
            block[start:, : out_ref.shape[1]]
        )


def heads_out_kernel(count, own, extra, meta_ref, *refs):
    blocks, rest = refs[:count], refs[count:]
    query_ref, key_ref, value_ref, proj_ref, gain_ref, held = rest
    here = meta_ref[0]
    pair = 2 * HD
    part = (blocks[0].shape[0] - own - extra) // 4
    gains = jnp.zeros(gain_ref.shape, jnp.float32)
    for bits in range(count):
        owner = lax.bitwise_xor(here, bits)
        block = wide(blocks[bits][...])
        query_ref[:, pl.ds(aligned(owner * pair, pair), pair)] = block[:own, :pair]
        held[owner] = block[:own, pair:]
        gains = gains + block[own : own + extra, :]
        for index in range(4):
            source = own + extra + index * part
            proj_ref[
                pl.ds(aligned(owner * part, part), part), index * 2 * pair : (index + 1) * 2 * pair
            ] = block[source : source + part, :]
    gain_ref[...] = gains
    first, _ = lane_masks(own)
    for index in range(count // 2):
        early, late = held[2 * index], held[2 * index + 1]
        lanes = slice(index * pair, (index + 1) * pair)
        key_ref[:, lanes] = jnp.where(first, early, pltpu.roll(late, HD, 1))
        value_ref[:, lanes] = jnp.where(first, pltpu.roll(early, HD, 1), late)


SCALARS = pl.BlockSpec(memory_space=pltpu.SMEM)
WHOLE = pl.BlockSpec(memory_space=pltpu.VMEM)
PLACED = pl.BlockSpec(memory_space=pl.ANY)
FAR = pl.BlockSpec(memory_space=pltpu.HBM)


def shaped(shape, kind=jnp.bfloat16):
    return jax.ShapeDtypeStruct(shape, kind)


def whole_call(kernel, outs, ins, flops, scratch=(), grant=24, specs=None):
    moved = sum(math.prod(out.shape) * out.dtype.itemsize for out in outs)
    return pl.pallas_call(
        kernel,
        out_shape=outs,
        in_specs=[SCALARS] + (specs or [WHOLE] * ins),
        out_specs=[WHOLE] * len(outs),
        scratch_shapes=list(scratch),
        cost_estimate=pl.CostEstimate(
            flops=int(flops), bytes_accessed=int(2 * moved), transcendentals=0
        ),
        compiler_params=pltpu.CompilerParams(vmem_limit_bytes=grant * 2**20),
    )


def rows_call(kernel, arrays, kept, outs, shared, rows, start, steps, flops, scratch=(), grant=24):
    specs = [SCALARS] + [WHOLE] * (len(arrays) - 1) + [PLACED] * len(kept)
    out_specs = [
        pl.BlockSpec((rows, out.shape[1]), lambda step: (start + step, 0)) for out in outs[:shared]
    ] + [WHOLE] * (len(outs) - shared)
    moved = sum(math.prod(out.shape) * out.dtype.itemsize for out in outs)
    return pl.pallas_call(
        kernel,
        grid=(steps,),
        out_shape=outs,
        in_specs=specs,
        out_specs=out_specs,
        scratch_shapes=list(scratch),
        input_output_aliases={len(arrays) + place: place for place in range(len(kept))},
        cost_estimate=pl.CostEstimate(
            flops=int(flops), bytes_accessed=int(moved), transcendentals=0
        ),
        compiler_params=pltpu.CompilerParams(vmem_limit_bytes=grant * 2**20),
    )(*arrays, *kept)


def local_heads(
    block_input, doc_starts, out_grad, query_weight, key_weight, value_weight, output_weight,
    gate_weight, up_weight, down_weight, mixer_gain, feed_gain, query_gain, key_gain,
):
    low = jnp.bfloat16
    tokens, width = block_input.shape[1:]
    count = lax.axis_size("ctx")
    shards = lax.axis_size("fsdp")
    here = lax.axis_index("ctx").astype(jnp.int32)
    shard = lax.axis_index("fsdp").astype(jnp.int32)
    stream = tokens * count
    docs = doc_starts.shape[1]
    pair = 2 * HD
    own_rows = width // shards
    extra = 16
    meta = jnp.concatenate([here[None], shard[None], doc_starts[0].astype(jnp.int32)])
    own_input = block_input[0]
    own_grad = out_grad[0]
    inner = down_weight.shape[0] // count
    wide_inner = inner * shards
    padded = -(-wide_inner // 128) * 128
    proj_rows = own_rows // count
    edges = [(0, 1), (3, 2)]
    middle = [(1, 2), (2, 1)]
    relay = [(1, 0), (2, 3)]

    def near(piece, bits):
        return shift_fsdp(piece, flipped(bits, shards))

    across, along, partner = gather_near(own_input)
    corner = swap_ctx(own_input, 6)
    piece_rows = own_rows + extra + 4 * proj_rows
    head_piece = whole_call(
        take_heads_kernel,
        [shaped((piece_rows, 2 * pair))],
        8,
        0,
        [
            pltpu.VMEM((extra, 2 * pair), jnp.float32),
            pltpu.VMEM((3, own_rows, pair), low),
            pltpu.VMEM((proj_rows, width), low),
            pltpu.SemaphoreType.DMA((4,)),
        ],
        grant=60,
        specs=[FAR] * 4 + [WHOLE] * 4,
    )(
        meta, query_weight, key_weight, value_weight, output_weight,
        mixer_gain[None], feed_gain[None], query_gain[None], key_gain[None],
    )[0]
    head_pieces = [head_piece] + [near(head_piece, bits) for bits in (1, 2, 3)]
    feed_rows = own_rows + inner
    feed_piece = whole_call(
        functools.partial(take_wide_kernel, shards),
        [shaped((feed_rows, 2 * wide_inner))],
        3,
        2 * own_rows * 2 * wide_inner * 2048,
        [
            pltpu.VMEM((2 * shards, own_rows, 256), low),
            pltpu.SemaphoreType.DMA((2 * shards,)),
            pltpu.VMEM((inner, width), low),
            pltpu.SemaphoreType.DMA(()),
        ],
        grant=60,
        specs=[FAR] * 3,
    )(behind(meta, head_piece), gate_weight, up_weight, down_weight)[0]
    feed_near = near(feed_piece, 1)
    feed_far = near(behind(feed_piece, *head_pieces[1:]), 2)
    others = gather_far(across, along, corner)
    input_blocks = [own_input, partner, across, others[0], along, others[1], corner, others[2]]

    where_at = jnp.arange(stream, dtype=jnp.int32)
    begins = doc_begin(doc_starts[0], where_at)
    lanes = jnp.arange(pair) % (HD // 2)
    frequency = ROPE_BASE ** (-(2.0 * lanes.astype(jnp.float32)) / HD)
    angles = (where_at - begins).astype(jnp.float32)[:, None] * frequency[None, :]
    cosine = jnp.cos(angles)
    sine = jnp.sin(angles) * jnp.where(jnp.arange(pair) % HD < HD // 2, -1.0, 1.0)[None, :]

    heads_weight, gain_mixer, gain_feed, gain_heads, proj_part = whole_call(
        functools.partial(arrange_heads_kernel, extra),
        [
            shaped((width, 2 * pair)),
            shaped((1, width), jnp.float32),
            shaped((1, width), jnp.float32),
            shaped((8, pair), jnp.float32),
            shaped((shards * proj_rows, width)),
        ],
        4,
        0,
        grant=8,
    )(behind(meta, cosine, sine), *head_pieces)

    kept = []
    for index in range(4):
        kept = rows_call(
            head_linear_kernel,
            [meta]
            + [input_blocks[bits] for bits in ORDER[2 * index : 2 * index + 2]]
            + [heads_weight, gain_mixer],
            kept,
            [shaped((stream, width)), shaped((stream, 2 * pair), jnp.float32)],
            2,
            2 * tokens,
            index,
            1,
            4 * tokens * width * 2 * pair,
            grant=6,
        )
    hidden_in, linear = kept

    pairs = stream * stream // 2
    extra_piece = behind(jnp.concatenate([own_grad, proj_part], axis=0), corner)
    extra_across, extra_along, extra_partner = gather_near(extra_piece)
    extra_corner = swap_ctx(extra_piece, 6)
    query_att, key_att, value_att, attn, lse, *attn_low = whole_call(
        functools.partial(attention_kernel, tokens, count, docs),
        [
            shaped((stream, pair)),
            shaped((stream, pair)),
            shaped((stream, pair)),
            shaped((stream, pair), jnp.float32),
            shaped((count, 1, 2 * tokens), jnp.float32),
        ]
        + [shaped((tokens, pair))] * count,
        4,
        8 * pairs * HD,
        [
            pltpu.VMEM((count, HD + 16, tokens), low),
            pltpu.VMEM((HD + 16, 2 * tokens), jnp.float32),
            pltpu.VMEM((stream, pair), low),
            pltpu.VMEM((pair, pair), low),
        ],
        grant=10,
    )(meta, linear, cosine, sine, gain_heads)

    attn_blocks = exchange_plane(attn_low)
    feed_middle = shift_fsdp(behind(feed_piece, attn_blocks[1]), middle)
    feed_relay = shift_fsdp(behind(feed_far, attn_blocks[1]), relay)
    extra_others = gather_far(extra_across, extra_along, extra_corner, attn_blocks[1])
    extra_blocks = [
        extra_piece, extra_partner, extra_across, extra_others[0],
        extra_along, extra_others[1], extra_corner, extra_others[2],
    ]
    full_proj, attn_rows, mixed, hidden_mid = whole_call(
        functools.partial(project_kernel, count, shards, tokens),
        [
            shaped((width, width)),
            shaped((tokens, width)),
            shaped((tokens, width), jnp.float32),
            shaped((tokens, width)),
        ],
        2 * count + 2,
        2 * tokens * width * width,
        [pltpu.VMEM((tokens, width), low)],
        grant=8,
    )(meta, *attn_blocks, *extra_blocks, own_input, gain_feed)

    hidden_across, hidden_along, hidden_partner = gather_near(hidden_mid)
    hidden_corner = swap_ctx(hidden_mid, 6)
    hidden_far = gather_far(hidden_across, hidden_along, hidden_corner)
    hidden_blocks = [
        hidden_mid, hidden_partner, hidden_across, hidden_far[0],
        hidden_along, hidden_far[1], hidden_corner, hidden_far[2],
    ]
    weight_piece = behind(heads_weight, hidden_far[2])
    weight_near = gather_near(weight_piece)
    weight_corner = swap_ctx(weight_piece, 6)
    act_all, grad_wide_all, hidden_all, grad_all, *parts = feed_call(
        meta,
        hidden_blocks,
        extra_blocks,
        (feed_piece, feed_near, feed_far, feed_middle, feed_relay),
        padded,
        60,
    )
    out_parts, back_parts = parts[:count], parts[count:]
    back_own, back_pairs = scatter_pair(back_parts)
    back_sums = back_own + scatter_links(back_pairs)

    def scatter_early(pieces):
        return shift_fsdp(pieces[3], edges), shift_fsdp(pieces[3], middle)

    def scatter_late(pieces, early, *ready):
        second = behind((wide(pieces[2]) + wide(early)).astype(low), *ready)
        return near(second, 2), near(behind(pieces[1], *ready), 1)

    grad_down = contract_rows(behind(act_all, *back_pairs), grad_all).astype(low)
    grad_wide = contract_rows(behind(hidden_all, grad_down), grad_wide_all).astype(low)
    feed_pieces = whole_call(
        pack_feed_kernel, [shaped((feed_rows, 2 * wide_inner))] * shards, 2, 0, grant=10
    )(meta, grad_wide, grad_down)
    wide_edge, wide_middle = scatter_early(feed_pieces)
    out_own, out_pairs = scatter_pair([behind(part, grad_wide) for part in out_parts])

    grad_mixed, grad_mixed_low, grad_feed, *grad_blocks = whole_call(
        functools.partial(feed_back_kernel, count),
        [
            shaped((tokens, width), jnp.float32),
            shaped((tokens, width)),
            shaped((1, width), jnp.float32),
        ]
        + [shaped((tokens, pair))] * count,
        9,
        2 * tokens * width * width,
        [pltpu.VMEM((tokens, width), low)],
        grant=8,
    )(meta, *back_sums, mixed, own_grad, full_proj, gain_feed)
    grad_attn = exchange_plane(grad_blocks)
    wide_late = scatter_late(feed_pieces, wide_edge, grad_blocks[0])
    proj_blocks = whole_call(
        functools.partial(proj_grad_kernel, shards),
        [shaped((shards * proj_rows, width))] * count,
        2,
        2 * tokens * width * width,
        [pltpu.VMEM((width, width), low)],
        grant=8,
    )(meta, attn_rows, grad_mixed_low)
    proj_own, proj_pairs = scatter_pair(proj_blocks)
    proj_parts = proj_own + scatter_links(proj_pairs)
    out_sums = out_own + scatter_links([behind(part, grad_blocks[0]) for part in out_pairs])

    back_outs = whole_call(
        functools.partial(attention_back_kernel, tokens, count, docs),
        [shaped((stream, 2 * pair)), shaped((8, pair), jnp.float32)]
        + [shaped((tokens, 2 * pair))] * count,
        9 + count,
        20 * pairs * HD,
        [
            pltpu.VMEM((count, HD, tokens), low),
            pltpu.VMEM((stream, pair), jnp.float32),
            pltpu.VMEM((stream, pair), jnp.float32),
            pltpu.VMEM((stream, pair), jnp.float32),
            pltpu.VMEM((HD, 2 * tokens), jnp.float32),
            pltpu.VMEM((stream, pair), low),
            pltpu.VMEM((pair, pair), low),
        ],
        grant=14,
    )(meta, linear, cosine, sine, gain_heads, query_att, key_att, value_att, attn, lse, *grad_attn)
    grad_linear, gain_sums, *token_blocks = back_outs

    token_grads = exchange_plane(token_blocks)
    weight_far = gather_far(weight_near[0], weight_near[1], weight_corner, token_grads[1])
    weight_all = [
        weight_piece, weight_near[2], weight_near[0], weight_far[0],
        weight_near[1], weight_far[1], weight_corner, weight_far[2],
    ]
    grad_heads, grad_mixer = pl.pallas_call(
        head_grads_kernel,
        grid=(4,),
        in_specs=[
            SCALARS,
            pl.BlockSpec((stream // 4, width), lambda step: (step, 0)),
            pl.BlockSpec((stream // 4, 2 * pair), lambda step: (step, 0)),
            pl.BlockSpec((width, 2 * pair), lambda step: (0, 0)),
        ],
        out_specs=[
            pl.BlockSpec((width, 2 * pair), lambda step: (0, 0)),
            pl.BlockSpec((1, width), lambda step: (0, 0)),
        ],
        out_shape=[shaped((width, 2 * pair)), shaped((1, width), jnp.float32)],
        scratch_shapes=[pltpu.VMEM((width, 2 * pair), jnp.float32)],
        cost_estimate=pl.CostEstimate(
            flops=8 * stream * width * pair, bytes_accessed=3 * stream * width, transcendentals=0
        ),
        compiler_params=pltpu.CompilerParams(vmem_limit_bytes=16 * 2**20),
        name="head_grads",
    )(behind(meta, token_grads[1]), hidden_in, grad_linear, heads_weight)
    packed = whole_call(
        functools.partial(pack_heads_kernel, extra),
        [shaped((piece_rows, 2 * pair))] * shards,
        10,
        0,
        [
            pltpu.VMEM((shards * proj_rows, width), low),
            pltpu.VMEM((1, width), jnp.float32),
            pltpu.VMEM((8, pair), jnp.float32),
            pltpu.VMEM((extra, 2 * pair), jnp.float32),
        ],
        grant=6,
    )(meta, grad_heads, grad_mixer, gain_mixer, grad_feed, gain_sums, *proj_parts)
    heads_sent = [near(packed[bits], bits) for bits in (1, 2, 3)]

    def total_of(first, *parts):
        return sum([wide(part) for part in parts], wide(first)).astype(low)

    def total_late(pieces, parts, *ready):
        return total_of(pieces[0], *[behind(part, *ready) for part in parts])

    wide_total = total_late(feed_pieces, (wide_middle,) + wide_late, grad_linear)
    wide_blocks = gather_plane(wide_total)
    input_grad = whole_call(
        functools.partial(input_grad_kernel, count),
        [shaped((tokens, width), jnp.float32)],
        2 * count + 3,
        2 * tokens * width * 2 * width,
        grant=10,
    )(meta, *token_grads, *weight_all, own_input, grad_mixed, gain_mixer)[0]
    heads_total = total_of(packed[0], *heads_sent)
    heads_blocks = gather_direct(heads_total)
    block_output = (
        mixed + sum(wide(behind(part, packed[0])) for part in out_sums)
    ).astype(low)

    out_down = whole_call(
        rows_out_kernel, [shaped((count * inner, width), jnp.float32)], count, 0
    )(meta, *wide_blocks)[0]
    tile = own_rows // 4
    out_gate, out_up = pl.pallas_call(
        functools.partial(wide_out_kernel, count, shards),
        grid=(4,),
        in_specs=[SCALARS]
        + [pl.BlockSpec((tile, 2 * wide_inner), lambda step: (step, 0))] * count,
        out_specs=[pl.BlockSpec((tile, wide_inner * count), lambda step: (step, 0))] * 2,
        out_shape=[shaped((own_rows, wide_inner * count), jnp.float32)] * 2,
        scratch_shapes=[pltpu.VMEM((count, tile, 2 * wide_inner), jnp.float32)],
        compiler_params=pltpu.CompilerParams(vmem_limit_bytes=24 * 2**20),
        name="wide_out",
    )(meta, *wide_blocks)
    out_query, out_key, out_value, out_proj, gain_out = whole_call(
        functools.partial(heads_out_kernel, count, own_rows, extra),
        [
            shaped((own_rows, width), jnp.float32),
            shaped((own_rows, KVH * HD), jnp.float32),
            shaped((own_rows, KVH * HD), jnp.float32),
            shaped((own_rows, width), jnp.float32),
            shaped((extra, 2 * pair), jnp.float32),
        ],
        count,
        0,
        [pltpu.VMEM((count, own_rows, pair), jnp.float32)],
    )(meta, *heads_blocks)
    return (
        block_output[None],
        input_grad[None],
        out_query,
        out_key,
        out_value,
        out_proj,
        out_gate,
        out_up,
        out_down,
        gain_out[0],
        gain_out[1],
        gain_out[2, : query_gain.shape[0]],
        gain_out[3, : key_gain.shape[0]],
    )


def divides_heads(mesh):
    return mesh.shape["ctx"] == KVH and mesh.shape["fsdp"] == 4 and H == 2 * KVH


def solution(mesh):
    in_specs = (
        P("fsdp", "ctx", None),
        P("fsdp", None),
        P("fsdp", "ctx", None),
        P("fsdp", None),
        P("fsdp", None),
        P("fsdp", None),
        P("fsdp", None),
        P("fsdp", None),
        P("fsdp", None),
        P("fsdp", None),
        P("fsdp"),
        P("fsdp"),
        P("fsdp"),
        P("fsdp"),
    )
    out_specs = (
        P("fsdp", "ctx", None),
        P("fsdp", "ctx", None),
        P("fsdp", None),
        P("fsdp", None),
        P("fsdp", None),
        P("fsdp", None),
        P("fsdp", None),
        P("fsdp", None),
        P("fsdp", None),
        P("fsdp"),
        P("fsdp"),
        P("fsdp"),
        P("fsdp"),
    )
    if not divides_heads(mesh):
        return jax.shard_map(
            local, mesh=mesh, in_specs=in_specs, out_specs=out_specs, check_vma=False
        )

    return jax.shard_map(local_heads, mesh=mesh, in_specs=in_specs, out_specs=out_specs, check_vma=False)
```

```python
import functools
import math

import jax
import jax.numpy as jnp
from jax import lax
from jax.experimental import pallas as pl
from jax.experimental.pallas import tpu as pltpu
from jax.sharding import PartitionSpec as P

H = 16
KVH = 8
HD = 64


EPSILON = 1e-05
ROPE_BASE = 1000000.0
FLOOR_SCORE = -1e30


def place_rows(row_index, tokens, ctx_count):
    half_rows = tokens // 2
    device = row_index // tokens
    offset = row_index % tokens
    early = device * half_rows + offset
    late = (2 * ctx_count - 1 - device) * half_rows + offset - half_rows
    return jnp.where(offset < half_rows, early, late)


def doc_begin(starts, where_at):
    started = starts[None, :] <= where_at[:, None]
    return jnp.max(jnp.where(started, starts[None, :], 0), axis=1)


def rotary(positions):
    half_dim = HD // 2
    frequency = ROPE_BASE ** (-(2.0 * jnp.arange(half_dim, dtype=jnp.float32)) / HD)
    angles = positions.astype(jnp.float32)[:, None] * frequency[None, :]
    angles = jnp.concatenate([angles, angles], axis=1)
    return (jnp.cos(angles)[:, None, :], jnp.sin(angles)[:, None, :])


def rotate_pairs(values, cosine, sine_part):
    half_dim = values.shape[-1] // 2
    rolled = jnp.concatenate([-values[..., half_dim:], values[..., :half_dim]], axis=-1)
    return values * cosine + rolled * sine_part


def rotate_back(grads, cosine, sine_part):
    half_dim = grads.shape[-1] // 2
    moved = grads * sine_part
    rolled = jnp.concatenate([moved[..., half_dim:], -moved[..., :half_dim]], axis=-1)
    return grads * cosine + rolled


def unit_norm(values):
    scaling = lax.rsqrt(jnp.mean(values * values, axis=-1, keepdims=True) + EPSILON)
    return (values * scaling, scaling)


def norm_back(grad_out, normed, scaling, gain_row):
    weighted = grad_out * gain_row
    grad_in = scaling * (weighted - normed * jnp.mean(weighted * normed, axis=-1, keepdims=True))
    grad_gain = jnp.sum((grad_out * normed).reshape(-1, normed.shape[-1]), axis=0)
    return (grad_in, grad_gain)


def score_block(query_rows, key_rows, scaling):
    return (
        jnp.einsum("igrd,jgd->grij", query_rows, key_rows, preferred_element_type=jnp.float32)
        * scaling
    )


def visible_pairs(query_at, query_doc, key_at, key_doc):
    return (query_doc[:, None] == key_doc[None, :]) & (key_at[None, :] <= query_at[:, None])


def any_visible(query_at, query_doc, key_at):
    return (jnp.min(key_at) <= jnp.max(query_at)) & (jnp.max(key_at) >= jnp.min(query_doc))


def contract_rows(left, right):
    return lax.dot_general(
        left, right, (((0,), (0,)), ((), ())), preferred_element_type=jnp.float32
    )


def contract_cols(left, right):
    return lax.dot_general(
        left, right, (((1,), (1,)), ((), ())), preferred_element_type=jnp.float32
    )


def keep_same(totals):
    return totals


def local(
    block_input,
    doc_starts,
    out_grad,
    query_weight,
    key_weight,
    value_weight,
    output_weight,
    gate_weight,
    up_weight,
    down_weight,
    mixer_gain,
    feed_gain,
    query_gain,
    key_gain,
):
    tokens = block_input.shape[1]
    ctx_count = lax.axis_size("ctx")
    repeat = H // KVH
    kv_width = KVH * HD
    scaling = HD ** (-0.5)
    inputs = block_input[0].astype(jnp.float32)
    starts = doc_starts[0]
    where_at = place_rows(
        lax.axis_index("ctx") * tokens + jnp.arange(tokens, dtype=jnp.int32), tokens, ctx_count
    )
    begins = doc_begin(starts, where_at)
    cosine, sine_part = rotary(where_at - begins)
    gathered = (
        lax.all_gather(query_weight, "fsdp", axis=0, tiled=True),
        lax.all_gather(key_weight, "fsdp", axis=0, tiled=True),
        lax.all_gather(value_weight, "fsdp", axis=0, tiled=True),
        lax.all_gather(output_weight, "fsdp", axis=0, tiled=True),
        lax.all_gather(gate_weight, "fsdp", axis=0, tiled=True),
        lax.all_gather(up_weight, "fsdp", axis=0, tiled=True),
        lax.all_gather(down_weight, "fsdp", axis=0, tiled=True),
        lax.all_gather(mixer_gain, "fsdp", axis=0, tiled=True),
        lax.all_gather(feed_gain, "fsdp", axis=0, tiled=True),
        lax.all_gather(query_gain, "fsdp", axis=0, tiled=True),
        lax.all_gather(key_gain, "fsdp", axis=0, tiled=True),
    )
    full_query, full_key, full_value, full_proj, full_gate, full_up, full_down = gathered[:7]
    gain_mixer, gain_feed, gain_query, gain_key = [
        entry.astype(jnp.float32) for entry in gathered[7:]
    ]
    normed_in, scale_in = unit_norm(inputs)
    hidden_in = (normed_in * gain_mixer).astype(jnp.bfloat16)
    query_lin = jnp.dot(hidden_in, full_query, preferred_element_type=jnp.float32)
    key_lin = jnp.dot(hidden_in, full_key, preferred_element_type=jnp.float32)
    value_lin = jnp.dot(hidden_in, full_value, preferred_element_type=jnp.float32)
    query_normed, query_scale = unit_norm(query_lin.reshape(tokens, H, HD))
    key_normed, key_scale = unit_norm(key_lin.reshape(tokens, KVH, HD))
    query_att = (
        rotate_pairs(query_normed * gain_query, cosine, sine_part)
        .reshape(tokens, H * HD)
        .astype(jnp.bfloat16)
    )
    key_att = (
        rotate_pairs(key_normed * gain_key, cosine, sine_part)
        .reshape(tokens, kv_width)
        .astype(jnp.bfloat16)
    )
    value_att = value_lin.astype(jnp.bfloat16)
    query_four = query_att.reshape(tokens, KVH, repeat, HD)
    start_state = (
        jnp.full((KVH, repeat, tokens), FLOOR_SCORE, jnp.float32),
        jnp.zeros((KVH, repeat, tokens), jnp.float32),
        jnp.zeros((tokens, H * HD), jnp.float32),
    )
    key_part = lax.all_gather(key_att, "ctx", axis=0, tiled=True)
    value_part = lax.all_gather(value_att, "ctx", axis=0, tiled=True)
    rows = key_part.shape[0]
    width = math.gcd(math.gcd(rows, tokens // 2), 512)

    def forward_key_block(block_index, totals):
        offset = block_index * width
        key_rows = lax.dynamic_slice_in_dim(key_part, offset, width, 0).reshape(width, KVH, HD)
        value_rows = lax.dynamic_slice_in_dim(value_part, offset, width, 0).reshape(width, KVH, HD)
        key_at = place_rows(offset + jnp.arange(width, dtype=jnp.int32), tokens, ctx_count)

        def attend(totals):
            highest, total_mass, accum = totals
            visible = visible_pairs(where_at, begins, key_at, doc_begin(starts, key_at))
            scores = jnp.where(visible, score_block(query_four, key_rows, scaling), FLOOR_SCORE)
            new_high = jnp.maximum(highest, jnp.max(scores, axis=-1))
            rescale = jnp.exp(highest - new_high)
            probable = jnp.where(visible, jnp.exp(scores - new_high[..., None]), 0.0)
            total_mass = total_mass * rescale + jnp.sum(probable, axis=-1)
            part_out = jnp.einsum(
                "grij,jgd->igrd",
                probable.astype(jnp.bfloat16),
                value_rows,
                preferred_element_type=jnp.float32,
            )
            accum = (
                accum.reshape(tokens, KVH, repeat, HD)
                * jnp.transpose(rescale, (2, 0, 1))[..., None]
                + part_out
            )
            return (new_high, total_mass, accum.reshape(tokens, H * HD))

        return lax.cond(any_visible(where_at, begins, key_at), attend, keep_same, totals)

    highest, total_mass, accum = lax.fori_loop(0, rows // width, forward_key_block, start_state)
    lse_heads = highest + jnp.log(total_mass)
    attn_raw = (
        accum.reshape(tokens, KVH, repeat, HD) / jnp.transpose(total_mass, (2, 0, 1))[..., None]
    ).reshape(tokens, H * HD)
    attn_low = attn_raw.astype(jnp.bfloat16)
    mixed = inputs + jnp.dot(attn_low, full_proj, preferred_element_type=jnp.float32)
    normed_mid, scale_mid = unit_norm(mixed)
    hidden_mid = (normed_mid * gain_feed).astype(jnp.bfloat16)
    gate_lin = jnp.dot(hidden_mid, full_gate, preferred_element_type=jnp.float32)
    up_lin = jnp.dot(hidden_mid, full_up, preferred_element_type=jnp.float32)
    sigmoid_gate = jax.nn.sigmoid(gate_lin)
    activated = (gate_lin * sigmoid_gate * up_lin).astype(jnp.bfloat16)
    block_output = (
        mixed + jnp.dot(activated, full_down, preferred_element_type=jnp.float32)
    ).astype(jnp.bfloat16)
    regathered = (
        lax.all_gather(query_weight, "fsdp", axis=0, tiled=True),
        lax.all_gather(key_weight, "fsdp", axis=0, tiled=True),
        lax.all_gather(value_weight, "fsdp", axis=0, tiled=True),
        lax.all_gather(output_weight, "fsdp", axis=0, tiled=True),
        lax.all_gather(gate_weight, "fsdp", axis=0, tiled=True),
        lax.all_gather(up_weight, "fsdp", axis=0, tiled=True),
        lax.all_gather(down_weight, "fsdp", axis=0, tiled=True),
        lax.all_gather(mixer_gain, "fsdp", axis=0, tiled=True),
        lax.all_gather(feed_gain, "fsdp", axis=0, tiled=True),
        lax.all_gather(query_gain, "fsdp", axis=0, tiled=True),
        lax.all_gather(key_gain, "fsdp", axis=0, tiled=True),
    )
    full_query, full_key, full_value, full_proj, full_gate, full_up, full_down = regathered[:7]
    gain_mixer, gain_feed, gain_query, gain_key = [
        entry.astype(jnp.float32) for entry in regathered[7:]
    ]
    grad_top = out_grad[0].astype(jnp.float32)
    grad_top_low = grad_top.astype(jnp.bfloat16)
    grad_down = contract_rows(activated, grad_top_low)
    grad_act = contract_cols(grad_top_low, full_down)
    grad_gate_low = (
        grad_act * up_lin * sigmoid_gate * (1.0 + gate_lin * (1.0 - sigmoid_gate))
    ).astype(jnp.bfloat16)
    grad_up_low = (grad_act * gate_lin * sigmoid_gate).astype(jnp.bfloat16)
    grad_gate = contract_rows(hidden_mid, grad_gate_low)
    grad_up = contract_rows(hidden_mid, grad_up_low)
    grad_hidden_mid = contract_cols(grad_gate_low, full_gate) + contract_cols(grad_up_low, full_up)
    grad_normed_mid, grad_feed = norm_back(grad_hidden_mid, normed_mid, scale_mid, gain_feed)
    grad_mixed = grad_top + grad_normed_mid
    grad_mixed_low = grad_mixed.astype(jnp.bfloat16)
    grad_proj = contract_rows(attn_low, grad_mixed_low)
    grad_attn = contract_cols(grad_mixed_low, full_proj).astype(jnp.bfloat16)
    grad_four = grad_attn.reshape(tokens, KVH, repeat, HD)
    delta_heads = jnp.sum(
        grad_four.astype(jnp.float32) * attn_raw.reshape(tokens, KVH, repeat, HD), axis=-1
    )
    delta_grid = jnp.transpose(delta_heads, (1, 2, 0))
    lse_rows = jnp.transpose(lse_heads, (2, 0, 1)).reshape(tokens, H)
    delta_rows = delta_heads.reshape(tokens, H)
    query_key_part = lax.all_gather(key_att, "ctx", axis=0, tiled=True)
    query_value_part = lax.all_gather(value_att, "ctx", axis=0, tiled=True)
    rows = query_key_part.shape[0]
    query_width = math.gcd(math.gcd(rows, tokens // 2), 512)

    def query_key_block(block_index, grad_query_acc):
        offset = block_index * query_width
        key_rows = lax.dynamic_slice_in_dim(query_key_part, offset, query_width, 0).reshape(
            query_width, KVH, HD
        )
        value_rows = lax.dynamic_slice_in_dim(query_value_part, offset, query_width, 0).reshape(
            query_width, KVH, HD
        )
        key_at = place_rows(offset + jnp.arange(query_width, dtype=jnp.int32), tokens, ctx_count)

        def attend(grad_query_acc):
            visible = visible_pairs(where_at, begins, key_at, doc_begin(starts, key_at))
            scores = score_block(query_four, key_rows, scaling)
            probable = jnp.where(visible, jnp.exp(scores - lse_heads[..., None]), 0.0)
            grad_prob = jnp.einsum(
                "igrd,jgd->grij", grad_four, value_rows, preferred_element_type=jnp.float32
            )
            grad_score = (probable * (grad_prob - delta_grid[..., None])).astype(jnp.bfloat16)
            added = (
                jnp.einsum(
                    "grij,jgd->igrd", grad_score, key_rows, preferred_element_type=jnp.float32
                )
                * scaling
            )
            return grad_query_acc + added.reshape(tokens, H * HD)

        return lax.cond(any_visible(where_at, begins, key_at), attend, keep_same, grad_query_acc)

    grad_query_att = lax.fori_loop(
        0, rows // query_width, query_key_block, jnp.zeros((tokens, H * HD), jnp.float32)
    )
    lse_all, delta_all = (
        lax.all_gather(lse_rows.astype(jnp.bfloat16), "ctx", axis=0, tiled=True).astype(
            lse_rows.dtype
        ),
        lax.all_gather(delta_rows.astype(jnp.bfloat16), "ctx", axis=0, tiled=True).astype(
            delta_rows.dtype
        ),
    )
    key_three = key_att.reshape(tokens, KVH, HD)
    value_three = value_att.reshape(tokens, KVH, HD)
    empty_keys = jnp.zeros((tokens, kv_width), jnp.float32)
    query_part = lax.all_gather(query_att, "ctx", axis=0, tiled=True)
    grad_part = lax.all_gather(grad_attn, "ctx", axis=0, tiled=True)
    rows = query_part.shape[0]
    key_width = math.gcd(math.gcd(rows, tokens // 2), 512)

    def query_block(block_index, totals):
        offset = block_index * key_width
        query_rows = lax.dynamic_slice_in_dim(query_part, offset, key_width, 0).reshape(
            key_width, KVH, repeat, HD
        )
        grad_rows = lax.dynamic_slice_in_dim(grad_part, offset, key_width, 0).reshape(
            key_width, KVH, repeat, HD
        )
        query_at = place_rows(offset + jnp.arange(key_width, dtype=jnp.int32), tokens, ctx_count)
        query_doc = doc_begin(starts, query_at)
        lse_block = jnp.transpose(
            lax.dynamic_slice_in_dim(lse_all, offset, key_width, 0).reshape(key_width, KVH, repeat),
            (1, 2, 0),
        )
        delta_block = jnp.transpose(
            lax.dynamic_slice_in_dim(delta_all, offset, key_width, 0).reshape(
                key_width, KVH, repeat
            ),
            (1, 2, 0),
        )

        def attend(totals):
            grad_key_acc, grad_value_acc = totals
            visible = visible_pairs(query_at, query_doc, where_at, begins)
            scores = score_block(query_rows, key_three, scaling)
            probable = jnp.where(visible, jnp.exp(scores - lse_block[..., None]), 0.0)
            grad_prob = jnp.einsum(
                "igrd,jgd->grij", grad_rows, value_three, preferred_element_type=jnp.float32
            )
            grad_score = (probable * (grad_prob - delta_block[..., None])).astype(jnp.bfloat16)
            value_added = jnp.einsum(
                "grij,igrd->jgd",
                probable.astype(jnp.bfloat16),
                grad_rows,
                preferred_element_type=jnp.float32,
            )
            key_added = (
                jnp.einsum(
                    "grij,igrd->jgd", grad_score, query_rows, preferred_element_type=jnp.float32
                )
                * scaling
            )
            return (
                grad_key_acc + key_added.reshape(tokens, kv_width),
                grad_value_acc + value_added.reshape(tokens, kv_width),
            )

        return lax.cond(any_visible(query_at, query_doc, where_at), attend, keep_same, totals)

    grad_key_att, grad_value_att = lax.fori_loop(
        0, rows // key_width, query_block, (empty_keys, empty_keys)
    )
    grad_query_unit = rotate_back(grad_query_att.reshape(tokens, H, HD), cosine, sine_part)
    grad_query_lin, grad_qgain = norm_back(grad_query_unit, query_normed, query_scale, gain_query)
    grad_key_unit = rotate_back(grad_key_att.reshape(tokens, KVH, HD), cosine, sine_part)
    grad_key_lin, grad_kgain = norm_back(grad_key_unit, key_normed, key_scale, gain_key)
    grad_query_low = grad_query_lin.reshape(tokens, H * HD).astype(jnp.bfloat16)
    grad_key_low = grad_key_lin.reshape(tokens, kv_width).astype(jnp.bfloat16)
    grad_value_low = grad_value_att.astype(jnp.bfloat16)
    grad_query = contract_rows(hidden_in, grad_query_low)
    grad_key = contract_rows(hidden_in, grad_key_low)
    grad_value = contract_rows(hidden_in, grad_value_low)
    grad_hidden_in = (
        contract_cols(grad_query_low, full_query)
        + contract_cols(grad_key_low, full_key)
        + contract_cols(grad_value_low, full_value)
    )
    grad_normed_in, grad_mixer = norm_back(grad_hidden_in, normed_in, scale_in, gain_mixer)
    input_grad = grad_mixed + grad_normed_in
    parts = (
        lax.psum_scatter(
            grad_query.astype(jnp.bfloat16), "fsdp", scatter_dimension=0, tiled=True
        ).astype(jnp.float32),
        lax.psum_scatter(
            grad_key.astype(jnp.bfloat16), "fsdp", scatter_dimension=0, tiled=True
        ).astype(jnp.float32),
        lax.psum_scatter(
            grad_value.astype(jnp.bfloat16), "fsdp", scatter_dimension=0, tiled=True
        ).astype(jnp.float32),
        lax.psum_scatter(
            grad_proj.astype(jnp.bfloat16), "fsdp", scatter_dimension=0, tiled=True
        ).astype(jnp.float32),
        lax.psum_scatter(
            grad_gate.astype(jnp.bfloat16), "fsdp", scatter_dimension=0, tiled=True
        ).astype(jnp.float32),
        lax.psum_scatter(
            grad_up.astype(jnp.bfloat16), "fsdp", scatter_dimension=0, tiled=True
        ).astype(jnp.float32),
        lax.psum_scatter(
            grad_down.astype(jnp.bfloat16), "fsdp", scatter_dimension=0, tiled=True
        ).astype(jnp.float32),
        lax.psum_scatter(
            grad_mixer.astype(jnp.bfloat16), "fsdp", scatter_dimension=0, tiled=True
        ).astype(jnp.float32),
        lax.psum_scatter(
            grad_feed.astype(jnp.bfloat16), "fsdp", scatter_dimension=0, tiled=True
        ).astype(jnp.float32),
        lax.psum_scatter(
            grad_qgain.astype(jnp.bfloat16), "fsdp", scatter_dimension=0, tiled=True
        ).astype(jnp.float32),
        lax.psum_scatter(
            grad_kgain.astype(jnp.bfloat16), "fsdp", scatter_dimension=0, tiled=True
        ).astype(jnp.float32),
    )
    summed = (
        lax.psum(parts[0].astype(jnp.bfloat16), "ctx").astype(jnp.float32),
        lax.psum(parts[1].astype(jnp.bfloat16), "ctx").astype(jnp.float32),
        lax.psum(parts[2].astype(jnp.bfloat16), "ctx").astype(jnp.float32),
        lax.psum(parts[3].astype(jnp.bfloat16), "ctx").astype(jnp.float32),
        lax.psum(parts[4].astype(jnp.bfloat16), "ctx").astype(jnp.float32),
        lax.psum(parts[5].astype(jnp.bfloat16), "ctx").astype(jnp.float32),
        lax.psum(parts[6].astype(jnp.bfloat16), "ctx").astype(jnp.float32),
        lax.psum(parts[7].astype(jnp.bfloat16), "ctx").astype(jnp.float32),
        lax.psum(parts[8].astype(jnp.bfloat16), "ctx").astype(jnp.float32),
        lax.psum(parts[9].astype(jnp.bfloat16), "ctx").astype(jnp.float32),
        lax.psum(parts[10].astype(jnp.bfloat16), "ctx").astype(jnp.float32),
    )
    return (
        block_output[None],
        input_grad[None],
        summed[0],
        summed[1],
        summed[2],
        summed[3],
        summed[4],
        summed[5],
        summed[6],
        summed[7],
        summed[8],
        summed[9],
        summed[10],
    )


ORDER = (0, 1, 2, 4, 3, 5, 6, 7)


def flipped(bits, count):
    return [(index, index ^ bits) for index in range(count)]


def swap_ctx(values, bits):
    return lax.ppermute(values, "ctx", flipped(bits, lax.axis_size("ctx")))


def behind(values, *ready):
    return lax.optimization_barrier((values,) + ready)[0]


def dot_nn(left, right):
    return lax.dot_general(
        left, right, (((1,), (0,)), ((), ())), preferred_element_type=jnp.float32
    )


def dot_nt(left, right):
    return lax.dot_general(
        left, right, (((1,), (1,)), ((), ())), preferred_element_type=jnp.float32
    )


def wide(values):
    return values.astype(jnp.float32)


def gather_near(block):
    return swap_ctx(block, 2), swap_ctx(block, 4), swap_ctx(block, 1)


def gather_corner(across, along):
    half = across.shape[0] // 2
    first = swap_ctx(along[:half], 2)
    second = swap_ctx(across[half:], 4)
    return jnp.concatenate([first, second], axis=0)


def gather_far(across, along, corner, *ready):
    return [swap_ctx(behind(part, *ready), 1) for part in (across, along, corner)]


def gather_plane(block, *ready):
    across, along, partner = gather_near(block)
    corner = gather_corner(across, along)
    others = gather_far(across, along, corner, *ready)
    return [block, partner, across, others[0], along, others[1], corner, others[2]]


def gather_direct(block, *ready):
    across, along, partner = gather_near(block)
    corner = swap_ctx(block, 6)
    others = gather_far(across, along, corner, *ready)
    return [block, partner, across, others[0], along, others[1], corner, others[2]]


def scatter_pair(blocks):
    got = [swap_ctx(blocks[bits], 1) for bits in (3, 5, 7, 1)]
    sums = [
        (wide(blocks[bits]) + wide(other)).astype(jnp.bfloat16)
        for bits, other in zip((2, 4, 6), got)
    ]
    return [blocks[0], got[3]], sums


def scatter_links(sums):
    return [swap_ctx(part, bits) for bits, part in zip((2, 4, 6), sums)]


def exchange_plane(blocks):
    return [blocks[0]] + [swap_ctx(blocks[bits], bits) for bits in range(1, 8)]


def shift_fsdp(values, pairs):
    return lax.ppermute(values, "fsdp", pairs)


def slot_of(bits):
    return jnp.where(bits == 3, 4, jnp.where(bits == 4, 3, bits))


def row_of(place, here, tokens, count):
    half = tokens // 2
    device = jnp.where(place < count, place, 2 * count - 1 - place)
    late = jnp.where(place < count, 0, half)
    return slot_of(lax.bitwise_xor(device, here)) * tokens + late


def swap_half(values, low_lane):
    return jnp.where(low_lane, pltpu.roll(values, 96, 1), pltpu.roll(values, 32, 1))


def head_blocks():
    shape = (2 * HD, 2 * HD)
    row = lax.broadcasted_iota(jnp.int32, shape, 0) < HD
    column = lax.broadcasted_iota(jnp.int32, shape, 1) < HD
    return jnp.where(row == column, 1.0 / HD, 0.0).astype(jnp.bfloat16)


def head_mean(values, blocks):
    high = values.astype(jnp.bfloat16)
    rest = (values - wide(high)).astype(jnp.bfloat16)
    return dot_nn(high, blocks) + dot_nn(rest, blocks)


def lane_masks(rows):
    lanes = lax.broadcasted_iota(jnp.int32, (rows, 2 * HD), 1)
    return lanes < HD, (lanes % HD) < (HD // 2)


def two_heads(values):
    first, _ = lane_masks(values.shape[0])
    zero = jnp.zeros_like(values)
    return jnp.concatenate(
        [jnp.where(first, values, zero), jnp.where(first, zero, values)], axis=0
    )


def begin_at(meta_ref, docs, where_at):
    begin = jnp.zeros_like(where_at)
    for doc in range(docs):
        begin = jnp.where(meta_ref[2 + doc] <= where_at, meta_ref[2 + doc], begin)
    return begin


def block_visible(meta_ref, docs, query_block, key_block, size):
    query_at = query_block * size + lax.broadcasted_iota(jnp.int32, (1, size), 1)
    begin = begin_at(meta_ref, docs, query_at)
    key_at = key_block * size + lax.broadcasted_iota(jnp.int32, (size, size), 0)
    return (key_at <= query_at) & (key_at >= begin)


def pair_tile(ref):
    return 2 * HD if ref.shape[0] % (4 * HD) == 0 else ref.shape[0] // 2


def aligned(value, size):
    return pl.multiple_of(value, size)


def take_heads_kernel(
    meta_ref, query_ref, key_ref, value_ref, proj_ref, mixer_ref, feed_ref, query_gain_ref, key_gain_ref,
    out_ref, gains, windows, proj, sem,
):
    here = meta_ref[0]
    rows = query_ref.shape[0]
    pair = 2 * HD
    start = aligned(lax.shift_right_logical(here, 1) * pair, pair)
    part = proj.shape[0]
    copies = [
        pltpu.make_async_copy(
            query_ref.at[:, pl.ds(aligned(here * pair, pair), pair)], windows.at[0], sem.at[0]
        ),
        pltpu.make_async_copy(key_ref.at[:, pl.ds(start, pair)], windows.at[1], sem.at[1]),
        pltpu.make_async_copy(value_ref.at[:, pl.ds(start, pair)], windows.at[2], sem.at[2]),
        pltpu.make_async_copy(
            proj_ref.at[pl.ds(aligned(here * part, part), part), :], proj, sem.at[3]
        ),
    ]
    for copy in copies:
        copy.start()
    gains[...] = jnp.zeros_like(gains)
    for row, ref in enumerate((mixer_ref, feed_ref, query_gain_ref, key_gain_ref)):
        gains[row : row + 1, : ref.shape[0]] = wide(ref[...]).reshape(1, ref.shape[0])
    extra = gains.shape[0]
    out_ref[rows : rows + extra, :] = gains[...].astype(jnp.bfloat16)
    for copy in copies:
        copy.wait()
    out_ref[:rows, :pair] = windows[0]
    odd = lax.bitwise_and(here, 1) == 1
    keys = wide(windows[1])
    values = wide(windows[2])
    first, _ = lane_masks(rows)
    keys = jnp.where(odd, pltpu.roll(keys, HD, 1), keys)
    values = jnp.where(odd, values, pltpu.roll(values, HD, 1))
    out_ref[:rows, pair:] = jnp.where(first, keys, values).astype(jnp.bfloat16)
    for index in range(proj.shape[1] // (2 * pair)):
        target = rows + extra + index * part
        out_ref[target : target + part, :] = proj[:, index * 2 * pair : (index + 1) * 2 * pair]


def arrange_heads_kernel(
    extra, meta_ref, *refs
):
    pieces, (weight_ref, mixer_ref, feed_ref, gains_ref, proj_ref) = refs[:4], refs[4:]
    shard = meta_ref[1]
    rows = weight_ref.shape[0] // 4
    pair = 2 * HD
    each = HD // 4
    gains = jnp.zeros((8, pair), jnp.float32)
    part = proj_ref.shape[0] // 4
    for bits, piece in enumerate(pieces):
        owner = lax.bitwise_xor(shard, bits)
        weight_ref[pl.ds(aligned(owner * rows, rows), rows), :] = piece[:rows, :]
        block = wide(piece[rows : rows + extra, :])
        lanes = pl.ds(aligned(owner * rows, rows), rows)
        mixer_ref[:, lanes] = block[0:1, :]
        feed_ref[:, lanes] = block[1:2, :]
        gains = gains + pltpu.roll(block[:8, :pair], owner * each, 1)
        for index in range(proj_ref.shape[1] // (2 * pair)):
            source = rows + extra + index * part
            proj_ref[
                pl.ds(aligned(owner * part, part), part), index * 2 * pair : (index + 1) * 2 * pair
            ] = piece[source : source + part, :]
    gains_ref[...] = gains + pltpu.roll(gains, HD, 1)


def take_wide_kernel(
    shards, meta_ref, gate_ref, up_ref, down_ref, out_ref, window, sem, rows, down_sem,
):
    here = meta_ref[0]
    own_rows = window.shape[1]
    inner = out_ref.shape[1] // 2
    piece = inner // shards
    span = window.shape[2]
    copies = []
    for kind, source in enumerate((gate_ref, up_ref)):
        for part in range(shards):
            start = aligned(part * (source.shape[1] // shards) + here * 128, 128)
            copies.append(
                pltpu.make_async_copy(
                    source.at[:, pl.ds(start, span)],
                    window.at[kind * shards + part],
                    sem.at[kind * shards + part],
                )
            )
    down = pltpu.make_async_copy(
        down_ref.at[pl.ds(aligned(here * rows.shape[0], 16), rows.shape[0]), :], rows, down_sem
    )
    for copy in copies:
        copy.start()
    down.start()
    main = inner // 128 * 128
    shift = span - here * (piece - 128)
    lasts = []
    for kind in range(2):
        parts = []
        for part in range(shards):
            copies[kind * shards + part].wait()
            moved = pltpu.roll(wide(window[kind * shards + part]), shift, 1)
            parts.append(moved[:, :piece])
        joined = jnp.concatenate(parts, axis=1)
        out_ref[:own_rows, kind * main : (kind + 1) * main] = joined[:, :main].astype(jnp.bfloat16)
        lasts.append(joined[:, main:])
    out_ref[:own_rows, 2 * main :] = jnp.concatenate(lasts, axis=1).astype(jnp.bfloat16)
    down.wait()
    out_ref[own_rows:, : rows.shape[1]] = rows[...]
    out_ref[own_rows:, rows.shape[1] :] = jnp.zeros_like(out_ref[own_rows:, rows.shape[1] :])


def head_linear_kernel(number, meta_ref, *refs):
    sources, (weight_ref, gain_ref, hidden_ref, linear_ref, rows, sem) = refs[:number], refs[number:]
    step = pl.program_id(0)

    def move(index):
        return pltpu.make_async_copy(sources[index], rows.at[index], sem.at[index])

    @pl.when(step == 0)
    def _():
        for index in range(number):
            move(index).start()

    for index in range(number):

        @pl.when(step == index)
        def _(index=index):
            move(index).wait()

    values = wide(rows[step])
    scale = lax.rsqrt(jnp.mean(values * values, axis=1, keepdims=True) + EPSILON)
    hidden_ref[...] = (values * scale * gain_ref[...]).astype(jnp.bfloat16)
    linear_ref[...] = dot_nn(hidden_ref[...], weight_ref[...])


def attention_kernel(
    tokens, count, docs,
    meta_ref, lin_ref, cos_ref, sin_ref, gains_ref,
    query_ref, key_ref, value_ref, attn_ref, lse_ref, *refs,
):
    low_refs, (value_t, accum, low, blocks_ref) = refs[:count], refs[count:]
    blocks_ref[...] = head_blocks()
    here = meta_ref[0]
    half = tokens // 2
    size = tokens
    blocks = count

    def prepare(place, carry):
        first, low_lane = lane_masks(half)
        source = aligned(row_of(place, here, tokens, count), half)
        target = aligned(place * half, half)
        cosine = cos_ref[pl.ds(target, half), :]
        sine = sin_ref[pl.ds(target, half), :]
        query = lin_ref[pl.ds(source, half), : 2 * HD]
        unit = query * lax.rsqrt(head_mean(query * query, blocks_ref[...]) + EPSILON) * gains_ref[2:3, :]
        turned = unit * cosine + swap_half(unit, low_lane) * sine
        query_ref[pl.ds(target, half), :] = (
            turned.astype(jnp.bfloat16).astype(jnp.float32) * (HD**-0.5)
        ).astype(jnp.bfloat16)
        both = lin_ref[pl.ds(source, half), 2 * HD :]
        unit = both * lax.rsqrt(head_mean(both * both, blocks_ref[...]) + EPSILON) * gains_ref[3:4, :]
        turned = unit * cosine + swap_half(unit, low_lane) * sine
        key_ref[pl.ds(target, half), :] = jnp.where(
            first, turned, pltpu.roll(turned, HD, 1)
        ).astype(jnp.bfloat16)
        values = jnp.where(first, pltpu.roll(both, HD, 1), both)
        value_ref[pl.ds(target, half), :] = values.astype(jnp.bfloat16)
        return carry

    lax.fori_loop(0, 2 * count, prepare, 0)

    def turn_values(block, carry):
        values = wide(value_ref[pl.ds(aligned(block * size, size), size), :])
        value_t[block, :HD, :] = values.T[:HD].astype(jnp.bfloat16)
        value_t[block, HD:, :] = jnp.ones((value_t.shape[1] - HD, size), jnp.bfloat16)
        return carry

    lax.fori_loop(0, blocks, turn_values, 0)

    def query_step(block, carry):
        query = two_heads(query_ref[pl.ds(aligned(block * size, size), size), :])
        accum[...] = jnp.zeros_like(accum)
        lowest = begin_at(meta_ref, docs, block * size) // size

        def key_step(other, carry):
            keys = key_ref[pl.ds(aligned(other * size, size), size), :]
            scores = dot_nt(keys, query)
            visible = block_visible(meta_ref, docs, block, other, size)
            probable = jnp.concatenate(
                [
                    jnp.where(visible, jnp.exp(scores[:, :size]), 0.0),
                    jnp.where(visible, jnp.exp(scores[:, size:]), 0.0),
                ],
                axis=1,
            ).astype(jnp.bfloat16)
            accum[...] += dot_nn(value_t[other], probable)
            return carry

        lax.fori_loop(lowest, block + 1, key_step, 0)
        mass = accum[HD : HD + 1, :]
        mixed = accum[:HD, :] / mass
        lse_ref[block] = jnp.log(mass)
        rows = jnp.concatenate([mixed[:, :size], mixed[:, size:]], axis=0).T
        attn_ref[pl.ds(aligned(block * size, size), size), :] = rows
        for part in range(2):
            target = aligned(row_of(2 * block + part, here, tokens, count), half)
            low[pl.ds(target, half), :] = rows[part * half : (part + 1) * half].astype(jnp.bfloat16)
        return carry

    lax.fori_loop(0, blocks, query_step, 0)
    for slot, bits in enumerate(ORDER):
        low_refs[bits][...] = low[slot * tokens : (slot + 1) * tokens, :]


def attention_back_kernel(
    tokens, count, docs,
    meta_ref, lin_ref, cos_ref, sin_ref, gains_ref,
    query_ref, key_ref, value_ref, attn_ref, lse_ref, *refs,
):
    grad_refs = refs[:count]
    out_ref, gain_ref = refs[count : count + 2]
    block_refs = refs[count + 2 : 2 * count + 2]
    key_t, grad_query, grad_key, grad_value, accum, grad_rows, blocks_ref = refs[2 * count + 2 :]
    blocks_ref[...] = head_blocks()
    here = meta_ref[0]
    half = tokens // 2
    size = tokens
    blocks = count
    grad_key[...] = jnp.zeros_like(grad_key)
    grad_value[...] = jnp.zeros_like(grad_value)
    gain_ref[...] = jnp.zeros_like(gain_ref)
    for slot, bits in enumerate(ORDER):
        grad_rows[slot * tokens : (slot + 1) * tokens, :] = grad_refs[bits][...]

    def turn_keys(block, carry):
        keys = wide(key_ref[pl.ds(aligned(block * size, size), size), :])
        key_t[block] = keys.T[:HD].astype(jnp.bfloat16)
        return carry

    lax.fori_loop(0, blocks, turn_keys, 0)

    def query_step(block, carry):
        here_rows = pl.ds(aligned(block * size, size), size)
        query = two_heads(query_ref[here_rows, :])
        parts = []
        for part in range(2):
            source = aligned(row_of(2 * block + part, here, tokens, count), half)
            parts.append(grad_rows[pl.ds(source, half), :])
        grads = jnp.concatenate(parts, axis=0)
        products = (wide(grads) * attn_ref[here_rows, :]).T
        deltas = (
            jnp.sum(products[:HD], axis=0, keepdims=True),
            jnp.sum(products[HD:], axis=0, keepdims=True),
        )
        grads = two_heads(grads)
        lse = lse_ref[block]
        accum[...] = jnp.zeros_like(accum)
        lowest = begin_at(meta_ref, docs, block * size) // size

        def key_step(other, carry):
            rows = pl.ds(aligned(other * size, size), size)
            scores = dot_nt(key_ref[rows, :], query)
            grad_prob = dot_nt(value_ref[rows, :], grads)
            visible = block_visible(meta_ref, docs, block, other, size)
            probs, grad_scores = [], []
            for head in range(2):
                cols = slice(head * size, (head + 1) * size)
                prob = jnp.where(visible, jnp.exp(scores[:, cols] - lse[:, cols]), 0.0)
                probs.append(prob)
                grad_scores.append(prob * (grad_prob[:, cols] - deltas[head]))
            probs = jnp.concatenate(probs, axis=1).astype(jnp.bfloat16)
            grad_scores = jnp.concatenate(grad_scores, axis=1).astype(jnp.bfloat16)
            grad_value[rows, :] += dot_nn(probs, grads)
            grad_key[rows, :] += dot_nn(grad_scores, query)
            accum[...] += dot_nn(key_t[other], grad_scores)
            return carry

        lax.fori_loop(lowest, block + 1, key_step, 0)
        total = accum[...] * (HD**-0.5)
        grad_query[here_rows, :] = jnp.concatenate([total[:, :size], total[:, size:]], axis=0).T
        return carry

    lax.fori_loop(0, blocks, query_step, 0)

    def finish(place, carry):
        first, low_lane = lane_masks(half)
        source = aligned(row_of(place, here, tokens, count), half)
        target = pl.ds(aligned(place * half, half), half)
        cosine = cos_ref[target, :]
        sine = sin_ref[target, :]

        def through(linear, grads, gain):
            scale = lax.rsqrt(head_mean(linear * linear, blocks_ref[...]) + EPSILON)
            normed = linear * scale
            turned = grads * cosine + swap_half(grads * sine, low_lane)
            weighted = turned * gain
            grad_in = scale * (weighted - normed * head_mean(weighted * normed, blocks_ref[...]))
            return grad_in, jnp.sum(turned * normed, axis=0, keepdims=True)

        grad_in, gain_row = through(
            lin_ref[pl.ds(source, half), : 2 * HD], grad_query[target, :], gains_ref[2:3, :]
        )
        out_ref[pl.ds(source, half), : 2 * HD] = grad_in.astype(jnp.bfloat16)
        gain_ref[0:1, :] += gain_row
        keys = grad_key[target, :]
        grad_in, gain_row = through(
            lin_ref[pl.ds(source, half), 2 * HD :], keys + pltpu.roll(keys, HD, 1), gains_ref[3:4, :]
        )
        gain_ref[1:2, :] += gain_row
        values = grad_value[target, :]
        values = values + pltpu.roll(values, HD, 1)
        out_ref[pl.ds(source, half), 2 * HD :] = jnp.where(first, grad_in, values).astype(
            jnp.bfloat16
        )
        return carry

    lax.fori_loop(0, 2 * count, finish, 0)
    for slot, bits in enumerate(ORDER):
        block_refs[bits][...] = out_ref[slot * tokens : (slot + 1) * tokens, :]


def proj_grad_kernel(parts, meta_ref, attn_ref, grad_ref, *refs):
    blocks, full = refs[:-1], refs[-1]
    count = len(blocks)
    here = meta_ref[0]
    tile = 2 * pair_tile(full)

    def outer(index, carry):
        part = pl.ds(aligned(index * tile, tile), tile)
        full[part, :] = contract_rows(attn_ref[:, part], grad_ref[...]).astype(jnp.bfloat16)
        return carry

    lax.fori_loop(0, full.shape[0] // tile, outer, 0)
    rows = blocks[0].shape[0] // parts
    for bits, block in enumerate(blocks):
        owner = lax.bitwise_xor(here, bits)
        for part in range(parts):
            source = aligned(part * count * rows + owner * rows, rows)
            block[part * rows : (part + 1) * rows, :] = full[pl.ds(source, rows), :]


def pack_heads_kernel(
    extra, meta_ref, heads_ref, mixer_ref, gain_ref, feed_ref, sums_ref, *refs
):
    proj_refs, pieces = refs[:5], refs[5:]
    shard = meta_ref[1]
    rows = heads_ref.shape[0] // 4
    pair = 2 * HD
    proj = wide(proj_refs[0][...])
    for other in proj_refs[1:]:
        proj = proj + wide(other[...])
    proj_low, mixer, _, gains = pieces[4:]
    pieces = pieces[:4]
    part = proj.shape[0] // 4
    proj_low[...] = proj.astype(jnp.bfloat16)
    mixer[...] = mixer_ref[...] / gain_ref[...]
    values = sums_ref[...]
    lower = lax.broadcasted_iota(jnp.int32, values.shape, 0) == 0
    values = values + jnp.where(lower, pltpu.roll(values, HD, 1), 0.0)
    each = HD // 4
    lanes = lax.broadcasted_iota(jnp.int32, values.shape, 1)
    for bits, piece in enumerate(pieces):
        owner = lax.bitwise_xor(shard, bits)
        piece[:rows, :] = heads_ref[pl.ds(aligned(owner * rows, rows), rows), :]
        gains[...] = jnp.zeros_like(gains)
        own = pl.ds(aligned(owner * rows, rows), rows)
        gains[0:1, :] = mixer[:, own]
        gains[1:2, :] = feed_ref[:, own]
        moved = pltpu.roll(values, pair - owner * each, 1)
        moved = jnp.where(lanes < each, moved, 0.0)
        gains[2:4, :pair] = moved[0:2, :]
        piece[rows : rows + extra, :] = gains[...].astype(jnp.bfloat16)
        for index in range(proj.shape[1] // (2 * pair)):
            target = rows + extra + index * part
            piece[target : target + part, :] = proj_low[
                pl.ds(aligned(owner * part, part), part), index * 2 * pair : (index + 1) * 2 * pair
            ]


def first_piece_kernel(meta_ref, hidden_ref, grad_ref, down_ref, piece_ref, total):
    step = pl.program_id(0)
    rows = total.shape[0]
    inner = piece_ref.shape[0] - rows
    width = down_ref.shape[1]
    product = contract_rows(hidden_ref[...], grad_ref[...])

    @pl.when(step == 0)
    def _():
        total[...] = product

    @pl.when(step > 0)
    def _():
        total[...] += product

    @pl.when(step == pl.num_programs(0) - 1)
    def _():
        owner = lax.bitwise_xor(meta_ref[1], 3)
        piece_ref[:rows, :] = total[...].astype(jnp.bfloat16)
        piece_ref[rows:, :width] = down_ref[pl.ds(aligned(owner * inner, 16), inner), :]
        piece_ref[rows:, width:] = jnp.zeros_like(piece_ref[rows:, width:])


def first_piece_call(meta, hidden, grads, down, rows, inner):
    stream, _ = hidden.shape
    columns = grads.shape[1]
    size = stream // 4
    return pl.pallas_call(
        first_piece_kernel,
        out_shape=shaped((rows + inner, columns)),
        grid_spec=pltpu.PrefetchScalarGridSpec(
            num_scalar_prefetch=1,
            grid=(4,),
            in_specs=[
                pl.BlockSpec((size, rows), lambda step, meta_ref: (step, lax.bitwise_xor(meta_ref[1], 3))),
                pl.BlockSpec((size, columns), lambda step, meta_ref: (step, 0)),
                pl.BlockSpec(down.shape, lambda step, meta_ref: (0, 0)),
            ],
            out_specs=pl.BlockSpec((rows + inner, columns), lambda step, meta_ref: (0, 0)),
            scratch_shapes=[pltpu.VMEM((rows, columns), jnp.float32)],
        ),
        cost_estimate=pl.CostEstimate(
            flops=2 * stream * rows * columns, bytes_accessed=stream * columns * 2, transcendentals=0
        ),
        compiler_params=pltpu.CompilerParams(vmem_limit_bytes=16 * 2**20),
        name="first_piece",
    )(meta, hidden, grads, down)


def pack_feed_kernel(meta_ref, wide_ref, down_ref, *pieces):
    shard = meta_ref[1]
    rows = wide_ref.shape[0] // 4
    inner = pieces[0].shape[0] - rows
    width = down_ref.shape[1]
    for bits, piece in enumerate(pieces):
        owner = lax.bitwise_xor(shard, bits)
        piece[:rows, :] = wide_ref[pl.ds(aligned(owner * rows, 16), rows), :]
        piece[rows:, :width] = down_ref[pl.ds(aligned(owner * inner, 16), inner), :]
        piece[rows:, width:] = jnp.zeros_like(piece[rows:, width:])


def input_grad_kernel(count, meta_ref, *refs):
    grads, weights = refs[:count], refs[count : 2 * count]
    input_ref, grad_ref, gain_ref, out_ref = refs[2 * count :]
    total = dot_nt(grads[0][...], weights[0][...])
    for left, right in zip(grads[1:], weights[1:]):
        total = total + dot_nt(left[...], right[...])
    values = wide(input_ref[...])
    scale = lax.rsqrt(jnp.mean(values * values, axis=1, keepdims=True) + EPSILON)
    normed = values * scale
    weighted = total * gain_ref[...]
    grad_in = scale * (weighted - normed * jnp.mean(weighted * normed, axis=1, keepdims=True))
    out_ref[...] = grad_ref[...] + grad_in


def project_kernel(count, parts, start, meta_ref, *refs):
    attn_refs, weight_refs, rest = refs[:count], refs[count : 2 * count], refs[2 * count :]
    input_ref, gain_ref, full_ref, attn_out_ref, mixed_ref, hidden_ref, _ = rest
    here = meta_ref[0]
    total = weight_refs[0].shape[0] - start
    rows = total // parts
    for bits in range(count):
        owner = lax.bitwise_xor(here, bits)
        for part in range(parts):
            target = aligned(part * count * rows + owner * rows, rows)
            source = start + part * rows
            full_ref[pl.ds(target, rows), :] = weight_refs[bits][source : source + rows, :]
        attn_out_ref[:, pl.ds(aligned(owner * 2 * HD, 2 * HD), 2 * HD)] = attn_refs[bits][...]
    tile = 2 * pair_tile(full_ref)

    def project(index, carry):
        part = pl.ds(aligned(index * tile, tile), tile)
        mixed_ref[:, part] = wide(input_ref[:, part]) + dot_nn(attn_out_ref[...], full_ref[:, part])
        return carry

    lax.fori_loop(0, full_ref.shape[1] // tile, project, 0)
    mixed = mixed_ref[...]
    scale = lax.rsqrt(jnp.mean(mixed * mixed, axis=1, keepdims=True) + EPSILON)
    hidden_ref[...] = (mixed * scale * gain_ref[...]).astype(jnp.bfloat16)


def feed_block(hidden_ref, grad_ref, wide_ref, down_ref, act_ref, grad_wide_ref, out_ref, back_ref):
    tokens = hidden_ref.shape[0]
    inner = wide_ref.shape[1] // 2
    main = inner // 128 * 128
    first, _ = lane_masks(tokens)

    def activate(gate, up, grad_act):
        sigmoid = 1.0 / (1.0 + jnp.exp(-gate))
        silu = gate * sigmoid
        grad_gate = grad_act * up * sigmoid * (1.0 + gate * (1.0 - sigmoid))
        return silu * up, grad_gate, grad_act * silu

    both = dot_nn(hidden_ref[...], wide_ref[...])
    grad_act = dot_nt(grad_ref[...], down_ref[...])
    act, grad_gate, grad_up = activate(
        both[:, :main], both[:, main : 2 * main], grad_act[:, :main]
    )
    act_ref[:, :main] = act.astype(jnp.bfloat16)
    grad_wide_ref[:, :main] = grad_gate.astype(jnp.bfloat16)
    grad_wide_ref[:, main : 2 * main] = grad_up.astype(jnp.bfloat16)
    last = both[:, 2 * main :]
    act, grad_gate, grad_up = activate(last, pltpu.roll(last, HD, 1), grad_act[:, main:])
    act_ref[:, main:] = jnp.where(first, act, 0.0).astype(jnp.bfloat16)
    grad_wide_ref[:, 2 * main :] = jnp.where(
        first, grad_gate, pltpu.roll(grad_up, HD, 1)
    ).astype(jnp.bfloat16)
    back_ref[...] = dot_nt(grad_wide_ref[...], wide_ref[...]).astype(jnp.bfloat16)
    out_ref[...] = dot_nn(act_ref[...], down_ref[...]).astype(jnp.bfloat16)


def feed_kernel(number, meta_ref, *refs):
    firsts, grads, pieces = refs[:number], refs[number : 2 * number], refs[2 * number : 2 * number + 5]
    refs = refs[2 * number + 5 :]
    act_ref, grad_wide_ref, hidden_all, grad_all = refs[:4]
    out_refs, back_refs = refs[4 : 4 + number], refs[4 + number : 4 + 2 * number]
    hidden, grad, out_low, back_low, wide_ref, down_ref, joined = refs[4 + 2 * number :][:7]
    in_sem, grad_sem, all_sem, grad_all_sem, out_sem, back_sem, piece_sem = refs[11 + 2 * number :]
    tokens, width = hidden.shape[1:]
    shard = meta_ref[1]
    rows = wide_ref.shape[0] // 4
    inner = joined.shape[1] - rows
    step = pl.program_id(0)

    def moves(index):
        filed = pl.ds(index * tokens, tokens)
        return (
            pltpu.make_async_copy(firsts[index], hidden.at[index], in_sem.at[index]),
            pltpu.make_async_copy(
                grads[index].at[pl.ds(0, tokens), :], grad.at[index], grad_sem.at[index]
            ),
            pltpu.make_async_copy(hidden.at[index], hidden_all.at[filed, :], all_sem.at[index]),
            pltpu.make_async_copy(grad.at[index], grad_all.at[filed, :], grad_all_sem.at[index]),
            pltpu.make_async_copy(out_low.at[index], out_refs[index], out_sem.at[index]),
            pltpu.make_async_copy(back_low.at[index], back_refs[index], back_sem.at[index]),
        )

    def places(bits):
        owner = lax.bitwise_xor(shard, bits)
        return (
            pl.ds(aligned(owner * rows, rows), rows),
            pl.ds(aligned(owner * inner, 16), inner),
        )

    @pl.when(step == 0)
    def _():
        copies = []
        for bits in range(3):
            upper, lower = places(bits)
            copies.append(
                pltpu.make_async_copy(
                    pieces[bits].at[pl.ds(0, rows), :], wide_ref.at[upper, :], piece_sem.at[2 * bits]
                )
            )
            copies.append(
                pltpu.make_async_copy(
                    pieces[bits].at[pl.ds(rows, inner), pl.ds(0, width)],
                    down_ref.at[lower, :],
                    piece_sem.at[2 * bits + 1],
                )
            )
        for index in range(2):
            copies.append(
                pltpu.make_async_copy(pieces[3 + index], joined.at[index], piece_sem.at[6 + index])
            )
        for copy in copies:
            copy.start()
        for index in range(number):
            for move in moves(index)[:2]:
                move.start()
        down_ref[4 * inner :, :] = jnp.zeros_like(down_ref[4 * inner :, :])
        for copy in copies:
            copy.wait()
        upper, lower = places(3)
        wide_ref[upper, :] = joined[0, :rows, :] + joined[1, :rows, :]
        down_ref[lower, :] = joined[0, rows:, :width] + joined[1, rows:, :width]

    for index in range(number):

        @pl.when(step == index)
        def _(index=index):
            for move in moves(index)[:2]:
                move.wait()
            for move in moves(index)[2:4]:
                move.start()

    feed_block(
        hidden.at[step], grad.at[step], wide_ref, down_ref,
        act_ref, grad_wide_ref, out_low.at[step], back_low.at[step],
    )

    for index in range(number):

        @pl.when(step == index)
        def _(index=index):
            for move in moves(index)[4:]:
                move.start()

    @pl.when(step == number - 1)
    def _():
        for index in range(number):
            for move in moves(index)[2:]:
                move.wait()


def feed_call(meta, hidden, grads, pieces, padded, grant):
    number = len(hidden)
    tokens, width = hidden[0].shape
    rows, inner = pieces[0].shape
    low = jnp.bfloat16
    outs = [shaped((number * tokens, columns)) for columns in (padded, inner, width, width)]
    outs += [shaped((tokens, width))] * (2 * number)
    return pl.pallas_call(
        functools.partial(feed_kernel, number),
        grid=(number,),
        out_shape=outs,
        in_specs=[SCALARS] + [PLACED] * (2 * number + 5),
        out_specs=[
            pl.BlockSpec((tokens, padded), lambda step: (step, 0)),
            pl.BlockSpec((tokens, inner), lambda step: (step, 0)),
        ]
        + [PLACED] * (2 + 2 * number),
        scratch_shapes=[pltpu.VMEM((number, tokens, width), low)] * 4
        + [
            pltpu.VMEM((width, inner), low),
            pltpu.VMEM((padded, width), low),
            pltpu.VMEM((2, rows, inner), low),
        ]
        + [pltpu.SemaphoreType.DMA((number,))] * 6
        + [pltpu.SemaphoreType.DMA((8,))],
        cost_estimate=pl.CostEstimate(
            flops=6 * number * tokens * width * inner,
            bytes_accessed=16 * number * tokens * width,
            transcendentals=0,
        ),
        compiler_params=pltpu.CompilerParams(vmem_limit_bytes=grant * 2**20),
        name="feed",
    )(meta, *hidden, *grads, *pieces)


def feed_back_kernel(count, meta_ref, *refs):
    sums, rest = refs[:5], refs[5:]
    mixed_ref, grad_ref, full_ref, gain_ref, grad_mixed_ref, grad_low_ref, grad_gain_ref = rest[:7]
    block_refs, attn = rest[7 : 7 + count], rest[7 + count]
    here = meta_ref[0]
    grad_hidden = wide(sums[0][...])
    for part in sums[1:]:
        grad_hidden = grad_hidden + wide(part[...])
    mixed = mixed_ref[...]
    scale = lax.rsqrt(jnp.mean(mixed * mixed, axis=1, keepdims=True) + EPSILON)
    normed = mixed * scale
    weighted = grad_hidden * gain_ref[...]
    grad_in = scale * (weighted - normed * jnp.mean(weighted * normed, axis=1, keepdims=True))
    grad_gain_ref[...] = jnp.sum(grad_hidden * normed, axis=0, keepdims=True)
    grad_mixed = wide(grad_ref[...]) + grad_in
    grad_mixed_ref[...] = grad_mixed
    grad_low_ref[...] = grad_mixed.astype(jnp.bfloat16)
    tile = 2 * pair_tile(full_ref)

    def project_back(index, carry):
        part = pl.ds(aligned(index * tile, tile), tile)
        attn[:, part] = dot_nt(grad_low_ref[...], full_ref[part, :]).astype(jnp.bfloat16)
        return carry

    lax.fori_loop(0, full_ref.shape[0] // tile, project_back, 0)
    for bits in range(count):
        owner = lax.bitwise_xor(here, bits)
        block_refs[bits][...] = attn[:, pl.ds(aligned(owner * 2 * HD, 2 * HD), 2 * HD)]


def wide_out_kernel(count, parts, meta_ref, *refs):
    blocks, (gate_ref, up_ref, down_ref, held, lower, sem, down_sem) = refs[:count], refs[count:]
    here = meta_ref[0]
    steps = 4
    tile = gate_ref.shape[0]
    rows = steps * tile
    inner = held.shape[3] // 2
    main = inner // 128 * 128
    piece = inner // parts
    width = down_ref.shape[1]
    each = count // steps
    step = pl.program_id(0)

    def moves(index):
        copies = []
        for bits in range(count):
            owner = lax.bitwise_xor(here, bits)
            copies.append(
                pltpu.make_async_copy(
                    blocks[bits].at[pl.ds(index * tile, tile), :],
                    held.at[index, owner],
                    sem.at[index * count + bits],
                )
            )
        return copies

    def down_move(bits):
        owner = lax.bitwise_xor(here, bits)
        return pltpu.make_async_copy(
            blocks[bits].at[pl.ds(rows, lower.shape[1]), pl.ds(0, width)],
            lower.at[owner],
            down_sem.at[bits],
        )

    @pl.when(step == 0)
    def _():
        for index in range(steps):
            for move in moves(index):
                move.start()
            if index == 0:
                for bits in range(count):
                    down_move(bits).start()
        for bits in range(count):
            down_move(bits).wait()

    for index in range(steps):

        @pl.when(step == index)
        def _(index=index):
            for move in moves(index):
                move.wait()

    for kind, out_ref in enumerate((gate_ref, up_ref)):
        for part in range(parts):
            columns = []
            for owner in range(count):
                start, stop = part * piece, (part + 1) * piece
                begin = kind * main
                if start < main:
                    columns.append(
                        wide(held[step, owner, :, begin + start : begin + min(stop, main)])
                    )
                if stop > main:
                    begin = main + kind * (inner - main)
                    columns.append(
                        wide(held[step, owner, :, begin + max(start, main) : begin + stop])
                    )
            out_ref[:, part * count * piece : (part + 1) * count * piece] = jnp.concatenate(
                columns, axis=1
            )
    size = lower.shape[1]
    for index in range(each):
        down_ref[index * size : (index + 1) * size, :] = wide(lower[step * each + index])


def heads_out_kernel(count, own, extra, meta_ref, *refs):
    blocks, rest = refs[:count], refs[count:]
    query_ref, key_ref, value_ref, proj_ref, gain_ref, held = rest
    here = meta_ref[0]
    pair = 2 * HD
    part = (blocks[0].shape[0] - own - extra) // 4
    gains = jnp.zeros(gain_ref.shape, jnp.float32)
    for bits in range(count):
        owner = lax.bitwise_xor(here, bits)
        block = wide(blocks[bits][...])
        query_ref[:, pl.ds(aligned(owner * pair, pair), pair)] = block[:own, :pair]
        held[owner] = block[:own, pair:]
        gains = gains + block[own : own + extra, :]
        for index in range(4):
            source = own + extra + index * part
            proj_ref[
                pl.ds(aligned(owner * part, part), part), index * 2 * pair : (index + 1) * 2 * pair
            ] = block[source : source + part, :]
    gain_ref[...] = gains
    first, _ = lane_masks(own)
    for index in range(count // 2):
        early, late = held[2 * index], held[2 * index + 1]
        lanes = slice(index * pair, (index + 1) * pair)
        key_ref[:, lanes] = jnp.where(first, early, pltpu.roll(late, HD, 1))
        value_ref[:, lanes] = jnp.where(first, pltpu.roll(early, HD, 1), late)


SCALARS = pl.BlockSpec(memory_space=pltpu.SMEM)
WHOLE = pl.BlockSpec(memory_space=pltpu.VMEM)
PLACED = pl.BlockSpec(memory_space=pl.ANY)
FAR = pl.BlockSpec(memory_space=pltpu.HBM)


def shaped(shape, kind=jnp.bfloat16):
    return jax.ShapeDtypeStruct(shape, kind)


def whole_call(kernel, outs, ins, flops, scratch=(), grant=24, specs=None):
    moved = sum(math.prod(out.shape) * out.dtype.itemsize for out in outs)
    return pl.pallas_call(
        kernel,
        out_shape=outs,
        in_specs=[SCALARS] + (specs or [WHOLE] * ins),
        out_specs=[WHOLE] * len(outs),
        scratch_shapes=list(scratch),
        cost_estimate=pl.CostEstimate(
            flops=int(flops), bytes_accessed=int(2 * moved), transcendentals=0
        ),
        compiler_params=pltpu.CompilerParams(vmem_limit_bytes=grant * 2**20),
    )


def local_heads(
    block_input, doc_starts, out_grad, query_weight, key_weight, value_weight, output_weight,
    gate_weight, up_weight, down_weight, mixer_gain, feed_gain, query_gain, key_gain,
):
    low = jnp.bfloat16
    tokens, width = block_input.shape[1:]
    count = lax.axis_size("ctx")
    shards = lax.axis_size("fsdp")
    here = lax.axis_index("ctx").astype(jnp.int32)
    shard = lax.axis_index("fsdp").astype(jnp.int32)
    stream = tokens * count
    docs = doc_starts.shape[1]
    pair = 2 * HD
    own_rows = width // shards
    extra = 16
    meta = jnp.concatenate([here[None], shard[None], doc_starts[0].astype(jnp.int32)])
    own_input = block_input[0]
    own_grad = out_grad[0]
    inner = down_weight.shape[0] // count
    wide_inner = inner * shards
    padded = -(-wide_inner // 128) * 128
    proj_rows = own_rows // count
    edges = [(0, 1), (3, 2)]
    middle = [(1, 2), (2, 1)]
    relay = [(1, 0), (2, 3)]

    def near(piece, bits):
        return shift_fsdp(piece, flipped(bits, shards))

    across, along, partner = gather_near(own_input)
    corner = swap_ctx(own_input, 6)
    piece_rows = own_rows + extra + 4 * proj_rows
    head_piece = whole_call(
        take_heads_kernel,
        [shaped((piece_rows, 2 * pair))],
        8,
        0,
        [
            pltpu.VMEM((extra, 2 * pair), jnp.float32),
            pltpu.VMEM((3, own_rows, pair), low),
            pltpu.VMEM((proj_rows, width), low),
            pltpu.SemaphoreType.DMA((4,)),
        ],
        grant=60,
        specs=[FAR] * 4 + [WHOLE] * 4,
    )(
        meta, query_weight, key_weight, value_weight, output_weight,
        mixer_gain, feed_gain, query_gain, key_gain,
    )[0]
    head_pieces = [head_piece] + [near(head_piece, bits) for bits in (1, 2, 3)]
    feed_rows = own_rows + inner
    feed_piece = whole_call(
        functools.partial(take_wide_kernel, shards),
        [shaped((feed_rows, 2 * wide_inner))],
        3,
        2 * own_rows * 2 * wide_inner * 2048,
        [
            pltpu.VMEM((2 * shards, own_rows, 256), low),
            pltpu.SemaphoreType.DMA((2 * shards,)),
            pltpu.VMEM((inner, width), low),
            pltpu.SemaphoreType.DMA(()),
        ],
        grant=60,
        specs=[FAR] * 3,
    )(behind(meta, head_piece), gate_weight, up_weight, down_weight)[0]
    feed_near = near(feed_piece, 1)
    feed_far = near(behind(feed_piece, *head_pieces[1:]), 2)
    others = gather_far(across, along, corner)
    input_blocks = [own_input, partner, across, others[0], along, others[1], corner, others[2]]

    where_at = jnp.arange(stream, dtype=jnp.int32)
    begins = doc_begin(doc_starts[0], where_at)
    lanes = jnp.arange(pair) % (HD // 2)
    frequency = ROPE_BASE ** (-(2.0 * lanes.astype(jnp.float32)) / HD)
    angles = (where_at - begins).astype(jnp.float32)[:, None] * frequency[None, :]
    cosine = jnp.cos(angles)
    sine = jnp.sin(angles) * jnp.where(jnp.arange(pair) % HD < HD // 2, -1.0, 1.0)[None, :]

    heads_weight, gain_mixer, gain_feed, gain_heads, proj_part = whole_call(
        functools.partial(arrange_heads_kernel, extra),
        [
            shaped((width, 2 * pair)),
            shaped((1, width), jnp.float32),
            shaped((1, width), jnp.float32),
            shaped((8, pair), jnp.float32),
            shaped((shards * proj_rows, width)),
        ],
        4,
        0,
        grant=8,
    )(behind(meta, cosine, sine), *head_pieces)

    hidden_in, linear = pl.pallas_call(
        functools.partial(head_linear_kernel, count),
        grid=(count,),
        in_specs=[SCALARS]
        + [PLACED] * count
        + [
            pl.BlockSpec((width, 2 * pair), lambda step: (0, 0)),
            pl.BlockSpec((1, width), lambda step: (0, 0)),
        ],
        out_specs=[
            pl.BlockSpec((tokens, width), lambda step: (step, 0)),
            pl.BlockSpec((tokens, 2 * pair), lambda step: (step, 0)),
        ],
        out_shape=[shaped((stream, width)), shaped((stream, 2 * pair), jnp.float32)],
        scratch_shapes=[
            pltpu.VMEM((count, tokens, width), low),
            pltpu.SemaphoreType.DMA((count,)),
        ],
        cost_estimate=pl.CostEstimate(
            flops=4 * stream * width * pair, bytes_accessed=6 * stream * width, transcendentals=0
        ),
        compiler_params=pltpu.CompilerParams(vmem_limit_bytes=60 * 2**20),
        name="head_linear",
    )(meta, *[input_blocks[bits] for bits in ORDER], heads_weight, gain_mixer)

    pairs = stream * stream // 2
    extra_piece = behind(jnp.concatenate([own_grad, proj_part], axis=0), corner)
    extra_across, extra_along, extra_partner = gather_near(extra_piece)
    extra_corner = swap_ctx(extra_piece, 6)
    query_att, key_att, value_att, attn, lse, *attn_low = whole_call(
        functools.partial(attention_kernel, tokens, count, docs),
        [
            shaped((stream, pair)),
            shaped((stream, pair)),
            shaped((stream, pair)),
            shaped((stream, pair), jnp.float32),
            shaped((count, 1, 2 * tokens), jnp.float32),
        ]
        + [shaped((tokens, pair))] * count,
        4,
        8 * pairs * HD,
        [
            pltpu.VMEM((count, HD + 16, tokens), low),
            pltpu.VMEM((HD + 16, 2 * tokens), jnp.float32),
            pltpu.VMEM((stream, pair), low),
            pltpu.VMEM((pair, pair), low),
        ],
        grant=10,
    )(meta, linear, cosine, sine, gain_heads)

    attn_blocks = exchange_plane(attn_low)
    feed_middle = shift_fsdp(behind(feed_piece, attn_blocks[1]), middle)
    feed_relay = shift_fsdp(behind(feed_far, attn_blocks[1]), relay)
    extra_others = gather_far(extra_across, extra_along, extra_corner, attn_blocks[1])
    extra_blocks = [
        extra_piece, extra_partner, extra_across, extra_others[0],
        extra_along, extra_others[1], extra_corner, extra_others[2],
    ]
    full_proj, attn_rows, mixed, hidden_mid = whole_call(
        functools.partial(project_kernel, count, shards, tokens),
        [
            shaped((width, width)),
            shaped((tokens, width)),
            shaped((tokens, width), jnp.float32),
            shaped((tokens, width)),
        ],
        2 * count + 2,
        2 * tokens * width * width,
        [pltpu.VMEM((tokens, width), low)],
        grant=8,
    )(meta, *attn_blocks, *extra_blocks, own_input, gain_feed)

    hidden_across, hidden_along, hidden_partner = gather_near(hidden_mid)
    hidden_corner = swap_ctx(hidden_mid, 6)
    hidden_far = gather_far(hidden_across, hidden_along, hidden_corner)
    hidden_blocks = [
        hidden_mid, hidden_partner, hidden_across, hidden_far[0],
        hidden_along, hidden_far[1], hidden_corner, hidden_far[2],
    ]
    weight_piece = behind(heads_weight, hidden_far[2])
    weight_near = gather_near(weight_piece)
    weight_corner = swap_ctx(weight_piece, 6)
    act_all, grad_wide_all, hidden_all, grad_all, *parts = feed_call(
        meta,
        hidden_blocks,
        extra_blocks,
        (feed_piece, feed_near, feed_far, feed_middle, feed_relay),
        padded,
        60,
    )
    out_parts, back_parts = parts[:count], parts[count:]
    back_own, back_pairs = scatter_pair(back_parts)
    back_sums = back_own + scatter_links(back_pairs)

    def scatter_early(pieces):
        return shift_fsdp(pieces[3], edges), shift_fsdp(pieces[3], middle)

    def scatter_late(pieces, early, *ready):
        second = behind((wide(pieces[2]) + wide(early)).astype(low), *ready)
        return near(second, 2), near(behind(pieces[1], *ready), 1)

    grad_down = contract_rows(behind(act_all, *back_pairs), grad_all).astype(low)
    first_piece = first_piece_call(meta, hidden_all, grad_wide_all, grad_down, own_rows, inner)
    grad_wide = contract_rows(behind(hidden_all, first_piece), grad_wide_all).astype(low)
    feed_pieces = whole_call(
        pack_feed_kernel, [shaped((feed_rows, 2 * wide_inner))] * 3, 2, 0, grant=16
    )(meta, grad_wide, grad_down)
    feed_pieces = [*feed_pieces, first_piece]
    wide_edge, wide_middle = scatter_early(feed_pieces)
    out_own, out_pairs = scatter_pair([behind(part, grad_wide) for part in out_parts])

    grad_mixed, grad_mixed_low, grad_feed, *grad_blocks = whole_call(
        functools.partial(feed_back_kernel, count),
        [
            shaped((tokens, width), jnp.float32),
            shaped((tokens, width)),
            shaped((1, width), jnp.float32),
        ]
        + [shaped((tokens, pair))] * count,
        9,
        2 * tokens * width * width,
        [pltpu.VMEM((tokens, width), low)],
        grant=8,
    )(meta, *back_sums, mixed, own_grad, full_proj, gain_feed)
    grad_attn = exchange_plane(grad_blocks)
    wide_late = scatter_late(feed_pieces, wide_edge, grad_blocks[0])
    proj_blocks = whole_call(
        functools.partial(proj_grad_kernel, shards),
        [shaped((shards * proj_rows, width))] * count,
        2,
        2 * tokens * width * width,
        [pltpu.VMEM((width, width), low)],
        grant=8,
    )(meta, attn_rows, grad_mixed_low)
    proj_own, proj_pairs = scatter_pair(proj_blocks)
    proj_parts = proj_own + scatter_links(proj_pairs)
    out_sums = out_own + scatter_links([behind(part, grad_blocks[0]) for part in out_pairs])

    back_outs = whole_call(
        functools.partial(attention_back_kernel, tokens, count, docs),
        [shaped((stream, 2 * pair)), shaped((8, pair), jnp.float32)]
        + [shaped((tokens, 2 * pair))] * count,
        9 + count,
        20 * pairs * HD,
        [
            pltpu.VMEM((count, HD, tokens), low),
            pltpu.VMEM((stream, pair), jnp.float32),
            pltpu.VMEM((stream, pair), jnp.float32),
            pltpu.VMEM((stream, pair), jnp.float32),
            pltpu.VMEM((HD, 2 * tokens), jnp.float32),
            pltpu.VMEM((stream, pair), low),
            pltpu.VMEM((pair, pair), low),
        ],
        grant=14,
    )(meta, linear, cosine, sine, gain_heads, query_att, key_att, value_att, attn, lse, *grad_attn)
    grad_linear, gain_sums, *token_blocks = back_outs

    token_grads = exchange_plane(token_blocks)
    weight_far = gather_far(weight_near[0], weight_near[1], weight_corner, token_grads[1])
    weight_all = [
        weight_piece, weight_near[2], weight_near[0], weight_far[0],
        weight_near[1], weight_far[1], weight_corner, weight_far[2],
    ]
    late_linear = behind(grad_linear, token_grads[1])
    grad_heads = contract_rows(hidden_in, late_linear).astype(low)
    grad_mixer = jnp.sum(
        contract_cols(late_linear, heads_weight) * wide(hidden_in), axis=0, keepdims=True
    )
    packed = whole_call(
        functools.partial(pack_heads_kernel, extra),
        [shaped((piece_rows, 2 * pair))] * shards,
        10,
        0,
        [
            pltpu.VMEM((shards * proj_rows, width), low),
            pltpu.VMEM((1, width), jnp.float32),
            pltpu.VMEM((8, pair), jnp.float32),
            pltpu.VMEM((extra, 2 * pair), jnp.float32),
        ],
        grant=6,
    )(meta, grad_heads, grad_mixer, gain_mixer, grad_feed, gain_sums, *proj_parts)
    heads_sent = [near(packed[bits], bits) for bits in (1, 2, 3)]

    def total_of(first, *parts):
        return sum([wide(part) for part in parts], wide(first)).astype(low)

    def total_late(pieces, parts, *ready):
        return total_of(pieces[0], *[behind(part, *ready) for part in parts])

    wide_total = total_late(feed_pieces, (wide_middle,) + wide_late, grad_linear)
    wide_blocks = gather_plane(wide_total)
    input_grad = whole_call(
        functools.partial(input_grad_kernel, count),
        [shaped((tokens, width), jnp.float32)],
        2 * count + 3,
        2 * tokens * width * 2 * width,
        grant=10,
    )(meta, *token_grads, *weight_all, own_input, grad_mixed, gain_mixer)[0]
    heads_total = total_of(packed[0], *heads_sent)
    heads_blocks = gather_direct(heads_total)
    block_output = (
        mixed + sum(wide(behind(part, packed[0])) for part in out_sums)
    ).astype(low)

    tile = own_rows // 4
    full = wide_inner * count
    out_gate, out_up, out_down = pl.pallas_call(
        functools.partial(wide_out_kernel, count, shards),
        grid=(4,),
        in_specs=[SCALARS] + [PLACED] * count,
        out_specs=[
            pl.BlockSpec((tile, full), lambda step: (step, 0)),
            pl.BlockSpec((tile, full), lambda step: (step, 0)),
            pl.BlockSpec((count * inner // 4, width), lambda step: (step, 0)),
        ],
        out_shape=[
            shaped((own_rows, full), jnp.float32),
            shaped((own_rows, full), jnp.float32),
            shaped((count * inner, width), jnp.float32),
        ],
        scratch_shapes=[
            pltpu.VMEM((4, count, tile, 2 * wide_inner), low),
            pltpu.VMEM((count, inner, width), low),
            pltpu.SemaphoreType.DMA((4 * count,)),
            pltpu.SemaphoreType.DMA((count,)),
        ],
        compiler_params=pltpu.CompilerParams(vmem_limit_bytes=60 * 2**20),
        name="wide_out",
    )(meta, *wide_blocks)
    out_query, out_key, out_value, out_proj, gain_out = whole_call(
        functools.partial(heads_out_kernel, count, own_rows, extra),
        [
            shaped((own_rows, width), jnp.float32),
            shaped((own_rows, KVH * HD), jnp.float32),
            shaped((own_rows, KVH * HD), jnp.float32),
            shaped((own_rows, width), jnp.float32),
            shaped((extra, 2 * pair), jnp.float32),
        ],
        count,
        0,
        [pltpu.VMEM((count, own_rows, pair), jnp.float32)],
    )(meta, *heads_blocks)
    return (
        block_output[None],
        input_grad[None],
        out_query,
        out_key,
        out_value,
        out_proj,
        out_gate,
        out_up,
        out_down,
        gain_out[0],
        gain_out[1],
        gain_out[2, : query_gain.shape[0]],
        gain_out[3, : key_gain.shape[0]],
    )


def divides_heads(mesh):
    return mesh.shape["ctx"] == KVH and mesh.shape["fsdp"] == 4 and H == 2 * KVH


def solution(mesh):
    in_specs = (
        P("fsdp", "ctx", None),
        P("fsdp", None),
        P("fsdp", "ctx", None),
        P("fsdp", None),
        P("fsdp", None),
        P("fsdp", None),
        P("fsdp", None),
        P("fsdp", None),
        P("fsdp", None),
        P("fsdp", None),
        P("fsdp"),
        P("fsdp"),
        P("fsdp"),
        P("fsdp"),
    )
    out_specs = (
        P("fsdp", "ctx", None),
        P("fsdp", "ctx", None),
        P("fsdp", None),
        P("fsdp", None),
        P("fsdp", None),
        P("fsdp", None),
        P("fsdp", None),
        P("fsdp", None),
        P("fsdp", None),
        P("fsdp"),
        P("fsdp"),
        P("fsdp"),
        P("fsdp"),
    )
    if not divides_heads(mesh):
        return jax.shard_map(
            local, mesh=mesh, in_specs=in_specs, out_specs=out_specs, check_vma=False
        )

    return jax.shard_map(local_heads, mesh=mesh, in_specs=in_specs, out_specs=out_specs, check_vma=False)
```

```python
import functools
import math

import jax
import jax.numpy as jnp
from jax import lax
from jax.experimental import pallas as pl
from jax.experimental.pallas import tpu as pltpu
from jax.sharding import PartitionSpec as P

H = 16
KVH = 8
HD = 64


EPSILON = 1e-05
ROPE_BASE = 1000000.0
FLOOR_SCORE = -1e30


def place_rows(row_index, tokens, ctx_count):
    half_rows = tokens // 2
    device = row_index // tokens
    offset = row_index % tokens
    early = device * half_rows + offset
    late = (2 * ctx_count - 1 - device) * half_rows + offset - half_rows
    return jnp.where(offset < half_rows, early, late)


def doc_begin(starts, where_at):
    started = starts[None, :] <= where_at[:, None]
    return jnp.max(jnp.where(started, starts[None, :], 0), axis=1)


def rotary(positions):
    half_dim = HD // 2
    frequency = ROPE_BASE ** (-(2.0 * jnp.arange(half_dim, dtype=jnp.float32)) / HD)
    angles = positions.astype(jnp.float32)[:, None] * frequency[None, :]
    angles = jnp.concatenate([angles, angles], axis=1)
    return (jnp.cos(angles)[:, None, :], jnp.sin(angles)[:, None, :])


def rotate_pairs(values, cosine, sine_part):
    half_dim = values.shape[-1] // 2
    rolled = jnp.concatenate([-values[..., half_dim:], values[..., :half_dim]], axis=-1)
    return values * cosine + rolled * sine_part


def rotate_back(grads, cosine, sine_part):
    half_dim = grads.shape[-1] // 2
    moved = grads * sine_part
    rolled = jnp.concatenate([moved[..., half_dim:], -moved[..., :half_dim]], axis=-1)
    return grads * cosine + rolled


def unit_norm(values):
    scaling = lax.rsqrt(jnp.mean(values * values, axis=-1, keepdims=True) + EPSILON)
    return (values * scaling, scaling)


def norm_back(grad_out, normed, scaling, gain_row):
    weighted = grad_out * gain_row
    grad_in = scaling * (weighted - normed * jnp.mean(weighted * normed, axis=-1, keepdims=True))
    grad_gain = jnp.sum((grad_out * normed).reshape(-1, normed.shape[-1]), axis=0)
    return (grad_in, grad_gain)


def score_block(query_rows, key_rows, scaling):
    return (
        jnp.einsum("igrd,jgd->grij", query_rows, key_rows, preferred_element_type=jnp.float32)
        * scaling
    )


def visible_pairs(query_at, query_doc, key_at, key_doc):
    return (query_doc[:, None] == key_doc[None, :]) & (key_at[None, :] <= query_at[:, None])


def any_visible(query_at, query_doc, key_at):
    return (jnp.min(key_at) <= jnp.max(query_at)) & (jnp.max(key_at) >= jnp.min(query_doc))


def contract_rows(left, right):
    return lax.dot_general(
        left, right, (((0,), (0,)), ((), ())), preferred_element_type=jnp.float32
    )


def contract_cols(left, right):
    return lax.dot_general(
        left, right, (((1,), (1,)), ((), ())), preferred_element_type=jnp.float32
    )


def keep_same(totals):
    return totals


def local(
    block_input,
    doc_starts,
    out_grad,
    query_weight,
    key_weight,
    value_weight,
    output_weight,
    gate_weight,
    up_weight,
    down_weight,
    mixer_gain,
    feed_gain,
    query_gain,
    key_gain,
):
    tokens = block_input.shape[1]
    ctx_count = lax.axis_size("ctx")
    repeat = H // KVH
    kv_width = KVH * HD
    scaling = HD ** (-0.5)
    inputs = block_input[0].astype(jnp.float32)
    starts = doc_starts[0]
    where_at = place_rows(
        lax.axis_index("ctx") * tokens + jnp.arange(tokens, dtype=jnp.int32), tokens, ctx_count
    )
    begins = doc_begin(starts, where_at)
    cosine, sine_part = rotary(where_at - begins)
    gathered = (
        lax.all_gather(query_weight, "fsdp", axis=0, tiled=True),
        lax.all_gather(key_weight, "fsdp", axis=0, tiled=True),
        lax.all_gather(value_weight, "fsdp", axis=0, tiled=True),
        lax.all_gather(output_weight, "fsdp", axis=0, tiled=True),
        lax.all_gather(gate_weight, "fsdp", axis=0, tiled=True),
        lax.all_gather(up_weight, "fsdp", axis=0, tiled=True),
        lax.all_gather(down_weight, "fsdp", axis=0, tiled=True),
        lax.all_gather(mixer_gain, "fsdp", axis=0, tiled=True),
        lax.all_gather(feed_gain, "fsdp", axis=0, tiled=True),
        lax.all_gather(query_gain, "fsdp", axis=0, tiled=True),
        lax.all_gather(key_gain, "fsdp", axis=0, tiled=True),
    )
    full_query, full_key, full_value, full_proj, full_gate, full_up, full_down = gathered[:7]
    gain_mixer, gain_feed, gain_query, gain_key = [
        entry.astype(jnp.float32) for entry in gathered[7:]
    ]
    normed_in, scale_in = unit_norm(inputs)
    hidden_in = (normed_in * gain_mixer).astype(jnp.bfloat16)
    query_lin = jnp.dot(hidden_in, full_query, preferred_element_type=jnp.float32)
    key_lin = jnp.dot(hidden_in, full_key, preferred_element_type=jnp.float32)
    value_lin = jnp.dot(hidden_in, full_value, preferred_element_type=jnp.float32)
    query_normed, query_scale = unit_norm(query_lin.reshape(tokens, H, HD))
    key_normed, key_scale = unit_norm(key_lin.reshape(tokens, KVH, HD))
    query_att = (
        rotate_pairs(query_normed * gain_query, cosine, sine_part)
        .reshape(tokens, H * HD)
        .astype(jnp.bfloat16)
    )
    key_att = (
        rotate_pairs(key_normed * gain_key, cosine, sine_part)
        .reshape(tokens, kv_width)
        .astype(jnp.bfloat16)
    )
    value_att = value_lin.astype(jnp.bfloat16)
    query_four = query_att.reshape(tokens, KVH, repeat, HD)
    start_state = (
        jnp.full((KVH, repeat, tokens), FLOOR_SCORE, jnp.float32),
        jnp.zeros((KVH, repeat, tokens), jnp.float32),
        jnp.zeros((tokens, H * HD), jnp.float32),
    )
    key_part = lax.all_gather(key_att, "ctx", axis=0, tiled=True)
    value_part = lax.all_gather(value_att, "ctx", axis=0, tiled=True)
    rows = key_part.shape[0]
    width = math.gcd(math.gcd(rows, tokens // 2), 512)

    def forward_key_block(block_index, totals):
        offset = block_index * width
        key_rows = lax.dynamic_slice_in_dim(key_part, offset, width, 0).reshape(width, KVH, HD)
        value_rows = lax.dynamic_slice_in_dim(value_part, offset, width, 0).reshape(width, KVH, HD)
        key_at = place_rows(offset + jnp.arange(width, dtype=jnp.int32), tokens, ctx_count)

        def attend(totals):
            highest, total_mass, accum = totals
            visible = visible_pairs(where_at, begins, key_at, doc_begin(starts, key_at))
            scores = jnp.where(visible, score_block(query_four, key_rows, scaling), FLOOR_SCORE)
            new_high = jnp.maximum(highest, jnp.max(scores, axis=-1))
            rescale = jnp.exp(highest - new_high)
            probable = jnp.where(visible, jnp.exp(scores - new_high[..., None]), 0.0)
            total_mass = total_mass * rescale + jnp.sum(probable, axis=-1)
            part_out = jnp.einsum(
                "grij,jgd->igrd",
                probable.astype(jnp.bfloat16),
                value_rows,
                preferred_element_type=jnp.float32,
            )
            accum = (
                accum.reshape(tokens, KVH, repeat, HD)
                * jnp.transpose(rescale, (2, 0, 1))[..., None]
                + part_out
            )
            return (new_high, total_mass, accum.reshape(tokens, H * HD))

        return lax.cond(any_visible(where_at, begins, key_at), attend, keep_same, totals)

    highest, total_mass, accum = lax.fori_loop(0, rows // width, forward_key_block, start_state)
    lse_heads = highest + jnp.log(total_mass)
    attn_raw = (
        accum.reshape(tokens, KVH, repeat, HD) / jnp.transpose(total_mass, (2, 0, 1))[..., None]
    ).reshape(tokens, H * HD)
    attn_low = attn_raw.astype(jnp.bfloat16)
    mixed = inputs + jnp.dot(attn_low, full_proj, preferred_element_type=jnp.float32)
    normed_mid, scale_mid = unit_norm(mixed)
    hidden_mid = (normed_mid * gain_feed).astype(jnp.bfloat16)
    gate_lin = jnp.dot(hidden_mid, full_gate, preferred_element_type=jnp.float32)
    up_lin = jnp.dot(hidden_mid, full_up, preferred_element_type=jnp.float32)
    sigmoid_gate = jax.nn.sigmoid(gate_lin)
    activated = (gate_lin * sigmoid_gate * up_lin).astype(jnp.bfloat16)
    block_output = (
        mixed + jnp.dot(activated, full_down, preferred_element_type=jnp.float32)
    ).astype(jnp.bfloat16)
    regathered = (
        lax.all_gather(query_weight, "fsdp", axis=0, tiled=True),
        lax.all_gather(key_weight, "fsdp", axis=0, tiled=True),
        lax.all_gather(value_weight, "fsdp", axis=0, tiled=True),
        lax.all_gather(output_weight, "fsdp", axis=0, tiled=True),
        lax.all_gather(gate_weight, "fsdp", axis=0, tiled=True),
        lax.all_gather(up_weight, "fsdp", axis=0, tiled=True),
        lax.all_gather(down_weight, "fsdp", axis=0, tiled=True),
        lax.all_gather(mixer_gain, "fsdp", axis=0, tiled=True),
        lax.all_gather(feed_gain, "fsdp", axis=0, tiled=True),
        lax.all_gather(query_gain, "fsdp", axis=0, tiled=True),
        lax.all_gather(key_gain, "fsdp", axis=0, tiled=True),
    )
    full_query, full_key, full_value, full_proj, full_gate, full_up, full_down = regathered[:7]
    gain_mixer, gain_feed, gain_query, gain_key = [
        entry.astype(jnp.float32) for entry in regathered[7:]
    ]
    grad_top = out_grad[0].astype(jnp.float32)
    grad_top_low = grad_top.astype(jnp.bfloat16)
    grad_down = contract_rows(activated, grad_top_low)
    grad_act = contract_cols(grad_top_low, full_down)
    grad_gate_low = (
        grad_act * up_lin * sigmoid_gate * (1.0 + gate_lin * (1.0 - sigmoid_gate))
    ).astype(jnp.bfloat16)
    grad_up_low = (grad_act * gate_lin * sigmoid_gate).astype(jnp.bfloat16)
    grad_gate = contract_rows(hidden_mid, grad_gate_low)
    grad_up = contract_rows(hidden_mid, grad_up_low)
    grad_hidden_mid = contract_cols(grad_gate_low, full_gate) + contract_cols(grad_up_low, full_up)
    grad_normed_mid, grad_feed = norm_back(grad_hidden_mid, normed_mid, scale_mid, gain_feed)
    grad_mixed = grad_top + grad_normed_mid
    grad_mixed_low = grad_mixed.astype(jnp.bfloat16)
    grad_proj = contract_rows(attn_low, grad_mixed_low)
    grad_attn = contract_cols(grad_mixed_low, full_proj).astype(jnp.bfloat16)
    grad_four = grad_attn.reshape(tokens, KVH, repeat, HD)
    delta_heads = jnp.sum(
        grad_four.astype(jnp.float32) * attn_raw.reshape(tokens, KVH, repeat, HD), axis=-1
    )
    delta_grid = jnp.transpose(delta_heads, (1, 2, 0))
    lse_rows = jnp.transpose(lse_heads, (2, 0, 1)).reshape(tokens, H)
    delta_rows = delta_heads.reshape(tokens, H)
    query_key_part = lax.all_gather(key_att, "ctx", axis=0, tiled=True)
    query_value_part = lax.all_gather(value_att, "ctx", axis=0, tiled=True)
    rows = query_key_part.shape[0]
    query_width = math.gcd(math.gcd(rows, tokens // 2), 512)

    def query_key_block(block_index, grad_query_acc):
        offset = block_index * query_width
        key_rows = lax.dynamic_slice_in_dim(query_key_part, offset, query_width, 0).reshape(
            query_width, KVH, HD
        )
        value_rows = lax.dynamic_slice_in_dim(query_value_part, offset, query_width, 0).reshape(
            query_width, KVH, HD
        )
        key_at = place_rows(offset + jnp.arange(query_width, dtype=jnp.int32), tokens, ctx_count)

        def attend(grad_query_acc):
            visible = visible_pairs(where_at, begins, key_at, doc_begin(starts, key_at))
            scores = score_block(query_four, key_rows, scaling)
            probable = jnp.where(visible, jnp.exp(scores - lse_heads[..., None]), 0.0)
            grad_prob = jnp.einsum(
                "igrd,jgd->grij", grad_four, value_rows, preferred_element_type=jnp.float32
            )
            grad_score = (probable * (grad_prob - delta_grid[..., None])).astype(jnp.bfloat16)
            added = (
                jnp.einsum(
                    "grij,jgd->igrd", grad_score, key_rows, preferred_element_type=jnp.float32
                )
                * scaling
            )
            return grad_query_acc + added.reshape(tokens, H * HD)

        return lax.cond(any_visible(where_at, begins, key_at), attend, keep_same, grad_query_acc)

    grad_query_att = lax.fori_loop(
        0, rows // query_width, query_key_block, jnp.zeros((tokens, H * HD), jnp.float32)
    )
    lse_all, delta_all = (
        lax.all_gather(lse_rows.astype(jnp.bfloat16), "ctx", axis=0, tiled=True).astype(
            lse_rows.dtype
        ),
        lax.all_gather(delta_rows.astype(jnp.bfloat16), "ctx", axis=0, tiled=True).astype(
            delta_rows.dtype
        ),
    )
    key_three = key_att.reshape(tokens, KVH, HD)
    value_three = value_att.reshape(tokens, KVH, HD)
    empty_keys = jnp.zeros((tokens, kv_width), jnp.float32)
    query_part = lax.all_gather(query_att, "ctx", axis=0, tiled=True)
    grad_part = lax.all_gather(grad_attn, "ctx", axis=0, tiled=True)
    rows = query_part.shape[0]
    key_width = math.gcd(math.gcd(rows, tokens // 2), 512)

    def query_block(block_index, totals):
        offset = block_index * key_width
        query_rows = lax.dynamic_slice_in_dim(query_part, offset, key_width, 0).reshape(
            key_width, KVH, repeat, HD
        )
        grad_rows = lax.dynamic_slice_in_dim(grad_part, offset, key_width, 0).reshape(
            key_width, KVH, repeat, HD
        )
        query_at = place_rows(offset + jnp.arange(key_width, dtype=jnp.int32), tokens, ctx_count)
        query_doc = doc_begin(starts, query_at)
        lse_block = jnp.transpose(
            lax.dynamic_slice_in_dim(lse_all, offset, key_width, 0).reshape(key_width, KVH, repeat),
            (1, 2, 0),
        )
        delta_block = jnp.transpose(
            lax.dynamic_slice_in_dim(delta_all, offset, key_width, 0).reshape(
                key_width, KVH, repeat
            ),
            (1, 2, 0),
        )

        def attend(totals):
            grad_key_acc, grad_value_acc = totals
            visible = visible_pairs(query_at, query_doc, where_at, begins)
            scores = score_block(query_rows, key_three, scaling)
            probable = jnp.where(visible, jnp.exp(scores - lse_block[..., None]), 0.0)
            grad_prob = jnp.einsum(
                "igrd,jgd->grij", grad_rows, value_three, preferred_element_type=jnp.float32
            )
            grad_score = (probable * (grad_prob - delta_block[..., None])).astype(jnp.bfloat16)
            value_added = jnp.einsum(
                "grij,igrd->jgd",
                probable.astype(jnp.bfloat16),
                grad_rows,
                preferred_element_type=jnp.float32,
            )
            key_added = (
                jnp.einsum(
                    "grij,igrd->jgd", grad_score, query_rows, preferred_element_type=jnp.float32
                )
                * scaling
            )
            return (
                grad_key_acc + key_added.reshape(tokens, kv_width),
                grad_value_acc + value_added.reshape(tokens, kv_width),
            )

        return lax.cond(any_visible(query_at, query_doc, where_at), attend, keep_same, totals)

    grad_key_att, grad_value_att = lax.fori_loop(
        0, rows // key_width, query_block, (empty_keys, empty_keys)
    )
    grad_query_unit = rotate_back(grad_query_att.reshape(tokens, H, HD), cosine, sine_part)
    grad_query_lin, grad_qgain = norm_back(grad_query_unit, query_normed, query_scale, gain_query)
    grad_key_unit = rotate_back(grad_key_att.reshape(tokens, KVH, HD), cosine, sine_part)
    grad_key_lin, grad_kgain = norm_back(grad_key_unit, key_normed, key_scale, gain_key)
    grad_query_low = grad_query_lin.reshape(tokens, H * HD).astype(jnp.bfloat16)
    grad_key_low = grad_key_lin.reshape(tokens, kv_width).astype(jnp.bfloat16)
    grad_value_low = grad_value_att.astype(jnp.bfloat16)
    grad_query = contract_rows(hidden_in, grad_query_low)
    grad_key = contract_rows(hidden_in, grad_key_low)
    grad_value = contract_rows(hidden_in, grad_value_low)
    grad_hidden_in = (
        contract_cols(grad_query_low, full_query)
        + contract_cols(grad_key_low, full_key)
        + contract_cols(grad_value_low, full_value)
    )
    grad_normed_in, grad_mixer = norm_back(grad_hidden_in, normed_in, scale_in, gain_mixer)
    input_grad = grad_mixed + grad_normed_in
    parts = (
        lax.psum_scatter(
            grad_query.astype(jnp.bfloat16), "fsdp", scatter_dimension=0, tiled=True
        ).astype(jnp.float32),
        lax.psum_scatter(
            grad_key.astype(jnp.bfloat16), "fsdp", scatter_dimension=0, tiled=True
        ).astype(jnp.float32),
        lax.psum_scatter(
            grad_value.astype(jnp.bfloat16), "fsdp", scatter_dimension=0, tiled=True
        ).astype(jnp.float32),
        lax.psum_scatter(
            grad_proj.astype(jnp.bfloat16), "fsdp", scatter_dimension=0, tiled=True
        ).astype(jnp.float32),
        lax.psum_scatter(
            grad_gate.astype(jnp.bfloat16), "fsdp", scatter_dimension=0, tiled=True
        ).astype(jnp.float32),
        lax.psum_scatter(
            grad_up.astype(jnp.bfloat16), "fsdp", scatter_dimension=0, tiled=True
        ).astype(jnp.float32),
        lax.psum_scatter(
            grad_down.astype(jnp.bfloat16), "fsdp", scatter_dimension=0, tiled=True
        ).astype(jnp.float32),
        lax.psum_scatter(
            grad_mixer.astype(jnp.bfloat16), "fsdp", scatter_dimension=0, tiled=True
        ).astype(jnp.float32),
        lax.psum_scatter(
            grad_feed.astype(jnp.bfloat16), "fsdp", scatter_dimension=0, tiled=True
        ).astype(jnp.float32),
        lax.psum_scatter(
            grad_qgain.astype(jnp.bfloat16), "fsdp", scatter_dimension=0, tiled=True
        ).astype(jnp.float32),
        lax.psum_scatter(
            grad_kgain.astype(jnp.bfloat16), "fsdp", scatter_dimension=0, tiled=True
        ).astype(jnp.float32),
    )
    summed = (
        lax.psum(parts[0].astype(jnp.bfloat16), "ctx").astype(jnp.float32),
        lax.psum(parts[1].astype(jnp.bfloat16), "ctx").astype(jnp.float32),
        lax.psum(parts[2].astype(jnp.bfloat16), "ctx").astype(jnp.float32),
        lax.psum(parts[3].astype(jnp.bfloat16), "ctx").astype(jnp.float32),
        lax.psum(parts[4].astype(jnp.bfloat16), "ctx").astype(jnp.float32),
        lax.psum(parts[5].astype(jnp.bfloat16), "ctx").astype(jnp.float32),
        lax.psum(parts[6].astype(jnp.bfloat16), "ctx").astype(jnp.float32),
        lax.psum(parts[7].astype(jnp.bfloat16), "ctx").astype(jnp.float32),
        lax.psum(parts[8].astype(jnp.bfloat16), "ctx").astype(jnp.float32),
        lax.psum(parts[9].astype(jnp.bfloat16), "ctx").astype(jnp.float32),
        lax.psum(parts[10].astype(jnp.bfloat16), "ctx").astype(jnp.float32),
    )
    return (
        block_output[None],
        input_grad[None],
        summed[0],
        summed[1],
        summed[2],
        summed[3],
        summed[4],
        summed[5],
        summed[6],
        summed[7],
        summed[8],
        summed[9],
        summed[10],
    )


ORDER = (0, 1, 2, 4, 3, 5, 6, 7)


def flipped(bits, count):
    return [(index, index ^ bits) for index in range(count)]


def swap_ctx(values, bits):
    return lax.ppermute(values, "ctx", flipped(bits, lax.axis_size("ctx")))


def behind(values, *ready):
    return lax.optimization_barrier((values,) + ready)[0]


def dot_nn(left, right):
    return lax.dot_general(
        left, right, (((1,), (0,)), ((), ())), preferred_element_type=jnp.float32
    )


def dot_nt(left, right):
    return lax.dot_general(
        left, right, (((1,), (1,)), ((), ())), preferred_element_type=jnp.float32
    )


def wide(values):
    return values.astype(jnp.float32)


def gather_near(block):
    return swap_ctx(block, 2), swap_ctx(block, 4), swap_ctx(block, 1)


def gather_corner(across, along):
    half = across.shape[0] // 2
    first = swap_ctx(along[:half], 2)
    second = swap_ctx(across[half:], 4)
    return jnp.concatenate([first, second], axis=0)


def gather_far(across, along, corner, *ready):
    return [swap_ctx(behind(part, *ready), 1) for part in (across, along, corner)]


def gather_plane(block, *ready):
    across, along, partner = gather_near(block)
    corner = gather_corner(across, along)
    others = gather_far(across, along, corner, *ready)
    return [block, partner, across, others[0], along, others[1], corner, others[2]]


def gather_direct(block, *ready):
    across, along, partner = gather_near(block)
    corner = swap_ctx(block, 6)
    others = gather_far(across, along, corner, *ready)
    return [block, partner, across, others[0], along, others[1], corner, others[2]]


def scatter_pair(blocks):
    got = [swap_ctx(blocks[bits], 1) for bits in (3, 5, 7, 1)]
    sums = [
        (wide(blocks[bits]) + wide(other)).astype(jnp.bfloat16)
        for bits, other in zip((2, 4, 6), got)
    ]
    return [blocks[0], got[3]], sums


def scatter_links(sums):
    return [swap_ctx(part, bits) for bits, part in zip((2, 4, 6), sums)]


def exchange_plane(blocks):
    return [blocks[0]] + [swap_ctx(blocks[bits], bits) for bits in range(1, 8)]


def shift_fsdp(values, pairs):
    return lax.ppermute(values, "fsdp", pairs)


def slot_of(bits):
    return jnp.where(bits == 3, 4, jnp.where(bits == 4, 3, bits))


def row_of(place, here, tokens, count):
    half = tokens // 2
    device = jnp.where(place < count, place, 2 * count - 1 - place)
    late = jnp.where(place < count, 0, half)
    return slot_of(lax.bitwise_xor(device, here)) * tokens + late


def swap_half(values, low_lane):
    return jnp.where(low_lane, pltpu.roll(values, 96, 1), pltpu.roll(values, 32, 1))


def head_blocks():
    shape = (2 * HD, 2 * HD)
    row = lax.broadcasted_iota(jnp.int32, shape, 0) < HD
    column = lax.broadcasted_iota(jnp.int32, shape, 1) < HD
    return jnp.where(row == column, 1.0 / HD, 0.0).astype(jnp.bfloat16)


def head_mean(values, blocks):
    high = values.astype(jnp.bfloat16)
    rest = (values - wide(high)).astype(jnp.bfloat16)
    return dot_nn(high, blocks) + dot_nn(rest, blocks)


def lane_masks(rows):
    lanes = lax.broadcasted_iota(jnp.int32, (rows, 2 * HD), 1)
    return lanes < HD, (lanes % HD) < (HD // 2)


def two_heads(values):
    first, _ = lane_masks(values.shape[0])
    zero = jnp.zeros_like(values)
    return jnp.concatenate(
        [jnp.where(first, values, zero), jnp.where(first, zero, values)], axis=0
    )


def begin_at(meta_ref, docs, where_at):
    begin = jnp.zeros_like(where_at)
    for doc in range(docs):
        begin = jnp.where(meta_ref[2 + doc] <= where_at, meta_ref[2 + doc], begin)
    return begin


def block_visible(meta_ref, docs, query_block, key_block, size):
    query_at = query_block * size + lax.broadcasted_iota(jnp.int32, (1, size), 1)
    begin = begin_at(meta_ref, docs, query_at)
    key_at = key_block * size + lax.broadcasted_iota(jnp.int32, (size, size), 0)
    return (key_at <= query_at) & (key_at >= begin)


def pair_tile(ref):
    return 2 * HD if ref.shape[0] % (4 * HD) == 0 else ref.shape[0] // 2


def aligned(value, size):
    return pl.multiple_of(value, size)


def take_heads_kernel(
    meta_ref, query_ref, key_ref, value_ref, proj_ref, mixer_ref, feed_ref, query_gain_ref, key_gain_ref,
    out_ref, gains, windows, proj, sem,
):
    here = meta_ref[0]
    rows = query_ref.shape[0]
    pair = 2 * HD
    start = aligned(lax.shift_right_logical(here, 1) * pair, pair)
    part = proj.shape[0]
    copies = [
        pltpu.make_async_copy(
            query_ref.at[:, pl.ds(aligned(here * pair, pair), pair)], windows.at[0], sem.at[0]
        ),
        pltpu.make_async_copy(key_ref.at[:, pl.ds(start, pair)], windows.at[1], sem.at[1]),
        pltpu.make_async_copy(value_ref.at[:, pl.ds(start, pair)], windows.at[2], sem.at[2]),
        pltpu.make_async_copy(
            proj_ref.at[pl.ds(aligned(here * part, part), part), :], proj, sem.at[3]
        ),
    ]
    for copy in copies:
        copy.start()
    gains[...] = jnp.zeros_like(gains)
    for row, ref in enumerate((mixer_ref, feed_ref, query_gain_ref, key_gain_ref)):
        gains[row : row + 1, : ref.shape[0]] = wide(ref[...]).reshape(1, ref.shape[0])
    extra = gains.shape[0]
    out_ref[rows : rows + extra, :] = gains[...].astype(jnp.bfloat16)
    for copy in copies:
        copy.wait()
    out_ref[:rows, :pair] = windows[0]
    odd = lax.bitwise_and(here, 1) == 1
    keys = wide(windows[1])
    values = wide(windows[2])
    first, _ = lane_masks(rows)
    keys = jnp.where(odd, pltpu.roll(keys, HD, 1), keys)
    values = jnp.where(odd, values, pltpu.roll(values, HD, 1))
    out_ref[:rows, pair:] = jnp.where(first, keys, values).astype(jnp.bfloat16)
    for index in range(proj.shape[1] // (2 * pair)):
        target = rows + extra + index * part
        out_ref[target : target + part, :] = proj[:, index * 2 * pair : (index + 1) * 2 * pair]


def arrange_heads_kernel(
    extra, meta_ref, *refs
):
    pieces, (weight_ref, mixer_ref, feed_ref, gains_ref, proj_ref) = refs[:4], refs[4:]
    shard = meta_ref[1]
    rows = weight_ref.shape[0] // 4
    pair = 2 * HD
    each = HD // 4
    gains = jnp.zeros((8, pair), jnp.float32)
    part = proj_ref.shape[0] // 4
    for bits, piece in enumerate(pieces):
        owner = lax.bitwise_xor(shard, bits)
        weight_ref[pl.ds(aligned(owner * rows, rows), rows), :] = piece[:rows, :]
        block = wide(piece[rows : rows + extra, :])
        lanes = pl.ds(aligned(owner * rows, rows), rows)
        mixer_ref[:, lanes] = block[0:1, :]
        feed_ref[:, lanes] = block[1:2, :]
        gains = gains + pltpu.roll(block[:8, :pair], owner * each, 1)
        for index in range(proj_ref.shape[1] // (2 * pair)):
            source = rows + extra + index * part
            proj_ref[
                pl.ds(aligned(owner * part, part), part), index * 2 * pair : (index + 1) * 2 * pair
            ] = piece[source : source + part, :]
    gains_ref[...] = gains + pltpu.roll(gains, HD, 1)


def take_wide_kernel(
    shards, meta_ref, gate_ref, up_ref, down_ref, out_ref, lasts, rows, sem, last_sem, down_sem,
):
    here = meta_ref[0]
    own_rows = lasts.shape[1]
    inner = out_ref.shape[1] // 2
    main = inner // 128 * 128
    each = (inner - main) // shards
    span = gate_ref.shape[1] // shards
    left = span - 128
    copies, last_copies = [], []
    for kind, source in enumerate((gate_ref, up_ref)):
        for part in range(shards):
            place = kind * shards + part
            copies.append(
                pltpu.make_async_copy(
                    source.at[:, pl.ds(aligned(part * span + here * 128, 128), 128)],
                    out_ref.at[pl.ds(0, own_rows), pl.ds(place * 128, 128)],
                    sem.at[place],
                )
            )
            last_copies.append(
                pltpu.make_async_copy(
                    source.at[:, pl.ds(part * span + left, 128)], lasts.at[place], last_sem.at[place]
                )
            )
    down_copies = [
        pltpu.make_async_copy(
            down_ref.at[pl.ds(aligned(here * 128, 128), 128), :],
            rows.at[pl.ds(0, 128), :],
            down_sem.at[0],
        ),
        pltpu.make_async_copy(
            down_ref.at[pl.ds(aligned(left + here * each, each), each), :],
            rows.at[pl.ds(128, each), :],
            down_sem.at[1],
        ),
    ]
    for copy in copies + last_copies + down_copies:
        copy.start()
    lanes = lax.broadcasted_iota(jnp.int32, (own_rows, 128), 1)
    total = jnp.zeros((own_rows, 128), jnp.float32)
    for place, copy in enumerate(last_copies):
        copy.wait()
        moved = pltpu.roll(wide(lasts[place]), 128 - here * each + place * each, 1)
        total = jnp.where((lanes >= place * each) & (lanes < (place + 1) * each), moved, total)
    out_ref[:own_rows, 2 * main :] = total.astype(jnp.bfloat16)
    for copy in copies + down_copies:
        copy.wait()
    out_ref[own_rows:, : rows.shape[1]] = rows[...]
    out_ref[own_rows:, rows.shape[1] :] = jnp.zeros_like(out_ref[own_rows:, rows.shape[1] :])


def head_linear_kernel(number, meta_ref, *refs):
    sources, (weight_ref, gain_ref, hidden_ref, linear_ref, rows, sem) = refs[:number], refs[number:]
    step = pl.program_id(0)
    size = sources[0].shape[0]

    def move(index):
        return pltpu.make_async_copy(
            sources[index], rows.at[index // 2, pl.ds(index % 2 * size, size), :], sem.at[index]
        )

    @pl.when(step == 0)
    def _():
        for index in range(number):
            move(index).start()

    for index in range(number // 2):

        @pl.when(step == index)
        def _(index=index):
            move(2 * index).wait()
            move(2 * index + 1).wait()

    values = wide(rows[step])
    scale = lax.rsqrt(jnp.mean(values * values, axis=1, keepdims=True) + EPSILON)
    hidden_ref[...] = (values * scale * gain_ref[...]).astype(jnp.bfloat16)
    linear_ref[...] = dot_nn(hidden_ref[...], weight_ref[...])


def attention_kernel(
    tokens, count, docs,
    meta_ref, lin_ref, cos_ref, sin_ref, gains_ref,
    query_ref, key_ref, value_ref, attn_ref, lse_ref, *refs,
):
    low_refs, (value_t, accum, low, blocks_ref) = refs[:count], refs[count:]
    blocks_ref[...] = head_blocks()
    here = meta_ref[0]
    half = tokens // 2
    size = tokens
    blocks = count

    def prepare(place, carry):
        first, low_lane = lane_masks(half)
        source = aligned(row_of(place, here, tokens, count), half)
        target = aligned(place * half, half)
        cosine = cos_ref[pl.ds(target, half), :]
        sine = sin_ref[pl.ds(target, half), :]
        query = lin_ref[pl.ds(source, half), : 2 * HD]
        unit = query * lax.rsqrt(head_mean(query * query, blocks_ref[...]) + EPSILON) * gains_ref[2:3, :]
        turned = unit * cosine + swap_half(unit, low_lane) * sine
        query_ref[pl.ds(target, half), :] = (
            turned.astype(jnp.bfloat16).astype(jnp.float32) * (HD**-0.5)
        ).astype(jnp.bfloat16)
        both = lin_ref[pl.ds(source, half), 2 * HD :]
        unit = both * lax.rsqrt(head_mean(both * both, blocks_ref[...]) + EPSILON) * gains_ref[3:4, :]
        turned = unit * cosine + swap_half(unit, low_lane) * sine
        key_ref[pl.ds(target, half), :] = jnp.where(
            first, turned, pltpu.roll(turned, HD, 1)
        ).astype(jnp.bfloat16)
        values = jnp.where(first, pltpu.roll(both, HD, 1), both)
        value_ref[pl.ds(target, half), :] = values.astype(jnp.bfloat16)
        return carry

    lax.fori_loop(0, 2 * count, prepare, 0)

    def turn_values(block, carry):
        values = wide(value_ref[pl.ds(aligned(block * size, size), size), :])
        value_t[block, :HD, :] = values.T[:HD].astype(jnp.bfloat16)
        value_t[block, HD:, :] = jnp.ones((value_t.shape[1] - HD, size), jnp.bfloat16)
        return carry

    lax.fori_loop(0, blocks, turn_values, 0)

    def query_step(block, carry):
        query = two_heads(query_ref[pl.ds(aligned(block * size, size), size), :])
        accum[...] = jnp.zeros_like(accum)
        lowest = begin_at(meta_ref, docs, block * size) // size

        def key_step(other, carry):
            keys = key_ref[pl.ds(aligned(other * size, size), size), :]
            scores = dot_nt(keys, query)
            visible = block_visible(meta_ref, docs, block, other, size)
            probable = jnp.concatenate(
                [
                    jnp.where(visible, jnp.exp(scores[:, :size]), 0.0),
                    jnp.where(visible, jnp.exp(scores[:, size:]), 0.0),
                ],
                axis=1,
            ).astype(jnp.bfloat16)
            accum[...] += dot_nn(value_t[other], probable)
            return carry

        lax.fori_loop(lowest, block + 1, key_step, 0)
        mass = accum[HD : HD + 1, :]
        mixed = accum[:HD, :] / mass
        lse_ref[block] = jnp.log(mass)
        rows = jnp.concatenate([mixed[:, :size], mixed[:, size:]], axis=0).T
        attn_ref[pl.ds(aligned(block * size, size), size), :] = rows
        for part in range(2):
            target = aligned(row_of(2 * block + part, here, tokens, count), half)
            low[pl.ds(target, half), :] = rows[part * half : (part + 1) * half].astype(jnp.bfloat16)
        return carry

    lax.fori_loop(0, blocks, query_step, 0)
    for slot, bits in enumerate(ORDER):
        low_refs[bits][...] = low[slot * tokens : (slot + 1) * tokens, :]


def attention_back_kernel(
    tokens, count, docs,
    meta_ref, lin_ref, cos_ref, sin_ref, gains_ref,
    query_ref, key_ref, value_ref, attn_ref, lse_ref, *refs,
):
    grad_refs = refs[:count]
    out_ref, gain_ref = refs[count : count + 2]
    block_refs = refs[count + 2 : 2 * count + 2]
    key_t, grad_query, grad_key, grad_value, accum, grad_rows, blocks_ref = refs[2 * count + 2 :]
    blocks_ref[...] = head_blocks()
    here = meta_ref[0]
    half = tokens // 2
    size = tokens
    blocks = count
    grad_key[...] = jnp.zeros_like(grad_key)
    grad_value[...] = jnp.zeros_like(grad_value)
    gain_ref[...] = jnp.zeros_like(gain_ref)
    for slot, bits in enumerate(ORDER):
        grad_rows[slot * tokens : (slot + 1) * tokens, :] = grad_refs[bits][...]

    def turn_keys(block, carry):
        keys = wide(key_ref[pl.ds(aligned(block * size, size), size), :])
        key_t[block] = keys.T[:HD].astype(jnp.bfloat16)
        return carry

    lax.fori_loop(0, blocks, turn_keys, 0)

    def query_step(block, carry):
        here_rows = pl.ds(aligned(block * size, size), size)
        query = two_heads(query_ref[here_rows, :])
        parts = []
        for part in range(2):
            source = aligned(row_of(2 * block + part, here, tokens, count), half)
            parts.append(grad_rows[pl.ds(source, half), :])
        grads = jnp.concatenate(parts, axis=0)
        products = (wide(grads) * attn_ref[here_rows, :]).T
        deltas = (
            jnp.sum(products[:HD], axis=0, keepdims=True),
            jnp.sum(products[HD:], axis=0, keepdims=True),
        )
        grads = two_heads(grads)
        lse = lse_ref[block]
        accum[...] = jnp.zeros_like(accum)
        lowest = begin_at(meta_ref, docs, block * size) // size

        def key_step(other, carry):
            rows = pl.ds(aligned(other * size, size), size)
            scores = dot_nt(key_ref[rows, :], query)
            grad_prob = dot_nt(value_ref[rows, :], grads)
            visible = block_visible(meta_ref, docs, block, other, size)
            probs, grad_scores = [], []
            for head in range(2):
                cols = slice(head * size, (head + 1) * size)
                prob = jnp.where(visible, jnp.exp(scores[:, cols] - lse[:, cols]), 0.0)
                probs.append(prob)
                grad_scores.append(prob * (grad_prob[:, cols] - deltas[head]))
            probs = jnp.concatenate(probs, axis=1).astype(jnp.bfloat16)
            grad_scores = jnp.concatenate(grad_scores, axis=1).astype(jnp.bfloat16)
            grad_value[rows, :] += dot_nn(probs, grads)
            grad_key[rows, :] += dot_nn(grad_scores, query)
            accum[...] += dot_nn(key_t[other], grad_scores)
            return carry

        lax.fori_loop(lowest, block + 1, key_step, 0)
        total = accum[...] * (HD**-0.5)
        grad_query[here_rows, :] = jnp.concatenate([total[:, :size], total[:, size:]], axis=0).T
        return carry

    lax.fori_loop(0, blocks, query_step, 0)

    def finish(place, carry):
        first, low_lane = lane_masks(half)
        source = aligned(row_of(place, here, tokens, count), half)
        target = pl.ds(aligned(place * half, half), half)
        cosine = cos_ref[target, :]
        sine = sin_ref[target, :]

        def through(linear, grads, gain):
            scale = lax.rsqrt(head_mean(linear * linear, blocks_ref[...]) + EPSILON)
            normed = linear * scale
            turned = grads * cosine + swap_half(grads * sine, low_lane)
            weighted = turned * gain
            grad_in = scale * (weighted - normed * head_mean(weighted * normed, blocks_ref[...]))
            return grad_in, jnp.sum(turned * normed, axis=0, keepdims=True)

        grad_in, gain_row = through(
            lin_ref[pl.ds(source, half), : 2 * HD], grad_query[target, :], gains_ref[2:3, :]
        )
        out_ref[pl.ds(source, half), : 2 * HD] = grad_in.astype(jnp.bfloat16)
        gain_ref[0:1, :] += gain_row
        keys = grad_key[target, :]
        grad_in, gain_row = through(
            lin_ref[pl.ds(source, half), 2 * HD :], keys + pltpu.roll(keys, HD, 1), gains_ref[3:4, :]
        )
        gain_ref[1:2, :] += gain_row
        values = grad_value[target, :]
        values = values + pltpu.roll(values, HD, 1)
        out_ref[pl.ds(source, half), 2 * HD :] = jnp.where(first, grad_in, values).astype(
            jnp.bfloat16
        )
        return carry

    lax.fori_loop(0, 2 * count, finish, 0)
    for slot, bits in enumerate(ORDER):
        block_refs[bits][...] = out_ref[slot * tokens : (slot + 1) * tokens, :]


def proj_grad_kernel(parts, meta_ref, attn_ref, grad_ref, *refs):
    blocks, full = refs[:-1], refs[-1]
    count = len(blocks)
    here = meta_ref[0]
    tile = 2 * pair_tile(full)

    def outer(index, carry):
        part = pl.ds(aligned(index * tile, tile), tile)
        full[part, :] = contract_rows(attn_ref[:, part], grad_ref[...]).astype(jnp.bfloat16)
        return carry

    lax.fori_loop(0, full.shape[0] // tile, outer, 0)
    rows = blocks[0].shape[0] // parts
    for bits, block in enumerate(blocks):
        owner = lax.bitwise_xor(here, bits)
        for part in range(parts):
            source = aligned(part * count * rows + owner * rows, rows)
            block[part * rows : (part + 1) * rows, :] = full[pl.ds(source, rows), :]


def pack_heads_kernel(
    extra, meta_ref, heads_ref, mixer_ref, gain_ref, feed_ref, sums_ref, *refs
):
    proj_refs, pieces = refs[:5], refs[5:]
    shard = meta_ref[1]
    rows = heads_ref.shape[0] // 4
    pair = 2 * HD
    proj = wide(proj_refs[0][...])
    for other in proj_refs[1:]:
        proj = proj + wide(other[...])
    proj_low, mixer, _, gains = pieces[4:]
    pieces = pieces[:4]
    part = proj.shape[0] // 4
    proj_low[...] = proj.astype(jnp.bfloat16)
    mixer[...] = mixer_ref[...] / gain_ref[...]
    values = sums_ref[...]
    lower = lax.broadcasted_iota(jnp.int32, values.shape, 0) == 0
    values = values + jnp.where(lower, pltpu.roll(values, HD, 1), 0.0)
    each = HD // 4
    lanes = lax.broadcasted_iota(jnp.int32, values.shape, 1)
    for bits, piece in enumerate(pieces):
        owner = lax.bitwise_xor(shard, bits)
        piece[:rows, :] = heads_ref[pl.ds(aligned(owner * rows, rows), rows), :]
        gains[...] = jnp.zeros_like(gains)
        own = pl.ds(aligned(owner * rows, rows), rows)
        gains[0:1, :] = mixer[:, own]
        gains[1:2, :] = feed_ref[:, own]
        moved = pltpu.roll(values, pair - owner * each, 1)
        moved = jnp.where(lanes < each, moved, 0.0)
        gains[2:4, :pair] = moved[0:2, :]
        piece[rows : rows + extra, :] = gains[...].astype(jnp.bfloat16)
        for index in range(proj.shape[1] // (2 * pair)):
            target = rows + extra + index * part
            piece[target : target + part, :] = proj_low[
                pl.ds(aligned(owner * part, part), part), index * 2 * pair : (index + 1) * 2 * pair
            ]


def file_down(piece_ref, down_ref, rows, owner):
    width = down_ref.shape[1]
    each = piece_ref.shape[0] - rows - 128
    piece_ref[rows : rows + 128, :width] = down_ref[pl.ds(aligned(owner * 128, 128), 128), :]
    piece_ref[rows + 128 :, :width] = down_ref[pl.ds(aligned(4 * 128 + owner * each, 16), each), :]
    piece_ref[rows:, width:] = jnp.zeros_like(piece_ref[rows:, width:])


def first_piece_kernel(meta_ref, hidden_ref, grad_ref, down_ref, piece_ref, total):
    step = pl.program_id(0)
    rows = total.shape[0]
    product = contract_rows(hidden_ref[...], grad_ref[...])

    @pl.when(step == 0)
    def _():
        total[...] = product

    @pl.when(step > 0)
    def _():
        total[...] += product

    @pl.when(step == pl.num_programs(0) - 1)
    def _():
        piece_ref[:rows, :] = total[...].astype(jnp.bfloat16)
        file_down(piece_ref, down_ref, rows, lax.bitwise_xor(meta_ref[1], 3))


def first_piece_call(meta, hidden, grads, down, rows, inner):
    stream, _ = hidden.shape
    columns = grads.shape[1]
    size = stream // 4
    return pl.pallas_call(
        first_piece_kernel,
        out_shape=shaped((rows + inner, columns)),
        grid_spec=pltpu.PrefetchScalarGridSpec(
            num_scalar_prefetch=1,
            grid=(4,),
            in_specs=[
                pl.BlockSpec((size, rows), lambda step, meta_ref: (step, lax.bitwise_xor(meta_ref[1], 3))),
                pl.BlockSpec((size, columns), lambda step, meta_ref: (step, 0)),
                pl.BlockSpec(down.shape, lambda step, meta_ref: (0, 0)),
            ],
            out_specs=pl.BlockSpec((rows + inner, columns), lambda step, meta_ref: (0, 0)),
            scratch_shapes=[pltpu.VMEM((rows, columns), jnp.float32)],
        ),
        cost_estimate=pl.CostEstimate(
            flops=2 * stream * rows * columns, bytes_accessed=stream * columns * 2, transcendentals=0
        ),
        compiler_params=pltpu.CompilerParams(vmem_limit_bytes=16 * 2**20),
        name="first_piece",
    )(meta, hidden, grads, down)


def pack_feed_kernel(meta_ref, wide_ref, down_ref, *pieces):
    shard = meta_ref[1]
    rows = wide_ref.shape[0] // 4
    for bits, piece in enumerate(pieces):
        owner = lax.bitwise_xor(shard, bits)
        piece[:rows, :] = wide_ref[pl.ds(aligned(owner * rows, 16), rows), :]
        file_down(piece, down_ref, rows, owner)


def input_grad_kernel(count, meta_ref, *refs):
    grads, weights = refs[:count], refs[count : 2 * count]
    input_ref, grad_ref, gain_ref, out_ref = refs[2 * count :]
    total = dot_nt(grads[0][...], weights[0][...])
    for left, right in zip(grads[1:], weights[1:]):
        total = total + dot_nt(left[...], right[...])
    values = wide(input_ref[...])
    scale = lax.rsqrt(jnp.mean(values * values, axis=1, keepdims=True) + EPSILON)
    normed = values * scale
    weighted = total * gain_ref[...]
    grad_in = scale * (weighted - normed * jnp.mean(weighted * normed, axis=1, keepdims=True))
    out_ref[...] = grad_ref[...] + grad_in


def project_kernel(count, parts, start, meta_ref, *refs):
    attn_refs, weight_refs, rest = refs[:count], refs[count : 2 * count], refs[2 * count :]
    input_ref, gain_ref, full_ref, attn_out_ref, mixed_ref, hidden_ref, attn_sem, weight_sem = rest
    here = meta_ref[0]
    rows = (weight_refs[0].shape[0] - start) // parts
    copies = []
    for bits in range(count):
        owner = lax.bitwise_xor(here, bits)
        copies.append(
            pltpu.make_async_copy(
                attn_refs[bits],
                attn_out_ref.at[:, pl.ds(aligned(owner * 2 * HD, 2 * HD), 2 * HD)],
                attn_sem.at[bits],
            )
        )
        for part in range(parts):
            target = aligned(part * count * rows + owner * rows, rows)
            copies.append(
                pltpu.make_async_copy(
                    weight_refs[bits].at[pl.ds(start + part * rows, rows), :],
                    full_ref.at[pl.ds(target, rows), :],
                    weight_sem.at[bits * parts + part],
                )
            )
    for copy in copies:
        copy.start()
    for copy in copies:
        copy.wait()
    tile = 2 * pair_tile(full_ref)

    def project(index, carry):
        part = pl.ds(aligned(index * tile, tile), tile)
        mixed_ref[:, part] = wide(input_ref[:, part]) + dot_nn(attn_out_ref[...], full_ref[:, part])
        return carry

    lax.fori_loop(0, full_ref.shape[1] // tile, project, 0)
    mixed = mixed_ref[...]
    scale = lax.rsqrt(jnp.mean(mixed * mixed, axis=1, keepdims=True) + EPSILON)
    hidden_ref[...] = (mixed * scale * gain_ref[...]).astype(jnp.bfloat16)


def feed_block(hidden_ref, grad_ref, wide_ref, down_ref, act_ref, grad_wide_ref, out_ref, back_ref):
    tokens = hidden_ref.shape[0]
    inner = wide_ref.shape[1] // 2
    main = inner // 128 * 128
    first, _ = lane_masks(tokens)

    def activate(gate, up, grad_act):
        sigmoid = 1.0 / (1.0 + jnp.exp(-gate))
        silu = gate * sigmoid
        grad_gate = grad_act * up * sigmoid * (1.0 + gate * (1.0 - sigmoid))
        return silu * up, grad_gate, grad_act * silu

    both = dot_nn(hidden_ref[...], wide_ref[...])
    grad_act = dot_nt(grad_ref[...], down_ref[...])
    act, grad_gate, grad_up = activate(
        both[:, :main], both[:, main : 2 * main], grad_act[:, :main]
    )
    act_ref[:, :main] = act.astype(jnp.bfloat16)
    grad_wide_ref[:, :main] = grad_gate.astype(jnp.bfloat16)
    grad_wide_ref[:, main : 2 * main] = grad_up.astype(jnp.bfloat16)
    last = both[:, 2 * main :]
    act, grad_gate, grad_up = activate(last, pltpu.roll(last, HD, 1), grad_act[:, main:])
    act_ref[:, main:] = jnp.where(first, act, 0.0).astype(jnp.bfloat16)
    grad_wide_ref[:, 2 * main :] = jnp.where(
        first, grad_gate, pltpu.roll(grad_up, HD, 1)
    ).astype(jnp.bfloat16)
    back_ref[...] = dot_nt(grad_wide_ref[...], wide_ref[...]).astype(jnp.bfloat16)
    out_ref[...] = dot_nn(act_ref[...], down_ref[...]).astype(jnp.bfloat16)


def feed_kernel(number, meta_ref, *refs):
    firsts, grads, pieces = refs[:number], refs[number : 2 * number], refs[2 * number : 2 * number + 5]
    refs = refs[2 * number + 5 :]
    act_ref, grad_wide_ref, hidden_all, grad_all = refs[:4]
    out_refs, back_refs = refs[4 : 4 + number], refs[4 + number : 4 + 2 * number]
    hidden, grad, out_low, back_low, wide_ref, down_ref, joined = refs[4 + 2 * number :][:7]
    in_sem, grad_sem, all_sem, grad_all_sem, out_sem, back_sem, piece_sem = refs[11 + 2 * number :]
    tokens, width = hidden.shape[1:]
    shard = meta_ref[1]
    rows = wide_ref.shape[0] // 4
    inner = joined.shape[1] - rows
    each = inner - 128
    step = pl.program_id(0)

    def moves(index):
        filed = pl.ds(index * tokens, tokens)
        return (
            pltpu.make_async_copy(firsts[index], hidden.at[index], in_sem.at[index]),
            pltpu.make_async_copy(
                grads[index].at[pl.ds(0, tokens), :], grad.at[index], grad_sem.at[index]
            ),
            pltpu.make_async_copy(hidden.at[index], hidden_all.at[filed, :], all_sem.at[index]),
            pltpu.make_async_copy(grad.at[index], grad_all.at[filed, :], grad_all_sem.at[index]),
            pltpu.make_async_copy(out_low.at[index], out_refs[index], out_sem.at[index]),
            pltpu.make_async_copy(back_low.at[index], back_refs[index], back_sem.at[index]),
        )

    def places(bits):
        owner = lax.bitwise_xor(shard, bits)
        return (
            pl.ds(aligned(owner * rows, rows), rows),
            pl.ds(aligned(owner * 128, 128), 128),
            pl.ds(aligned(4 * 128 + owner * each, 16), each),
        )

    @pl.when(step == 0)
    def _():
        copies = []
        for bits in range(3):
            upper, lower, last = places(bits)
            for place, (source, target) in enumerate(
                (
                    (pieces[bits].at[pl.ds(0, rows), :], wide_ref.at[upper, :]),
                    (pieces[bits].at[pl.ds(rows, 128), pl.ds(0, width)], down_ref.at[lower, :]),
                    (pieces[bits].at[pl.ds(rows + 128, each), pl.ds(0, width)], down_ref.at[last, :]),
                )
            ):
                copies.append(
                    pltpu.make_async_copy(source, target, piece_sem.at[3 * bits + place])
                )
        for index in range(2):
            copies.append(
                pltpu.make_async_copy(pieces[3 + index], joined.at[index], piece_sem.at[9 + index])
            )
        for copy in copies:
            copy.start()
        for index in range(number):
            for move in moves(index)[:2]:
                move.start()
        down_ref[4 * inner :, :] = jnp.zeros_like(down_ref[4 * inner :, :])
        for copy in copies:
            copy.wait()
        upper, lower, last = places(3)
        wide_ref[upper, :] = joined[0, :rows, :] + joined[1, :rows, :]
        middle = rows + 128
        down_ref[lower, :] = joined[0, rows:middle, :width] + joined[1, rows:middle, :width]
        down_ref[last, :] = joined[0, middle:, :width] + joined[1, middle:, :width]

    for index in range(number):

        @pl.when(step == index)
        def _(index=index):
            for move in moves(index)[:2]:
                move.wait()
            for move in moves(index)[2:4]:
                move.start()

    feed_block(
        hidden.at[step], grad.at[step], wide_ref, down_ref,
        act_ref, grad_wide_ref, out_low.at[step], back_low.at[step],
    )

    for index in range(number):

        @pl.when(step == index)
        def _(index=index):
            for move in moves(index)[4:]:
                move.start()

    @pl.when(step == number - 1)
    def _():
        for index in range(number):
            for move in moves(index)[2:]:
                move.wait()


def feed_call(meta, hidden, grads, pieces, padded, grant):
    number = len(hidden)
    tokens, width = hidden[0].shape
    rows, inner = pieces[0].shape
    low = jnp.bfloat16
    outs = [shaped((number * tokens, columns)) for columns in (padded, inner, width, width)]
    outs += [shaped((tokens, width))] * (2 * number)
    return pl.pallas_call(
        functools.partial(feed_kernel, number),
        grid=(number,),
        out_shape=outs,
        in_specs=[SCALARS] + [PLACED] * (2 * number + 5),
        out_specs=[
            pl.BlockSpec((tokens, padded), lambda step: (step, 0)),
            pl.BlockSpec((tokens, inner), lambda step: (step, 0)),
        ]
        + [PLACED] * (2 + 2 * number),
        scratch_shapes=[pltpu.VMEM((number, tokens, width), low)] * 4
        + [
            pltpu.VMEM((width, inner), low),
            pltpu.VMEM((padded, width), low),
            pltpu.VMEM((2, rows, inner), low),
        ]
        + [pltpu.SemaphoreType.DMA((number,))] * 6
        + [pltpu.SemaphoreType.DMA((11,))],
        cost_estimate=pl.CostEstimate(
            flops=6 * number * tokens * width * inner,
            bytes_accessed=16 * number * tokens * width,
            transcendentals=0,
        ),
        compiler_params=pltpu.CompilerParams(vmem_limit_bytes=grant * 2**20),
        name="feed",
    )(meta, *hidden, *grads, *pieces)


def feed_back_kernel(count, meta_ref, *refs):
    sums, rest = refs[:5], refs[5:]
    mixed_ref, grad_ref, full_ref, gain_ref, grad_mixed_ref, grad_low_ref, grad_gain_ref = rest[:7]
    block_refs, attn = rest[7 : 7 + count], rest[7 + count]
    here = meta_ref[0]
    grad_hidden = wide(sums[0][...])
    for part in sums[1:]:
        grad_hidden = grad_hidden + wide(part[...])
    mixed = mixed_ref[...]
    scale = lax.rsqrt(jnp.mean(mixed * mixed, axis=1, keepdims=True) + EPSILON)
    normed = mixed * scale
    weighted = grad_hidden * gain_ref[...]
    grad_in = scale * (weighted - normed * jnp.mean(weighted * normed, axis=1, keepdims=True))
    grad_gain_ref[...] = jnp.sum(grad_hidden * normed, axis=0, keepdims=True)
    grad_mixed = wide(grad_ref[...]) + grad_in
    grad_mixed_ref[...] = grad_mixed
    grad_low_ref[...] = grad_mixed.astype(jnp.bfloat16)
    tile = 2 * pair_tile(full_ref)

    def project_back(index, carry):
        part = pl.ds(aligned(index * tile, tile), tile)
        attn[:, part] = dot_nt(grad_low_ref[...], full_ref[part, :]).astype(jnp.bfloat16)
        return carry

    lax.fori_loop(0, full_ref.shape[0] // tile, project_back, 0)
    for bits in range(count):
        owner = lax.bitwise_xor(here, bits)
        block_refs[bits][...] = attn[:, pl.ds(aligned(owner * 2 * HD, 2 * HD), 2 * HD)]


def wide_out_kernel(count, parts, meta_ref, *refs):
    blocks, lowers, (gate_ref, up_ref, down_ref) = refs[:count], refs[count : 2 * count], refs[2 * count :]
    here = meta_ref[0]
    tile = gate_ref.shape[0]
    inner = blocks[0].shape[1] // 2
    main = inner // 128 * 128
    each = (inner - main) // parts
    span = gate_ref.shape[1] // parts
    left = span - 128
    lanes = lax.broadcasted_iota(jnp.int32, (tile, 128), 1)
    owners = [lax.bitwise_xor(here, bits) for bits in range(count)]
    for kind, out_ref in enumerate((gate_ref, up_ref)):
        for part in range(parts):
            place = kind * parts + part
            for bits, owner in enumerate(owners):
                target = pl.ds(aligned(part * span + owner * 128, 128), 128)
                out_ref[:, target] = wide(blocks[bits][:, place * 128 : (place + 1) * 128])
    lasts = [wide(block[:, 2 * main :]) for block in blocks]
    for kind, out_ref in enumerate((gate_ref, up_ref)):
        for part in range(parts):
            place = kind * parts + part
            total = jnp.zeros((tile, 128), jnp.float32)
            for bits, owner in enumerate(owners):
                moved = pltpu.roll(lasts[bits], 128 + (owner - place) * each, 1)
                total = jnp.where((lanes >= owner * each) & (lanes < (owner + 1) * each), moved, total)
            out_ref[:, part * span + left : part * span + left + 128] = total

    @pl.when(pl.program_id(0) == 0)
    def _():
        rows = count * 128
        for bits, owner in enumerate(owners):
            low = wide(lowers[bits][:, : down_ref.shape[1]])
            down_ref[pl.ds(aligned(owner * 128, 128), 128), :] = low[:128]
            down_ref[pl.ds(aligned(rows + owner * each, 16), each), :] = low[128:]


def heads_out_kernel(count, own, extra, meta_ref, *refs):
    blocks, rest = refs[:count], refs[count:]
    query_ref, key_ref, value_ref, proj_ref, gain_ref, held = rest
    here = meta_ref[0]
    pair = 2 * HD
    part = (blocks[0].shape[0] - own - extra) // 4
    gains = jnp.zeros(gain_ref.shape, jnp.float32)
    for bits in range(count):
        owner = lax.bitwise_xor(here, bits)
        block = wide(blocks[bits][...])
        query_ref[:, pl.ds(aligned(owner * pair, pair), pair)] = block[:own, :pair]
        held[owner] = block[:own, pair:]
        gains = gains + block[own : own + extra, :]
        for index in range(4):
            source = own + extra + index * part
            proj_ref[
                pl.ds(aligned(owner * part, part), part), index * 2 * pair : (index + 1) * 2 * pair
            ] = block[source : source + part, :]
    gain_ref[...] = gains
    first, _ = lane_masks(own)
    for index in range(count // 2):
        early, late = held[2 * index], held[2 * index + 1]
        lanes = slice(index * pair, (index + 1) * pair)
        key_ref[:, lanes] = jnp.where(first, early, pltpu.roll(late, HD, 1))
        value_ref[:, lanes] = jnp.where(first, pltpu.roll(early, HD, 1), late)


SCALARS = pl.BlockSpec(memory_space=pltpu.SMEM)
WHOLE = pl.BlockSpec(memory_space=pltpu.VMEM)
PLACED = pl.BlockSpec(memory_space=pl.ANY)
FAR = pl.BlockSpec(memory_space=pltpu.HBM)


def shaped(shape, kind=jnp.bfloat16):
    return jax.ShapeDtypeStruct(shape, kind)


def whole_call(kernel, outs, ins, flops, scratch=(), grant=24, specs=None):
    moved = sum(math.prod(out.shape) * out.dtype.itemsize for out in outs)
    return pl.pallas_call(
        kernel,
        out_shape=outs,
        in_specs=[SCALARS] + (specs or [WHOLE] * ins),
        out_specs=[WHOLE] * len(outs),
        scratch_shapes=list(scratch),
        cost_estimate=pl.CostEstimate(
            flops=int(flops), bytes_accessed=int(2 * moved), transcendentals=0
        ),
        compiler_params=pltpu.CompilerParams(vmem_limit_bytes=grant * 2**20),
    )


def local_heads(
    block_input, doc_starts, out_grad, query_weight, key_weight, value_weight, output_weight,
    gate_weight, up_weight, down_weight, mixer_gain, feed_gain, query_gain, key_gain,
):
    low = jnp.bfloat16
    tokens, width = block_input.shape[1:]
    count = lax.axis_size("ctx")
    shards = lax.axis_size("fsdp")
    here = lax.axis_index("ctx").astype(jnp.int32)
    shard = lax.axis_index("fsdp").astype(jnp.int32)
    stream = tokens * count
    docs = doc_starts.shape[1]
    pair = 2 * HD
    own_rows = width // shards
    extra = 16
    meta = jnp.concatenate([here[None], shard[None], doc_starts[0].astype(jnp.int32)])
    own_input = block_input[0]
    own_grad = out_grad[0]
    inner = down_weight.shape[0] // count
    wide_inner = inner * shards
    padded = -(-wide_inner // 128) * 128
    proj_rows = own_rows // count
    edges = [(0, 1), (3, 2)]
    middle = [(1, 2), (2, 1)]
    relay = [(1, 0), (2, 3)]

    def near(piece, bits):
        return shift_fsdp(piece, flipped(bits, shards))

    across, along, partner = gather_near(own_input)
    corner = swap_ctx(own_input, 6)
    piece_rows = own_rows + extra + 4 * proj_rows
    head_piece = whole_call(
        take_heads_kernel,
        [shaped((piece_rows, 2 * pair))],
        8,
        0,
        [
            pltpu.VMEM((extra, 2 * pair), jnp.float32),
            pltpu.VMEM((3, own_rows, pair), low),
            pltpu.VMEM((proj_rows, width), low),
            pltpu.SemaphoreType.DMA((4,)),
        ],
        grant=60,
        specs=[FAR] * 4 + [WHOLE] * 4,
    )(
        meta, query_weight, key_weight, value_weight, output_weight,
        mixer_gain, feed_gain, query_gain, key_gain,
    )[0]
    head_pieces = [head_piece] + [near(head_piece, bits) for bits in (1, 2, 3)]
    feed_rows = own_rows + inner
    feed_piece = whole_call(
        functools.partial(take_wide_kernel, shards),
        [shaped((feed_rows, 2 * wide_inner))],
        3,
        2 * own_rows * 2 * wide_inner * 2048,
        [
            pltpu.VMEM((2 * shards, own_rows, 128), low),
            pltpu.VMEM((inner, width), low),
            pltpu.SemaphoreType.DMA((2 * shards,)),
            pltpu.SemaphoreType.DMA((2 * shards,)),
            pltpu.SemaphoreType.DMA((2,)),
        ],
        grant=60,
        specs=[FAR] * 3,
    )(behind(meta, head_piece), gate_weight, up_weight, down_weight)[0]
    feed_near = near(feed_piece, 1)
    feed_far = near(behind(feed_piece, *head_pieces[1:]), 2)
    others = gather_far(across, along, corner)
    input_blocks = [own_input, partner, across, others[0], along, others[1], corner, others[2]]

    where_at = jnp.arange(stream, dtype=jnp.int32)
    begins = doc_begin(doc_starts[0], where_at)
    lanes = jnp.arange(pair) % (HD // 2)
    frequency = ROPE_BASE ** (-(2.0 * lanes.astype(jnp.float32)) / HD)
    angles = (where_at - begins).astype(jnp.float32)[:, None] * frequency[None, :]
    cosine = jnp.cos(angles)
    sine = jnp.sin(angles) * jnp.where(jnp.arange(pair) % HD < HD // 2, -1.0, 1.0)[None, :]

    heads_weight, gain_mixer, gain_feed, gain_heads, proj_part = whole_call(
        functools.partial(arrange_heads_kernel, extra),
        [
            shaped((width, 2 * pair)),
            shaped((1, width), jnp.float32),
            shaped((1, width), jnp.float32),
            shaped((8, pair), jnp.float32),
            shaped((shards * proj_rows, width)),
        ],
        4,
        0,
        grant=8,
    )(behind(meta, cosine, sine), *head_pieces)

    hidden_in, linear = pl.pallas_call(
        functools.partial(head_linear_kernel, count),
        grid=(count // 2,),
        in_specs=[SCALARS]
        + [PLACED] * count
        + [
            pl.BlockSpec((width, 2 * pair), lambda step: (0, 0)),
            pl.BlockSpec((1, width), lambda step: (0, 0)),
        ],
        out_specs=[
            pl.BlockSpec((2 * tokens, width), lambda step: (step, 0)),
            pl.BlockSpec((2 * tokens, 2 * pair), lambda step: (step, 0)),
        ],
        out_shape=[shaped((stream, width)), shaped((stream, 2 * pair), jnp.float32)],
        scratch_shapes=[
            pltpu.VMEM((count // 2, 2 * tokens, width), low),
            pltpu.SemaphoreType.DMA((count,)),
        ],
        cost_estimate=pl.CostEstimate(
            flops=4 * stream * width * pair, bytes_accessed=6 * stream * width, transcendentals=0
        ),
        compiler_params=pltpu.CompilerParams(vmem_limit_bytes=60 * 2**20),
        name="head_linear",
    )(meta, *[input_blocks[bits] for bits in ORDER], heads_weight, gain_mixer)

    pairs = stream * stream // 2
    extra_piece = behind(jnp.concatenate([own_grad, proj_part], axis=0), corner)
    extra_across, extra_along, extra_partner = gather_near(extra_piece)
    extra_corner = swap_ctx(extra_piece, 6)
    query_att, key_att, value_att, attn, lse, *attn_low = whole_call(
        functools.partial(attention_kernel, tokens, count, docs),
        [
            shaped((stream, pair)),
            shaped((stream, pair)),
            shaped((stream, pair)),
            shaped((stream, pair), jnp.float32),
            shaped((count, 1, 2 * tokens), jnp.float32),
        ]
        + [shaped((tokens, pair))] * count,
        4,
        8 * pairs * HD,
        [
            pltpu.VMEM((count, HD + 16, tokens), low),
            pltpu.VMEM((HD + 16, 2 * tokens), jnp.float32),
            pltpu.VMEM((stream, pair), low),
            pltpu.VMEM((pair, pair), low),
        ],
        grant=60,
    )(meta, linear, cosine, sine, gain_heads)

    attn_blocks = exchange_plane(attn_low)
    feed_middle = shift_fsdp(behind(feed_piece, attn_blocks[1]), middle)
    feed_relay = shift_fsdp(behind(feed_far, attn_blocks[1]), relay)
    extra_others = gather_far(extra_across, extra_along, extra_corner, attn_blocks[1])
    extra_blocks = [
        extra_piece, extra_partner, extra_across, extra_others[0],
        extra_along, extra_others[1], extra_corner, extra_others[2],
    ]
    full_proj, attn_rows, mixed, hidden_mid = whole_call(
        functools.partial(project_kernel, count, shards, tokens),
        [
            shaped((width, width)),
            shaped((tokens, width)),
            shaped((tokens, width), jnp.float32),
            shaped((tokens, width)),
        ],
        2 * count + 2,
        2 * tokens * width * width,
        [pltpu.SemaphoreType.DMA((count,)), pltpu.SemaphoreType.DMA((shards * count,))],
        grant=60,
        specs=[PLACED] * (2 * count) + [WHOLE] * 2,
    )(meta, *attn_blocks, *extra_blocks, own_input, gain_feed)

    hidden_across, hidden_along, hidden_partner = gather_near(hidden_mid)
    hidden_corner = swap_ctx(hidden_mid, 6)
    hidden_far = gather_far(hidden_across, hidden_along, hidden_corner)
    hidden_blocks = [
        hidden_mid, hidden_partner, hidden_across, hidden_far[0],
        hidden_along, hidden_far[1], hidden_corner, hidden_far[2],
    ]
    weight_piece = behind(heads_weight, hidden_far[2])
    weight_near = gather_near(weight_piece)
    weight_corner = swap_ctx(weight_piece, 6)
    act_all, grad_wide_all, hidden_all, grad_all, *parts = feed_call(
        meta,
        hidden_blocks,
        extra_blocks,
        (feed_piece, feed_near, feed_far, feed_middle, feed_relay),
        padded,
        60,
    )
    out_parts, back_parts = parts[:count], parts[count:]
    back_own, back_pairs = scatter_pair(back_parts)
    back_sums = back_own + scatter_links(back_pairs)

    def scatter_early(pieces):
        return shift_fsdp(pieces[3], edges), shift_fsdp(pieces[3], middle)

    def scatter_late(pieces, early, *ready):
        second = behind((wide(pieces[2]) + wide(early)).astype(low), *ready)
        return near(second, 2), near(behind(pieces[1], *ready), 1)

    grad_down = contract_rows(behind(act_all, *back_pairs), grad_all).astype(low)
    first_piece = first_piece_call(meta, hidden_all, grad_wide_all, grad_down, own_rows, inner)
    grad_wide = contract_rows(behind(hidden_all, first_piece), grad_wide_all).astype(low)
    feed_pieces = whole_call(
        pack_feed_kernel, [shaped((feed_rows, 2 * wide_inner))] * 3, 2, 0, grant=16
    )(meta, grad_wide, grad_down)
    feed_pieces = [*feed_pieces, first_piece]
    wide_edge, wide_middle = scatter_early(feed_pieces)
    out_own, out_pairs = scatter_pair([behind(part, grad_wide) for part in out_parts])

    grad_mixed, grad_mixed_low, grad_feed, *grad_blocks = whole_call(
        functools.partial(feed_back_kernel, count),
        [
            shaped((tokens, width), jnp.float32),
            shaped((tokens, width)),
            shaped((1, width), jnp.float32),
        ]
        + [shaped((tokens, pair))] * count,
        9,
        2 * tokens * width * width,
        [pltpu.VMEM((tokens, width), low)],
        grant=8,
    )(meta, *back_sums, mixed, own_grad, full_proj, gain_feed)
    grad_attn = exchange_plane(grad_blocks)
    wide_late = scatter_late(feed_pieces, wide_edge, grad_blocks[0])
    proj_blocks = whole_call(
        functools.partial(proj_grad_kernel, shards),
        [shaped((shards * proj_rows, width))] * count,
        2,
        2 * tokens * width * width,
        [pltpu.VMEM((width, width), low)],
        grant=8,
    )(meta, attn_rows, grad_mixed_low)
    proj_own, proj_pairs = scatter_pair(proj_blocks)
    proj_parts = proj_own + scatter_links(proj_pairs)
    out_sums = out_own + scatter_links([behind(part, grad_blocks[0]) for part in out_pairs])

    back_outs = whole_call(
        functools.partial(attention_back_kernel, tokens, count, docs),
        [shaped((stream, 2 * pair)), shaped((8, pair), jnp.float32)]
        + [shaped((tokens, 2 * pair))] * count,
        9 + count,
        20 * pairs * HD,
        [
            pltpu.VMEM((count, HD, tokens), low),
            pltpu.VMEM((stream, pair), jnp.float32),
            pltpu.VMEM((stream, pair), jnp.float32),
            pltpu.VMEM((stream, pair), jnp.float32),
            pltpu.VMEM((HD, 2 * tokens), jnp.float32),
            pltpu.VMEM((stream, pair), low),
            pltpu.VMEM((pair, pair), low),
        ],
        grant=14,
    )(meta, linear, cosine, sine, gain_heads, query_att, key_att, value_att, attn, lse, *grad_attn)
    grad_linear, gain_sums, *token_blocks = back_outs

    token_grads = exchange_plane(token_blocks)
    weight_far = gather_far(weight_near[0], weight_near[1], weight_corner, token_grads[1])
    weight_all = [
        weight_piece, weight_near[2], weight_near[0], weight_far[0],
        weight_near[1], weight_far[1], weight_corner, weight_far[2],
    ]
    late_linear = behind(grad_linear, token_grads[1])
    grad_heads = contract_rows(hidden_in, late_linear).astype(low)
    grad_mixer = jnp.sum(
        contract_cols(late_linear, heads_weight) * wide(hidden_in), axis=0, keepdims=True
    )
    packed = whole_call(
        functools.partial(pack_heads_kernel, extra),
        [shaped((piece_rows, 2 * pair))] * shards,
        10,
        0,
        [
            pltpu.VMEM((shards * proj_rows, width), low),
            pltpu.VMEM((1, width), jnp.float32),
            pltpu.VMEM((8, pair), jnp.float32),
            pltpu.VMEM((extra, 2 * pair), jnp.float32),
        ],
        grant=6,
    )(meta, grad_heads, grad_mixer, gain_mixer, grad_feed, gain_sums, *proj_parts)
    heads_sent = [near(packed[bits], bits) for bits in (1, 2, 3)]

    def total_of(first, *parts):
        return sum([wide(part) for part in parts], wide(first)).astype(low)

    def total_late(pieces, parts, *ready):
        return total_of(pieces[0], *[behind(part, *ready) for part in parts])

    wide_total = total_late(feed_pieces, (wide_middle,) + wide_late, grad_linear)
    wide_blocks = gather_plane(wide_total)
    input_grad = whole_call(
        functools.partial(input_grad_kernel, count),
        [shaped((tokens, width), jnp.float32)],
        2 * count + 3,
        2 * tokens * width * 2 * width,
        grant=10,
    )(meta, *token_grads, *weight_all, own_input, grad_mixed, gain_mixer)[0]
    heads_total = total_of(packed[0], *heads_sent)
    heads_blocks = gather_direct(heads_total)
    block_output = (
        mixed + sum(wide(behind(part, packed[0])) for part in out_sums)
    ).astype(low)

    tile = own_rows // 4
    full = wide_inner * count
    out_gate, out_up, out_down = pl.pallas_call(
        functools.partial(wide_out_kernel, count, shards),
        grid=(4,),
        in_specs=[SCALARS]
        + [pl.BlockSpec((tile, 2 * wide_inner), lambda step: (step, 0))] * count
        + [pl.BlockSpec((pl.Element(inner), pl.Element(2 * wide_inner)), lambda step: (own_rows, 0))]
        * count,
        out_specs=[
            pl.BlockSpec((tile, full), lambda step: (step, 0)),
            pl.BlockSpec((tile, full), lambda step: (step, 0)),
            pl.BlockSpec((count * inner, width), lambda step: (0, 0)),
        ],
        out_shape=[
            shaped((own_rows, full), jnp.float32),
            shaped((own_rows, full), jnp.float32),
            shaped((count * inner, width), jnp.float32),
        ],
        compiler_params=pltpu.CompilerParams(vmem_limit_bytes=40 * 2**20),
        name="wide_out",
    )(meta, *wide_blocks, *wide_blocks)
    out_query, out_key, out_value, out_proj, gain_out = whole_call(
        functools.partial(heads_out_kernel, count, own_rows, extra),
        [
            shaped((own_rows, width), jnp.float32),
            shaped((own_rows, KVH * HD), jnp.float32),
            shaped((own_rows, KVH * HD), jnp.float32),
            shaped((own_rows, width), jnp.float32),
            shaped((extra, 2 * pair), jnp.float32),
        ],
        count,
        0,
        [pltpu.VMEM((count, own_rows, pair), jnp.float32)],
    )(meta, *heads_blocks)
    return (
        block_output[None],
        input_grad[None],
        out_query,
        out_key,
        out_value,
        out_proj,
        out_gate,
        out_up,
        out_down,
        gain_out[0],
        gain_out[1],
        gain_out[2, : query_gain.shape[0]],
        gain_out[3, : key_gain.shape[0]],
    )


def divides_heads(mesh):
    return mesh.shape["ctx"] == KVH and mesh.shape["fsdp"] == 4 and H == 2 * KVH


def solution(mesh):
    in_specs = (
        P("fsdp", "ctx", None),
        P("fsdp", None),
        P("fsdp", "ctx", None),
        P("fsdp", None),
        P("fsdp", None),
        P("fsdp", None),
        P("fsdp", None),
        P("fsdp", None),
        P("fsdp", None),
        P("fsdp", None),
        P("fsdp"),
        P("fsdp"),
        P("fsdp"),
        P("fsdp"),
    )
    out_specs = (
        P("fsdp", "ctx", None),
        P("fsdp", "ctx", None),
        P("fsdp", None),
        P("fsdp", None),
        P("fsdp", None),
        P("fsdp", None),
        P("fsdp", None),
        P("fsdp", None),
        P("fsdp", None),
        P("fsdp"),
        P("fsdp"),
        P("fsdp"),
        P("fsdp"),
    )
    if not divides_heads(mesh):
        return jax.shard_map(
            local, mesh=mesh, in_specs=in_specs, out_specs=out_specs, check_vma=False
        )

    return jax.shard_map(local_heads, mesh=mesh, in_specs=in_specs, out_specs=out_specs, check_vma=False)
```

```python
import functools
import math

import jax
import jax.numpy as jnp
from jax import lax
from jax.experimental import pallas as pl
from jax.experimental.pallas import tpu as pltpu
from jax.sharding import PartitionSpec as P

H = 16
KVH = 8
HD = 64


EPSILON = 1e-05
ROPE_BASE = 1000000.0
FLOOR_SCORE = -1e30


def place_rows(row_index, tokens, ctx_count):
    half_rows = tokens // 2
    device = row_index // tokens
    offset = row_index % tokens
    early = device * half_rows + offset
    late = (2 * ctx_count - 1 - device) * half_rows + offset - half_rows
    return jnp.where(offset < half_rows, early, late)


def doc_begin(starts, where_at):
    started = starts[None, :] <= where_at[:, None]
    return jnp.max(jnp.where(started, starts[None, :], 0), axis=1)


def rotary(positions):
    half_dim = HD // 2
    frequency = ROPE_BASE ** (-(2.0 * jnp.arange(half_dim, dtype=jnp.float32)) / HD)
    angles = positions.astype(jnp.float32)[:, None] * frequency[None, :]
    angles = jnp.concatenate([angles, angles], axis=1)
    return (jnp.cos(angles)[:, None, :], jnp.sin(angles)[:, None, :])


def rotate_pairs(values, cosine, sine_part):
    half_dim = values.shape[-1] // 2
    rolled = jnp.concatenate([-values[..., half_dim:], values[..., :half_dim]], axis=-1)
    return values * cosine + rolled * sine_part


def rotate_back(grads, cosine, sine_part):
    half_dim = grads.shape[-1] // 2
    moved = grads * sine_part
    rolled = jnp.concatenate([moved[..., half_dim:], -moved[..., :half_dim]], axis=-1)
    return grads * cosine + rolled


def unit_norm(values):
    scaling = lax.rsqrt(jnp.mean(values * values, axis=-1, keepdims=True) + EPSILON)
    return (values * scaling, scaling)


def norm_back(grad_out, normed, scaling, gain_row):
    weighted = grad_out * gain_row
    grad_in = scaling * (weighted - normed * jnp.mean(weighted * normed, axis=-1, keepdims=True))
    grad_gain = jnp.sum((grad_out * normed).reshape(-1, normed.shape[-1]), axis=0)
    return (grad_in, grad_gain)


def score_block(query_rows, key_rows, scaling):
    return (
        jnp.einsum("igrd,jgd->grij", query_rows, key_rows, preferred_element_type=jnp.float32)
        * scaling
    )


def visible_pairs(query_at, query_doc, key_at, key_doc):
    return (query_doc[:, None] == key_doc[None, :]) & (key_at[None, :] <= query_at[:, None])


def any_visible(query_at, query_doc, key_at):
    return (jnp.min(key_at) <= jnp.max(query_at)) & (jnp.max(key_at) >= jnp.min(query_doc))


def contract_rows(left, right):
    return lax.dot_general(
        left, right, (((0,), (0,)), ((), ())), preferred_element_type=jnp.float32
    )


def contract_cols(left, right):
    return lax.dot_general(
        left, right, (((1,), (1,)), ((), ())), preferred_element_type=jnp.float32
    )


def keep_same(totals):
    return totals


def local(
    block_input,
    doc_starts,
    out_grad,
    query_weight,
    key_weight,
    value_weight,
    output_weight,
    gate_weight,
    up_weight,
    down_weight,
    mixer_gain,
    feed_gain,
    query_gain,
    key_gain,
):
    tokens = block_input.shape[1]
    ctx_count = lax.axis_size("ctx")
    repeat = H // KVH
    kv_width = KVH * HD
    scaling = HD ** (-0.5)
    inputs = block_input[0].astype(jnp.float32)
    starts = doc_starts[0]
    where_at = place_rows(
        lax.axis_index("ctx") * tokens + jnp.arange(tokens, dtype=jnp.int32), tokens, ctx_count
    )
    begins = doc_begin(starts, where_at)
    cosine, sine_part = rotary(where_at - begins)
    gathered = (
        lax.all_gather(query_weight, "fsdp", axis=0, tiled=True),
        lax.all_gather(key_weight, "fsdp", axis=0, tiled=True),
        lax.all_gather(value_weight, "fsdp", axis=0, tiled=True),
        lax.all_gather(output_weight, "fsdp", axis=0, tiled=True),
        lax.all_gather(gate_weight, "fsdp", axis=0, tiled=True),
        lax.all_gather(up_weight, "fsdp", axis=0, tiled=True),
        lax.all_gather(down_weight, "fsdp", axis=0, tiled=True),
        lax.all_gather(mixer_gain, "fsdp", axis=0, tiled=True),
        lax.all_gather(feed_gain, "fsdp", axis=0, tiled=True),
        lax.all_gather(query_gain, "fsdp", axis=0, tiled=True),
        lax.all_gather(key_gain, "fsdp", axis=0, tiled=True),
    )
    full_query, full_key, full_value, full_proj, full_gate, full_up, full_down = gathered[:7]
    gain_mixer, gain_feed, gain_query, gain_key = [
        entry.astype(jnp.float32) for entry in gathered[7:]
    ]
    normed_in, scale_in = unit_norm(inputs)
    hidden_in = (normed_in * gain_mixer).astype(jnp.bfloat16)
    query_lin = jnp.dot(hidden_in, full_query, preferred_element_type=jnp.float32)
    key_lin = jnp.dot(hidden_in, full_key, preferred_element_type=jnp.float32)
    value_lin = jnp.dot(hidden_in, full_value, preferred_element_type=jnp.float32)
    query_normed, query_scale = unit_norm(query_lin.reshape(tokens, H, HD))
    key_normed, key_scale = unit_norm(key_lin.reshape(tokens, KVH, HD))
    query_att = (
        rotate_pairs(query_normed * gain_query, cosine, sine_part)
        .reshape(tokens, H * HD)
        .astype(jnp.bfloat16)
    )
    key_att = (
        rotate_pairs(key_normed * gain_key, cosine, sine_part)
        .reshape(tokens, kv_width)
        .astype(jnp.bfloat16)
    )
    value_att = value_lin.astype(jnp.bfloat16)
    query_four = query_att.reshape(tokens, KVH, repeat, HD)
    start_state = (
        jnp.full((KVH, repeat, tokens), FLOOR_SCORE, jnp.float32),
        jnp.zeros((KVH, repeat, tokens), jnp.float32),
        jnp.zeros((tokens, H * HD), jnp.float32),
    )
    key_part = lax.all_gather(key_att, "ctx", axis=0, tiled=True)
    value_part = lax.all_gather(value_att, "ctx", axis=0, tiled=True)
    rows = key_part.shape[0]
    width = math.gcd(math.gcd(rows, tokens // 2), 512)

    def forward_key_block(block_index, totals):
        offset = block_index * width
        key_rows = lax.dynamic_slice_in_dim(key_part, offset, width, 0).reshape(width, KVH, HD)
        value_rows = lax.dynamic_slice_in_dim(value_part, offset, width, 0).reshape(width, KVH, HD)
        key_at = place_rows(offset + jnp.arange(width, dtype=jnp.int32), tokens, ctx_count)

        def attend(totals):
            highest, total_mass, accum = totals
            visible = visible_pairs(where_at, begins, key_at, doc_begin(starts, key_at))
            scores = jnp.where(visible, score_block(query_four, key_rows, scaling), FLOOR_SCORE)
            new_high = jnp.maximum(highest, jnp.max(scores, axis=-1))
            rescale = jnp.exp(highest - new_high)
            probable = jnp.where(visible, jnp.exp(scores - new_high[..., None]), 0.0)
            total_mass = total_mass * rescale + jnp.sum(probable, axis=-1)
            part_out = jnp.einsum(
                "grij,jgd->igrd",
                probable.astype(jnp.bfloat16),
                value_rows,
                preferred_element_type=jnp.float32,
            )
            accum = (
                accum.reshape(tokens, KVH, repeat, HD)
                * jnp.transpose(rescale, (2, 0, 1))[..., None]
                + part_out
            )
            return (new_high, total_mass, accum.reshape(tokens, H * HD))

        return lax.cond(any_visible(where_at, begins, key_at), attend, keep_same, totals)

    highest, total_mass, accum = lax.fori_loop(0, rows // width, forward_key_block, start_state)
    lse_heads = highest + jnp.log(total_mass)
    attn_raw = (
        accum.reshape(tokens, KVH, repeat, HD) / jnp.transpose(total_mass, (2, 0, 1))[..., None]
    ).reshape(tokens, H * HD)
    attn_low = attn_raw.astype(jnp.bfloat16)
    mixed = inputs + jnp.dot(attn_low, full_proj, preferred_element_type=jnp.float32)
    normed_mid, scale_mid = unit_norm(mixed)
    hidden_mid = (normed_mid * gain_feed).astype(jnp.bfloat16)
    gate_lin = jnp.dot(hidden_mid, full_gate, preferred_element_type=jnp.float32)
    up_lin = jnp.dot(hidden_mid, full_up, preferred_element_type=jnp.float32)
    sigmoid_gate = jax.nn.sigmoid(gate_lin)
    activated = (gate_lin * sigmoid_gate * up_lin).astype(jnp.bfloat16)
    block_output = (
        mixed + jnp.dot(activated, full_down, preferred_element_type=jnp.float32)
    ).astype(jnp.bfloat16)
    regathered = (
        lax.all_gather(query_weight, "fsdp", axis=0, tiled=True),
        lax.all_gather(key_weight, "fsdp", axis=0, tiled=True),
        lax.all_gather(value_weight, "fsdp", axis=0, tiled=True),
        lax.all_gather(output_weight, "fsdp", axis=0, tiled=True),
        lax.all_gather(gate_weight, "fsdp", axis=0, tiled=True),
        lax.all_gather(up_weight, "fsdp", axis=0, tiled=True),
        lax.all_gather(down_weight, "fsdp", axis=0, tiled=True),
        lax.all_gather(mixer_gain, "fsdp", axis=0, tiled=True),
        lax.all_gather(feed_gain, "fsdp", axis=0, tiled=True),
        lax.all_gather(query_gain, "fsdp", axis=0, tiled=True),
        lax.all_gather(key_gain, "fsdp", axis=0, tiled=True),
    )
    full_query, full_key, full_value, full_proj, full_gate, full_up, full_down = regathered[:7]
    gain_mixer, gain_feed, gain_query, gain_key = [
        entry.astype(jnp.float32) for entry in regathered[7:]
    ]
    grad_top = out_grad[0].astype(jnp.float32)
    grad_top_low = grad_top.astype(jnp.bfloat16)
    grad_down = contract_rows(activated, grad_top_low)
    grad_act = contract_cols(grad_top_low, full_down)
    grad_gate_low = (
        grad_act * up_lin * sigmoid_gate * (1.0 + gate_lin * (1.0 - sigmoid_gate))
    ).astype(jnp.bfloat16)
    grad_up_low = (grad_act * gate_lin * sigmoid_gate).astype(jnp.bfloat16)
    grad_gate = contract_rows(hidden_mid, grad_gate_low)
    grad_up = contract_rows(hidden_mid, grad_up_low)
    grad_hidden_mid = contract_cols(grad_gate_low, full_gate) + contract_cols(grad_up_low, full_up)
    grad_normed_mid, grad_feed = norm_back(grad_hidden_mid, normed_mid, scale_mid, gain_feed)
    grad_mixed = grad_top + grad_normed_mid
    grad_mixed_low = grad_mixed.astype(jnp.bfloat16)
    grad_proj = contract_rows(attn_low, grad_mixed_low)
    grad_attn = contract_cols(grad_mixed_low, full_proj).astype(jnp.bfloat16)
    grad_four = grad_attn.reshape(tokens, KVH, repeat, HD)
    delta_heads = jnp.sum(
        grad_four.astype(jnp.float32) * attn_raw.reshape(tokens, KVH, repeat, HD), axis=-1
    )
    delta_grid = jnp.transpose(delta_heads, (1, 2, 0))
    lse_rows = jnp.transpose(lse_heads, (2, 0, 1)).reshape(tokens, H)
    delta_rows = delta_heads.reshape(tokens, H)
    query_key_part = lax.all_gather(key_att, "ctx", axis=0, tiled=True)
    query_value_part = lax.all_gather(value_att, "ctx", axis=0, tiled=True)
    rows = query_key_part.shape[0]
    query_width = math.gcd(math.gcd(rows, tokens // 2), 512)

    def query_key_block(block_index, grad_query_acc):
        offset = block_index * query_width
        key_rows = lax.dynamic_slice_in_dim(query_key_part, offset, query_width, 0).reshape(
            query_width, KVH, HD
        )
        value_rows = lax.dynamic_slice_in_dim(query_value_part, offset, query_width, 0).reshape(
            query_width, KVH, HD
        )
        key_at = place_rows(offset + jnp.arange(query_width, dtype=jnp.int32), tokens, ctx_count)

        def attend(grad_query_acc):
            visible = visible_pairs(where_at, begins, key_at, doc_begin(starts, key_at))
            scores = score_block(query_four, key_rows, scaling)
            probable = jnp.where(visible, jnp.exp(scores - lse_heads[..., None]), 0.0)
            grad_prob = jnp.einsum(
                "igrd,jgd->grij", grad_four, value_rows, preferred_element_type=jnp.float32
            )
            grad_score = (probable * (grad_prob - delta_grid[..., None])).astype(jnp.bfloat16)
            added = (
                jnp.einsum(
                    "grij,jgd->igrd", grad_score, key_rows, preferred_element_type=jnp.float32
                )
                * scaling
            )
            return grad_query_acc + added.reshape(tokens, H * HD)

        return lax.cond(any_visible(where_at, begins, key_at), attend, keep_same, grad_query_acc)

    grad_query_att = lax.fori_loop(
        0, rows // query_width, query_key_block, jnp.zeros((tokens, H * HD), jnp.float32)
    )
    lse_all, delta_all = (
        lax.all_gather(lse_rows.astype(jnp.bfloat16), "ctx", axis=0, tiled=True).astype(
            lse_rows.dtype
        ),
        lax.all_gather(delta_rows.astype(jnp.bfloat16), "ctx", axis=0, tiled=True).astype(
            delta_rows.dtype
        ),
    )
    key_three = key_att.reshape(tokens, KVH, HD)
    value_three = value_att.reshape(tokens, KVH, HD)
    empty_keys = jnp.zeros((tokens, kv_width), jnp.float32)
    query_part = lax.all_gather(query_att, "ctx", axis=0, tiled=True)
    grad_part = lax.all_gather(grad_attn, "ctx", axis=0, tiled=True)
    rows = query_part.shape[0]
    key_width = math.gcd(math.gcd(rows, tokens // 2), 512)

    def query_block(block_index, totals):
        offset = block_index * key_width
        query_rows = lax.dynamic_slice_in_dim(query_part, offset, key_width, 0).reshape(
            key_width, KVH, repeat, HD
        )
        grad_rows = lax.dynamic_slice_in_dim(grad_part, offset, key_width, 0).reshape(
            key_width, KVH, repeat, HD
        )
        query_at = place_rows(offset + jnp.arange(key_width, dtype=jnp.int32), tokens, ctx_count)
        query_doc = doc_begin(starts, query_at)
        lse_block = jnp.transpose(
            lax.dynamic_slice_in_dim(lse_all, offset, key_width, 0).reshape(key_width, KVH, repeat),
            (1, 2, 0),
        )
        delta_block = jnp.transpose(
            lax.dynamic_slice_in_dim(delta_all, offset, key_width, 0).reshape(
                key_width, KVH, repeat
            ),
            (1, 2, 0),
        )

        def attend(totals):
            grad_key_acc, grad_value_acc = totals
            visible = visible_pairs(query_at, query_doc, where_at, begins)
            scores = score_block(query_rows, key_three, scaling)
            probable = jnp.where(visible, jnp.exp(scores - lse_block[..., None]), 0.0)
            grad_prob = jnp.einsum(
                "igrd,jgd->grij", grad_rows, value_three, preferred_element_type=jnp.float32
            )
            grad_score = (probable * (grad_prob - delta_block[..., None])).astype(jnp.bfloat16)
            value_added = jnp.einsum(
                "grij,igrd->jgd",
                probable.astype(jnp.bfloat16),
                grad_rows,
                preferred_element_type=jnp.float32,
            )
            key_added = (
                jnp.einsum(
                    "grij,igrd->jgd", grad_score, query_rows, preferred_element_type=jnp.float32
                )
                * scaling
            )
            return (
                grad_key_acc + key_added.reshape(tokens, kv_width),
                grad_value_acc + value_added.reshape(tokens, kv_width),
            )

        return lax.cond(any_visible(query_at, query_doc, where_at), attend, keep_same, totals)

    grad_key_att, grad_value_att = lax.fori_loop(
        0, rows // key_width, query_block, (empty_keys, empty_keys)
    )
    grad_query_unit = rotate_back(grad_query_att.reshape(tokens, H, HD), cosine, sine_part)
    grad_query_lin, grad_qgain = norm_back(grad_query_unit, query_normed, query_scale, gain_query)
    grad_key_unit = rotate_back(grad_key_att.reshape(tokens, KVH, HD), cosine, sine_part)
    grad_key_lin, grad_kgain = norm_back(grad_key_unit, key_normed, key_scale, gain_key)
    grad_query_low = grad_query_lin.reshape(tokens, H * HD).astype(jnp.bfloat16)
    grad_key_low = grad_key_lin.reshape(tokens, kv_width).astype(jnp.bfloat16)
    grad_value_low = grad_value_att.astype(jnp.bfloat16)
    grad_query = contract_rows(hidden_in, grad_query_low)
    grad_key = contract_rows(hidden_in, grad_key_low)
    grad_value = contract_rows(hidden_in, grad_value_low)
    grad_hidden_in = (
        contract_cols(grad_query_low, full_query)
        + contract_cols(grad_key_low, full_key)
        + contract_cols(grad_value_low, full_value)
    )
    grad_normed_in, grad_mixer = norm_back(grad_hidden_in, normed_in, scale_in, gain_mixer)
    input_grad = grad_mixed + grad_normed_in
    parts = (
        lax.psum_scatter(
            grad_query.astype(jnp.bfloat16), "fsdp", scatter_dimension=0, tiled=True
        ).astype(jnp.float32),
        lax.psum_scatter(
            grad_key.astype(jnp.bfloat16), "fsdp", scatter_dimension=0, tiled=True
        ).astype(jnp.float32),
        lax.psum_scatter(
            grad_value.astype(jnp.bfloat16), "fsdp", scatter_dimension=0, tiled=True
        ).astype(jnp.float32),
        lax.psum_scatter(
            grad_proj.astype(jnp.bfloat16), "fsdp", scatter_dimension=0, tiled=True
        ).astype(jnp.float32),
        lax.psum_scatter(
            grad_gate.astype(jnp.bfloat16), "fsdp", scatter_dimension=0, tiled=True
        ).astype(jnp.float32),
        lax.psum_scatter(
            grad_up.astype(jnp.bfloat16), "fsdp", scatter_dimension=0, tiled=True
        ).astype(jnp.float32),
        lax.psum_scatter(
            grad_down.astype(jnp.bfloat16), "fsdp", scatter_dimension=0, tiled=True
        ).astype(jnp.float32),
        lax.psum_scatter(
            grad_mixer.astype(jnp.bfloat16), "fsdp", scatter_dimension=0, tiled=True
        ).astype(jnp.float32),
        lax.psum_scatter(
            grad_feed.astype(jnp.bfloat16), "fsdp", scatter_dimension=0, tiled=True
        ).astype(jnp.float32),
        lax.psum_scatter(
            grad_qgain.astype(jnp.bfloat16), "fsdp", scatter_dimension=0, tiled=True
        ).astype(jnp.float32),
        lax.psum_scatter(
            grad_kgain.astype(jnp.bfloat16), "fsdp", scatter_dimension=0, tiled=True
        ).astype(jnp.float32),
    )
    summed = (
        lax.psum(parts[0].astype(jnp.bfloat16), "ctx").astype(jnp.float32),
        lax.psum(parts[1].astype(jnp.bfloat16), "ctx").astype(jnp.float32),
        lax.psum(parts[2].astype(jnp.bfloat16), "ctx").astype(jnp.float32),
        lax.psum(parts[3].astype(jnp.bfloat16), "ctx").astype(jnp.float32),
        lax.psum(parts[4].astype(jnp.bfloat16), "ctx").astype(jnp.float32),
        lax.psum(parts[5].astype(jnp.bfloat16), "ctx").astype(jnp.float32),
        lax.psum(parts[6].astype(jnp.bfloat16), "ctx").astype(jnp.float32),
        lax.psum(parts[7].astype(jnp.bfloat16), "ctx").astype(jnp.float32),
        lax.psum(parts[8].astype(jnp.bfloat16), "ctx").astype(jnp.float32),
        lax.psum(parts[9].astype(jnp.bfloat16), "ctx").astype(jnp.float32),
        lax.psum(parts[10].astype(jnp.bfloat16), "ctx").astype(jnp.float32),
    )
    return (
        block_output[None],
        input_grad[None],
        summed[0],
        summed[1],
        summed[2],
        summed[3],
        summed[4],
        summed[5],
        summed[6],
        summed[7],
        summed[8],
        summed[9],
        summed[10],
    )


ORDER = (0, 1, 2, 4, 3, 5, 6, 7)


def flipped(bits, count):
    return [(index, index ^ bits) for index in range(count)]


def swap_ctx(values, bits):
    return lax.ppermute(values, "ctx", flipped(bits, lax.axis_size("ctx")))


def behind(values, *ready):
    return lax.optimization_barrier((values,) + ready)[0]


def dot_nn(left, right):
    return lax.dot_general(
        left, right, (((1,), (0,)), ((), ())), preferred_element_type=jnp.float32
    )


def dot_nt(left, right):
    return lax.dot_general(
        left, right, (((1,), (1,)), ((), ())), preferred_element_type=jnp.float32
    )


def wide(values):
    return values.astype(jnp.float32)


def gather_near(block):
    return swap_ctx(block, 2), swap_ctx(block, 4), swap_ctx(block, 1)


def gather_corner(across, along):
    half = across.shape[0] // 2
    first = swap_ctx(along[:half], 2)
    second = swap_ctx(across[half:], 4)
    return jnp.concatenate([first, second], axis=0)


def gather_far(across, along, corner, *ready):
    return [swap_ctx(behind(part, *ready), 1) for part in (across, along, corner)]


def gather_plane(block, *ready):
    across, along, partner = gather_near(block)
    corner = gather_corner(across, along)
    others = gather_far(across, along, corner, *ready)
    return [block, partner, across, others[0], along, others[1], corner, others[2]]


def gather_direct(block, *ready):
    across, along, partner = gather_near(block)
    corner = swap_ctx(block, 6)
    others = gather_far(across, along, corner, *ready)
    return [block, partner, across, others[0], along, others[1], corner, others[2]]


def scatter_pair(blocks):
    got = [swap_ctx(blocks[bits], 1) for bits in (3, 5, 7, 1)]
    sums = [
        (wide(blocks[bits]) + wide(other)).astype(jnp.bfloat16)
        for bits, other in zip((2, 4, 6), got)
    ]
    return [blocks[0], got[3]], sums


def scatter_links(sums):
    return [swap_ctx(part, bits) for bits, part in zip((2, 4, 6), sums)]


def exchange_plane(blocks):
    return [blocks[0]] + [swap_ctx(blocks[bits], bits) for bits in range(1, 8)]


def shift_fsdp(values, pairs):
    return lax.ppermute(values, "fsdp", pairs)


def slot_of(bits):
    return jnp.where(bits == 3, 4, jnp.where(bits == 4, 3, bits))


def row_of(place, here, tokens, count):
    half = tokens // 2
    device = jnp.where(place < count, place, 2 * count - 1 - place)
    late = jnp.where(place < count, 0, half)
    return slot_of(lax.bitwise_xor(device, here)) * tokens + late


def swap_half(values, low_lane):
    return jnp.where(low_lane, pltpu.roll(values, 96, 1), pltpu.roll(values, 32, 1))


def head_blocks():
    shape = (2 * HD, 2 * HD)
    row = lax.broadcasted_iota(jnp.int32, shape, 0) < HD
    column = lax.broadcasted_iota(jnp.int32, shape, 1) < HD
    return jnp.where(row == column, 1.0 / HD, 0.0).astype(jnp.bfloat16)


def head_mean(values, blocks):
    high = values.astype(jnp.bfloat16)
    rest = (values - wide(high)).astype(jnp.bfloat16)
    return dot_nn(high, blocks) + dot_nn(rest, blocks)


def lane_masks(rows):
    lanes = lax.broadcasted_iota(jnp.int32, (rows, 2 * HD), 1)
    return lanes < HD, (lanes % HD) < (HD // 2)


def two_heads(values):
    first, _ = lane_masks(values.shape[0])
    zero = jnp.zeros_like(values)
    return jnp.concatenate(
        [jnp.where(first, values, zero), jnp.where(first, zero, values)], axis=0
    )


def begin_at(meta_ref, docs, where_at):
    begin = jnp.zeros_like(where_at)
    for doc in range(docs):
        begin = jnp.where(meta_ref[2 + doc] <= where_at, meta_ref[2 + doc], begin)
    return begin


def block_visible(meta_ref, docs, query_block, key_block, size):
    query_at = query_block * size + lax.broadcasted_iota(jnp.int32, (1, size), 1)
    begin = begin_at(meta_ref, docs, query_at)
    key_at = key_block * size + lax.broadcasted_iota(jnp.int32, (size, size), 0)
    return (key_at <= query_at) & (key_at >= begin)


def pair_tile(ref):
    return 2 * HD if ref.shape[0] % (4 * HD) == 0 else ref.shape[0] // 2


def aligned(value, size):
    return pl.multiple_of(value, size)


def take_heads_kernel(
    meta_ref, query_ref, key_ref, value_ref, proj_ref, mixer_ref, feed_ref, query_gain_ref, key_gain_ref,
    out_ref, gains, windows, proj, sem,
):
    here = meta_ref[0]
    rows = query_ref.shape[0]
    pair = 2 * HD
    start = aligned(lax.shift_right_logical(here, 1) * pair, pair)
    part = proj.shape[0]
    copies = [
        pltpu.make_async_copy(
            query_ref.at[:, pl.ds(aligned(here * pair, pair), pair)], windows.at[0], sem.at[0]
        ),
        pltpu.make_async_copy(key_ref.at[:, pl.ds(start, pair)], windows.at[1], sem.at[1]),
        pltpu.make_async_copy(value_ref.at[:, pl.ds(start, pair)], windows.at[2], sem.at[2]),
        pltpu.make_async_copy(
            proj_ref.at[pl.ds(aligned(here * part, part), part), :], proj, sem.at[3]
        ),
    ]
    for copy in copies:
        copy.start()
    gains[...] = jnp.zeros_like(gains)
    for row, ref in enumerate((mixer_ref, feed_ref, query_gain_ref, key_gain_ref)):
        gains[row : row + 1, : ref.shape[0]] = wide(ref[...]).reshape(1, ref.shape[0])
    extra = gains.shape[0]
    out_ref[rows : rows + extra, :] = gains[...].astype(jnp.bfloat16)
    for copy in copies:
        copy.wait()
    out_ref[:rows, :pair] = windows[0]
    odd = lax.bitwise_and(here, 1) == 1
    keys = wide(windows[1])
    values = wide(windows[2])
    first, _ = lane_masks(rows)
    keys = jnp.where(odd, pltpu.roll(keys, HD, 1), keys)
    values = jnp.where(odd, values, pltpu.roll(values, HD, 1))
    out_ref[:rows, pair:] = jnp.where(first, keys, values).astype(jnp.bfloat16)
    for index in range(proj.shape[1] // (2 * pair)):
        target = rows + extra + index * part
        out_ref[target : target + part, :] = proj[:, index * 2 * pair : (index + 1) * 2 * pair]


def arrange_heads_kernel(
    extra, meta_ref, *refs
):
    pieces, (weight_ref, mixer_ref, feed_ref, gains_ref, proj_ref) = refs[:4], refs[4:]
    shard = meta_ref[1]
    rows = weight_ref.shape[0] // 4
    pair = 2 * HD
    each = HD // 4
    gains = jnp.zeros((8, pair), jnp.float32)
    part = proj_ref.shape[0] // 4
    for bits, piece in enumerate(pieces):
        owner = lax.bitwise_xor(shard, bits)
        weight_ref[pl.ds(aligned(owner * rows, rows), rows), :] = piece[:rows, :]
        block = wide(piece[rows : rows + extra, :])
        lanes = pl.ds(aligned(owner * rows, rows), rows)
        mixer_ref[:, lanes] = block[0:1, :]
        feed_ref[:, lanes] = block[1:2, :]
        gains = gains + pltpu.roll(block[:8, :pair], owner * each, 1)
        for index in range(proj_ref.shape[1] // (2 * pair)):
            source = rows + extra + index * part
            proj_ref[
                pl.ds(aligned(owner * part, part), part), index * 2 * pair : (index + 1) * 2 * pair
            ] = piece[source : source + part, :]
    gains_ref[...] = gains + pltpu.roll(gains, HD, 1)


def take_wide_kernel(
    shards, meta_ref, gate_ref, up_ref, down_ref, out_ref, lasts, rows, sem, last_sem, down_sem,
):
    here = meta_ref[0]
    own_rows = lasts.shape[1]
    inner = out_ref.shape[1] // 2
    main = inner // 128 * 128
    each = (inner - main) // shards
    span = gate_ref.shape[1] // shards
    left = span - 128
    copies, last_copies = [], []
    for kind, source in enumerate((gate_ref, up_ref)):
        for part in range(shards):
            place = kind * shards + part
            copies.append(
                pltpu.make_async_copy(
                    source.at[:, pl.ds(aligned(part * span + here * 128, 128), 128)],
                    out_ref.at[pl.ds(0, own_rows), pl.ds(place * 128, 128)],
                    sem.at[place],
                )
            )
            last_copies.append(
                pltpu.make_async_copy(
                    source.at[:, pl.ds(part * span + left, 128)], lasts.at[place], last_sem.at[place]
                )
            )
    down_copies = [
        pltpu.make_async_copy(
            down_ref.at[pl.ds(aligned(here * 128, 128), 128), :],
            rows.at[pl.ds(0, 128), :],
            down_sem.at[0],
        ),
        pltpu.make_async_copy(
            down_ref.at[pl.ds(aligned(left + here * each, each), each), :],
            rows.at[pl.ds(128, each), :],
            down_sem.at[1],
        ),
    ]
    for copy in copies + last_copies + down_copies:
        copy.start()
    lanes = lax.broadcasted_iota(jnp.int32, (own_rows, 128), 1)
    total = jnp.zeros((own_rows, 128), jnp.float32)
    for place, copy in enumerate(last_copies):
        copy.wait()
        moved = pltpu.roll(wide(lasts[place]), 128 - here * each + place * each, 1)
        total = jnp.where((lanes >= place * each) & (lanes < (place + 1) * each), moved, total)
    out_ref[:own_rows, 2 * main :] = total.astype(jnp.bfloat16)
    for copy in copies + down_copies:
        copy.wait()
    out_ref[own_rows:, : rows.shape[1]] = rows[...]
    out_ref[own_rows:, rows.shape[1] :] = jnp.zeros_like(out_ref[own_rows:, rows.shape[1] :])


def head_linear_kernel(number, meta_ref, *refs):
    sources, (weight_ref, gain_ref, hidden_ref, linear_ref, rows, sem) = refs[:number], refs[number:]
    step = pl.program_id(0)
    size = sources[0].shape[0]

    def move(index):
        return pltpu.make_async_copy(
            sources[index], rows.at[index // 2, pl.ds(index % 2 * size, size), :], sem.at[index]
        )

    @pl.when(step == 0)
    def _():
        for index in range(number):
            move(index).start()

    for index in range(number // 2):

        @pl.when(step == index)
        def _(index=index):
            move(2 * index).wait()
            move(2 * index + 1).wait()

    values = wide(rows[step])
    scale = lax.rsqrt(jnp.mean(values * values, axis=1, keepdims=True) + EPSILON)
    hidden_ref[...] = (values * scale * gain_ref[...]).astype(jnp.bfloat16)
    linear_ref[...] = dot_nn(hidden_ref[...], weight_ref[...])


def attention_kernel(
    tokens, count, docs,
    meta_ref, lin_ref, cos_ref, sin_ref, gains_ref,
    query_ref, key_ref, value_ref, attn_ref, lse_ref, *refs,
):
    low_refs, (value_t, accum, low, blocks_ref) = refs[:count], refs[count:]
    blocks_ref[...] = head_blocks()
    here = meta_ref[0]
    half = tokens // 2
    size = tokens
    blocks = count

    def prepare(place, carry):
        first, low_lane = lane_masks(half)
        source = aligned(row_of(place, here, tokens, count), half)
        target = aligned(place * half, half)
        cosine = cos_ref[pl.ds(target, half), :]
        sine = sin_ref[pl.ds(target, half), :]
        query = lin_ref[pl.ds(source, half), : 2 * HD]
        unit = query * lax.rsqrt(head_mean(query * query, blocks_ref[...]) + EPSILON) * gains_ref[2:3, :]
        turned = unit * cosine + swap_half(unit, low_lane) * sine
        query_ref[pl.ds(target, half), :] = (
            turned.astype(jnp.bfloat16).astype(jnp.float32) * (HD**-0.5)
        ).astype(jnp.bfloat16)
        both = lin_ref[pl.ds(source, half), 2 * HD :]
        unit = both * lax.rsqrt(head_mean(both * both, blocks_ref[...]) + EPSILON) * gains_ref[3:4, :]
        turned = unit * cosine + swap_half(unit, low_lane) * sine
        key_ref[pl.ds(target, half), :] = jnp.where(
            first, turned, pltpu.roll(turned, HD, 1)
        ).astype(jnp.bfloat16)
        values = jnp.where(first, pltpu.roll(both, HD, 1), both)
        value_ref[pl.ds(target, half), :] = values.astype(jnp.bfloat16)
        return carry

    lax.fori_loop(0, 2 * count, prepare, 0)

    def turn_values(block, carry):
        values = wide(value_ref[pl.ds(aligned(block * size, size), size), :])
        value_t[block, :HD, :] = values.T[:HD].astype(jnp.bfloat16)
        value_t[block, HD:, :] = jnp.ones((value_t.shape[1] - HD, size), jnp.bfloat16)
        return carry

    lax.fori_loop(0, blocks, turn_values, 0)

    def query_step(block, carry):
        query = two_heads(query_ref[pl.ds(aligned(block * size, size), size), :])
        accum[...] = jnp.zeros_like(accum)
        lowest = begin_at(meta_ref, docs, block * size) // size

        def key_step(other, carry):
            keys = key_ref[pl.ds(aligned(other * size, size), size), :]
            scores = dot_nt(keys, query)
            visible = block_visible(meta_ref, docs, block, other, size)
            probable = jnp.concatenate(
                [
                    jnp.where(visible, jnp.exp(scores[:, :size]), 0.0),
                    jnp.where(visible, jnp.exp(scores[:, size:]), 0.0),
                ],
                axis=1,
            ).astype(jnp.bfloat16)
            accum[...] += dot_nn(value_t[other], probable)
            return carry

        lax.fori_loop(lowest, block + 1, key_step, 0)
        mass = accum[HD : HD + 1, :]
        mixed = accum[:HD, :] / mass
        lse_ref[block] = jnp.log(mass)
        rows = jnp.concatenate([mixed[:, :size], mixed[:, size:]], axis=0).T
        attn_ref[pl.ds(aligned(block * size, size), size), :] = rows
        for part in range(2):
            target = aligned(row_of(2 * block + part, here, tokens, count), half)
            low[pl.ds(target, half), :] = rows[part * half : (part + 1) * half].astype(jnp.bfloat16)
        return carry

    lax.fori_loop(0, blocks, query_step, 0)
    for slot, bits in enumerate(ORDER):
        low_refs[bits][...] = low[slot * tokens : (slot + 1) * tokens, :]


def attention_back_kernel(
    tokens, count, docs,
    meta_ref, lin_ref, cos_ref, sin_ref, gains_ref,
    query_ref, key_ref, value_ref, attn_ref, lse_ref, *refs,
):
    grad_refs = refs[:count]
    out_ref, gain_ref = refs[count : count + 2]
    block_refs = refs[count + 2 : 2 * count + 2]
    key_t, grad_query, grad_key, grad_value, accum, grad_rows, blocks_ref = refs[2 * count + 2 :]
    blocks_ref[...] = head_blocks()
    here = meta_ref[0]
    half = tokens // 2
    size = tokens
    blocks = count
    grad_key[...] = jnp.zeros_like(grad_key)
    grad_value[...] = jnp.zeros_like(grad_value)
    gain_ref[...] = jnp.zeros_like(gain_ref)
    for slot, bits in enumerate(ORDER):
        grad_rows[slot * tokens : (slot + 1) * tokens, :] = grad_refs[bits][...]

    def turn_keys(block, carry):
        keys = wide(key_ref[pl.ds(aligned(block * size, size), size), :])
        key_t[block] = keys.T[:HD].astype(jnp.bfloat16)
        return carry

    lax.fori_loop(0, blocks, turn_keys, 0)

    def query_step(block, carry):
        here_rows = pl.ds(aligned(block * size, size), size)
        query = two_heads(query_ref[here_rows, :])
        parts = []
        for part in range(2):
            source = aligned(row_of(2 * block + part, here, tokens, count), half)
            parts.append(grad_rows[pl.ds(source, half), :])
        grads = jnp.concatenate(parts, axis=0)
        products = (wide(grads) * attn_ref[here_rows, :]).T
        deltas = (
            jnp.sum(products[:HD], axis=0, keepdims=True),
            jnp.sum(products[HD:], axis=0, keepdims=True),
        )
        grads = two_heads(grads)
        lse = lse_ref[block]
        accum[...] = jnp.zeros_like(accum)
        lowest = begin_at(meta_ref, docs, block * size) // size

        def key_step(other, carry):
            rows = pl.ds(aligned(other * size, size), size)
            scores = dot_nt(key_ref[rows, :], query)
            grad_prob = dot_nt(value_ref[rows, :], grads)
            visible = block_visible(meta_ref, docs, block, other, size)
            probs, grad_scores = [], []
            for head in range(2):
                cols = slice(head * size, (head + 1) * size)
                prob = jnp.where(visible, jnp.exp(scores[:, cols] - lse[:, cols]), 0.0)
                probs.append(prob)
                grad_scores.append(prob * (grad_prob[:, cols] - deltas[head]))
            probs = jnp.concatenate(probs, axis=1).astype(jnp.bfloat16)
            grad_scores = jnp.concatenate(grad_scores, axis=1).astype(jnp.bfloat16)
            grad_value[rows, :] += dot_nn(probs, grads)
            grad_key[rows, :] += dot_nn(grad_scores, query)
            accum[...] += dot_nn(key_t[other], grad_scores)
            return carry

        lax.fori_loop(lowest, block + 1, key_step, 0)
        total = accum[...] * (HD**-0.5)
        grad_query[here_rows, :] = jnp.concatenate([total[:, :size], total[:, size:]], axis=0).T
        return carry

    lax.fori_loop(0, blocks, query_step, 0)

    def finish(place, carry):
        first, low_lane = lane_masks(half)
        source = aligned(row_of(place, here, tokens, count), half)
        target = pl.ds(aligned(place * half, half), half)
        cosine = cos_ref[target, :]
        sine = sin_ref[target, :]

        def through(linear, grads, gain):
            scale = lax.rsqrt(head_mean(linear * linear, blocks_ref[...]) + EPSILON)
            normed = linear * scale
            turned = grads * cosine + swap_half(grads * sine, low_lane)
            weighted = turned * gain
            grad_in = scale * (weighted - normed * head_mean(weighted * normed, blocks_ref[...]))
            return grad_in, jnp.sum(turned * normed, axis=0, keepdims=True)

        grad_in, gain_row = through(
            lin_ref[pl.ds(source, half), : 2 * HD], grad_query[target, :], gains_ref[2:3, :]
        )
        out_ref[pl.ds(source, half), : 2 * HD] = grad_in.astype(jnp.bfloat16)
        gain_ref[0:1, :] += gain_row
        keys = grad_key[target, :]
        grad_in, gain_row = through(
            lin_ref[pl.ds(source, half), 2 * HD :], keys + pltpu.roll(keys, HD, 1), gains_ref[3:4, :]
        )
        gain_ref[1:2, :] += gain_row
        values = grad_value[target, :]
        values = values + pltpu.roll(values, HD, 1)
        out_ref[pl.ds(source, half), 2 * HD :] = jnp.where(first, grad_in, values).astype(
            jnp.bfloat16
        )
        return carry

    lax.fori_loop(0, 2 * count, finish, 0)
    for slot, bits in enumerate(ORDER):
        block_refs[bits][...] = out_ref[slot * tokens : (slot + 1) * tokens, :]


def proj_grad_kernel(parts, meta_ref, attn_ref, grad_ref, *refs):
    blocks, full = refs[:-1], refs[-1]
    count = len(blocks)
    here = meta_ref[0]
    tile = 2 * pair_tile(full)

    def outer(index, carry):
        part = pl.ds(aligned(index * tile, tile), tile)
        full[part, :] = contract_rows(attn_ref[:, part], grad_ref[...]).astype(jnp.bfloat16)
        return carry

    lax.fori_loop(0, full.shape[0] // tile, outer, 0)
    rows = blocks[0].shape[0] // parts
    for bits, block in enumerate(blocks):
        owner = lax.bitwise_xor(here, bits)
        for part in range(parts):
            source = aligned(part * count * rows + owner * rows, rows)
            block[part * rows : (part + 1) * rows, :] = full[pl.ds(source, rows), :]


def pack_heads_kernel(
    extra, meta_ref, heads_ref, mixer_ref, gain_ref, feed_ref, sums_ref, *refs
):
    proj_refs, pieces = refs[:5], refs[5:]
    shard = meta_ref[1]
    rows = heads_ref.shape[0] // 4
    pair = 2 * HD
    proj = wide(proj_refs[0][...])
    for other in proj_refs[1:]:
        proj = proj + wide(other[...])
    proj_low, mixer, _, gains = pieces[4:]
    pieces = pieces[:4]
    part = proj.shape[0] // 4
    proj_low[...] = proj.astype(jnp.bfloat16)
    mixer[...] = mixer_ref[...] / gain_ref[...]
    values = sums_ref[...]
    lower = lax.broadcasted_iota(jnp.int32, values.shape, 0) == 0
    values = values + jnp.where(lower, pltpu.roll(values, HD, 1), 0.0)
    each = HD // 4
    lanes = lax.broadcasted_iota(jnp.int32, values.shape, 1)
    for bits, piece in enumerate(pieces):
        owner = lax.bitwise_xor(shard, bits)
        piece[:rows, :] = heads_ref[pl.ds(aligned(owner * rows, rows), rows), :]
        gains[...] = jnp.zeros_like(gains)
        own = pl.ds(aligned(owner * rows, rows), rows)
        gains[0:1, :] = mixer[:, own]
        gains[1:2, :] = feed_ref[:, own]
        moved = pltpu.roll(values, pair - owner * each, 1)
        moved = jnp.where(lanes < each, moved, 0.0)
        gains[2:4, :pair] = moved[0:2, :]
        piece[rows : rows + extra, :] = gains[...].astype(jnp.bfloat16)
        for index in range(proj.shape[1] // (2 * pair)):
            target = rows + extra + index * part
            piece[target : target + part, :] = proj_low[
                pl.ds(aligned(owner * part, part), part), index * 2 * pair : (index + 1) * 2 * pair
            ]


def file_down(piece_ref, down_ref, rows, owner):
    width = down_ref.shape[1]
    each = piece_ref.shape[0] - rows - 128
    piece_ref[rows : rows + 128, :width] = down_ref[pl.ds(aligned(owner * 128, 128), 128), :]
    piece_ref[rows + 128 :, :width] = down_ref[pl.ds(aligned(4 * 128 + owner * each, 16), each), :]
    piece_ref[rows:, width:] = jnp.zeros_like(piece_ref[rows:, width:])


def first_piece_kernel(meta_ref, hidden_ref, grad_ref, down_ref, piece_ref, total):
    step = pl.program_id(0)
    rows = total.shape[0]
    product = contract_rows(hidden_ref[...], grad_ref[...])

    @pl.when(step == 0)
    def _():
        total[...] = product

    @pl.when(step > 0)
    def _():
        total[...] += product

    @pl.when(step == pl.num_programs(0) - 1)
    def _():
        piece_ref[:rows, :] = total[...].astype(jnp.bfloat16)
        file_down(piece_ref, down_ref, rows, lax.bitwise_xor(meta_ref[1], 3))


def first_piece_call(meta, hidden, grads, down, rows, inner):
    stream, _ = hidden.shape
    columns = grads.shape[1]
    size = stream // 4
    return pl.pallas_call(
        first_piece_kernel,
        out_shape=shaped((rows + inner, columns)),
        grid_spec=pltpu.PrefetchScalarGridSpec(
            num_scalar_prefetch=1,
            grid=(4,),
            in_specs=[
                pl.BlockSpec((size, rows), lambda step, meta_ref: (step, lax.bitwise_xor(meta_ref[1], 3))),
                pl.BlockSpec((size, columns), lambda step, meta_ref: (step, 0)),
                pl.BlockSpec(down.shape, lambda step, meta_ref: (0, 0)),
            ],
            out_specs=pl.BlockSpec((rows + inner, columns), lambda step, meta_ref: (0, 0)),
            scratch_shapes=[pltpu.VMEM((rows, columns), jnp.float32)],
        ),
        cost_estimate=pl.CostEstimate(
            flops=2 * stream * rows * columns, bytes_accessed=stream * columns * 2, transcendentals=0
        ),
        compiler_params=pltpu.CompilerParams(vmem_limit_bytes=16 * 2**20),
        name="first_piece",
    )(meta, hidden, grads, down)


def pack_feed_kernel(meta_ref, wide_ref, down_ref, *pieces):
    shard = meta_ref[1]
    rows = wide_ref.shape[0] // 4
    for bits, piece in enumerate(pieces):
        owner = lax.bitwise_xor(shard, bits)
        piece[:rows, :] = wide_ref[pl.ds(aligned(owner * rows, 16), rows), :]
        file_down(piece, down_ref, rows, owner)


def input_grad_kernel(count, meta_ref, *refs):
    grads, weights = refs[:count], refs[count : 2 * count]
    input_ref, grad_ref, gain_ref, out_ref = refs[2 * count :]
    total = dot_nt(grads[0][...], weights[0][...])
    for left, right in zip(grads[1:], weights[1:]):
        total = total + dot_nt(left[...], right[...])
    values = wide(input_ref[...])
    scale = lax.rsqrt(jnp.mean(values * values, axis=1, keepdims=True) + EPSILON)
    normed = values * scale
    weighted = total * gain_ref[...]
    grad_in = scale * (weighted - normed * jnp.mean(weighted * normed, axis=1, keepdims=True))
    out_ref[...] = grad_ref[...] + grad_in


def project_kernel(count, parts, start, meta_ref, *refs):
    attn_refs, weight_refs, rest = refs[:count], refs[count : 2 * count], refs[2 * count :]
    input_ref, gain_ref, full_ref, attn_out_ref, mixed_ref, hidden_ref, attn_sem, weight_sem = rest
    here = meta_ref[0]
    rows = (weight_refs[0].shape[0] - start) // parts
    copies = []
    for bits in range(count):
        owner = lax.bitwise_xor(here, bits)
        copies.append(
            pltpu.make_async_copy(
                attn_refs[bits],
                attn_out_ref.at[:, pl.ds(aligned(owner * 2 * HD, 2 * HD), 2 * HD)],
                attn_sem.at[bits],
            )
        )
        for part in range(parts):
            target = aligned(part * count * rows + owner * rows, rows)
            copies.append(
                pltpu.make_async_copy(
                    weight_refs[bits].at[pl.ds(start + part * rows, rows), :],
                    full_ref.at[pl.ds(target, rows), :],
                    weight_sem.at[bits * parts + part],
                )
            )
    for copy in copies:
        copy.start()
    for copy in copies:
        copy.wait()
    tile = 2 * pair_tile(full_ref)

    def project(index, carry):
        part = pl.ds(aligned(index * tile, tile), tile)
        mixed_ref[:, part] = wide(input_ref[:, part]) + dot_nn(attn_out_ref[...], full_ref[:, part])
        return carry

    lax.fori_loop(0, full_ref.shape[1] // tile, project, 0)
    mixed = mixed_ref[...]
    scale = lax.rsqrt(jnp.mean(mixed * mixed, axis=1, keepdims=True) + EPSILON)
    hidden_ref[...] = (mixed * scale * gain_ref[...]).astype(jnp.bfloat16)


def feed_block(hidden_ref, grad_ref, wide_ref, down_ref, act_ref, grad_wide_ref, out_ref, back_ref):
    tokens = hidden_ref.shape[0]
    inner = wide_ref.shape[1] // 2
    main = inner // 128 * 128
    first, _ = lane_masks(tokens)

    def activate(gate, up, grad_act):
        sigmoid = 1.0 / (1.0 + jnp.exp(-gate))
        silu = gate * sigmoid
        grad_gate = grad_act * up * sigmoid * (1.0 + gate * (1.0 - sigmoid))
        return silu * up, grad_gate, grad_act * silu

    both = dot_nn(hidden_ref[...], wide_ref[...])
    grad_act = dot_nt(grad_ref[...], down_ref[...])
    act, grad_gate, grad_up = activate(
        both[:, :main], both[:, main : 2 * main], grad_act[:, :main]
    )
    act_ref[:, :main] = act.astype(jnp.bfloat16)
    grad_wide_ref[:, :main] = grad_gate.astype(jnp.bfloat16)
    grad_wide_ref[:, main : 2 * main] = grad_up.astype(jnp.bfloat16)
    last = both[:, 2 * main :]
    act, grad_gate, grad_up = activate(last, pltpu.roll(last, HD, 1), grad_act[:, main:])
    act_ref[:, main:] = jnp.where(first, act, 0.0).astype(jnp.bfloat16)
    grad_wide_ref[:, 2 * main :] = jnp.where(
        first, grad_gate, pltpu.roll(grad_up, HD, 1)
    ).astype(jnp.bfloat16)
    back_ref[...] = dot_nt(grad_wide_ref[...], wide_ref[...]).astype(jnp.bfloat16)
    out_ref[...] = dot_nn(act_ref[...], down_ref[...]).astype(jnp.bfloat16)


def feed_kernel(number, base, first_call, meta_ref, *refs):
    sources = 5 if first_call else 2
    kept = 0 if first_call else 4
    firsts, grads = refs[:number], refs[number : 2 * number]
    pieces = refs[2 * number : 2 * number + sources]
    refs = refs[2 * number + sources + kept :]
    if first_call:
        weight_sem, refs = refs[-1], refs[:-1]
        handed, refs = refs[4 + 2 * number : 6 + 2 * number], (
            refs[: 4 + 2 * number] + refs[6 + 2 * number :]
        )
    act_ref, grad_wide_ref, hidden_all, grad_all = refs[:4]
    out_refs, back_refs = refs[4 : 4 + number], refs[4 + number : 4 + 2 * number]
    hidden, grad, out_low, back_low, wide_ref, down_ref, joined = refs[4 + 2 * number :][:7]
    in_sem, grad_sem, all_sem, grad_all_sem, out_sem, back_sem, piece_sem = refs[11 + 2 * number :]
    tokens, _ = hidden.shape[1:]
    shard = meta_ref[1]
    step = pl.program_id(0)

    def moves(index):
        filed = pl.ds((base + index) * tokens, tokens)
        return (
            pltpu.make_async_copy(firsts[index], hidden.at[index], in_sem.at[index]),
            pltpu.make_async_copy(
                grads[index].at[pl.ds(0, tokens), :], grad.at[index], grad_sem.at[index]
            ),
            pltpu.make_async_copy(hidden.at[index], hidden_all.at[filed, :], all_sem.at[index]),
            pltpu.make_async_copy(grad.at[index], grad_all.at[filed, :], grad_all_sem.at[index]),
            pltpu.make_async_copy(out_low.at[index], out_refs[index], out_sem.at[index]),
            pltpu.make_async_copy(back_low.at[index], back_refs[index], back_sem.at[index]),
        )

    def hand_on():
        return [
            pltpu.make_async_copy(source, target, weight_sem.at[place])
            for place, (source, target) in enumerate(zip((wide_ref, down_ref), handed))
        ]

    @pl.when(step == 0)
    def _():
        if first_call:
            copies = piece_copies(pieces, wide_ref, down_ref, joined, piece_sem, shard)
        else:
            copies = [
                pltpu.make_async_copy(source, target, piece_sem.at[place])
                for place, (source, target) in enumerate(zip(pieces, (wide_ref, down_ref)))
            ]
        for copy in copies:
            copy.start()
        for index in range(number):
            for move in moves(index)[:2]:
                move.start()
        for copy in copies:
            copy.wait()
        if first_call:
            add_last_piece(wide_ref, down_ref, joined, shard)
            for copy in hand_on():
                copy.start()

    for index in range(number):

        @pl.when(step == index)
        def _(index=index):
            for move in moves(index)[:2]:
                move.wait()
            for move in moves(index)[2:4]:
                move.start()

    feed_block(
        hidden.at[step], grad.at[step], wide_ref, down_ref,
        act_ref, grad_wide_ref, out_low.at[step], back_low.at[step],
    )

    for index in range(number):

        @pl.when(step == index)
        def _(index=index):
            for move in moves(index)[4:]:
                move.start()

    @pl.when(step == number - 1)
    def _():
        for index in range(number):
            for move in moves(index)[2:]:
                move.wait()
        if first_call:
            for copy in hand_on():
                copy.wait()


def piece_places(shard, bits, rows, each):
    owner = lax.bitwise_xor(shard, bits)
    return (
        pl.ds(aligned(owner * rows, rows), rows),
        pl.ds(aligned(owner * 128, 128), 128),
        pl.ds(aligned(4 * 128 + owner * each, 16), each),
    )


def piece_copies(pieces, wide_ref, down_ref, joined, sem, shard):
    rows, width = wide_ref.shape[0] // 4, down_ref.shape[1]
    each = joined.shape[1] - rows - 128
    copies = []
    for bits in range(3):
        upper, lower, last = piece_places(shard, bits, rows, each)
        for place, (source, target) in enumerate(
            (
                (pieces[bits].at[pl.ds(0, rows), :], wide_ref.at[upper, :]),
                (pieces[bits].at[pl.ds(rows, 128), pl.ds(0, width)], down_ref.at[lower, :]),
                (pieces[bits].at[pl.ds(rows + 128, each), pl.ds(0, width)], down_ref.at[last, :]),
            )
        ):
            copies.append(pltpu.make_async_copy(source, target, sem.at[3 * bits + place]))
    for index in range(2):
        copies.append(pltpu.make_async_copy(pieces[3 + index], joined.at[index], sem.at[9 + index]))
    return copies


def add_last_piece(wide_ref, down_ref, joined, shard):
    rows, width = wide_ref.shape[0] // 4, down_ref.shape[1]
    middle = rows + 128
    each = joined.shape[1] - middle
    upper, lower, last = piece_places(shard, 3, rows, each)
    wide_ref[upper, :] = joined[0, :rows, :] + joined[1, :rows, :]
    down_ref[lower, :] = joined[0, rows:middle, :width] + joined[1, rows:middle, :width]
    down_ref[last, :] = joined[0, middle:, :width] + joined[1, middle:, :width]
    down_ref[4 * (middle - rows + each) :, :] = jnp.zeros_like(
        down_ref[4 * (middle - rows + each) :, :]
    )


def feed_call(meta, hidden, grads, pieces, kept, blocks, base, padded, grant):
    number = len(hidden)
    first_call = not kept
    tokens, width = hidden[0].shape
    inner = pieces[0].shape[1]
    rows = pieces[0].shape[0] if first_call else 16
    weights = [shaped((width, inner)), shaped((padded, width))] if first_call else []
    low = jnp.bfloat16
    outs = [shaped((blocks * tokens, columns)) for columns in (padded, inner, width, width)]
    outs += [shaped((tokens, width))] * (2 * number) + weights
    return pl.pallas_call(
        functools.partial(feed_kernel, number, base, first_call),
        grid=(number,),
        out_shape=outs,
        in_specs=[SCALARS] + [PLACED] * (2 * number + len(pieces) + len(kept)),
        out_specs=[
            pl.BlockSpec((tokens, padded), lambda step: (base + step, 0)),
            pl.BlockSpec((tokens, inner), lambda step: (base + step, 0)),
        ]
        + [PLACED] * (2 + 2 * number + len(weights)),
        scratch_shapes=[pltpu.VMEM((number, tokens, width), low)] * 4
        + [
            pltpu.VMEM((width, inner), low),
            pltpu.VMEM((padded, width), low),
            pltpu.VMEM((2, rows, inner), low),
        ]
        + [pltpu.SemaphoreType.DMA((number,))] * 6
        + [pltpu.SemaphoreType.DMA((11,))]
        + [pltpu.SemaphoreType.DMA((2,))] * first_call,
        input_output_aliases={
            1 + 2 * number + len(pieces) + place: place for place in range(len(kept))
        },
        cost_estimate=pl.CostEstimate(
            flops=6 * number * tokens * width * inner,
            bytes_accessed=16 * number * tokens * width,
            transcendentals=0,
        ),
        compiler_params=pltpu.CompilerParams(vmem_limit_bytes=grant * 2**20),
        name="feed",
    )(meta, *hidden, *grads, *pieces, *kept)


def feed_back_kernel(count, meta_ref, *refs):
    sums, rest = refs[:5], refs[5:]
    mixed_ref, grad_ref, full_ref, gain_ref, grad_mixed_ref, grad_low_ref, grad_gain_ref = rest[:7]
    block_refs, attn = rest[7 : 7 + count], rest[7 + count]
    here = meta_ref[0]
    grad_hidden = wide(sums[0][...])
    for part in sums[1:]:
        grad_hidden = grad_hidden + wide(part[...])
    mixed = mixed_ref[...]
    scale = lax.rsqrt(jnp.mean(mixed * mixed, axis=1, keepdims=True) + EPSILON)
    normed = mixed * scale
    weighted = grad_hidden * gain_ref[...]
    grad_in = scale * (weighted - normed * jnp.mean(weighted * normed, axis=1, keepdims=True))
    grad_gain_ref[...] = jnp.sum(grad_hidden * normed, axis=0, keepdims=True)
    grad_mixed = wide(grad_ref[...]) + grad_in
    grad_mixed_ref[...] = grad_mixed
    grad_low_ref[...] = grad_mixed.astype(jnp.bfloat16)
    tile = 2 * pair_tile(full_ref)

    def project_back(index, carry):
        part = pl.ds(aligned(index * tile, tile), tile)
        attn[:, part] = dot_nt(grad_low_ref[...], full_ref[part, :]).astype(jnp.bfloat16)
        return carry

    lax.fori_loop(0, full_ref.shape[0] // tile, project_back, 0)
    for bits in range(count):
        owner = lax.bitwise_xor(here, bits)
        block_refs[bits][...] = attn[:, pl.ds(aligned(owner * 2 * HD, 2 * HD), 2 * HD)]


def wide_out_kernel(count, parts, meta_ref, *refs):
    blocks, lowers = refs[:count], refs[count : 2 * count]
    gate_ref, up_ref, down_out, down_ref, down_sem = refs[2 * count :]
    here = meta_ref[0]
    tile = gate_ref.shape[0]
    inner = blocks[0].shape[1] // 2
    main = inner // 128 * 128
    each = (inner - main) // parts
    span = gate_ref.shape[1] // parts
    left = span - 128
    lanes = lax.broadcasted_iota(jnp.int32, (tile, 128), 1)
    owners = [lax.bitwise_xor(here, bits) for bits in range(count)]
    for kind, out_ref in enumerate((gate_ref, up_ref)):
        for part in range(parts):
            place = kind * parts + part
            for bits, owner in enumerate(owners):
                target = pl.ds(aligned(part * span + owner * 128, 128), 128)
                out_ref[:, target] = wide(blocks[bits][:, place * 128 : (place + 1) * 128])
    lasts = [wide(block[:, 2 * main :]) for block in blocks]
    for kind, out_ref in enumerate((gate_ref, up_ref)):
        for part in range(parts):
            place = kind * parts + part
            total = jnp.zeros((tile, 128), jnp.float32)
            for bits, owner in enumerate(owners):
                moved = pltpu.roll(lasts[bits], 128 + (owner - place) * each, 1)
                total = jnp.where((lanes >= owner * each) & (lanes < (owner + 1) * each), moved, total)
            out_ref[:, part * span + left : part * span + left + 128] = total

    @pl.when(pl.program_id(0) == 0)
    def _():
        rows = count * 128
        for bits, owner in enumerate(owners):
            low = wide(lowers[bits][:, : down_ref.shape[1]])
            down_ref[pl.ds(aligned(owner * 128, 128), 128), :] = low[:128]
            down_ref[pl.ds(aligned(rows + owner * each, 16), each), :] = low[128:]
        pltpu.make_async_copy(down_ref, down_out, down_sem).start()

    @pl.when(pl.program_id(0) == pl.num_programs(0) - 1)
    def _():
        pltpu.make_async_copy(down_ref, down_out, down_sem).wait()


def heads_out_kernel(count, own, extra, meta_ref, *refs):
    blocks, rest = refs[:count], refs[count:]
    query_ref, key_ref, value_ref, proj_ref, gain_ref, held = rest
    here = meta_ref[0]
    pair = 2 * HD
    part = (blocks[0].shape[0] - own - extra) // 4
    gains = jnp.zeros(gain_ref.shape, jnp.float32)
    for bits in range(count):
        owner = lax.bitwise_xor(here, bits)
        block = wide(blocks[bits][...])
        query_ref[:, pl.ds(aligned(owner * pair, pair), pair)] = block[:own, :pair]
        held[owner] = block[:own, pair:]
        gains = gains + block[own : own + extra, :]
        for index in range(4):
            source = own + extra + index * part
            proj_ref[
                pl.ds(aligned(owner * part, part), part), index * 2 * pair : (index + 1) * 2 * pair
            ] = block[source : source + part, :]
    gain_ref[...] = gains
    first, _ = lane_masks(own)
    for index in range(count // 2):
        early, late = held[2 * index], held[2 * index + 1]
        lanes = slice(index * pair, (index + 1) * pair)
        key_ref[:, lanes] = jnp.where(first, early, pltpu.roll(late, HD, 1))
        value_ref[:, lanes] = jnp.where(first, pltpu.roll(early, HD, 1), late)


SCALARS = pl.BlockSpec(memory_space=pltpu.SMEM)
WHOLE = pl.BlockSpec(memory_space=pltpu.VMEM)
PLACED = pl.BlockSpec(memory_space=pl.ANY)
FAR = pl.BlockSpec(memory_space=pltpu.HBM)


def shaped(shape, kind=jnp.bfloat16):
    return jax.ShapeDtypeStruct(shape, kind)


def whole_call(kernel, outs, ins, flops, scratch=(), grant=24, specs=None):
    moved = sum(math.prod(out.shape) * out.dtype.itemsize for out in outs)
    return pl.pallas_call(
        kernel,
        out_shape=outs,
        in_specs=[SCALARS] + (specs or [WHOLE] * ins),
        out_specs=[WHOLE] * len(outs),
        scratch_shapes=list(scratch),
        cost_estimate=pl.CostEstimate(
            flops=int(flops), bytes_accessed=int(2 * moved), transcendentals=0
        ),
        compiler_params=pltpu.CompilerParams(vmem_limit_bytes=grant * 2**20),
    )


def local_heads(
    block_input, doc_starts, out_grad, query_weight, key_weight, value_weight, output_weight,
    gate_weight, up_weight, down_weight, mixer_gain, feed_gain, query_gain, key_gain,
):
    low = jnp.bfloat16
    tokens, width = block_input.shape[1:]
    count = lax.axis_size("ctx")
    shards = lax.axis_size("fsdp")
    here = lax.axis_index("ctx").astype(jnp.int32)
    shard = lax.axis_index("fsdp").astype(jnp.int32)
    stream = tokens * count
    docs = doc_starts.shape[1]
    pair = 2 * HD
    own_rows = width // shards
    extra = 16
    meta = jnp.concatenate([here[None], shard[None], doc_starts[0].astype(jnp.int32)])
    own_input = block_input[0]
    own_grad = out_grad[0]
    inner = down_weight.shape[0] // count
    wide_inner = inner * shards
    padded = -(-wide_inner // 128) * 128
    proj_rows = own_rows // count
    edges = [(0, 1), (3, 2)]
    middle = [(1, 2), (2, 1)]
    relay = [(1, 0), (2, 3)]

    def near(piece, bits):
        return shift_fsdp(piece, flipped(bits, shards))

    across, along, partner = gather_near(own_input)
    corner = swap_ctx(own_input, 6)
    piece_rows = own_rows + extra + 4 * proj_rows
    head_piece = whole_call(
        take_heads_kernel,
        [shaped((piece_rows, 2 * pair))],
        8,
        0,
        [
            pltpu.VMEM((extra, 2 * pair), jnp.float32),
            pltpu.VMEM((3, own_rows, pair), low),
            pltpu.VMEM((proj_rows, width), low),
            pltpu.SemaphoreType.DMA((4,)),
        ],
        grant=60,
        specs=[FAR] * 4 + [WHOLE] * 4,
    )(
        meta, query_weight, key_weight, value_weight, output_weight,
        mixer_gain, feed_gain, query_gain, key_gain,
    )[0]
    head_pieces = [head_piece] + [near(head_piece, bits) for bits in (1, 2, 3)]
    feed_rows = own_rows + inner
    feed_piece = whole_call(
        functools.partial(take_wide_kernel, shards),
        [shaped((feed_rows, 2 * wide_inner))],
        3,
        2 * own_rows * 2 * wide_inner * 2048,
        [
            pltpu.VMEM((2 * shards, own_rows, 128), low),
            pltpu.VMEM((inner, width), low),
            pltpu.SemaphoreType.DMA((2 * shards,)),
            pltpu.SemaphoreType.DMA((2 * shards,)),
            pltpu.SemaphoreType.DMA((2,)),
        ],
        grant=60,
        specs=[FAR] * 3,
    )(behind(meta, head_piece), gate_weight, up_weight, down_weight)[0]
    feed_near = near(feed_piece, 1)
    feed_far = near(behind(feed_piece, *head_pieces[1:]), 2)
    others = gather_far(across, along, corner)
    input_blocks = [own_input, partner, across, others[0], along, others[1], corner, others[2]]

    where_at = jnp.arange(stream, dtype=jnp.int32)
    begins = doc_begin(doc_starts[0], where_at)
    lanes = jnp.arange(pair) % (HD // 2)
    frequency = ROPE_BASE ** (-(2.0 * lanes.astype(jnp.float32)) / HD)
    angles = (where_at - begins).astype(jnp.float32)[:, None] * frequency[None, :]
    cosine = jnp.cos(angles)
    sine = jnp.sin(angles) * jnp.where(jnp.arange(pair) % HD < HD // 2, -1.0, 1.0)[None, :]

    heads_weight, gain_mixer, gain_feed, gain_heads, proj_part = whole_call(
        functools.partial(arrange_heads_kernel, extra),
        [
            shaped((width, 2 * pair)),
            shaped((1, width), jnp.float32),
            shaped((1, width), jnp.float32),
            shaped((8, pair), jnp.float32),
            shaped((shards * proj_rows, width)),
        ],
        4,
        0,
        grant=8,
    )(behind(meta, cosine, sine), *head_pieces)

    hidden_in, linear = pl.pallas_call(
        functools.partial(head_linear_kernel, count),
        grid=(count // 2,),
        in_specs=[SCALARS]
        + [PLACED] * count
        + [
            pl.BlockSpec((width, 2 * pair), lambda step: (0, 0)),
            pl.BlockSpec((1, width), lambda step: (0, 0)),
        ],
        out_specs=[
            pl.BlockSpec((2 * tokens, width), lambda step: (step, 0)),
            pl.BlockSpec((2 * tokens, 2 * pair), lambda step: (step, 0)),
        ],
        out_shape=[shaped((stream, width)), shaped((stream, 2 * pair), jnp.float32)],
        scratch_shapes=[
            pltpu.VMEM((count // 2, 2 * tokens, width), low),
            pltpu.SemaphoreType.DMA((count,)),
        ],
        cost_estimate=pl.CostEstimate(
            flops=4 * stream * width * pair, bytes_accessed=6 * stream * width, transcendentals=0
        ),
        compiler_params=pltpu.CompilerParams(vmem_limit_bytes=60 * 2**20),
        name="head_linear",
    )(meta, *[input_blocks[bits] for bits in ORDER], heads_weight, gain_mixer)

    pairs = stream * stream // 2
    extra_piece = behind(jnp.concatenate([own_grad, proj_part], axis=0), corner)
    extra_across, extra_along, extra_partner = gather_near(extra_piece)
    extra_corner = swap_ctx(extra_piece, 6)
    query_att, key_att, value_att, attn, lse, *attn_low = whole_call(
        functools.partial(attention_kernel, tokens, count, docs),
        [
            shaped((stream, pair)),
            shaped((stream, pair)),
            shaped((stream, pair)),
            shaped((stream, pair), jnp.float32),
            shaped((count, 1, 2 * tokens), jnp.float32),
        ]
        + [shaped((tokens, pair))] * count,
        4,
        8 * pairs * HD,
        [
            pltpu.VMEM((count, HD + 16, tokens), low),
            pltpu.VMEM((HD + 16, 2 * tokens), jnp.float32),
            pltpu.VMEM((stream, pair), low),
            pltpu.VMEM((pair, pair), low),
        ],
        grant=60,
    )(meta, linear, cosine, sine, gain_heads)

    attn_blocks = exchange_plane(attn_low)
    feed_middle = shift_fsdp(behind(feed_piece, attn_blocks[1]), middle)
    feed_relay = shift_fsdp(behind(feed_far, attn_blocks[1]), relay)
    extra_others = gather_far(extra_across, extra_along, extra_corner, attn_blocks[1])
    extra_blocks = [
        extra_piece, extra_partner, extra_across, extra_others[0],
        extra_along, extra_others[1], extra_corner, extra_others[2],
    ]
    full_proj, attn_rows, mixed, hidden_mid = whole_call(
        functools.partial(project_kernel, count, shards, tokens),
        [
            shaped((width, width)),
            shaped((tokens, width)),
            shaped((tokens, width), jnp.float32),
            shaped((tokens, width)),
        ],
        2 * count + 2,
        2 * tokens * width * width,
        [pltpu.SemaphoreType.DMA((count,)), pltpu.SemaphoreType.DMA((shards * count,))],
        grant=60,
        specs=[PLACED] * (2 * count) + [WHOLE] * 2,
    )(meta, *attn_blocks, *extra_blocks, own_input, gain_feed)

    hidden_across, hidden_along, hidden_partner = gather_near(hidden_mid)
    hidden_corner = swap_ctx(hidden_mid, 6)
    *kept, out_0, out_1, back_0, back_1, wide_weight, down_part = feed_call(
        meta,
        [hidden_mid, hidden_partner],
        extra_blocks[:2],
        (feed_piece, feed_near, feed_far, feed_middle, feed_relay),
        [],
        count,
        count - 2,
        padded,
        60,
    )
    hidden_far = gather_far(hidden_across, hidden_along, hidden_corner, out_0)
    weight_piece = behind(heads_weight, hidden_far[2])
    weight_near = gather_near(weight_piece)
    weight_corner = swap_ctx(weight_piece, 6)
    act_all, grad_wide_all, hidden_all, grad_all, *parts = feed_call(
        meta,
        [hidden_across, hidden_far[0], hidden_along, hidden_far[1], hidden_corner, hidden_far[2]],
        extra_blocks[2:],
        (wide_weight, down_part),
        kept,
        count,
        0,
        padded,
        60,
    )
    out_parts = [out_0, out_1, *parts[: count - 2]]
    back_parts = [back_0, back_1, *parts[count - 2 :]]
    back_own, back_pairs = scatter_pair(back_parts)
    back_sums = back_own + scatter_links(back_pairs)

    def scatter_early(pieces):
        return shift_fsdp(pieces[3], edges), shift_fsdp(pieces[3], middle)

    def scatter_late(pieces, early, *ready):
        second = behind((wide(pieces[2]) + wide(early)).astype(low), *ready)
        return near(second, 2), near(behind(pieces[1], *ready), 1)

    grad_down = contract_rows(behind(act_all, *back_pairs), grad_all).astype(low)
    first_piece = first_piece_call(meta, hidden_all, grad_wide_all, grad_down, own_rows, inner)
    grad_wide = contract_rows(behind(hidden_all, first_piece), grad_wide_all).astype(low)
    feed_pieces = whole_call(
        pack_feed_kernel, [shaped((feed_rows, 2 * wide_inner))] * 3, 2, 0, grant=16
    )(meta, grad_wide, grad_down)
    feed_pieces = [*feed_pieces, first_piece]
    wide_edge, wide_middle = scatter_early(feed_pieces)
    out_own, out_pairs = scatter_pair([behind(part, grad_wide) for part in out_parts])

    grad_mixed, grad_mixed_low, grad_feed, *grad_blocks = whole_call(
        functools.partial(feed_back_kernel, count),
        [
            shaped((tokens, width), jnp.float32),
            shaped((tokens, width)),
            shaped((1, width), jnp.float32),
        ]
        + [shaped((tokens, pair))] * count,
        9,
        2 * tokens * width * width,
        [pltpu.VMEM((tokens, width), low)],
        grant=8,
    )(meta, *back_sums, mixed, own_grad, full_proj, gain_feed)
    grad_attn = exchange_plane(grad_blocks)
    wide_late = scatter_late(feed_pieces, wide_edge, grad_blocks[0])
    proj_blocks = whole_call(
        functools.partial(proj_grad_kernel, shards),
        [shaped((shards * proj_rows, width))] * count,
        2,
        2 * tokens * width * width,
        [pltpu.VMEM((width, width), low)],
        grant=8,
    )(meta, attn_rows, grad_mixed_low)
    proj_own, proj_pairs = scatter_pair(proj_blocks)
    proj_parts = proj_own + scatter_links(proj_pairs)
    out_sums = out_own + scatter_links([behind(part, grad_blocks[0]) for part in out_pairs])

    back_outs = whole_call(
        functools.partial(attention_back_kernel, tokens, count, docs),
        [shaped((stream, 2 * pair)), shaped((8, pair), jnp.float32)]
        + [shaped((tokens, 2 * pair))] * count,
        9 + count,
        20 * pairs * HD,
        [
            pltpu.VMEM((count, HD, tokens), low),
            pltpu.VMEM((stream, pair), jnp.float32),
            pltpu.VMEM((stream, pair), jnp.float32),
            pltpu.VMEM((stream, pair), jnp.float32),
            pltpu.VMEM((HD, 2 * tokens), jnp.float32),
            pltpu.VMEM((stream, pair), low),
            pltpu.VMEM((pair, pair), low),
        ],
        grant=14,
    )(meta, linear, cosine, sine, gain_heads, query_att, key_att, value_att, attn, lse, *grad_attn)
    grad_linear, gain_sums, *token_blocks = back_outs

    token_grads = exchange_plane(token_blocks)
    weight_far = gather_far(weight_near[0], weight_near[1], weight_corner, token_grads[1])
    weight_all = [
        weight_piece, weight_near[2], weight_near[0], weight_far[0],
        weight_near[1], weight_far[1], weight_corner, weight_far[2],
    ]
    late_linear = behind(grad_linear, token_grads[1])
    grad_heads = contract_rows(hidden_in, late_linear).astype(low)
    grad_mixer = jnp.sum(
        contract_cols(late_linear, heads_weight) * wide(hidden_in), axis=0, keepdims=True
    )
    packed = whole_call(
        functools.partial(pack_heads_kernel, extra),
        [shaped((piece_rows, 2 * pair))] * shards,
        10,
        0,
        [
            pltpu.VMEM((shards * proj_rows, width), low),
            pltpu.VMEM((1, width), jnp.float32),
            pltpu.VMEM((8, pair), jnp.float32),
            pltpu.VMEM((extra, 2 * pair), jnp.float32),
        ],
        grant=6,
    )(meta, grad_heads, grad_mixer, gain_mixer, grad_feed, gain_sums, *proj_parts)
    heads_sent = [near(packed[bits], bits) for bits in (1, 2, 3)]

    def total_of(first, *parts):
        return sum([wide(part) for part in parts], wide(first)).astype(low)

    def total_late(pieces, parts, *ready):
        return total_of(pieces[0], *[behind(part, *ready) for part in parts])

    wide_total = total_late(feed_pieces, (wide_middle,) + wide_late, grad_linear)
    wide_blocks = gather_plane(wide_total)
    input_grad = whole_call(
        functools.partial(input_grad_kernel, count),
        [shaped((tokens, width), jnp.float32)],
        2 * count + 3,
        2 * tokens * width * 2 * width,
        grant=10,
    )(meta, *token_grads, *weight_all, own_input, grad_mixed, gain_mixer)[0]
    heads_total = total_of(packed[0], *heads_sent)
    heads_blocks = gather_direct(heads_total)
    block_output = (
        mixed + sum(wide(behind(part, packed[0])) for part in out_sums)
    ).astype(low)[None]

    steps = 8
    tile = own_rows // steps
    full = wide_inner * count
    out_gate, out_up, out_down = pl.pallas_call(
        functools.partial(wide_out_kernel, count, shards),
        grid=(steps,),
        in_specs=[SCALARS]
        + [pl.BlockSpec((tile, 2 * wide_inner), lambda step: (step, 0))] * count
        + [pl.BlockSpec((pl.Element(inner), pl.Element(2 * wide_inner)), lambda step: (own_rows, 0))]
        * count,
        out_specs=[
            pl.BlockSpec((tile, full), lambda step: (step, 0)),
            pl.BlockSpec((tile, full), lambda step: (step, 0)),
            PLACED,
        ],
        out_shape=[
            shaped((own_rows, full), jnp.float32),
            shaped((own_rows, full), jnp.float32),
            shaped((count * inner, width), jnp.float32),
        ],
        scratch_shapes=[
            pltpu.VMEM((count * inner, width), jnp.float32),
            pltpu.SemaphoreType.DMA(()),
        ],
        compiler_params=pltpu.CompilerParams(vmem_limit_bytes=40 * 2**20),
        name="wide_out",
    )(meta, *wide_blocks, *wide_blocks)
    out_query, out_key, out_value, out_proj, gain_out = whole_call(
        functools.partial(heads_out_kernel, count, own_rows, extra),
        [
            shaped((own_rows, width), jnp.float32),
            shaped((own_rows, KVH * HD), jnp.float32),
            shaped((own_rows, KVH * HD), jnp.float32),
            shaped((own_rows, width), jnp.float32),
            shaped((extra, 2 * pair), jnp.float32),
        ],
        count,
        0,
        [pltpu.VMEM((count, own_rows, pair), jnp.float32)],
    )(meta, *heads_blocks)
    return (
        block_output,
        input_grad[None],
        out_query,
        out_key,
        out_value,
        out_proj,
        out_gate,
        out_up,
        out_down,
        gain_out[0],
        gain_out[1],
        gain_out[2, : query_gain.shape[0]],
        gain_out[3, : key_gain.shape[0]],
    )


def divides_heads(mesh):
    return mesh.shape["ctx"] == KVH and mesh.shape["fsdp"] == 4 and H == 2 * KVH


def solution(mesh):
    in_specs = (
        P("fsdp", "ctx", None),
        P("fsdp", None),
        P("fsdp", "ctx", None),
        P("fsdp", None),
        P("fsdp", None),
        P("fsdp", None),
        P("fsdp", None),
        P("fsdp", None),
        P("fsdp", None),
        P("fsdp", None),
        P("fsdp"),
        P("fsdp"),
        P("fsdp"),
        P("fsdp"),
    )
    out_specs = (
        P("fsdp", "ctx", None),
        P("fsdp", "ctx", None),
        P("fsdp", None),
        P("fsdp", None),
        P("fsdp", None),
        P("fsdp", None),
        P("fsdp", None),
        P("fsdp", None),
        P("fsdp", None),
        P("fsdp"),
        P("fsdp"),
        P("fsdp"),
        P("fsdp"),
    )
    if not divides_heads(mesh):
        return jax.shard_map(
            local, mesh=mesh, in_specs=in_specs, out_specs=out_specs, check_vma=False
        )

    return jax.shard_map(local_heads, mesh=mesh, in_specs=in_specs, out_specs=out_specs, check_vma=False)
```
